32 devices in a mesh: ctx: 16 (over z, x, core), wsh: 2 (over y).
Axes of the slice: x: 2, y: 2, z: 4, core: 2. Of those that a mesh axis runs over, the one named last changes fastest.
Arguments:
- inputs: bfloat16 [2, 4096, 512], P('wsh', 'ctx'), may hold values from -6 to 6
- block_perm: int32 [2, 32], P('wsh'), may hold values from 0 to 31, as said below
- seq_lengths: int32 [2, 8], P('wsh'), may hold values from 1 to 2048, 4096 in all within a row
- loss_mask: int32 [2, 4096], P('wsh', 'ctx'), may hold values from 0 to 1
- teacher: bfloat16 [2, 4096, 512], P('wsh', 'ctx'), may hold values from -4 to 4
- out_grad: bfloat16 [2, 4096, 512], P('wsh', 'ctx'), may hold values from -6 to 6
- gain_one: bfloat16 [512], P('wsh'), may hold values from 0.5 to 1.5
- bias_one: bfloat16 [512], P('wsh'), may hold values from -1.75 to 1.75
- w_query: bfloat16 [512, 512], P('wsh'), may hold values from -0.375 to 0.375
- w_key: bfloat16 [512, 512], P('wsh'), may hold values from -0.375 to 0.375
- w_value: bfloat16 [512, 512], P('wsh'), may hold values from -0.25 to 0.25
- w_output: bfloat16 [512, 512], P('wsh'), may hold values from -1 to 1
- w_pos: bfloat16 [512, 512], P('wsh'), may hold values from -0.25 to 0.25
- content_bias: bfloat16 [512], P('wsh'), may hold values from -3 to 3
- position_bias: bfloat16 [512], P('wsh'), may hold values from -3 to 3
- gain_two: bfloat16 [512], P('wsh'), may hold values from 0.5 to 1.5
- bias_two: bfloat16 [512], P('wsh'), may hold values from -1.75 to 1.75
- w_up: bfloat16 [512, 2048], P('wsh'), may hold values from -0.25 to 0.25
- bias_up: bfloat16 [2048], P('wsh'), may hold values from -1.75 to 1.75
- w_down: bfloat16 [2048, 512], P('wsh'), may hold values from -0.125 to 0.125
- bias_down: bfloat16 [512], P('wsh'), may hold values from -1.75 to 1.75
Outputs:
- output: bfloat16 [2, 4096, 512], P('wsh', 'ctx')
- loss: float32 [], replicated
- grad_input: float32 [2, 4096, 512], P('wsh', 'ctx')
- grad_gain_one: float32 [512], P('wsh')
- grad_bias_one: float32 [512], P('wsh')
- grad_w_query: float32 [512, 512], P('wsh')
- grad_w_key: float32 [512, 512], P('wsh')
- grad_w_value: float32 [512, 512], P('wsh')
- grad_w_output: float32 [512, 512], P('wsh')
- grad_w_pos: float32 [512, 512], P('wsh')
- grad_content_bias: float32 [512], P('wsh')
- grad_position_bias: float32 [512], P('wsh')
- grad_gain_two: float32 [512], P('wsh')
- grad_bias_two: float32 [512], P('wsh')
- grad_w_up: float32 [512, 2048], P('wsh')
- grad_bias_up: float32 [2048], P('wsh')
- grad_w_down: float32 [2048, 512], P('wsh')
- grad_bias_down: float32 [512], P('wsh')
The draws below stay inside these ranges and needn't reach their ends.
Inputs may be any that keep to these rules, and one draw needn't show every extreme that they name: `block_perm`: each group's row is a permutation of 0 to 31 in which slots 2c and 2c + 1 hold blocks b and 31 - b for some b. `seq_lengths`: each group's lengths add up to 4096.
All inputs are finite; a program needn't handle non-finite values.
Results may differ from the reference program's by a relative error of at most 0.028.
Values may be sent and summed in bfloat16 or wider, within the bound.
A program may use at most 384 MiB of HBM per device.

```python
import math
import jax
import jax.numpy as jnp
import numpy as np
from jax import lax

D = 512
HEADS = 8
HEAD = 64
FF = 2048
NSEQ = 8
GROUP_TOKENS = 4096
LONGEST = 2048
GROUPS = 2
BLOCKS = 32


def draw_block_perm(key, part):
    half_count = BLOCKS // 2

    def one_group(group_key):
        order_key, swap_key = jax.random.split(group_key)
        pairing = jax.random.permutation(order_key, half_count).astype(jnp.int32)
        swapped = jax.random.randint(swap_key, (half_count,), 0, 2, dtype=jnp.int32)
        early = pairing
        later = BLOCKS - 1 - pairing
        first_slot = jnp.where(swapped == 1, later, early)
        second_slot = jnp.where(swapped == 1, early, later)
        return jnp.stack([first_slot, second_slot], axis=1).reshape(BLOCKS)
    return jax.vmap(one_group)(jax.random.split(key, GROUPS)).astype(jnp.int32)


def draw_loss_mask(key, part):
    places = jnp.arange(GROUP_TOKENS, dtype=jnp.int32)
    threshold = 250 + 500 * places // (GROUP_TOKENS - 1)
    picks = jax.random.randint(key, (GROUPS, GROUP_TOKENS), 0, 1000, dtype=jnp.int32)
    return (picks < threshold[None, :]).astype(jnp.int32)


def draw_teacher(key, part):
    array_shape = (GROUPS, GROUP_TOKENS, D)
    rising = jnp.arange(GROUP_TOKENS, dtype=jnp.float32).reshape(1, GROUP_TOKENS, 1) / (GROUP_TOKENS - 1)
    return jnp.clip(jax.random.normal(key, array_shape, jnp.float32) * (0.3 + 2.7 * rising), -4.0, 4.0).astype(jnp.bfloat16)


def steps_of(own_key, extent, pieces, least, top_value):
    level, own = 1.0, jax.random.fold_in(own_key, 6)
    for dim, shards_of in pieces:
        steps = jnp.exp(jax.random.uniform(jax.random.fold_in(own, dim), (shards_of,), jnp.float32, least / len(pieces), top_value / len(pieces)))
        level = level * jnp.repeat(steps, extent[dim] // shards_of).reshape([-1 if axis == dim else 1 for axis in range(len(extent))])
    return level


def length_profile(amount, total, reach, skew):
    portions = [(1 << 20) // math.isqrt(standing ** skew) + 1 for standing in range(2, amount + 1)]
    spare, counts = total - reach - (amount - 1), [1] * (amount - 1)
    while spare > 0:
        candidates = [i for i in range(amount - 1) if counts[i] < reach]
        pool, budget = sum([portions[i] for i in candidates]), spare
        for i in candidates:
            more = min(reach - counts[i], max(1, budget * portions[i] // pool), spare)
            counts[i] = counts[i] + more
            spare = spare - more
    return np.array([reach] + counts)


def uneven(stream_key, number_of, total, bound, lean):
    if number_of == 2:
        one = jax.random.randint(stream_key, (), max(1, total - bound), min(bound, total - 1) + 1)
        return jnp.stack([one, total - one])
    sizes = jnp.asarray(length_profile(number_of, total, bound, lean), jnp.int32)
    twos = (number_of - 1) // 2
    donor, sink = sizes[1:1 + 2 * twos:2], sizes[2:2 + 2 * twos:2]
    slack = jnp.minimum(donor - 1, bound - sink)
    shifted = jax.random.randint(jax.random.fold_in(stream_key, 1), (twos,), 0, 1 << 20) % (slack + 1)
    sizes = sizes.at[1:1 + 2 * twos:2].set(donor - shifted).at[2:2 + 2 * twos:2].set(sink + shifted)
    return sizes[jax.random.permutation(jax.random.fold_in(stream_key, 2), number_of)]


def bell_draw(own_key, extent, scale, reach, cuts=(), kind=jnp.bfloat16):
    values = scale * jax.random.normal(own_key, extent, jnp.float32)
    if cuts:
        values = values * steps_of(own_key, extent, cuts, -0.22, 0.18)
    return jnp.clip(values, -reach, reach).astype(kind)


def setup_inputs(seed: int = 0) -> dict:
    key_of = jax.random.split(jax.random.key(seed), 22)
    inputs = bell_draw(key_of[0], (GROUPS, GROUP_TOKENS, D), 1.0, 6.0, ((0, 2), (1, 16)))
    block_perm = draw_block_perm(jax.random.fold_in(key_of[21], 71), 0)
    seq_lengths = jax.vmap(lambda own: uneven(own, NSEQ, GROUP_TOKENS, LONGEST, 2))(jax.random.split(key_of[2], GROUPS)).reshape((GROUPS, NSEQ)).astype(jnp.int32)
    loss_mask = draw_loss_mask(jax.random.fold_in(key_of[21], 71), 0)
    teacher = draw_teacher(jax.random.fold_in(key_of[21], 71), 0)
    out_grad = bell_draw(key_of[5], (GROUPS, GROUP_TOKENS, D), 1.0, 6.0, ((0, 2), (1, 16)))
    gain_one = jnp.clip(1.0 + 0.1 * jax.random.normal(key_of[6], (D,), jnp.float32), 0.5, 1.5).astype(jnp.bfloat16)
    bias_one = bell_draw(key_of[7], (D,), 0.3, 1.75, ((0, 2),))
    w_query = bell_draw(key_of[8], (D, D), (D // 2) ** -0.5, 0.375, ((0, 2),))
    w_key = bell_draw(key_of[9], (D, D), (D // 2) ** -0.5, 0.375, ((0, 2),))
    w_value = bell_draw(key_of[10], (D, D), D ** -0.5, 0.25, ((0, 2),))
    w_output = bell_draw(key_of[11], (D, D), 32 ** -0.5, 1.0, ((0, 2),))
    w_pos = bell_draw(key_of[12], (D, D), D ** -0.5, 0.25, ((0, 2),))
    content_bias = bell_draw(key_of[13], (D,), 0.5, 3.0, ((0, 2),))
    position_bias = bell_draw(key_of[14], (D,), 0.5, 3.0, ((0, 2),))
    gain_two = jnp.clip(1.0 + 0.1 * jax.random.normal(key_of[15], (D,), jnp.float32), 0.5, 1.5).astype(jnp.bfloat16)
    bias_two = bell_draw(key_of[16], (D,), 0.3, 1.75, ((0, 2),))
    w_up = bell_draw(key_of[17], (D, FF), D ** -0.5, 0.25, ((0, 2),))
    bias_up = bell_draw(key_of[18], (FF,), 0.3, 1.75, ((0, 2),))
    w_down = bell_draw(key_of[19], (FF, D), FF ** -0.5, 0.125, ((0, 2),))
    bias_down = bell_draw(key_of[20], (D,), 0.3, 1.75, ((0, 2),))
    return {"inputs": inputs, "block_perm": block_perm, "seq_lengths": seq_lengths, "loss_mask": loss_mask, "teacher": teacher, "out_grad": out_grad, "gain_one": gain_one, "bias_one": bias_one, "w_query": w_query, "w_key": w_key, "w_value": w_value, "w_output": w_output, "w_pos": w_pos, "content_bias": content_bias, "position_bias": position_bias, "gain_two": gain_two, "bias_two": bias_two, "w_up": w_up, "bias_up": bias_up, "w_down": w_down, "bias_down": bias_down}


epsilon = 1e-05
highest = lax.Precision.HIGHEST
masked_score = -1e+30

@jax.custom_vjp
def low(v):
    return lax.optimization_barrier(v.astype(jnp.bfloat16)).astype(jnp.float32)

@jax.custom_vjp
def low_back(v):
    return v

def low_keep(v):
    return (low(v), None)

def low_pass(kept, grad):
    return (grad,)

def back_keep(v):
    return (v, None)

def back_low(kept, grad):
    return (low(grad),)
low.defvjp(low_keep, low_pass)
low_back.defvjp(back_keep, back_low)

def product(left_side, right_side):
    return jnp.dot(left_side, right_side, precision=highest, preferred_element_type=jnp.float32)

def sinus_table(distance, width):
    halves = width // 2
    frequency = jnp.exp(jnp.arange(halves, dtype=jnp.float32) * (-2.0 * math.log(10000.0) / width))
    angles = distance.astype(jnp.float32)[:, None] * frequency[None, :]
    return jnp.concatenate([jnp.sin(angles), jnp.cos(angles)], axis=1)

def layer_norm(values, gain, offset_bias):
    center = values - lax.optimization_barrier(jnp.mean(values, axis=-1, keepdims=True))
    spread = lax.optimization_barrier(jnp.mean(center * center, axis=-1, keepdims=True))
    return center * lax.rsqrt(spread + epsilon) * gain + offset_bias

def attend(queries, keys, values, pos_keys, key_term, pos_term, position, segment):
    group_rows = queries.shape[0]
    block_rows = min(512, group_rows)
    scale = HEAD ** (-0.5)

    def one_block(start):
        rows_query = lax.dynamic_slice_in_dim(queries, start, block_rows, 0)
        rows_pos = lax.dynamic_slice_in_dim(position, start, block_rows, 0)
        rows_seg = lax.dynamic_slice_in_dim(segment, start, block_rows, 0)
        distance = rows_pos[:, None] - position[None, :]
        valid = (distance >= 0) & (rows_seg[:, None] == segment[None, :])
        lookup = jnp.broadcast_to(jnp.clip(distance, 0, LONGEST - 1)[None], (HEADS, block_rows, group_rows)).astype(jnp.int32)
        content = jnp.einsum('ihe,jhe->hij', rows_query, keys, precision=highest)
        along = jnp.einsum('ihe,dhe->hid', rows_query, pos_keys, precision=highest) + pos_term[:, None, :]
        relative = jnp.take_along_axis(along, lookup, axis=2)
        scores = low_back(scale * (content + relative + key_term[:, None, :]))
        scores = jnp.where(valid[None], scores, masked_score)
        top = lax.optimization_barrier(jnp.max(scores, axis=2, keepdims=True))
        weights_exp = jnp.where(valid[None], jnp.exp(scores - top), 0.0)
        probs = weights_exp / lax.optimization_barrier(jnp.sum(weights_exp, axis=2, keepdims=True))
        return jnp.einsum('hij,jhe->ihe', low(probs), values, precision=highest)
    starts = jnp.arange(group_rows // block_rows, dtype=jnp.int32) * block_rows
    mixed = lax.map(jax.checkpoint(one_block), starts)
    return mixed.reshape(group_rows, HEADS * HEAD)

def group_layer(layer_in, teacher_rows, mask_row, lengths, perm_row, weights):
    gain_one, bias_one, w_query, w_key, w_value, w_output, w_pos, content_bias, position_bias, gain_two, bias_two, w_up, bias_up, w_down, bias_down = weights
    group_rows = layer_in.shape[0]
    block_rows = group_rows // perm_row.shape[0]
    slots = jnp.arange(group_rows, dtype=jnp.int32)
    position = (perm_row[slots // block_rows] * block_rows + slots % block_rows).astype(jnp.int32)
    ends = jnp.cumsum(lengths).astype(jnp.int32)
    segment = lax.optimization_barrier(jnp.sum((position[:, None] >= ends[None, :]).astype(jnp.int32), axis=1))
    normed_one = low(layer_norm(layer_in, gain_one, bias_one))
    queries = low(low_back(product(normed_one, w_query))).reshape(group_rows, HEADS, HEAD)
    keys = low(low_back(product(normed_one, w_key))).reshape(group_rows, HEADS, HEAD)
    values = low(low_back(product(normed_one, w_value))).reshape(group_rows, HEADS, HEAD)
    table = low(sinus_table(jnp.arange(LONGEST, dtype=jnp.int32), D))
    pos_keys = low(product(table, w_pos)).reshape(LONGEST, HEADS, HEAD)
    key_term = jnp.einsum('jhe,he->hj', keys, content_bias.reshape(HEADS, HEAD), precision=highest)
    pos_term = jnp.einsum('dhe,he->hd', pos_keys, position_bias.reshape(HEADS, HEAD), precision=highest)
    mixed = low(low_back(attend(queries, keys, values, pos_keys, key_term, pos_term, position, segment)))
    hidden_one = layer_in + low_back(product(mixed, w_output))
    normed_two = low(layer_norm(hidden_one, gain_two, bias_two))
    pre_act = low_back(product(normed_two, w_up) + bias_up)
    activated = low(jax.nn.gelu(pre_act, approximate=True))
    result = hidden_one + low_back(product(activated, w_down) + bias_down)
    error = result - teacher_rows
    return (result, jnp.sum(mask_row[:, None] * error * error))

def reference(inputs, block_perm, seq_lengths, loss_mask, teacher, out_grad, gain_one, bias_one, w_query, w_key, w_value, w_output, w_pos, content_bias, position_bias, gain_two, bias_two, w_up, bias_up, w_down, bias_down):
    params = tuple((item.astype(jnp.float32) for item in (gain_one, bias_one, w_query, w_key, w_value, w_output, w_pos, content_bias, position_bias, gain_two, bias_two, w_up, bias_up, w_down, bias_down)))
    inputs_wide = inputs.astype(jnp.float32)
    teacher_wide = teacher.astype(jnp.float32)
    mask_wide = loss_mask.astype(jnp.float32)
    count = jnp.sum(mask_wide)

    def whole(layer_in, weights):

        def per_group(items):
            return group_layer(items[0], items[1], items[2], items[3], items[4], weights)
        results, squares = lax.map(jax.checkpoint(per_group), (layer_in, teacher_wide, mask_wide, seq_lengths, block_perm))
        return (results, jnp.sum(squares) / (count * D))
    (result, loss), pullback = jax.vjp(whole, inputs_wide, params)
    grad_input, grads = pullback((out_grad.astype(jnp.float32), jnp.ones((), jnp.float32)))
    return (result.astype(jnp.bfloat16), loss, grad_input, grads[0], grads[1], grads[2], grads[3], grads[4], grads[5], grads[6], grads[7], grads[8], grads[9], grads[10], grads[11], grads[12], grads[13], grads[14])
```

```python
import functools
import math

import jax
import jax.numpy as jnp
from jax import lax
from jax.experimental import pallas as pl
from jax.experimental.pallas import tpu as pltpu
from jax.sharding import PartitionSpec as P

HEADS = 8
HEAD = 64
PAIRS = HEADS // 2
BLK = 128
ROWS = HEADS * BLK
NEG = -1e30
epsilon = 1e-05
F32 = jnp.float32
BF16 = jnp.bfloat16


def dot_nt(a, b):
    return lax.dot_general(a, b, (((1,), (1,)), ((), ())), preferred_element_type=F32)


def dot_nn(a, b):
    return lax.dot_general(a, b, (((1,), (0,)), ((), ())), preferred_element_type=F32)


def iotas():
    row = lax.broadcasted_iota(jnp.int32, (BLK, BLK), 0)
    col = lax.broadcasted_iota(jnp.int32, (BLK, BLK), 1)
    return row, col


def block_range(meta, a, blocks, limit):
    qb = meta[a]
    first = qb * BLK
    low = jnp.int32(0)
    for e in range(meta.shape[0] - 2 - blocks):
        end = meta[2 + blocks + e]
        low = jnp.where(first >= end, jnp.maximum(low, end), low)
    lowest = low // BLK
    return qb, lowest, jnp.minimum(qb - lowest + 1, limit)


def stack_heads(pair):
    lane = lax.broadcasted_iota(jnp.int32, pair.shape, 1)
    zero = jnp.zeros_like(pair)
    return jnp.concatenate([jnp.where(lane < HEAD, pair, zero), jnp.where(lane >= HEAD, pair, zero)], axis=0)


def flip_rows(x):
    index = 7 - lax.broadcasted_iota(jnp.int32, (8, BLK), 0)
    slabs = [jnp.take_along_axis(x[8 * g : 8 * g + 8], index, axis=0) for g in reversed(range(BLK // 8))]
    return jnp.concatenate(slabs, axis=0)


def flip_two(x):
    return jnp.concatenate([flip_rows(x[:BLK]), flip_rows(x[BLK:])], axis=0)


def attn_fwd_kernel(
    blocks, limit, meta, qc_ref, qp_ref, k_ref, v_ref, pk_ref, mixed_ref, linv_ref, p_ref,
    q2c, q2p, prev, top, total, acc, s_scr, p_buf, p_sem,
):
    row, col = iotas()
    tri = col <= row

    def p_copy(slot, index):
        return pltpu.make_async_copy(p_buf.at[slot], p_ref.at[index], p_sem.at[slot])

    def one_query_block(a, _):
        qb, lowest, count = block_range(meta, a, blocks, limit)
        rows_a = pl.ds(pl.multiple_of(a * BLK, BLK), BLK)
        pos = qb * BLK + row
        start = jnp.zeros((BLK, BLK), jnp.int32)
        for e in range(meta.shape[0] - 2 - blocks):
            end = meta[2 + blocks + e]
            start = jnp.where(pos >= end, jnp.maximum(start, end), start)
        for hp in range(PAIRS):
            lanes = slice(hp * BLK, (hp + 1) * BLK)
            q2c[hp] = stack_heads(qc_ref[rows_a, lanes].astype(F32)).astype(BF16)
            q2p[hp] = stack_heads(qp_ref[rows_a, lanes].astype(F32)).astype(BF16)
        prev[...] = jnp.zeros_like(prev)
        top[...] = jnp.full_like(top, NEG)
        total[...] = jnp.zeros_like(total)
        acc[...] = jnp.zeros_like(acc)

        def score_step(d, _):
            kb = qb - d
            off = pl.multiple_of(meta[2 + kb] * BLK, BLK)
            place = kb * BLK + col
            bias = jnp.where((place >= start) & (place <= pos), 0.0, NEG).astype(F32)
            drow = pl.multiple_of(d * BLK, BLK)
            for hp in range(PAIRS):
                lanes = slice(hp * BLK, (hp + 1) * BLK)
                s = dot_nt(q2c[hp], k_ref[pl.ds(off, BLK), lanes])
                r = dot_nt(q2p[hp], pk_ref[pl.ds(drow, BLK), lanes])
                for half in range(2):
                    part = slice(half * BLK, (half + 1) * BLK)
                    rows = slice((2 * hp + half) * BLK, (2 * hp + half + 1) * BLK)
                    rot = pltpu.roll(r[part], 1, 1, stride=1, stride_axis=0)
                    score = s[part] + jnp.where(tri, rot, prev[rows]) + bias
                    prev[rows] = rot
                    s_scr[d, rows] = score
                    top[rows] = jnp.maximum(top[rows], score)
            return 0

        lax.fori_loop(0, count, score_step, 0)
        for h in range(HEADS):
            rows = slice(h * BLK, (h + 1) * BLK)
            top[rows] = jnp.broadcast_to(jnp.max(top[rows], axis=1, keepdims=True), (BLK, BLK))

        def mix_step(d, _):
            kb = qb - d
            off = pl.multiple_of(meta[2 + kb] * BLK, BLK)
            slot = lax.rem(d, 2)

            @pl.when(d >= 2)
            def _():
                p_copy(slot, 0).wait()

            for hp in range(PAIRS):
                lanes = slice(hp * BLK, (hp + 1) * BLK)
                rows = slice(2 * hp * BLK, 2 * (hp + 1) * BLK)
                p = jnp.exp(s_scr[d, rows] - top[rows])
                total[rows] += p
                p_buf[slot, rows] = flip_two(p).astype(BF16)
                acc[hp] += dot_nn(p.astype(BF16), v_ref[pl.ds(off, BLK), lanes])
            p_copy(slot, a * limit + d).start()
            return 0

        lax.fori_loop(0, count, mix_step, 0)
        p_copy(lax.rem(count - 1, 2), 0).wait()

        @pl.when(count >= 2)
        def _():
            p_copy(lax.rem(count, 2), 0).wait()

        lane = lax.broadcasted_iota(jnp.int32, (BLK, BLK), 1)
        for hp in range(PAIRS):
            lanes = slice(hp * BLK, (hp + 1) * BLK)
            parts = []
            for half in range(2):
                h = 2 * hp + half
                rows = slice(h * BLK, (h + 1) * BLK)
                inv = 1.0 / jnp.sum(total[rows], axis=1, keepdims=True)
                inv = jnp.broadcast_to(inv, (BLK, BLK))
                linv_ref[a, rows] = inv
                parts.append(acc[hp, half * BLK : (half + 1) * BLK] * inv)
            mixed_ref[rows_a, lanes] = jnp.where(lane < HEAD, parts[0], parts[1])
        return 0

    lax.fori_loop(0, 2, one_query_block, 0)


def attn_fwd(meta, qc, qp, k, v, pk, blocks, limit):
    tokens, width = qc.shape
    vmem = pl.BlockSpec(memory_space=pltpu.VMEM)
    return pl.pallas_call(
        functools.partial(attn_fwd_kernel, blocks, limit),
        out_shape=(
            jax.ShapeDtypeStruct((tokens, width), F32),
            jax.ShapeDtypeStruct((2, ROWS, BLK), F32),
            jax.ShapeDtypeStruct((2 * limit, ROWS, BLK), BF16),
        ),
        in_specs=[pl.BlockSpec(memory_space=pltpu.SMEM)] + [vmem] * 5,
        out_specs=(vmem, vmem, pl.BlockSpec(memory_space=pl.ANY)),
        scratch_shapes=[
            pltpu.VMEM((PAIRS, 2 * BLK, BLK), BF16),
            pltpu.VMEM((PAIRS, 2 * BLK, BLK), BF16),
            pltpu.VMEM((ROWS, BLK), F32),
            pltpu.VMEM((ROWS, BLK), F32),
            pltpu.VMEM((ROWS, BLK), F32),
            pltpu.VMEM((PAIRS, 2 * BLK, BLK), F32),
            pltpu.VMEM((limit, ROWS, BLK), F32),
            pltpu.VMEM((2, ROWS, BLK), BF16),
            pltpu.SemaphoreType.DMA((2,)),
        ],
        compiler_params=pltpu.CompilerParams(vmem_limit_bytes=56 * 2**20),
        cost_estimate=pl.CostEstimate(flops=3 * 10**9, bytes_accessed=20 * 2**20, transcendentals=4 * 10**6),
        name="attn_fwd",
    )(meta, qc, qp, k, v, pk)


def attn_bwd_kernel(
    blocks, limit, meta, qc_ref, qp_ref, k_ref, v_ref, pk_ref, p_ref, linv_ref, gm_ref, mixed_ref,
    dq_ref, bias_ref, dk_ref, dv_ref, dpk_ref,
    q2c_t, q2p_t, gm2, gm2_t, dd, carry, dqk, dqp, dpk, p_buf, p_sem,
):
    row, col = iotas()
    tri = col <= BLK - 1 - row
    dk_ref[...] = jnp.zeros_like(dk_ref)
    dv_ref[...] = jnp.zeros_like(dv_ref)
    dpk[...] = jnp.zeros_like(dpk)
    bias_ref[...] = jnp.zeros_like(bias_ref)

    def p_copy(slot, index):
        return pltpu.make_async_copy(p_ref.at[index], p_buf.at[slot], p_sem.at[slot])

    def one_query_block(a, _):
        qb, lowest, count = block_range(meta, a, blocks, limit)
        rows_a = pl.ds(pl.multiple_of(a * BLK, BLK), BLK)
        p_copy(0, a * limit + count - 1).start()
        for hp in range(PAIRS):
            lanes = slice(hp * BLK, (hp + 1) * BLK)
            rows = slice(2 * hp * BLK, 2 * (hp + 1) * BLK)
            q2c_t[hp] = stack_heads(flip_rows(qc_ref[rows_a, lanes].astype(F32))).T.astype(BF16)
            q2p_t[hp] = stack_heads(flip_rows(qp_ref[rows_a, lanes].astype(F32))).T.astype(BF16)
            g = stack_heads(gm_ref[rows_a, lanes].astype(F32))
            scaled = flip_two(g * linv_ref[a, rows])
            gm2[hp] = scaled.astype(BF16)
            gm2_t[hp] = scaled.T.astype(BF16)
            pair = flip_rows(mixed_ref[rows_a, lanes])
            dd[rows] = jnp.broadcast_to(
                jnp.sum(scaled * jnp.concatenate([pair, pair], axis=0), axis=1, keepdims=True), (2 * BLK, BLK)
            )
        carry[...] = jnp.zeros_like(carry)
        dqk[...] = jnp.zeros_like(dqk)
        dqp[...] = jnp.zeros_like(dqp)

        def step(t, _):
            d = count - 1 - t
            kb = qb - d
            off = pl.multiple_of(meta[2 + kb] * BLK, BLK)
            keys = pl.ds(off, BLK)
            drow = pl.ds(pl.multiple_of(d * BLK, BLK), BLK)
            slot = lax.rem(t, 2)
            p_copy(slot, 0).wait()

            @pl.when(d >= 1)
            def _():
                p_copy(1 - slot, a * limit + d - 1).start()

            for hp in range(PAIRS):
                lanes = slice(hp * BLK, (hp + 1) * BLK)
                rows = slice(2 * hp * BLK, 2 * (hp + 1) * BLK)
                p = p_buf[slot, rows]
                g = dot_nt(gm2[hp], v_ref[keys, lanes])
                gs = p.astype(F32) * (g - dd[rows])
                gs_low = gs.astype(BF16)
                gs = gs_low.astype(F32)
                rots = []
                for half in range(2):
                    part = slice(half * BLK, (half + 1) * BLK)
                    crow = slice((2 * hp + half) * BLK, (2 * hp + half + 1) * BLK)
                    both = jnp.where(tri, gs[part], carry[crow])
                    carry[crow] = gs[part]
                    rots.append(pltpu.roll(both, 0, 1, stride=1, stride_axis=0))
                rot = jnp.concatenate(rots, axis=0).astype(BF16)
                dqk[hp] += dot_nn(gs_low, k_ref[keys, lanes])
                dqp[hp] += dot_nn(rot, pk_ref[drow, lanes])
                dk_ref[lanes, keys] = (dk_ref[lanes, keys].astype(F32) + dot_nn(q2c_t[hp], gs_low)).astype(BF16)
                dv_ref[lanes, keys] = (dv_ref[lanes, keys].astype(F32) + dot_nn(gm2_t[hp], p)).astype(BF16)
                dpk[lanes, drow] += dot_nn(q2p_t[hp], rot)
            return 0

        lax.fori_loop(0, count, step, 0)
        lane = lax.broadcasted_iota(jnp.int32, (BLK, BLK), 1)
        for hp in range(PAIRS):
            lanes = slice(hp * BLK, (hp + 1) * BLK)
            ck = jnp.where(lane < HEAD, dqk[hp, :BLK], dqk[hp, BLK:]) * 0.125
            cp = jnp.where(lane < HEAD, dqp[hp, :BLK], dqp[hp, BLK:]) * 0.125
            dq_ref[rows_a, lanes] = flip_rows(ck + cp).astype(BF16)
            bias_ref[0:1, lanes] += jnp.sum(ck, axis=0, keepdims=True)
            bias_ref[1:2, lanes] += jnp.sum(cp, axis=0, keepdims=True)
        return 0

    lax.fori_loop(0, 2, one_query_block, 0)
    dpk_ref[...] = dpk[...].astype(BF16)


def attn_bwd(meta, qc, qp, k, v, pk, p, linv, gm, mixed, blocks, limit):
    tokens, width = qc.shape
    keys = k.shape[0]
    span = pk.shape[0]
    vmem = pl.BlockSpec(memory_space=pltpu.VMEM)
    return pl.pallas_call(
        functools.partial(attn_bwd_kernel, blocks, limit),
        out_shape=(
            jax.ShapeDtypeStruct((tokens, width), BF16),
            jax.ShapeDtypeStruct((8, width), F32),
            jax.ShapeDtypeStruct((width, keys), BF16),
            jax.ShapeDtypeStruct((width, keys), BF16),
            jax.ShapeDtypeStruct((width, span), BF16),
        ),
        in_specs=[pl.BlockSpec(memory_space=pltpu.SMEM)]
        + [vmem] * 5
        + [pl.BlockSpec(memory_space=pl.ANY)]
        + [vmem] * 3,
        out_specs=(vmem,) * 5,
        scratch_shapes=[
            pltpu.VMEM((PAIRS, BLK, 2 * BLK), BF16),
            pltpu.VMEM((PAIRS, BLK, 2 * BLK), BF16),
            pltpu.VMEM((PAIRS, 2 * BLK, BLK), BF16),
            pltpu.VMEM((PAIRS, BLK, 2 * BLK), BF16),
            pltpu.VMEM((ROWS, BLK), F32),
            pltpu.VMEM((ROWS, BLK), F32),
            pltpu.VMEM((PAIRS, 2 * BLK, BLK), F32),
            pltpu.VMEM((PAIRS, 2 * BLK, BLK), F32),
            pltpu.VMEM((width, span), F32),
            pltpu.VMEM((2, ROWS, BLK), BF16),
            pltpu.SemaphoreType.DMA((2,)),
        ],
        compiler_params=pltpu.CompilerParams(vmem_limit_bytes=60 * 2**20),
        cost_estimate=pl.CostEstimate(flops=6 * 10**9, bytes_accessed=30 * 2**20, transcendentals=0),
        name="attn_bwd",
    )(meta, qc, qp, k, v, pk, p, linv, gm, mixed)


def sinus_rows(distance, width):
    halves = width // 2
    frequency = jnp.exp(jnp.arange(halves, dtype=F32) * (-2.0 * math.log(10000.0) / width))
    angles = distance.astype(F32)[:, None] * frequency[None, :]
    return jnp.concatenate([jnp.sin(angles), jnp.cos(angles)], axis=1)


def norm_forward(values, gain, offset_bias):
    center = values - jnp.mean(values, axis=1, keepdims=True)
    inverse = lax.rsqrt(jnp.mean(center * center, axis=1, keepdims=True) + epsilon)
    unit_rows = center * inverse
    return (unit_rows * gain + offset_bias, unit_rows, inverse)


def norm_backward(grad_out, unit_rows, inverse, gain):
    scaled = grad_out * gain
    grad_in = inverse * (
        scaled
        - jnp.mean(scaled, axis=1, keepdims=True)
        - unit_rows * jnp.mean(scaled * unit_rows, axis=1, keepdims=True)
    )
    return (grad_in, jnp.sum(grad_out * unit_rows, axis=0), jnp.sum(grad_out, axis=0))


def gelu_tanh(values):
    return jax.nn.gelu(values, approximate=True)


def product(left_side, right_side):
    return jnp.dot(left_side, right_side, preferred_element_type=F32)


def transposed_times(left_side, right_side):
    return lax.dot_general(left_side, right_side, (((0,), (0,)), ((), ())), preferred_element_type=F32)


def body(
    inputs, block_perm, seq_lengths, loss_mask, teacher, out_grad, gain_one, bias_one, w_query, w_key, w_value,
    w_output, w_pos, content_bias, position_bias, gain_two, bias_two, w_up, bias_up, w_down, bias_down,
):
    def whole(part):
        return lax.all_gather(part, "wsh", axis=0, tiled=True)

    tokens, width = inputs.shape[1:]
    shards = lax.axis_size("wsh")
    members = lax.axis_size("ctx")
    hidden = bias_up.shape[0] * shards
    perm_row = block_perm[0]
    blocks = perm_row.shape[0]
    group_rows = blocks * BLK
    limit = group_rows // 2 // BLK + 1
    span = limit * BLK
    device = lax.axis_index("ctx")

    x_all = lax.all_gather(inputs[0], "ctx", axis=0, tiled=True)
    attn_w = whole(jnp.concatenate([w_query, w_key, w_value, w_pos], axis=1))
    w_q, w_k, w_v, w_p = (attn_w[:, i * width : (i + 1) * width] for i in range(4))
    vector_sizes = [width] * 7 + [hidden]
    vectors = (gain_one, bias_one, content_bias, position_bias, gain_two, bias_two, bias_down, bias_up)
    packed = lax.all_gather(jnp.concatenate(vectors), "wsh", axis=0).astype(F32)
    full = []
    begin = 0
    for size in vector_sizes:
        part = size // shards
        full.append(packed[:, begin : begin + part].reshape(size))
        begin += part
    g1, b1, cb, pb, g2, b2, b_down, b_up = full
    w_o, w_u, w_d = whole(w_output), whole(w_up), whole(w_down)

    inverse_perm = jnp.sum(
        jnp.where(perm_row[None, :] == jnp.arange(blocks, dtype=jnp.int32)[:, None], jnp.arange(blocks, dtype=jnp.int32), 0),
        axis=1,
    )
    own_blocks = lax.dynamic_slice_in_dim(perm_row, 2 * device, 2, 0)
    meta = jnp.concatenate([own_blocks, inverse_perm, jnp.cumsum(seq_lengths[0])]).astype(jnp.int32)

    normed_all = norm_forward(x_all.astype(F32), g1, b1)[0].astype(BF16)
    rows_in = inputs[0].astype(F32)
    normed, unit_one, inverse_one = norm_forward(rows_in, g1, b1)
    normed_low = normed.astype(BF16)
    keys = product(normed_all, w_k).astype(BF16)
    values = product(normed_all, w_v).astype(BF16)
    queries = product(normed_low, w_q).astype(BF16).astype(F32)
    qc = ((queries + cb) * 0.125).astype(BF16)
    qp = ((queries + pb) * 0.125).astype(BF16)
    order = jnp.arange(span, dtype=jnp.int32)
    table = sinus_rows((order // BLK) * BLK + BLK - 1 - order % BLK, width).astype(BF16)
    pos_keys = product(table, w_p).astype(BF16)

    mixed, linv, probs = attn_fwd(meta, qc, qp, keys, values, pos_keys, blocks, limit)

    mixed_low = mixed.astype(BF16)
    hidden_one = rows_in + product(mixed_low, w_o)
    normed_two, unit_two, inverse_two = norm_forward(hidden_one, g2, b2)
    normed_two_low = normed_two.astype(BF16)
    pre_act = product(normed_two_low, w_u) + b_up
    activated, gelu_pull = jax.vjp(gelu_tanh, pre_act)
    activated_low = activated.astype(BF16)
    result = hidden_one + (product(activated_low, w_d) + b_down)
    mask_rows = loss_mask[0].astype(F32)
    error = result - teacher[0].astype(F32)
    count = lax.psum(jnp.sum(mask_rows), ("ctx", "wsh"))
    square_sum = lax.psum(jnp.sum(mask_rows[:, None] * error * error), ("ctx", "wsh"))
    loss = square_sum / (count * width)
    grad_result = out_grad[0].astype(F32) + 2.0 / (count * width) * mask_rows[:, None] * error
    branch_low = grad_result.astype(BF16)
    grad_down_bias = jnp.sum(branch_low.astype(F32), axis=0)
    grad_down = transposed_times(activated_low, branch_low)
    grad_pre = gelu_pull(dot_nt(branch_low, w_d))[0].astype(BF16)
    grad_up_bias = jnp.sum(grad_pre.astype(F32), axis=0)
    grad_up = transposed_times(normed_two_low, grad_pre)
    grad_norm_two, grad_second_gain, grad_second_bias = norm_backward(dot_nt(grad_pre, w_u), unit_two, inverse_two, g2)
    grad_hidden = grad_result + grad_norm_two
    attn_low = grad_hidden.astype(BF16)
    grad_output = transposed_times(mixed_low, attn_low)
    grad_mixed = dot_nt(attn_low, w_o).astype(BF16)

    early = jnp.concatenate(
        [
            grad_up.astype(BF16).reshape(shards, -1, hidden // width, width).transpose(0, 2, 1, 3).reshape(shards, -1, width),
            grad_down.astype(BF16).reshape(shards, -1, width),
            grad_output.astype(BF16).reshape(shards, -1, width),
        ],
        axis=1,
    )
    rows_up = hidden // shards
    rows_out = width // shards
    early = lax.psum_scatter(early, "wsh", scatter_dimension=0, tiled=True)[0]
    early = lax.psum_scatter(early, "ctx", scatter_dimension=0, tiled=True)
    early = lax.all_gather(early, "ctx", axis=0, tiled=True).astype(F32)
    total_up = early[:rows_up].reshape(hidden // width, rows_out, width).transpose(1, 0, 2).reshape(rows_out, hidden)
    total_down = early[rows_up : 2 * rows_up]
    total_output = early[2 * rows_up :]

    grad_query, bias_grads, dk_t, dv_t, dpk_t = attn_bwd(
        meta, qc, qp, keys, values, pos_keys, probs, linv, grad_mixed, mixed, blocks, limit
    )
    grad_normed_part = lax.dot_general(dk_t, w_k, (((0,), (1,)), ((), ())), preferred_element_type=F32) + lax.dot_general(
        dv_t, w_v, (((0,), (1,)), ((), ())), preferred_element_type=F32
    )
    grad_normed = lax.psum_scatter(grad_normed_part.astype(BF16), "ctx", scatter_dimension=0, tiled=True).astype(F32)
    grad_normed = grad_normed + dot_nt(grad_query, w_q)
    late = jnp.stack(
        [
            transposed_times(normed_low, grad_query),
            lax.dot_general(normed_all, dk_t, (((0,), (1,)), ((), ())), preferred_element_type=F32),
            lax.dot_general(normed_all, dv_t, (((0,), (1,)), ((), ())), preferred_element_type=F32),
            lax.dot_general(table, dpk_t, (((0,), (1,)), ((), ())), preferred_element_type=F32),
        ]
    ).astype(BF16)
    late = late.reshape(4, shards, rows_out, width).transpose(1, 0, 2, 3).reshape(shards, 4 * rows_out, width)
    late = lax.psum_scatter(late, "wsh", scatter_dimension=0, tiled=True)[0]
    late = lax.psum(late, "ctx").astype(F32).reshape(4, rows_out, width)

    grad_rows, grad_first_gain, grad_first_bias = norm_backward(grad_normed, unit_one, inverse_one, g1)
    grad_input = grad_hidden + grad_rows
    vector_grads = (
        grad_first_gain, grad_first_bias, bias_grads[0], bias_grads[1], grad_second_gain, grad_second_bias,
        grad_down_bias, grad_up_bias,
    )
    packed = jnp.concatenate([v.reshape(shards, -1) for v in vector_grads], axis=1)
    packed = lax.psum(packed, ("ctx", "wsh"))
    own = lax.dynamic_index_in_dim(packed, lax.axis_index("wsh"), 0, keepdims=False)
    vectors_out = []
    begin = 0
    for size in vector_sizes:
        part = size // shards
        vectors_out.append(own[begin : begin + part])
        begin += part
    v_g1, v_b1, v_cb, v_pb, v_g2, v_b2, v_bd, v_bu = vectors_out
    return (
        result.astype(BF16)[None], loss, grad_input[None], v_g1, v_b1, late[0], late[1], late[2], total_output, late[3],
        v_cb, v_pb, v_g2, v_b2, total_up, v_bu, total_down, v_bd,
    )


def solution(mesh):
    rows = P("wsh", "ctx", None)
    vector = P("wsh")
    matrix = P("wsh", None)
    placed = (
        rows, matrix, matrix, P("wsh", "ctx"), rows, rows, vector, vector, matrix, matrix, matrix, matrix, matrix,
        vector, vector, vector, vector, matrix, vector, matrix, vector,
    )
    out = (
        rows, P(), rows, vector, vector, matrix, matrix, matrix, matrix, matrix, vector, vector, vector, vector,
        matrix, vector, matrix, vector,
    )
    return jax.shard_map(body, mesh=mesh, in_specs=placed, out_specs=out, check_vma=False)
```

```python
import functools
import math

import jax
import jax.numpy as jnp
from jax import lax
from jax.experimental import pallas as pl
from jax.experimental.pallas import tpu as pltpu
from jax.sharding import PartitionSpec as P

HEADS = 8
HEAD = 64
PAIRS = HEADS // 2
BLK = 128
ROWS = HEADS * BLK
NEG = -1e30
epsilon = 1e-05
F32 = jnp.float32
BF16 = jnp.bfloat16


def dot_nt(a, b):
    return lax.dot_general(a, b, (((1,), (1,)), ((), ())), preferred_element_type=F32)


def dot_nn(a, b):
    return lax.dot_general(a, b, (((1,), (0,)), ((), ())), preferred_element_type=F32)


def dot_tn(a, b):
    return lax.dot_general(a, b, (((0,), (0,)), ((), ())), preferred_element_type=F32)


def iotas():
    row = lax.broadcasted_iota(jnp.int32, (BLK, BLK), 0)
    col = lax.broadcasted_iota(jnp.int32, (BLK, BLK), 1)
    return row, col


def block_range(meta, a, blocks, limit):
    qb = meta[a]
    first = qb * BLK
    low = jnp.int32(0)
    for e in range(meta.shape[0] - 2 - blocks):
        end = meta[2 + blocks + e]
        low = jnp.where(first >= end, jnp.maximum(low, end), low)
    lowest = low // BLK
    return qb, lowest, jnp.minimum(qb - lowest + 1, limit)


def stack_heads(pair):
    lane = lax.broadcasted_iota(jnp.int32, pair.shape, 1)
    zero = jnp.zeros_like(pair)
    return jnp.concatenate([jnp.where(lane < HEAD, pair, zero), jnp.where(lane >= HEAD, pair, zero)], axis=0)


def flip_rows(x):
    index = 7 - lax.broadcasted_iota(jnp.int32, (8, BLK), 0)
    slabs = [jnp.take_along_axis(x[8 * g : 8 * g + 8], index, axis=0) for g in reversed(range(BLK // 8))]
    return jnp.concatenate(slabs, axis=0)


def flip_two(x):
    return jnp.concatenate([flip_rows(x[:BLK]), flip_rows(x[BLK:])], axis=0)


def attn_fwd_kernel(
    blocks, limit, meta, qc_ref, qp_ref, k_ref, v_ref, pk_ref, mixed_ref, linv_ref, p_ref,
    q2c, q2p, prev, top, total, acc, s_scr, p_buf, p_sem,
):
    row, col = iotas()
    tri = col <= row

    def p_copy(slot, index):
        return pltpu.make_async_copy(p_buf.at[slot], p_ref.at[index], p_sem.at[slot])

    def one_query_block(a, _):
        qb, lowest, count = block_range(meta, a, blocks, limit)
        rows_a = pl.ds(pl.multiple_of(a * BLK, BLK), BLK)
        pos = qb * BLK + row
        start = jnp.zeros((BLK, BLK), jnp.int32)
        for e in range(meta.shape[0] - 2 - blocks):
            end = meta[2 + blocks + e]
            start = jnp.where(pos >= end, jnp.maximum(start, end), start)
        for hp in range(PAIRS):
            lanes = slice(hp * BLK, (hp + 1) * BLK)
            q2c[hp] = stack_heads(qc_ref[rows_a, lanes].astype(F32)).astype(BF16)
            q2p[hp] = stack_heads(qp_ref[rows_a, lanes].astype(F32)).astype(BF16)
        prev[...] = jnp.zeros_like(prev)
        top[...] = jnp.full_like(top, NEG)
        total[...] = jnp.zeros_like(total)
        acc[...] = jnp.zeros_like(acc)

        def score_step(d, _):
            kb = qb - d
            off = pl.multiple_of(meta[2 + kb] * BLK, BLK)
            place = kb * BLK + col
            bias = jnp.where((place >= start) & (place <= pos), 0.0, NEG).astype(F32)
            drow = pl.multiple_of(d * BLK, BLK)
            for hp in range(PAIRS):
                lanes = slice(hp * BLK, (hp + 1) * BLK)
                s = dot_nt(q2c[hp], k_ref[pl.ds(off, BLK), lanes])
                r = dot_nt(q2p[hp], pk_ref[pl.ds(drow, BLK), lanes])
                for half in range(2):
                    part = slice(half * BLK, (half + 1) * BLK)
                    rows = slice((2 * hp + half) * BLK, (2 * hp + half + 1) * BLK)
                    rot = pltpu.roll(r[part], 1, 1, stride=1, stride_axis=0)
                    score = s[part] + jnp.where(tri, rot, prev[rows]) + bias
                    prev[rows] = rot
                    s_scr[d, rows] = score
                    top[rows] = jnp.maximum(top[rows], score)
            return 0

        lax.fori_loop(0, count, score_step, 0)
        for h in range(HEADS):
            rows = slice(h * BLK, (h + 1) * BLK)
            top[rows] = jnp.broadcast_to(jnp.max(top[rows], axis=1, keepdims=True), (BLK, BLK))

        def mix_step(d, _):
            kb = qb - d
            off = pl.multiple_of(meta[2 + kb] * BLK, BLK)
            slot = lax.rem(d, 2)

            @pl.when(d >= 2)
            def _():
                p_copy(slot, 0).wait()

            for hp in range(PAIRS):
                lanes = slice(hp * BLK, (hp + 1) * BLK)
                rows = slice(2 * hp * BLK, 2 * (hp + 1) * BLK)
                p = jnp.exp(s_scr[d, rows] - top[rows])
                total[rows] += p
                p_buf[slot, rows] = flip_two(p).astype(BF16)
                acc[hp] += dot_nn(p.astype(BF16), v_ref[pl.ds(off, BLK), lanes])
            p_copy(slot, a * limit + d).start()
            return 0

        lax.fori_loop(0, count, mix_step, 0)
        p_copy(lax.rem(count - 1, 2), 0).wait()

        @pl.when(count >= 2)
        def _():
            p_copy(lax.rem(count, 2), 0).wait()

        lane = lax.broadcasted_iota(jnp.int32, (BLK, BLK), 1)
        for hp in range(PAIRS):
            lanes = slice(hp * BLK, (hp + 1) * BLK)
            parts = []
            for half in range(2):
                h = 2 * hp + half
                rows = slice(h * BLK, (h + 1) * BLK)
                inv = 1.0 / jnp.sum(total[rows], axis=1, keepdims=True)
                inv = jnp.broadcast_to(inv, (BLK, BLK))
                linv_ref[a, rows] = inv
                parts.append(acc[hp, half * BLK : (half + 1) * BLK] * inv)
            mixed_ref[rows_a, lanes] = jnp.where(lane < HEAD, parts[0], parts[1])
        return 0

    lax.fori_loop(0, 2, one_query_block, 0)


def attn_fwd(meta, qc, qp, k, v, pk, blocks, limit):
    tokens, width = qc.shape
    vmem = pl.BlockSpec(memory_space=pltpu.VMEM)
    return pl.pallas_call(
        functools.partial(attn_fwd_kernel, blocks, limit),
        out_shape=(
            jax.ShapeDtypeStruct((tokens, width), F32),
            jax.ShapeDtypeStruct((2, ROWS, BLK), F32),
            jax.ShapeDtypeStruct((2 * limit, ROWS, BLK), BF16),
        ),
        in_specs=[pl.BlockSpec(memory_space=pltpu.SMEM)] + [vmem] * 5,
        out_specs=(vmem, vmem, pl.BlockSpec(memory_space=pl.ANY)),
        scratch_shapes=[
            pltpu.VMEM((PAIRS, 2 * BLK, BLK), BF16),
            pltpu.VMEM((PAIRS, 2 * BLK, BLK), BF16),
            pltpu.VMEM((ROWS, BLK), F32),
            pltpu.VMEM((ROWS, BLK), F32),
            pltpu.VMEM((ROWS, BLK), F32),
            pltpu.VMEM((PAIRS, 2 * BLK, BLK), F32),
            pltpu.VMEM((limit, ROWS, BLK), F32),
            pltpu.VMEM((2, ROWS, BLK), BF16),
            pltpu.SemaphoreType.DMA((2,)),
        ],
        compiler_params=pltpu.CompilerParams(vmem_limit_bytes=56 * 2**20),
        cost_estimate=pl.CostEstimate(flops=3 * 10**9, bytes_accessed=20 * 2**20, transcendentals=4 * 10**6),
        name="attn_fwd",
    )(meta, qc, qp, k, v, pk)


def attn_bwd_kernel(
    blocks, limit, meta, qc_ref, qp_ref, k_ref, v_ref, pk_ref, p_ref, linv_ref, gm_ref, mixed_ref,
    dq_ref, bias_ref, dk_ref, dv_ref, dpk_ref,
    q2c_t, q2p_t, gm2, gm2_t, dd, carry, dqk, dqp, dpk, p_buf, p_sem,
):
    row, col = iotas()
    tri = col <= BLK - 1 - row
    dk_ref[...] = jnp.zeros_like(dk_ref)
    dv_ref[...] = jnp.zeros_like(dv_ref)
    dpk[...] = jnp.zeros_like(dpk)
    bias_ref[...] = jnp.zeros_like(bias_ref)

    def p_copy(slot, index):
        return pltpu.make_async_copy(p_ref.at[index], p_buf.at[slot], p_sem.at[slot])

    def one_query_block(a, _):
        qb, lowest, count = block_range(meta, a, blocks, limit)
        rows_a = pl.ds(pl.multiple_of(a * BLK, BLK), BLK)
        p_copy(0, a * limit + count - 1).start()
        for hp in range(PAIRS):
            lanes = slice(hp * BLK, (hp + 1) * BLK)
            rows = slice(2 * hp * BLK, 2 * (hp + 1) * BLK)
            q2c_t[hp] = stack_heads(flip_rows(qc_ref[rows_a, lanes].astype(F32))).T.astype(BF16)
            q2p_t[hp] = stack_heads(flip_rows(qp_ref[rows_a, lanes].astype(F32))).T.astype(BF16)
            g = stack_heads(gm_ref[rows_a, lanes].astype(F32))
            scaled = flip_two(g * linv_ref[a, rows])
            gm2[hp] = scaled.astype(BF16)
            gm2_t[hp] = scaled.T.astype(BF16)
            pair = flip_rows(mixed_ref[rows_a, lanes])
            dd[rows] = jnp.broadcast_to(
                jnp.sum(scaled * jnp.concatenate([pair, pair], axis=0), axis=1, keepdims=True), (2 * BLK, BLK)
            )
        carry[...] = jnp.zeros_like(carry)
        dqk[...] = jnp.zeros_like(dqk)
        dqp[...] = jnp.zeros_like(dqp)

        def step(t, _):
            d = count - 1 - t
            kb = qb - d
            off = pl.multiple_of(meta[2 + kb] * BLK, BLK)
            keys = pl.ds(off, BLK)
            drow = pl.ds(pl.multiple_of(d * BLK, BLK), BLK)
            slot = lax.rem(t, 2)
            p_copy(slot, 0).wait()

            @pl.when(d >= 1)
            def _():
                p_copy(1 - slot, a * limit + d - 1).start()

            for hp in range(PAIRS):
                lanes = slice(hp * BLK, (hp + 1) * BLK)
                rows = slice(2 * hp * BLK, 2 * (hp + 1) * BLK)
                p = p_buf[slot, rows]
                g = dot_nt(gm2[hp], v_ref[keys, lanes])
                gs = p.astype(F32) * (g - dd[rows])
                gs_low = gs.astype(BF16)
                gs = gs_low.astype(F32)
                rots = []
                for half in range(2):
                    part = slice(half * BLK, (half + 1) * BLK)
                    crow = slice((2 * hp + half) * BLK, (2 * hp + half + 1) * BLK)
                    both = jnp.where(tri, gs[part], carry[crow])
                    carry[crow] = gs[part]
                    rots.append(pltpu.roll(both, 0, 1, stride=1, stride_axis=0))
                rot = jnp.concatenate(rots, axis=0).astype(BF16)
                dqk[hp] += dot_nn(gs_low, k_ref[keys, lanes])
                dqp[hp] += dot_nn(rot, pk_ref[drow, lanes])
                dk_ref[lanes, keys] = (dk_ref[lanes, keys].astype(F32) + dot_nn(q2c_t[hp], gs_low)).astype(BF16)
                dv_ref[lanes, keys] = (dv_ref[lanes, keys].astype(F32) + dot_nn(gm2_t[hp], p)).astype(BF16)
                dpk[lanes, drow] += dot_nn(q2p_t[hp], rot)
            return 0

        lax.fori_loop(0, count, step, 0)
        lane = lax.broadcasted_iota(jnp.int32, (BLK, BLK), 1)
        for hp in range(PAIRS):
            lanes = slice(hp * BLK, (hp + 1) * BLK)
            ck = jnp.where(lane < HEAD, dqk[hp, :BLK], dqk[hp, BLK:]) * 0.125
            cp = jnp.where(lane < HEAD, dqp[hp, :BLK], dqp[hp, BLK:]) * 0.125
            dq_ref[rows_a, lanes] = flip_rows(ck + cp).astype(BF16)
            bias_ref[0:1, lanes] += jnp.sum(ck, axis=0, keepdims=True)
            bias_ref[1:2, lanes] += jnp.sum(cp, axis=0, keepdims=True)
        return 0

    lax.fori_loop(0, 2, one_query_block, 0)
    dpk_ref[...] = dpk[...].astype(BF16)


def attn_bwd(meta, qc, qp, k, v, pk, p, linv, gm, mixed, blocks, limit):
    tokens, width = qc.shape
    keys = k.shape[0]
    span = pk.shape[0]
    vmem = pl.BlockSpec(memory_space=pltpu.VMEM)
    return pl.pallas_call(
        functools.partial(attn_bwd_kernel, blocks, limit),
        out_shape=(
            jax.ShapeDtypeStruct((tokens, width), BF16),
            jax.ShapeDtypeStruct((8, width), F32),
            jax.ShapeDtypeStruct((width, keys), BF16),
            jax.ShapeDtypeStruct((width, keys), BF16),
            jax.ShapeDtypeStruct((width, span), BF16),
        ),
        in_specs=[pl.BlockSpec(memory_space=pltpu.SMEM)]
        + [vmem] * 5
        + [pl.BlockSpec(memory_space=pl.ANY)]
        + [vmem] * 3,
        out_specs=(vmem,) * 5,
        scratch_shapes=[
            pltpu.VMEM((PAIRS, BLK, 2 * BLK), BF16),
            pltpu.VMEM((PAIRS, BLK, 2 * BLK), BF16),
            pltpu.VMEM((PAIRS, 2 * BLK, BLK), BF16),
            pltpu.VMEM((PAIRS, BLK, 2 * BLK), BF16),
            pltpu.VMEM((ROWS, BLK), F32),
            pltpu.VMEM((ROWS, BLK), F32),
            pltpu.VMEM((PAIRS, 2 * BLK, BLK), F32),
            pltpu.VMEM((PAIRS, 2 * BLK, BLK), F32),
            pltpu.VMEM((width, span), F32),
            pltpu.VMEM((2, ROWS, BLK), BF16),
            pltpu.SemaphoreType.DMA((2,)),
        ],
        compiler_params=pltpu.CompilerParams(vmem_limit_bytes=60 * 2**20),
        cost_estimate=pl.CostEstimate(flops=6 * 10**9, bytes_accessed=30 * 2**20, transcendentals=0),
        name="attn_bwd",
    )(meta, qc, qp, k, v, pk, p, linv, gm, mixed)


MESH = pl.DeviceIdType.MESH


def fold_rows(x):
    return jnp.broadcast_to(x, (x.shape[0], BLK)).T[0:1]


def aligned(begin, size):
    return pl.ds(pl.multiple_of(begin, math.gcd(size, 16)), size)


def finish_kernel(
    lines, shards, rows_f, rows_l,
    gf_ref, dk_ref, dv_ref, unit_all_ref, dpk_ref, table_ref, weights_ref, dq_ref, x_ref,
    vectors_ref, cols_ref, vec_ref, bias_ref, hidden_ref,
    grad_ref, total_ref, vsum_ref,
    dk_buf, dv_buf, un_buf, in_sem, gl_src, mt_k, mt_v, cs_k, cs_v, dxp, bx0, bx1, bx2, vbuf, vacc,
    *rest,
):
    groups = rest[: 4 * (len(rows_f) + 1)]
    send_sem, recv_sem = rest[4 * (len(rows_f) + 1) :]
    wk_ref, wv_ref, wq_ref = weights_ref.at[0], weights_ref.at[1], weights_ref.at[3]
    tokens, width = dq_ref.shape
    ctx = lax.axis_index("ctx")
    w = lax.axis_index("wsh")
    core = lax.rem(ctx, 2)
    b = lax.rem(ctx // 2, 2)
    a = ctx // 4

    def at(a_to, b_to, core_to):
        return (a_to * 2 + b_to) * 2 + core_to

    def line_peer(s):
        return (at(lax.rem(a + s, lines), b, core), w)

    def shard_peer(s):
        return (ctx, lax.rem(w + s, shards))

    core_peer = (at(a, b, 1 - core), w)
    b_peer = (at(a, 1 - b, core), w)
    peers = [core_peer, b_peer] + [line_peer(s) for s in range(1, lines)] + [shard_peer(s) for s in range(1, shards)]

    barrier = pltpu.get_barrier_semaphore()
    for peer in peers:
        pl.semaphore_signal(barrier, inc=1, device_id=peer, device_id_type=MESH)

    counter = [0]

    def take(number):
        begin = counter[0]
        counter[0] += number
        return begin

    def remote(src, dst, index, peer):
        return pltpu.make_async_remote_copy(
            src_ref=src, dst_ref=dst, send_sem=send_sem.at[index], recv_sem=recv_sem.at[index],
            device_id=peer, device_id_type=MESH,
        )

    def fetch(j, q, slot):
        a_to = lax.rem(a + 1 + j, lines)
        b_to = b if q % 2 == 1 else 1 - b
        core_to = core if q >= 2 else 1 - core
        begin = pl.multiple_of(at(a_to, b_to, core_to) * tokens, tokens)
        return (
            pltpu.make_async_copy(dk_ref.at[:, pl.ds(begin, tokens)], dk_buf.at[slot], in_sem.at[slot, 0]),
            pltpu.make_async_copy(dv_ref.at[:, pl.ds(begin, tokens)], dv_buf.at[slot], in_sem.at[slot, 1]),
            pltpu.make_async_copy(unit_all_ref.at[pl.ds(begin, tokens)], un_buf.at[slot], in_sem.at[slot, 2]),
        )

    for q in range(2):
        for copy in fetch(0, q, q):
            copy.start()
    pl.semaphore_wait(barrier, len(peers))

    class Group:
        def __init__(self, src, begin, rows, out_begin, bufs):
            self.src, self.begin, self.rows, self.out = src, begin, rows, out_begin
            self.b0, self.b1, self.b2, self.b3 = bufs
            self.rc, self.rb, self.ra = rows // 2, rows // 4, rows // 4 // lines
            self.pending = []

        def s0(self):
            copy = remote(
                self.src.at[:, aligned(self.begin + (1 - core) * self.rc, self.rc)], self.b0, take(1), core_peer
            )
            copy.start()
            self.pending = [copy]

        def done(self):
            for copy in self.pending:
                copy.wait()

        def s1(self):
            self.done()
            mine = self.src[:, aligned(self.begin + core * self.rc, self.rc)]
            self.b0[...] = (self.b0[...].astype(F32) + mine.astype(F32)).astype(BF16)
            first = take(shards - 1)
            self.pending = []
            for s in range(1, shards):
                copy = remote(self.b0.at[lax.rem(w + s, shards)], self.b1.at[s - 1], first + s - 1, shard_peer(s))
                copy.start()
                self.pending.append(copy)

        def s2(self):
            self.done()
            total = self.b0[w].astype(F32)
            for s in range(shards - 1):
                total = total + self.b1[s].astype(F32)
            self.b1[0] = total.astype(BF16)
            copy = remote(self.b1.at[0, aligned((1 - b) * self.rb, self.rb)], self.b2, take(1), b_peer)
            copy.start()
            self.pending = [copy]

        def s3(self):
            self.done()
            self.b2[...] = (self.b2[...].astype(F32) + self.b1[0, aligned(b * self.rb, self.rb)].astype(F32)).astype(BF16)
            first = take(lines - 1)
            self.pending = []
            for s in range(1, lines):
                share = aligned(lax.rem(a + s, lines) * self.ra, self.ra)
                copy = remote(self.b2.at[share], self.b3.at[s - 1], first + s - 1, line_peer(s))
                copy.start()
                self.pending.append(copy)

        def s4(self):
            self.done()
            total = self.b2[aligned(a * self.ra, self.ra)].astype(F32)
            for s in range(lines - 1):
                total = total + self.b3[s].astype(F32)
            own = aligned(self.out + core * self.rc + b * self.rb + a * self.ra, self.ra)
            total_ref[own] = total.astype(BF16)
            first = take(lines - 1)
            self.pending = []
            for s in range(1, lines):
                copy = remote(total_ref.at[own], total_ref.at[own], first + s - 1, line_peer(s))
                copy.start()
                self.pending.append(copy)

        def s5(self):
            self.done()
            own = aligned(self.out + core * self.rc + b * self.rb, self.rb)
            copy = remote(total_ref.at[own], total_ref.at[own], take(1), b_peer)
            copy.start()
            self.pending = [copy]

        def s6(self):
            self.done()
            own = aligned(self.out + core * self.rc, self.rc)
            copy = remote(total_ref.at[own], total_ref.at[own], take(1), core_peer)
            copy.start()
            self.pending = [copy]

    parts = []
    begin = 0
    for index, rows in enumerate(rows_f):
        parts.append(Group(gf_ref, begin, rows, begin, groups[4 * index : 4 * index + 4]))
        begin += rows
    late = Group(gl_src, 0, rows_l, begin, groups[4 * len(rows_f) :])

    for part in parts:
        part.s0()
    for part in parts:
        part.s1()

    mt_k[...] = jnp.zeros_like(mt_k)
    mt_v[...] = jnp.zeros_like(mt_v)
    cs_k[...] = jnp.zeros_like(cs_k)
    cs_v[...] = jnp.zeros_like(cs_v)
    x0, x1, x2 = take(lines), take(lines), take(lines - 1)

    def copy_x0(j):
        return remote(dxp.at[j, pl.ds(0, 2)], bx0.at[j], x0 + j, core_peer)

    def copy_x1(j):
        return remote(bx0.at[j, 0], bx1.at[j], x1 + j, b_peer)

    def copy_x2(j):
        return remote(bx1.at[j], bx2.at[j], x2 + j, (at(lax.rem(a + 1 + j, lines), b, core), w))

    def after_x0(j):
        copy_x0(j).wait()
        bx0[j] = (bx0[j].astype(F32) + dxp[j, 2:4].astype(F32)).astype(BF16)
        copy_x1(j).start()

    def after_x1(j):
        copy_x1(j).wait()
        bx1[j] = (bx1[j].astype(F32) + bx0[j, 1].astype(F32)).astype(BF16)

        @pl.when(j < lines - 1)
        def _():
            copy_x2(j).start()

    def line_step(j, _):
        for q in range(4):
            slot = q % 2
            for copy in fetch(j, q, slot):
                copy.wait()
            dk, dv, un = dk_buf[slot], dv_buf[slot], un_buf[slot]
            dxp[j, q] = (dot_nn(wk_ref[...], dk) + dot_nn(wv_ref[...], dv)).astype(BF16)
            mt_k[...] += dot_nn(dk, un)
            mt_v[...] += dot_nn(dv, un)
            for half in range(tokens // BLK):
                cs_k[...] += dk[:, half * BLK : (half + 1) * BLK].astype(F32)
                cs_v[...] += dv[:, half * BLK : (half + 1) * BLK].astype(F32)
            if q < 2:
                for copy in fetch(j, q + 2, slot):
                    copy.start()
            else:

                @pl.when(j < lines - 1)
                def _():
                    for copy in fetch(j + 1, q - 2, slot):
                        copy.start()

            if q == 1:
                copy_x0(j).start()

        @pl.when(j >= 1)
        def _():
            after_x0(j - 1)

        @pl.when(j >= 2)
        def _():
            after_x1(j - 2)

        return 0

    lax.fori_loop(0, lines, line_step, 0)

    dq = dq_ref[...]
    values = x_ref[...].astype(F32)
    center = values - jnp.mean(values, axis=1, keepdims=True)
    inverse = lax.rsqrt(jnp.mean(center * center, axis=1, keepdims=True) + epsilon)
    unit = center * inverse
    unit_low = unit.astype(BF16)
    m_q = lax.dot_general(unit_low, dq, (((0,), (0,)), ((), ())), preferred_element_type=F32)
    csq = jnp.sum(dq.astype(F32), axis=0, keepdims=True)
    csk_col = jnp.sum(cs_k[...], axis=1, keepdims=True)
    csv_col = jnp.sum(cs_v[...], axis=1, keepdims=True)
    csk, csv = fold_rows(csk_col), fold_rows(csv_col)
    m_k, m_v = mt_k[...].T, mt_v[...].T
    gain_col, bias_col = cols_ref[:, 0:1], cols_ref[:, 1:2]
    rows_out = width // shards
    for m, grad in enumerate(
        (
            gain_col * m_q + bias_col * csq,
            gain_col * m_k + bias_col * csk,
            gain_col * m_v + bias_col * csv,
            dot_nn(dpk_ref[...], table_ref[...]).T,
        )
    ):
        for s in range(shards):
            gl_src[s, m * rows_out : (m + 1) * rows_out] = grad[s * rows_out : (s + 1) * rows_out].astype(BF16)
    used = 4 * rows_out
    if used < rows_l:
        gl_src[:, used:] = jnp.zeros((shards, rows_l - used, width), BF16)
    late.s0()
    gain_grad = m_q * wq_ref[...].astype(F32) + m_k * wk_ref[...].astype(F32) + m_v * wv_ref[...].astype(F32)
    vacc[0:16] = vec_ref[...]
    vacc[2:4] = bias_ref[0:2]
    vacc[0:1] = fold_rows(jnp.sum(gain_grad, axis=1, keepdims=True))
    sums = [jnp.broadcast_to(x, (8, width)).astype(BF16) for x in (csq, csk, csv)]
    vacc[1:2] = (dot_nt(sums[0], wq_ref[...]) + dot_nt(sums[1], wk_ref[...]) + dot_nt(sums[2], wv_ref[...]))[0:1]

    vstages = [[core_peer], [b_peer], [line_peer(s) for s in range(1, lines)], [shard_peer(s) for s in range(1, shards)]]
    vslots = []
    place = 0
    for stage in vstages:
        vslots.append(place)
        place += len(stage)
    vbegin = take(place)

    def v_copy(stage, index):
        slot = vslots[stage] + index
        return remote(vacc.at[pl.ds(stage * 16, 16)], vbuf.at[slot], vbegin + slot, vstages[stage][index])

    def v_start(stage):
        for index in range(len(vstages[stage])):
            v_copy(stage, index).start()

    def v_finish(stage):
        total = vacc[stage * 16 : stage * 16 + 16]
        for index in range(len(vstages[stage])):
            v_copy(stage, index).wait()
            total = total + vbuf[vslots[stage] + index]
        vacc[(stage + 1) * 16 : (stage + 2) * 16] = total

    v_start(0)
    late.s1()
    after_x0(lines - 1)
    after_x1(lines - 2)
    v_finish(0)
    v_start(1)
    parts[0].s2()
    after_x1(lines - 1)
    for part in parts[1:]:
        part.s2()
    v_finish(1)
    v_start(2)
    parts[0].s3()
    late.s2()
    for part in parts[1:]:
        part.s3()
    own = bx1[lines - 1].astype(F32)
    for j in range(lines - 1):
        copy_x2(j).wait()
        own = own + bx2[j].astype(F32)
    e = own.T + dot_nt(dq, wq_ref[...])
    scaled = e * vectors_ref[0:1]
    grad_ref[...] = hidden_ref[...] + inverse * (
        scaled
        - jnp.mean(scaled, axis=1, keepdims=True)
        - unit * jnp.mean(scaled * unit, axis=1, keepdims=True)
    )
    v_finish(2)
    v_start(3)
    parts[0].s4()
    late.s3()
    for part in parts[1:]:
        part.s4()
    parts[0].s5()
    late.s4()
    for part in parts[1:]:
        part.s5()
    parts[0].s6()
    late.s5()
    for part in parts[1:]:
        part.s6()
    late.s6()
    v_finish(3)
    vsum_ref[...] = vacc[4 * 16 : 5 * 16]
    for part in parts:
        part.done()
    late.done()


def finish(lines, shards, rows_f, rows_l, cid, gf, dk, dv, unit_all, dpk, table, weights, dq, x, vectors, cols, vec, bias, hidden):
    tokens, width = dq.shape
    vmem = pl.BlockSpec(memory_space=pltpu.VMEM)
    hbm = pl.BlockSpec(memory_space=pl.ANY)
    group_bufs = []
    for rows in tuple(rows_f) + (rows_l,):
        rc, rb = rows // 2, rows // 4
        group_bufs += [
            pltpu.VMEM((shards, rc, width), BF16),
            pltpu.VMEM((shards - 1, rc, width), BF16),
            pltpu.VMEM((rb, width), BF16),
            pltpu.VMEM((lines - 1, rb // lines, width), BF16),
        ]
    copies = (len(rows_f) + 1) * (shards + 2 * lines + 1) + 3 * lines + 2 + lines + shards
    total_rows = sum(rows_f) + rows_l
    stages = 1 + 1 + (lines - 1) + (shards - 1)
    return pl.pallas_call(
        functools.partial(finish_kernel, lines, shards, tuple(rows_f), rows_l),
        out_shape=(
            jax.ShapeDtypeStruct((tokens, width), F32),
            jax.ShapeDtypeStruct((total_rows, width), BF16),
            jax.ShapeDtypeStruct((16, width), F32),
        ),
        in_specs=[vmem] + [hbm] * 3 + [vmem] * 10,
        out_specs=(vmem,) * 3,
        scratch_shapes=[
            pltpu.VMEM((2, width, tokens), BF16),
            pltpu.VMEM((2, width, tokens), BF16),
            pltpu.VMEM((2, tokens, width), BF16),
            pltpu.SemaphoreType.DMA((2, 3)),
            pltpu.VMEM((shards, rows_l, width), BF16),
            pltpu.VMEM((width, width), F32),
            pltpu.VMEM((width, width), F32),
            pltpu.VMEM((width, BLK), F32),
            pltpu.VMEM((width, BLK), F32),
            pltpu.VMEM((lines, 4, width, tokens), BF16),
            pltpu.VMEM((lines, 2, width, tokens), BF16),
            pltpu.VMEM((lines, width, tokens), BF16),
            pltpu.VMEM((lines - 1, width, tokens), BF16),
            pltpu.VMEM((stages, 16, width), F32),
            pltpu.VMEM((5 * 16, width), F32),
        ]
        + group_bufs
        + [pltpu.SemaphoreType.DMA((copies,)), pltpu.SemaphoreType.DMA((copies,))],
        compiler_params=pltpu.CompilerParams(
            collective_id=cid, has_side_effects=True, vmem_limit_bytes=63 * 2**20
        ),
        cost_estimate=pl.CostEstimate(flops=10**10, bytes_accessed=30 * 2**20, transcendentals=0),
        name="finish",
    )(
        gf, dk, dv, unit_all, dpk, table, weights, dq, x, vectors, cols, vec, bias, hidden
    )


def start_kernel(
    lines, shards, x_ref, wq_ref, wk_ref, wv_ref, wp_ref, vec_ref, count_ref, far_ref, near_ref,
    k_ref, v_ref, unit_ref, pk_ref, table_ref, qc_ref, qp_ref, weights_ref, vectors_ref, total_ref,
    x_all, k_buf, v_buf, u_buf, pk_buf, t_buf, vec_buf, cnt_buf, cnt_acc,
    up_send, up_recv, down_send, down_recv, b_send, b_recv, c_send, c_recv,
    y_send, y_recv, yc_send, yc_recv, s_send, s_recv, out_sem, pos_sem,
):
    tokens, width = x_ref.shape
    half = width // 2
    chunks = pk_buf.shape[0] // BLK
    ctx = lax.axis_index("ctx")
    w = lax.axis_index("wsh")
    core = lax.rem(ctx, 2)
    b = lax.rem(ctx // 2, 2)
    a = ctx // 4

    def at(a_to, b_to, core_to):
        return (a_to * 2 + b_to) * 2 + core_to

    def shard_peer(s):
        return (ctx, lax.rem(w + s, shards))

    def line_peer(s):
        return (at(lax.rem(a + s, lines), b, core), w)

    core_peer = (at(a, b, 1 - core), w)
    b_peer = (at(a, 1 - b, core), w)
    peers = [core_peer, b_peer] + [line_peer(s) for s in range(1, lines)] + [shard_peer(s) for s in range(1, shards)]
    barrier = pltpu.get_barrier_semaphore()
    for peer in peers:
        pl.semaphore_signal(barrier, inc=1, device_id=peer, device_id_type=MESH)

    def remote(src, dst, send, recv, peer):
        return pltpu.make_async_remote_copy(
            src_ref=src, dst_ref=dst, send_sem=send, recv_sem=recv, device_id=peer, device_id_type=MESH
        )

    def block(slot):
        return aligned(slot * tokens, tokens)

    x_all[block(ctx)] = x_ref[...]
    rows_out = wq_ref.shape[0]
    quarter = rows_out // 2
    shard_refs = (wk_ref, wv_ref, wp_ref, wq_ref)
    for m, ref in enumerate(shard_refs):
        weights_ref[m, aligned(w * rows_out, rows_out)] = ref[...]
    pl.semaphore_wait(barrier, len(peers))

    def x_copy(slot, send, recv, peer):
        return remote(x_all.at[block(slot)], x_all.at[block(slot)], send, recv, peer)

    def up_copy(p):
        return x_copy(at(p, b, core), up_send.at[p], up_recv.at[p], (at(jnp.minimum(a + 1, lines - 1), b, core), w))

    def down_copy(p):
        return x_copy(at(p, b, core), down_send.at[p], down_recv.at[p], (at(jnp.maximum(a - 1, 0), b, core), w))

    def b_copy(p, b_from):
        return x_copy(at(p, b_from, core), b_send.at[p], b_recv.at[p], b_peer)

    def c_copy(p, far, b_from, core_from):
        return x_copy(at(p, b_from, core_from), c_send.at[far, p], c_recv.at[far, p], core_peer)

    def weight_copy(m, s):
        rows = aligned(w * rows_out + core * quarter, quarter)
        return remote(
            weights_ref.at[m, rows], weights_ref.at[m, rows], y_send.at[m, s - 1], y_recv.at[m, s - 1], shard_peer(s)
        )

    def weight_pass(m, s):
        rows = aligned(lax.rem(w + shards - s, shards) * rows_out + core * quarter, quarter)
        return remote(
            weights_ref.at[m, rows], weights_ref.at[m, rows], yc_send.at[m, s - 1], yc_recv.at[m, s - 1], core_peer
        )

    def vec_copy(s):
        return remote(vec_ref, vec_buf.at[s - 1], s_send.at[s - 1], s_recv.at[s - 1], shard_peer(s))

    @pl.when(a + 1 < lines)
    def _():
        up_copy(a).start()

    @pl.when(a >= 1)
    def _():
        down_copy(a).start()

    b_copy(a, b).start()
    c_copy(a, 0, b, core).start()
    for s in range(1, shards):
        vec_copy(s).start()
    for m in range(4):
        for s in range(1, shards):
            weight_copy(m, s).start()

    stages = [[core_peer], [b_peer], [line_peer(s) for s in range(1, lines)], [shard_peer(s) for s in range(1, shards)]]
    slots = []
    place = 0
    for stage in stages:
        slots.append(place)
        place += len(stage)
    cnt_acc[0:8] = count_ref[...]

    def cnt_copy(stage, index):
        slot = slots[stage] + index
        sem = shards - 1 + slot
        return remote(cnt_acc.at[pl.ds(stage * 8, 8)], cnt_buf.at[slot], s_send.at[sem], s_recv.at[sem], stages[stage][index])

    def cnt_start(stage):
        for index in range(len(stages[stage])):
            cnt_copy(stage, index).start()

    def cnt_finish(stage):
        total = cnt_acc[stage * 8 : stage * 8 + 8]
        for index in range(len(stages[stage])):
            cnt_copy(stage, index).wait()
            total = total + cnt_buf[slots[stage] + index]
        cnt_acc[(stage + 1) * 8 : (stage + 2) * 8] = total

    cnt_start(0)

    def table_step(d, _):
        sin_far, cos_far = far_ref[0, pl.ds(d, 1)], far_ref[1, pl.ds(d, 1)]
        sin_near, cos_near = near_ref[0], near_ref[1]
        rows = aligned(d * BLK, BLK)
        t_buf[rows, :half] = (sin_far * cos_near - cos_far * sin_near).astype(BF16)
        t_buf[rows, half:] = (cos_far * cos_near + sin_far * sin_near).astype(BF16)
        return 0

    lax.fori_loop(0, chunks, table_step, 0)
    table_out = pltpu.make_async_copy(t_buf, table_ref, pos_sem.at[0])
    table_out.start()
    cnt_finish(0)
    cnt_start(1)
    vectors = vec_ref[...]
    for s in range(1, shards):
        vec_copy(s).wait()
        vectors = vectors + vec_buf[s - 1]
    vectors_ref[...] = vectors
    gain, offset = vectors_ref[0:1], vectors_ref[1:2]
    cnt_finish(1)
    cnt_start(2)
    for m in range(2):
        for s in range(1, shards):
            weight_copy(m, s).wait()
            weight_pass(m, s).start()
    for m in range(2):
        for s in range(1, shards):
            weight_pass(m, s).wait()

    def unit_of(rows):
        values = rows.astype(F32)
        center = values - jnp.mean(values, axis=1, keepdims=True)
        return center * lax.rsqrt(jnp.mean(center * center, axis=1, keepdims=True) + epsilon)

    def out_copies(slot):
        rows = block(slot)
        return (
            pltpu.make_async_copy(k_buf.at[rows], k_ref.at[rows], out_sem.at[0, slot]),
            pltpu.make_async_copy(v_buf.at[rows], v_ref.at[rows], out_sem.at[1, slot]),
            pltpu.make_async_copy(u_buf.at[rows], unit_ref.at[rows], out_sem.at[2, slot]),
        )

    def project(p):
        def one(q, _):
            other_b = lax.rem(q, 2)
            other_core = q // 2

            @pl.when(q == 1)
            def _():
                b_copy(p, b).wait()
                c_copy(p, 1, 1 - b, core).start()

            @pl.when(q == 2)
            def _():
                c_copy(p, 0, b, core).wait()

            @pl.when(q == 3)
            def _():
                c_copy(p, 1, 1 - b, core).wait()

            slot = at(p, b + other_b - 2 * b * other_b, core + other_core - 2 * core * other_core)
            rows = block(slot)
            unit = unit_of(x_all[rows])
            u_buf[rows] = unit.astype(BF16)
            normed = (unit * gain + offset).astype(BF16)
            k_buf[rows] = dot_nn(normed, weights_ref[0]).astype(BF16)
            v_buf[rows] = dot_nn(normed, weights_ref[1]).astype(BF16)
            for copy in out_copies(slot):
                copy.start()
            return 0

        lax.fori_loop(0, 4, one, 0)

    def pos_step(d, _):
        rows = aligned(d * BLK, BLK)
        pk_buf[rows] = dot_nn(t_buf[rows], weights_ref[2]).astype(BF16)
        return 0

    def line_step(s, _):
        low, high = a - 1 - s, a + 1 + s

        @pl.when((s < lines - 1) & (low >= 0))
        def _():
            p = jnp.maximum(low, 0)
            up_copy(p).wait_recv()

            @pl.when(a + 1 < lines)
            def _():
                up_copy(p).start()

            b_copy(p, b).start()
            c_copy(p, 0, b, core).start()

        @pl.when((s < lines - 1) & (high < lines))
        def _():
            p = jnp.minimum(high, lines - 1)
            down_copy(p).wait_recv()

            @pl.when(a >= 1)
            def _():
                down_copy(p).start()

            b_copy(p, b).start()
            c_copy(p, 0, b, core).start()

        @pl.when(s == 0)
        def _():
            for m in range(2, 4):
                for t in range(1, shards):
                    weight_copy(m, t).wait()
                    weight_pass(m, t).start()

        @pl.when(s == 1)
        def _():
            for m in range(2, 4):
                for t in range(1, shards):
                    weight_pass(m, t).wait()

        @pl.when(a - s >= 0)
        def _():
            project(jnp.maximum(a - s, 0))

        @pl.when((s >= 1) & (a + s < lines))
        def _():
            project(jnp.minimum(a + s, lines - 1))

        @pl.when(s >= 1)
        def _():
            lax.fori_loop(chunks * (s - 1) // (lines - 1), chunks * s // (lines - 1), pos_step, 0)

        return 0

    lax.fori_loop(0, lines, line_step, 0)
    pos_out = pltpu.make_async_copy(pk_buf, pk_ref, pos_sem.at[1])
    pos_out.start()
    normed = (unit_of(x_ref[...]) * gain + offset).astype(BF16)
    queries = dot_nn(normed, weights_ref[3]).astype(BF16).astype(F32)
    qc_ref[...] = ((queries + vectors_ref[2:3]) * 0.125).astype(BF16)
    qp_ref[...] = ((queries + vectors_ref[3:4]) * 0.125).astype(BF16)
    cnt_finish(2)
    cnt_start(3)

    def sends_done(p, _):
        @pl.when((a + 1 < lines) & (p <= a))
        def _():
            up_copy(p).wait_send()

        @pl.when((a >= 1) & (p >= a))
        def _():
            down_copy(p).wait_send()

        return 0

    lax.fori_loop(0, lines, sends_done, 0)

    def outs_done(slot, _):
        for copy in out_copies(slot):
            copy.wait()
        return 0

    lax.fori_loop(0, 4 * lines, outs_done, 0)
    table_out.wait()
    pos_out.wait()
    cnt_finish(3)
    total_ref[...] = cnt_acc[4 * 8 : 5 * 8]


def start(lines, shards, cid, limit, x, wq, wk, wv, wp, vec, count, far, near):
    tokens, width = x.shape
    members = 4 * lines
    keys = members * tokens
    span = limit * BLK
    vmem = pl.BlockSpec(memory_space=pltpu.VMEM)
    hbm = pl.BlockSpec(memory_space=pl.ANY)
    small = 2 * (shards - 1) + 1 + 1 + lines - 1
    dma = pltpu.SemaphoreType.DMA
    return pl.pallas_call(
        functools.partial(start_kernel, lines, shards),
        out_shape=(
            jax.ShapeDtypeStruct((keys, width), BF16),
            jax.ShapeDtypeStruct((keys, width), BF16),
            jax.ShapeDtypeStruct((keys, width), BF16),
            jax.ShapeDtypeStruct((span, width), BF16),
            jax.ShapeDtypeStruct((span, width), BF16),
            jax.ShapeDtypeStruct((tokens, width), BF16),
            jax.ShapeDtypeStruct((tokens, width), BF16),
            jax.ShapeDtypeStruct((4, width, width), BF16),
            jax.ShapeDtypeStruct((16, width), F32),
            jax.ShapeDtypeStruct((8, BLK), F32),
        ),
        in_specs=[vmem] * 9,
        out_specs=(hbm,) * 5 + (vmem,) * 5,
        scratch_shapes=[
            pltpu.VMEM((keys, width), BF16),
            pltpu.VMEM((keys, width), BF16),
            pltpu.VMEM((keys, width), BF16),
            pltpu.VMEM((keys, width), BF16),
            pltpu.VMEM((span, width), BF16),
            pltpu.VMEM((span, width), BF16),
            pltpu.VMEM((shards - 1, 16, width), F32),
            pltpu.VMEM((lines + shards, 8, BLK), F32),
            pltpu.VMEM((5 * 8, BLK), F32),
            dma((lines,)), dma((lines,)), dma((lines,)), dma((lines,)), dma((lines,)), dma((lines,)),
            dma((2, lines)), dma((2, lines)),
            dma((4, shards - 1)), dma((4, shards - 1)), dma((4, shards - 1)), dma((4, shards - 1)),
            dma((small,)), dma((small,)),
            dma((3, members)), dma((2,)),
        ],
        compiler_params=pltpu.CompilerParams(collective_id=cid, has_side_effects=True, vmem_limit_bytes=60 * 2**20),
        cost_estimate=pl.CostEstimate(flops=6 * 10**9, bytes_accessed=20 * 2**20, transcendentals=0),
        name="start",
    )(x, wq, wk, wv, wp, vec, count, far, near)


GELU_SCALE = math.sqrt(2.0 / math.pi)


def middle_kernel(
    shards, rows_f, mask_ref, x_ref, mixed_ref, teacher_ref, out_grad_ref, vectors_ref, total_ref, *rest,
):
    wo_refs = rest[:shards]
    wu_refs = rest[shards : 2 * shards]
    wd_refs = rest[2 * shards : 3 * shards]
    out_ref, hidden_ref, gm_ref, gf_ref, vec_ref, wo, wu, wd, slope, act, sem = rest[3 * shards :]
    tokens, width = x_ref.shape
    parts = wu.shape[1] // width
    w = lax.axis_index("wsh")
    copies = []
    for s in range(shards):
        owner = lax.rem(w + s, shards)
        for m, (refs, full) in enumerate(((wo_refs, wo), (wu_refs, wu), (wd_refs, wd))):
            rows = full.shape[0] // shards
            copies.append(pltpu.make_async_copy(refs[s], full.at[aligned(owner * rows, rows)], sem.at[m, s]))
    for copy in copies:
        copy.start()
    for copy in copies:
        copy.wait()
    gain, offset, down_bias = vectors_ref[4:5], vectors_ref[5:6], vectors_ref[6:7]
    mixed = mixed_ref[...].astype(BF16)
    hidden = x_ref[...].astype(F32) + dot_nn(mixed, wo[...])
    center = hidden - jnp.mean(hidden, axis=1, keepdims=True)
    inverse = lax.rsqrt(jnp.mean(center * center, axis=1, keepdims=True) + epsilon)
    unit = center * inverse
    normed = (unit * gain + offset).astype(BF16)
    result = hidden + down_bias
    for c in range(parts):
        cols = slice(c * width, (c + 1) * width)
        v = dot_nn(normed, wu[:, cols]) + vectors_ref[7 + c : 8 + c]
        square = v * v
        t = jnp.tanh(GELU_SCALE * (v + 0.044715 * (square * v)))
        act[:, cols] = (0.5 * v * (1.0 + t)).astype(BF16)
        slope[:, cols] = 0.5 * (1.0 + t) + 0.5 * v * (1.0 - t * t) * (GELU_SCALE * (1.0 + 3.0 * 0.044715 * square))
        result = result + dot_nn(act[:, cols], wd[cols])
    out_ref[...] = result.astype(BF16)
    mask = mask_ref[...]
    error = result - teacher_ref[...].astype(F32)
    masked = mask * error
    count = jnp.sum(total_ref[0:1, 0:1], axis=1, keepdims=True)
    grad_result = out_grad_ref[...].astype(F32) + (2.0 / (count * width)) * masked
    branch = grad_result.astype(BF16)
    vec_ref[...] = jnp.zeros_like(vec_ref)
    vec_ref[7 + parts : 8 + parts] = jnp.broadcast_to(
        jnp.sum(jnp.sum(masked * error, axis=1, keepdims=True), axis=0, keepdims=True), (1, width)
    )
    vec_ref[6:7] = jnp.sum(branch.astype(F32), axis=0, keepdims=True)
    rows_up = wd.shape[0] // shards
    rows_out = width // shards
    used = 2 * rows_up + rows_out
    if used < rows_f:
        gf_ref[:, used:] = jnp.zeros((shards, rows_f - used, width), BF16)
    grad_normed = jnp.zeros((tokens, width), F32)
    for c in range(parts):
        cols = slice(c * width, (c + 1) * width)
        grad_pre = (dot_nt(branch, wd[cols]) * slope[:, cols]).astype(BF16)
        vec_ref[7 + c : 8 + c] = jnp.sum(grad_pre.astype(F32), axis=0, keepdims=True)
        grad_normed = grad_normed + dot_nt(grad_pre, wu[:, cols])
        up = dot_tn(normed, grad_pre).astype(BF16)
        down = dot_tn(act[:, cols], branch).astype(BF16)
        for s in range(shards):
            gf_ref[s, c * rows_out : (c + 1) * rows_out] = up[s * rows_out : (s + 1) * rows_out]
        step = min(rows_up, width)
        for begin in range(0, width, step):
            row = c * width + begin
            place = rows_up + row % rows_up
            gf_ref[row // rows_up, place : place + step] = down[begin : begin + step]
    vec_ref[4:5] = jnp.sum(grad_normed * unit, axis=0, keepdims=True)
    vec_ref[5:6] = jnp.sum(grad_normed, axis=0, keepdims=True)
    scaled = grad_normed * gain
    grad_hidden = grad_result + inverse * (
        scaled - jnp.mean(scaled, axis=1, keepdims=True) - unit * jnp.mean(scaled * unit, axis=1, keepdims=True)
    )
    hidden_ref[...] = grad_hidden
    attn = grad_hidden.astype(BF16)
    gm_ref[...] = dot_nt(attn, wo[...]).astype(BF16)
    outer = dot_tn(mixed, attn).astype(BF16)
    for s in range(shards):
        gf_ref[s, 2 * rows_up : used] = outer[s * rows_out : (s + 1) * rows_out]


def middle(shards, rows_f, mask, x, mixed, teacher, out_grad, vectors, total, wo_parts, wu_parts, wd_parts):
    tokens, width = x.shape
    hidden = wu_parts[0].shape[1]
    vmem = pl.BlockSpec(memory_space=pltpu.VMEM)
    hbm = pl.BlockSpec(memory_space=pl.ANY)
    return pl.pallas_call(
        functools.partial(middle_kernel, shards, rows_f),
        out_shape=(
            jax.ShapeDtypeStruct((tokens, width), BF16),
            jax.ShapeDtypeStruct((tokens, width), F32),
            jax.ShapeDtypeStruct((tokens, width), BF16),
            jax.ShapeDtypeStruct((shards, rows_f, width), BF16),
            jax.ShapeDtypeStruct((16, width), F32),
        ),
        in_specs=[vmem] * 7 + [hbm] * (3 * shards),
        out_specs=(vmem,) * 5,
        scratch_shapes=[
            pltpu.VMEM((width, width), BF16),
            pltpu.VMEM((width, hidden), BF16),
            pltpu.VMEM((hidden, width), BF16),
            pltpu.VMEM((tokens, hidden), F32),
            pltpu.VMEM((tokens, hidden), BF16),
            pltpu.SemaphoreType.DMA((3, shards)),
        ],
        compiler_params=pltpu.CompilerParams(vmem_limit_bytes=48 * 2**20),
        cost_estimate=pl.CostEstimate(flops=4 * 10**9, bytes_accessed=20 * 2**20, transcendentals=10**6),
        name="middle",
    )(mask, x, mixed, teacher, out_grad, vectors, total, *wo_parts, *wu_parts, *wd_parts)


def body(
    inputs, block_perm, seq_lengths, loss_mask, teacher, out_grad, gain_one, bias_one, w_query, w_key, w_value,
    w_output, w_pos, content_bias, position_bias, gain_two, bias_two, w_up, bias_up, w_down, bias_down,
):
    tokens, width = inputs.shape[1:]
    shards = lax.axis_size("wsh")
    lines = lax.axis_size("ctx") // 4
    hidden = bias_up.shape[0] * shards
    perm_row = block_perm[0]
    blocks = perm_row.shape[0]
    limit = blocks * BLK // 2 // BLK + 1
    device, own = lax.axis_index("ctx"), lax.axis_index("wsh")
    rows_up, rows_out = hidden // shards, width // shards

    def pieces_of(part):
        pieces = [part]
        for s in range(1, shards):
            pieces.append(lax.ppermute(part, "wsh", [((i + s) % shards, i) for i in range(shards)]))
        return pieces

    wo_parts, wu_parts, wd_parts = pieces_of(w_output), pieces_of(w_up), pieces_of(w_down)

    inverse_perm = jnp.sum(
        jnp.where(perm_row[None, :] == jnp.arange(blocks, dtype=jnp.int32)[:, None], jnp.arange(blocks, dtype=jnp.int32), 0),
        axis=1,
    )
    own_blocks = lax.dynamic_slice_in_dim(perm_row, 2 * device, 2, 0)
    meta = jnp.concatenate([own_blocks, inverse_perm, jnp.cumsum(seq_lengths[0])]).astype(jnp.int32)

    rows = [gain_one, bias_one, content_bias, position_bias, gain_two, bias_two, bias_down]
    placed = lax.dynamic_update_slice(jnp.zeros((7, width), F32), jnp.stack(rows).astype(F32), (0, own * rows_out))
    ups = lax.dynamic_update_slice(jnp.zeros((hidden,), F32), bias_up.astype(F32), (own * rows_up,))
    vec = jnp.concatenate([placed, ups.reshape(hidden // width, width), jnp.zeros((9 - hidden // width, width), F32)])
    mask_rows = loss_mask[0].astype(F32)
    count = jnp.broadcast_to(jnp.sum(mask_rows), (8, BLK))

    frequency = jnp.exp(jnp.arange(width // 2, dtype=F32) * (-2.0 * math.log(10000.0) / width))
    padded = -(-limit // 8) * 8
    far_angle = (jnp.arange(padded, dtype=F32) * BLK + (BLK - 1))[:, None] * frequency[None]
    near_angle = jnp.arange(BLK, dtype=F32)[:, None] * frequency[None]
    far = jnp.stack([jnp.sin(far_angle), jnp.cos(far_angle)])
    near = jnp.stack([jnp.sin(near_angle), jnp.cos(near_angle)])

    keys, values, unit_all, pos_keys, table, qc, qp, weights, vectors, total = start(
        lines, shards, 0, limit, inputs[0], w_query, w_key, w_value, w_pos, vec, count, far, near
    )
    mixed, linv, probs = attn_fwd(meta, qc, qp, keys, values, pos_keys, blocks, limit)

    unit_rows = 64 * lines
    used = 2 * rows_up + rows_out
    pieces = -(-used // unit_rows)
    split = min(3, pieces)
    rows_f = tuple((pieces * (i + 1) // split - pieces * i // split) * unit_rows for i in range(split))
    rows_l = -(-4 * rows_out // unit_rows) * unit_rows
    output, grad_hidden, grad_mixed, early, vec = middle(
        shards, pieces * unit_rows, mask_rows[:, None], inputs[0], mixed, teacher[0], out_grad[0], vectors, total,
        wo_parts, wu_parts, wd_parts,
    )
    grad_query, bias_grads, dk_t, dv_t, dpk_t = attn_bwd(
        meta, qc, qp, keys, values, pos_keys, probs, linv, grad_mixed, mixed, blocks, limit
    )
    grad_input, sums_low, sums = finish(
        lines, shards, rows_f, rows_l, 1, early, dk_t, dv_t, unit_all, dpk_t, table, weights, grad_query,
        inputs[0], vectors, vectors[:2].T, vec, bias_grads, grad_hidden,
    )
    loss = sums[7 + hidden // width, 0] / (total[0, 0] * width)
    wide = sums_low.astype(F32)
    total_up = wide[:rows_up].reshape(hidden // width, rows_out, width).transpose(1, 0, 2).reshape(rows_out, hidden)
    total_down = wide[rows_up : 2 * rows_up]
    total_output = wide[2 * rows_up : used]
    late = wide[pieces * unit_rows :]
    late = [late[i * rows_out : (i + 1) * rows_out] for i in range(4)]

    def share(part):
        size = part.size // shards
        return lax.dynamic_slice_in_dim(part.reshape(-1), own * size, size, 0)

    v_g1, v_b1, v_cb, v_pb, v_g2, v_b2, v_bd = (share(sums[i]) for i in range(7))
    v_bu = share(sums[7 : 7 + hidden // width])
    return (
        output[None], loss, grad_input[None], v_g1, v_b1, late[0], late[1], late[2], total_output, late[3],
        v_cb, v_pb, v_g2, v_b2, total_up, v_bu, total_down, v_bd,
    )


def solution(mesh):
    rows = P("wsh", "ctx", None)
    vector = P("wsh")
    matrix = P("wsh", None)
    placed = (
        rows, matrix, matrix, P("wsh", "ctx"), rows, rows, vector, vector, matrix, matrix, matrix, matrix, matrix,
        vector, vector, vector, vector, matrix, vector, matrix, vector,
    )
    out = (
        rows, P(), rows, vector, vector, matrix, matrix, matrix, matrix, matrix, vector, vector, vector, vector,
        matrix, vector, matrix, vector,
    )
    return jax.shard_map(body, mesh=mesh, in_specs=placed, out_specs=out, check_vma=False)
```

```python
import functools
import math

import jax
import jax.numpy as jnp
import numpy as np
from jax import lax
from jax.experimental import pallas as pl
from jax.experimental.pallas import tpu as pltpu
from jax.sharding import PartitionSpec as P

HEADS = 8
HEAD = 64
PAIRS = HEADS // 2
BLK = 128
ROWS = HEADS * BLK
NEG = -1e30
epsilon = 1e-05
F32 = jnp.float32
BF16 = jnp.bfloat16


def dot_nt(a, b):
    return lax.dot_general(a, b, (((1,), (1,)), ((), ())), preferred_element_type=F32)


def dot_nn(a, b):
    return lax.dot_general(a, b, (((1,), (0,)), ((), ())), preferred_element_type=F32)


def dot_tn(a, b):
    return lax.dot_general(a, b, (((0,), (0,)), ((), ())), preferred_element_type=F32)


def iotas():
    row = lax.broadcasted_iota(jnp.int32, (BLK, BLK), 0)
    col = lax.broadcasted_iota(jnp.int32, (BLK, BLK), 1)
    return row, col


def read_places(perm_ref, lengths_ref, meta, blocks, count):
    device = lax.axis_index("ctx")
    meta[0] = perm_ref[0, 2 * device]
    meta[1] = perm_ref[0, 2 * device + 1]

    def place(slot, _):
        meta[2 + perm_ref[0, slot]] = slot
        return 0

    lax.fori_loop(0, blocks, place, 0)
    end = jnp.int32(0)
    for e in range(count):
        end = end + lengths_ref[0, e]
        meta[2 + blocks + e] = end


def block_range(meta, a, blocks, limit):
    qb = meta[a]
    first = qb * BLK
    low = jnp.int32(0)
    for e in range(meta.shape[0] - 2 - blocks):
        end = meta[2 + blocks + e]
        low = jnp.where(first >= end, jnp.maximum(low, end), low)
    lowest = low // BLK
    return qb, lowest, jnp.minimum(qb - lowest + 1, limit)


def stack_heads(pair):
    lane = lax.broadcasted_iota(jnp.int32, pair.shape, 1)
    zero = jnp.zeros_like(pair)
    return jnp.concatenate([jnp.where(lane < HEAD, pair, zero), jnp.where(lane >= HEAD, pair, zero)], axis=0)


def flip_rows(x):
    index = 7 - lax.broadcasted_iota(jnp.int32, (8, BLK), 0)
    slabs = [jnp.take_along_axis(x[8 * g : 8 * g + 8], index, axis=0) for g in reversed(range(BLK // 8))]
    return jnp.concatenate(slabs, axis=0)


def flip_two(x):
    return jnp.concatenate([flip_rows(x[:BLK]), flip_rows(x[BLK:])], axis=0)


def attn_fwd_kernel(
    blocks, limit, perm_ref, lengths_ref, qc_ref, qp_ref, k_ref, v_ref, pk_ref, mixed_ref, linv_ref, p_ref,
    meta, q2c, q2p, prev, top, total, acc, s_scr, p_buf, p_sem,
):
    read_places(perm_ref, lengths_ref, meta, blocks, lengths_ref.shape[1])
    row, col = iotas()
    tri = col <= row

    def p_copy(slot, index):
        return pltpu.make_async_copy(p_buf.at[slot], p_ref.at[index], p_sem.at[slot])

    def one_query_block(a, _):
        qb, lowest, count = block_range(meta, a, blocks, limit)
        rows_a = pl.ds(pl.multiple_of(a * BLK, BLK), BLK)
        pos = qb * BLK + row
        start = jnp.zeros((BLK, BLK), jnp.int32)
        for e in range(meta.shape[0] - 2 - blocks):
            end = meta[2 + blocks + e]
            start = jnp.where(pos >= end, jnp.maximum(start, end), start)
        for hp in range(PAIRS):
            lanes = slice(hp * BLK, (hp + 1) * BLK)
            q2c[hp] = stack_heads(qc_ref[rows_a, lanes].astype(F32)).astype(BF16)
            q2p[hp] = stack_heads(qp_ref[rows_a, lanes].astype(F32)).astype(BF16)
        prev[...] = jnp.zeros_like(prev)
        top[...] = jnp.full_like(top, NEG)
        total[...] = jnp.zeros_like(total)
        acc[...] = jnp.zeros_like(acc)

        def score_step(d, _):
            kb = qb - d
            off = pl.multiple_of(meta[2 + kb] * BLK, BLK)
            place = kb * BLK + col
            bias = jnp.where((place >= start) & (place <= pos), 0.0, NEG).astype(F32)
            drow = pl.multiple_of(d * BLK, BLK)
            for hp in range(PAIRS):
                lanes = slice(hp * BLK, (hp + 1) * BLK)
                s = dot_nt(q2c[hp], k_ref[pl.ds(off, BLK), lanes])
                r = dot_nt(q2p[hp], pk_ref[pl.ds(drow, BLK), lanes])
                for half in range(2):
                    part = slice(half * BLK, (half + 1) * BLK)
                    rows = slice((2 * hp + half) * BLK, (2 * hp + half + 1) * BLK)
                    rot = pltpu.roll(r[part], 1, 1, stride=1, stride_axis=0)
                    score = s[part] + jnp.where(tri, rot, prev[rows]) + bias
                    prev[rows] = rot
                    s_scr[d, rows] = score
                    top[rows] = jnp.maximum(top[rows], score)
            return 0

        lax.fori_loop(0, count, score_step, 0)
        for h in range(HEADS):
            rows = slice(h * BLK, (h + 1) * BLK)
            top[rows] = jnp.broadcast_to(jnp.max(top[rows], axis=1, keepdims=True), (BLK, BLK))

        def mix_step(d, _):
            kb = qb - d
            off = pl.multiple_of(meta[2 + kb] * BLK, BLK)
            slot = lax.rem(d, 2)

            @pl.when(d >= 2)
            def _():
                p_copy(slot, 0).wait()

            for hp in range(PAIRS):
                lanes = slice(hp * BLK, (hp + 1) * BLK)
                rows = slice(2 * hp * BLK, 2 * (hp + 1) * BLK)
                p = jnp.exp(s_scr[d, rows] - top[rows])
                total[rows] += p
                p_buf[slot, rows] = flip_two(p).astype(BF16)
                acc[hp] += dot_nn(p.astype(BF16), v_ref[pl.ds(off, BLK), lanes])
            p_copy(slot, a * limit + d).start()
            return 0

        lax.fori_loop(0, count, mix_step, 0)
        p_copy(lax.rem(count - 1, 2), 0).wait()

        @pl.when(count >= 2)
        def _():
            p_copy(lax.rem(count, 2), 0).wait()

        lane = lax.broadcasted_iota(jnp.int32, (BLK, BLK), 1)
        for hp in range(PAIRS):
            lanes = slice(hp * BLK, (hp + 1) * BLK)
            parts = []
            for half in range(2):
                h = 2 * hp + half
                rows = slice(h * BLK, (h + 1) * BLK)
                inv = 1.0 / jnp.sum(total[rows], axis=1, keepdims=True)
                inv = jnp.broadcast_to(inv, (BLK, BLK))
                linv_ref[a, rows] = inv
                parts.append(acc[hp, half * BLK : (half + 1) * BLK] * inv)
            mixed_ref[rows_a, lanes] = jnp.where(lane < HEAD, parts[0], parts[1])
        return 0

    lax.fori_loop(0, 2, one_query_block, 0)


def attn_fwd(perm, lengths, qc, qp, k, v, pk, blocks, limit):
    tokens, width = qc.shape
    vmem = pl.BlockSpec(memory_space=pltpu.VMEM)
    return pl.pallas_call(
        functools.partial(attn_fwd_kernel, blocks, limit),
        out_shape=(
            jax.ShapeDtypeStruct((tokens, width), F32),
            jax.ShapeDtypeStruct((2, ROWS, BLK), F32),
            jax.ShapeDtypeStruct((2 * limit, ROWS, BLK), BF16),
        ),
        in_specs=[pl.BlockSpec(memory_space=pltpu.SMEM)] * 2 + [vmem] * 5,
        out_specs=(vmem, vmem, pl.BlockSpec(memory_space=pl.ANY)),
        scratch_shapes=[
            pltpu.SMEM((2 + blocks + lengths.shape[1],), jnp.int32),
            pltpu.VMEM((PAIRS, 2 * BLK, BLK), BF16),
            pltpu.VMEM((PAIRS, 2 * BLK, BLK), BF16),
            pltpu.VMEM((ROWS, BLK), F32),
            pltpu.VMEM((ROWS, BLK), F32),
            pltpu.VMEM((ROWS, BLK), F32),
            pltpu.VMEM((PAIRS, 2 * BLK, BLK), F32),
            pltpu.VMEM((limit, ROWS, BLK), F32),
            pltpu.VMEM((2, ROWS, BLK), BF16),
            pltpu.SemaphoreType.DMA((2,)),
        ],
        compiler_params=pltpu.CompilerParams(vmem_limit_bytes=56 * 2**20),
        cost_estimate=pl.CostEstimate(flops=3 * 10**9, bytes_accessed=20 * 2**20, transcendentals=4 * 10**6),
        name="attn_fwd",
    )(perm, lengths, qc, qp, k, v, pk)


def attn_bwd_kernel(
    blocks, limit, perm_ref, lengths_ref, qc_ref, qp_ref, k_ref, v_ref, pk_ref, p_ref, linv_ref, gm_ref, mixed_ref,
    dq_ref, bias_ref, dk_ref, dv_ref, dpk_ref,
    meta, q2c_t, q2p_t, gm2, gm2_t, dd, carry, dqk, dqp, dpk, p_buf, p_sem,
):
    read_places(perm_ref, lengths_ref, meta, blocks, lengths_ref.shape[1])
    row, col = iotas()
    tri = col <= BLK - 1 - row
    dk_ref[...] = jnp.zeros_like(dk_ref)
    dv_ref[...] = jnp.zeros_like(dv_ref)
    dpk[...] = jnp.zeros_like(dpk)
    bias_ref[...] = jnp.zeros_like(bias_ref)

    def p_copy(slot, index):
        return pltpu.make_async_copy(p_ref.at[index], p_buf.at[slot], p_sem.at[slot])

    def one_query_block(a, _):
        qb, lowest, count = block_range(meta, a, blocks, limit)
        rows_a = pl.ds(pl.multiple_of(a * BLK, BLK), BLK)
        p_copy(0, a * limit + count - 1).start()
        for hp in range(PAIRS):
            lanes = slice(hp * BLK, (hp + 1) * BLK)
            rows = slice(2 * hp * BLK, 2 * (hp + 1) * BLK)
            q2c_t[hp] = stack_heads(flip_rows(qc_ref[rows_a, lanes].astype(F32))).T.astype(BF16)
            q2p_t[hp] = stack_heads(flip_rows(qp_ref[rows_a, lanes].astype(F32))).T.astype(BF16)
            g = stack_heads(gm_ref[rows_a, lanes].astype(F32))
            scaled = flip_two(g * linv_ref[a, rows])
            gm2[hp] = scaled.astype(BF16)
            gm2_t[hp] = scaled.T.astype(BF16)
            pair = flip_rows(mixed_ref[rows_a, lanes])
            dd[rows] = jnp.broadcast_to(
                jnp.sum(scaled * jnp.concatenate([pair, pair], axis=0), axis=1, keepdims=True), (2 * BLK, BLK)
            )
        carry[...] = jnp.zeros_like(carry)
        dqk[...] = jnp.zeros_like(dqk)
        dqp[...] = jnp.zeros_like(dqp)

        def step(t, _):
            d = count - 1 - t
            kb = qb - d
            off = pl.multiple_of(meta[2 + kb] * BLK, BLK)
            keys = pl.ds(off, BLK)
            drow = pl.ds(pl.multiple_of(d * BLK, BLK), BLK)
            slot = lax.rem(t, 2)
            p_copy(slot, 0).wait()

            @pl.when(d >= 1)
            def _():
                p_copy(1 - slot, a * limit + d - 1).start()

            for hp in range(PAIRS):
                lanes = slice(hp * BLK, (hp + 1) * BLK)
                rows = slice(2 * hp * BLK, 2 * (hp + 1) * BLK)
                p = p_buf[slot, rows]
                g = dot_nt(gm2[hp], v_ref[keys, lanes])
                gs = p.astype(F32) * (g - dd[rows])
                gs_low = gs.astype(BF16)
                gs = gs_low.astype(F32)
                rots = []
                for half in range(2):
                    part = slice(half * BLK, (half + 1) * BLK)
                    crow = slice((2 * hp + half) * BLK, (2 * hp + half + 1) * BLK)
                    both = jnp.where(tri, gs[part], carry[crow])
                    carry[crow] = gs[part]
                    rots.append(pltpu.roll(both, 0, 1, stride=1, stride_axis=0))
                rot = jnp.concatenate(rots, axis=0).astype(BF16)
                dqk[hp] += dot_nn(gs_low, k_ref[keys, lanes])
                dqp[hp] += dot_nn(rot, pk_ref[drow, lanes])
                dk_ref[lanes, keys] = (dk_ref[lanes, keys].astype(F32) + dot_nn(q2c_t[hp], gs_low)).astype(BF16)
                dv_ref[lanes, keys] = (dv_ref[lanes, keys].astype(F32) + dot_nn(gm2_t[hp], p)).astype(BF16)
                dpk[lanes, drow] += dot_nn(q2p_t[hp], rot)
            return 0

        lax.fori_loop(0, count, step, 0)
        lane = lax.broadcasted_iota(jnp.int32, (BLK, BLK), 1)
        for hp in range(PAIRS):
            lanes = slice(hp * BLK, (hp + 1) * BLK)
            ck = jnp.where(lane < HEAD, dqk[hp, :BLK], dqk[hp, BLK:]) * 0.125
            cp = jnp.where(lane < HEAD, dqp[hp, :BLK], dqp[hp, BLK:]) * 0.125
            dq_ref[rows_a, lanes] = flip_rows(ck + cp).astype(BF16)
            bias_ref[0:1, lanes] += jnp.sum(ck, axis=0, keepdims=True)
            bias_ref[1:2, lanes] += jnp.sum(cp, axis=0, keepdims=True)
        return 0

    lax.fori_loop(0, 2, one_query_block, 0)
    dpk_ref[...] = dpk[...].astype(BF16)


def attn_bwd(perm, lengths, qc, qp, k, v, pk, p, linv, gm, mixed, blocks, limit):
    tokens, width = qc.shape
    keys = k.shape[0]
    span = pk.shape[0]
    vmem = pl.BlockSpec(memory_space=pltpu.VMEM)
    return pl.pallas_call(
        functools.partial(attn_bwd_kernel, blocks, limit),
        out_shape=(
            jax.ShapeDtypeStruct((tokens, width), BF16),
            jax.ShapeDtypeStruct((8, width), F32),
            jax.ShapeDtypeStruct((width, keys), BF16),
            jax.ShapeDtypeStruct((width, keys), BF16),
            jax.ShapeDtypeStruct((width, span), BF16),
        ),
        in_specs=[pl.BlockSpec(memory_space=pltpu.SMEM)] * 2
        + [vmem] * 5
        + [pl.BlockSpec(memory_space=pl.ANY)]
        + [vmem] * 3,
        out_specs=(vmem,) * 5,
        scratch_shapes=[
            pltpu.SMEM((2 + blocks + lengths.shape[1],), jnp.int32),
            pltpu.VMEM((PAIRS, BLK, 2 * BLK), BF16),
            pltpu.VMEM((PAIRS, BLK, 2 * BLK), BF16),
            pltpu.VMEM((PAIRS, 2 * BLK, BLK), BF16),
            pltpu.VMEM((PAIRS, BLK, 2 * BLK), BF16),
            pltpu.VMEM((ROWS, BLK), F32),
            pltpu.VMEM((ROWS, BLK), F32),
            pltpu.VMEM((PAIRS, 2 * BLK, BLK), F32),
            pltpu.VMEM((PAIRS, 2 * BLK, BLK), F32),
            pltpu.VMEM((width, span), F32),
            pltpu.VMEM((2, ROWS, BLK), BF16),
            pltpu.SemaphoreType.DMA((2,)),
        ],
        compiler_params=pltpu.CompilerParams(vmem_limit_bytes=60 * 2**20),
        cost_estimate=pl.CostEstimate(flops=6 * 10**9, bytes_accessed=30 * 2**20, transcendentals=0),
        name="attn_bwd",
    )(perm, lengths, qc, qp, k, v, pk, p, linv, gm, mixed)


MESH = pl.DeviceIdType.MESH


def fold_rows(x):
    return jnp.broadcast_to(x, (x.shape[0], BLK)).T[0:1]


def aligned(begin, size):
    return pl.ds(pl.multiple_of(begin, math.gcd(size, 16)), size)


def finish_kernel(
    lines, shards, chunks_f, rows_l,
    mine_ref, come_ref, dk_ref, dv_ref, unit_all_ref, dpk_ref, table_ref, weights_ref, dq_ref, x_ref,
    vectors_ref, total_ref, vec_ref, bias_ref, hidden_ref,
    grad_ref, sums_ref, vsum_ref,
    dk_buf, dv_buf, un_buf, in_sem, dpk_buf, table_buf, pos_sem, mt_k, mt_v, cs_k, cs_v, dxp, bx0, bx1, bx2, vbuf, vacc,
    *rest,
):
    wk_ref, wv_ref, wq_ref = weights_ref.at[0], weights_ref.at[1], weights_ref.at[3]
    tokens, width = dq_ref.shape
    count_f = len(chunks_f)
    bufs_f, bufs_l = rest[: 3 * count_f], rest[3 * count_f : 3 * count_f + 10]
    send_sem, recv_sem = rest[3 * count_f + 10 :]
    ctx = lax.axis_index("ctx")
    w = lax.axis_index("wsh")
    core = lax.rem(ctx, 2)
    b = lax.rem(ctx // 2, 2)
    a = ctx // 4

    def at(a_to, b_to, core_to):
        return (a_to * 2 + b_to) * 2 + core_to

    def line_peer(s):
        return (at(lax.rem(a + s, lines), b, core), w)

    def shard_peer(s):
        return (ctx, lax.rem(w + s, shards))

    core_peer = (at(a, b, 1 - core), w)
    b_peer = (at(a, 1 - b, core), w)
    peers = [core_peer, b_peer] + [line_peer(s) for s in range(1, lines)] + [shard_peer(s) for s in range(1, shards)]
    barrier = pltpu.get_barrier_semaphore()
    for peer in peers:
        pl.semaphore_signal(barrier, inc=1, device_id=peer, device_id_type=MESH)

    counter = [0]

    def take(number):
        begin = counter[0]
        counter[0] += number
        return begin

    def remote(src, dst, index, peer):
        return pltpu.make_async_remote_copy(
            src_ref=src, dst_ref=dst, send_sem=send_sem.at[index], recv_sem=recv_sem.at[index],
            device_id=peer, device_id_type=MESH,
        )

    def fetch(j, q, slot):
        a_to = lax.rem(a + 1 + j, lines)
        b_to = b if q % 2 == 1 else 1 - b
        core_to = core if q >= 2 else 1 - core
        begin = pl.multiple_of(at(a_to, b_to, core_to) * tokens, tokens)
        return (
            pltpu.make_async_copy(dk_ref.at[:, pl.ds(begin, tokens)], dk_buf.at[slot], in_sem.at[slot, 0]),
            pltpu.make_async_copy(dv_ref.at[:, pl.ds(begin, tokens)], dv_buf.at[slot], in_sem.at[slot, 1]),
            pltpu.make_async_copy(unit_all_ref.at[pl.ds(begin, tokens)], un_buf.at[slot], in_sem.at[slot, 2]),
        )

    pos_copies = [
        pltpu.make_async_copy(dpk_ref, dpk_buf, pos_sem.at[0]),
        pltpu.make_async_copy(table_ref, table_buf, pos_sem.at[1]),
    ]
    for copy in pos_copies:
        copy.start()
    for q in range(2):
        for copy in fetch(0, q, q):
            copy.start()

    def start_all(copies):
        for copy in copies:
            copy.start()

    def wait_all(copies):
        for copy in copies:
            copy.wait()

    class Feed:
        def __init__(self, begin, rows, total_rows, bufs):
            self.begin, self.rows, self.share = begin, rows, rows // lines
            self.rc, self.rb = total_rows // 2, total_rows // 4
            self.b0, self.b1, self.b3 = bufs
            self.iy, self.irs, self.iag, self.ix, self.ic = take(shards - 1), take(lines - 1), take(lines - 1), take(1), take(2)

        def y_copies(self):
            return [
                remote(self.b0.at[lax.rem(w + s, shards)], self.b1.at[s - 1], self.iy + s - 1, shard_peer(s))
                for s in range(1, shards)
            ]

        def rs_copies(self):
            return [
                remote(
                    self.b1.at[0, aligned(lax.rem(a + s, lines) * self.share, self.share)],
                    self.b3.at[s - 1], self.irs + s - 1, line_peer(s),
                )
                for s in range(1, lines)
            ]

        def place(self, b_of, begin, size):
            return aligned(core * self.rc + b_of * self.rb + self.begin + begin, size)

        def ag_copies(self):
            own = self.place(b, a * self.share, self.share)
            return [remote(sums_ref.at[own], sums_ref.at[own], self.iag + s - 1, line_peer(s)) for s in range(1, lines)]

        def x_copies(self):
            own = self.place(b, 0, self.rows)
            return [remote(sums_ref.at[own], sums_ref.at[own], self.ix, b_peer)]

        def c_copies(self):
            return [
                remote(sums_ref.at[rows], sums_ref.at[rows], self.ic + k, core_peer)
                for k, rows in enumerate((self.place(b, 0, self.rows), self.place(1 - b, 0, self.rows)))
            ]

        def y(self):
            rows = pl.ds(self.begin, self.rows)
            self.b0[...] = (mine_ref[:, rows].astype(F32) + come_ref[:, rows].astype(F32)).astype(BF16)
            start_all(self.y_copies())

        def rs(self):
            wait_all(self.y_copies())
            total = self.b0[w].astype(F32)
            for s in range(shards - 1):
                total = total + self.b1[s].astype(F32)
            self.b1[0] = total.astype(BF16)
            start_all(self.rs_copies())

        def ag(self):
            wait_all(self.rs_copies())
            total = self.b1[0, aligned(a * self.share, self.share)].astype(F32)
            for s in range(lines - 1):
                total = total + self.b3[s].astype(F32)
            sums_ref[self.place(b, a * self.share, self.share)] = total.astype(BF16)
            start_all(self.ag_copies())

        def x(self):
            wait_all(self.ag_copies())
            start_all(self.x_copies())

        def c(self):
            wait_all(self.x_copies())
            start_all(self.c_copies())

        def done(self):
            wait_all(self.c_copies())

    class Late:
        def __init__(self, out, rows, bufs):
            self.out, self.rows = out, rows
            self.src, self.b0, self.b1, self.b2, self.b3 = bufs
            self.rc, self.rb, self.share = rows // 2, rows // 4, rows // 4 // lines
            self.i0, self.iy, self.i2 = take(1), take(shards - 1), take(1)
            self.irs, self.iag, self.ix, self.ic = take(lines - 1), take(lines - 1), take(1), take(1)

        def c0_copies(self):
            return [remote(self.src.at[:, aligned((1 - core) * self.rc, self.rc)], self.b0, self.i0, core_peer)]

        def y_copies(self):
            return [
                remote(self.b0.at[lax.rem(w + s, shards)], self.b1.at[s - 1], self.iy + s - 1, shard_peer(s))
                for s in range(1, shards)
            ]

        def x0_copies(self):
            return [remote(self.b1.at[0, aligned((1 - b) * self.rb, self.rb)], self.b2, self.i2, b_peer)]

        def rs_copies(self):
            return [
                remote(
                    self.b2.at[aligned(lax.rem(a + s, lines) * self.share, self.share)],
                    self.b3.at[s - 1], self.irs + s - 1, line_peer(s),
                )
                for s in range(1, lines)
            ]

        def ag_copies(self):
            own = aligned(self.out + core * self.rc + b * self.rb + a * self.share, self.share)
            return [remote(sums_ref.at[own], sums_ref.at[own], self.iag + s - 1, line_peer(s)) for s in range(1, lines)]

        def x_copies(self):
            own = aligned(self.out + core * self.rc + b * self.rb, self.rb)
            return [remote(sums_ref.at[own], sums_ref.at[own], self.ix, b_peer)]

        def c_copies(self):
            own = aligned(self.out + core * self.rc, self.rc)
            return [remote(sums_ref.at[own], sums_ref.at[own], self.ic, core_peer)]

        def c0(self):
            start_all(self.c0_copies())

        def y(self):
            wait_all(self.c0_copies())
            own = self.src[:, aligned(core * self.rc, self.rc)]
            self.b0[...] = (self.b0[...].astype(F32) + own.astype(F32)).astype(BF16)
            start_all(self.y_copies())

        def x0(self):
            wait_all(self.y_copies())
            total = self.b0[w].astype(F32)
            for s in range(shards - 1):
                total = total + self.b1[s].astype(F32)
            self.b1[0] = total.astype(BF16)
            start_all(self.x0_copies())

        def rs(self):
            wait_all(self.x0_copies())
            own = self.b1[0, aligned(b * self.rb, self.rb)]
            self.b2[...] = (self.b2[...].astype(F32) + own.astype(F32)).astype(BF16)
            start_all(self.rs_copies())

        def ag(self):
            wait_all(self.rs_copies())
            total = self.b2[aligned(a * self.share, self.share)].astype(F32)
            for s in range(lines - 1):
                total = total + self.b3[s].astype(F32)
            own = aligned(self.out + core * self.rc + b * self.rb + a * self.share, self.share)
            sums_ref[own] = total.astype(BF16)
            start_all(self.ag_copies())

        def x(self):
            wait_all(self.ag_copies())
            start_all(self.x_copies())

        def c(self):
            wait_all(self.x_copies())
            start_all(self.c_copies())

        def done(self):
            wait_all(self.c_copies())

    rows_f = 4 * sum(chunks_f)
    feeds = []
    begin = 0
    for index, rows in enumerate(chunks_f):
        feeds.append(Feed(begin, rows, rows_f, bufs_f[3 * index : 3 * index + 3]))
        begin += rows
    first = Late(rows_f, rows_l, bufs_l[:5])
    second = Late(rows_f + rows_l, rows_l, bufs_l[5:])

    mt_k[...] = jnp.zeros_like(mt_k)
    mt_v[...] = jnp.zeros_like(mt_v)
    cs_k[...] = jnp.zeros_like(cs_k)
    cs_v[...] = jnp.zeros_like(cs_v)
    pl.semaphore_wait(barrier, len(peers))
    for feed in feeds:
        feed.y()

    rows_out = width // shards

    def fill(group, grads):
        for m, grad in enumerate(grads):
            for s in range(shards):
                group.src[s, m * rows_out : (m + 1) * rows_out] = grad[s * rows_out : (s + 1) * rows_out].astype(BF16)
        used = len(grads) * rows_out
        if used < rows_l:
            group.src[:, used:] = jnp.zeros((shards, rows_l - used, width), BF16)

    values = x_ref[...].astype(F32)
    center = values - jnp.mean(values, axis=1, keepdims=True)
    inverse = lax.rsqrt(jnp.mean(center * center, axis=1, keepdims=True) + epsilon)
    unit = center * inverse
    cols = vectors_ref[0:8].T
    gain_col, bias_col = cols[:, 0:1], cols[:, 1:2]
    dq = dq_ref[...]
    m_q = dot_tn(unit.astype(BF16), dq)
    csq = jnp.sum(dq.astype(F32), axis=0, keepdims=True)
    wait_all(pos_copies)
    fill(first, (gain_col * m_q + bias_col * csq, dot_nn(dpk_buf[...], table_buf[...]).T))
    first.c0()

    i_x0, i_x1, i_x2 = take(lines), take(lines), take(lines - 1)

    def copy_x0(j):
        return remote(dxp.at[j, pl.ds(0, 2)], bx0.at[j], i_x0 + j, core_peer)

    def copy_x1(j):
        return remote(bx0.at[j, 0], bx1.at[j], i_x1 + j, b_peer)

    def copy_x2(j):
        return remote(bx1.at[j], bx2.at[j], i_x2 + j, (at(lax.rem(a + 1 + j, lines), b, core), w))

    def after_x0(j):
        copy_x0(j).wait()
        bx0[j] = (bx0[j].astype(F32) + dxp[j, 2:4].astype(F32)).astype(BF16)
        copy_x1(j).start()

    def after_x1(j):
        copy_x1(j).wait()
        bx1[j] = (bx1[j].astype(F32) + bx0[j, 1].astype(F32)).astype(BF16)

        @pl.when(j < lines - 1)
        def _():
            copy_x2(j).start()

    events = {0: [first.y], 1: [], 2: [], 3: [first.x0]}
    for index, feed in enumerate(feeds):
        events[min(index, 3)].append(feed.rs)
        events[min(index + 2, 3)].append(feed.ag)

    def line_step(j, _):
        for q in range(4):
            slot = q % 2
            wait_all(fetch(j, q, slot))
            dk, dv, un = dk_buf[slot], dv_buf[slot], un_buf[slot]
            dxp[j, q] = (dot_nn(wk_ref[...], dk) + dot_nn(wv_ref[...], dv)).astype(BF16)
            mt_k[...] += dot_nn(dk, un)
            mt_v[...] += dot_nn(dv, un)
            for half in range(tokens // BLK):
                cs_k[...] += dk[:, half * BLK : (half + 1) * BLK].astype(F32)
                cs_v[...] += dv[:, half * BLK : (half + 1) * BLK].astype(F32)
            if q < 2:
                start_all(fetch(j, q + 2, slot))
            else:

                @pl.when(j < lines - 1)
                def _():
                    start_all(fetch(j + 1, q - 2, slot))

            if q == 1:
                copy_x0(j).start()

        @pl.when(j >= 1)
        def _():
            after_x0(j - 1)

        @pl.when(j >= 2)
        def _():
            after_x1(j - 2)

        for when, works in events.items():
            if when < lines - 1:

                @pl.when(j == when)
                def _():
                    for work in works:
                        work()

        return 0

    lax.fori_loop(0, lines, line_step, 0)
    after_x0(lines - 1)
    for when, works in events.items():
        if when >= lines - 1:
            for work in works:
                work()
    csk_col = jnp.sum(cs_k[...], axis=1, keepdims=True)
    csv_col = jnp.sum(cs_v[...], axis=1, keepdims=True)
    csk, csv = fold_rows(csk_col), fold_rows(csv_col)
    m_k, m_v = mt_k[...].T, mt_v[...].T
    fill(second, (gain_col * m_k + bias_col * csk, gain_col * m_v + bias_col * csv))
    second.c0()
    gain_grad = m_q * wq_ref[...].astype(F32) + m_k * wk_ref[...].astype(F32) + m_v * wv_ref[...].astype(F32)
    vacc[0:16] = vec_ref[...]
    vacc[2:4] = bias_ref[0:2]
    vacc[0:1] = fold_rows(jnp.sum(gain_grad, axis=1, keepdims=True))
    sums = [jnp.broadcast_to(x, (8, width)).astype(BF16) for x in (csq, csk, csv)]
    vacc[1:2] = (dot_nt(sums[0], wq_ref[...]) + dot_nt(sums[1], wk_ref[...]) + dot_nt(sums[2], wv_ref[...]))[0:1]

    vstages = [[core_peer], [b_peer], [line_peer(s) for s in range(1, lines)], [shard_peer(s) for s in range(1, shards)]]
    vslots = []
    place = 0
    for stage in vstages:
        vslots.append(place)
        place += len(stage)
    vbegin = take(place)

    def v_copy(stage, index):
        slot = vslots[stage] + index
        return remote(vacc.at[pl.ds(stage * 16, 16)], vbuf.at[slot], vbegin + slot, vstages[stage][index])

    def v_start(stage):
        for index in range(len(vstages[stage])):
            v_copy(stage, index).start()

    def v_finish(stage):
        total = vacc[stage * 16 : stage * 16 + 16]
        for index in range(len(vstages[stage])):
            v_copy(stage, index).wait()
            total = total + vbuf[vslots[stage] + index]
        vacc[(stage + 1) * 16 : (stage + 2) * 16] = total

    v_start(0)
    second.y()
    after_x1(lines - 2)
    v_finish(0)
    v_start(1)
    feeds[0].x()
    first.rs()
    after_x1(lines - 1)
    for feed in feeds[1:2]:
        feed.x()
    v_finish(1)
    v_start(2)
    first.ag()
    second.x0()
    for feed in feeds[2:]:
        feed.x()
    feeds[0].c()
    v_finish(2)
    v_start(3)
    second.rs()
    first.x()
    for feed in feeds[1:2]:
        feed.c()
    second.ag()
    own = bx1[lines - 1].astype(F32)
    for j in range(lines - 1):
        copy_x2(j).wait()
        own = own + bx2[j].astype(F32)
    scaled = own.T + dot_nt(dq, wq_ref[...])
    scaled = scaled * vectors_ref[0:1]
    grad_ref[...] = hidden_ref[...] + inverse * (
        scaled - jnp.mean(scaled, axis=1, keepdims=True) - unit * jnp.mean(scaled * unit, axis=1, keepdims=True)
    )
    for feed in feeds[2:]:
        feed.c()
    first.c()
    v_finish(3)
    totals = vacc[4 * 16 : 5 * 16]
    vsum_ref[...] = totals
    second.x()
    second.c()
    for feed in feeds:
        feed.done()
    first.done()
    second.done()


def finish(lines, shards, chunks_f, rows_l, cid, mine, come, dk, dv, unit_all, dpk, table, weights, dq, x, vectors, total, vec, bias, hidden):
    tokens, width = dq.shape
    vmem = pl.BlockSpec(memory_space=pltpu.VMEM)
    hbm = pl.BlockSpec(memory_space=pl.ANY)
    bufs = []
    for rows in chunks_f:
        bufs += [
            pltpu.VMEM((shards, rows, width), BF16),
            pltpu.VMEM((shards - 1, rows, width), BF16),
            pltpu.VMEM((lines - 1, rows // lines, width), BF16),
        ]
    for group in range(2):
        bufs += [
            pltpu.VMEM((shards, rows_l, width), BF16),
            pltpu.VMEM((shards, rows_l // 2, width), BF16),
            pltpu.VMEM((shards - 1, rows_l // 2, width), BF16),
            pltpu.VMEM((rows_l // 4, width), BF16),
            pltpu.VMEM((lines - 1, rows_l // 4 // lines, width), BF16),
        ]
    hops = shards - 1 + 2 * (lines - 1)
    copies = len(chunks_f) * (hops + 3) + 2 * (hops + 4) + 3 * lines - 1 + 2 + lines - 1 + shards - 1
    total_rows = 4 * sum(chunks_f) + 2 * rows_l
    stages = 1 + 1 + (lines - 1) + (shards - 1)
    span = dpk.shape[1]
    return pl.pallas_call(
        functools.partial(finish_kernel, lines, shards, tuple(chunks_f), rows_l),
        out_shape=(
            jax.ShapeDtypeStruct((tokens, width), F32),
            jax.ShapeDtypeStruct((total_rows, width), BF16),
            jax.ShapeDtypeStruct((16, width), F32),
        ),
        in_specs=[vmem] * 2 + [hbm] * 5 + [vmem] * 8,
        out_specs=(vmem,) * 3,
        scratch_shapes=[
            pltpu.VMEM((2, width, tokens), BF16),
            pltpu.VMEM((2, width, tokens), BF16),
            pltpu.VMEM((2, tokens, width), BF16),
            pltpu.SemaphoreType.DMA((2, 3)),
            pltpu.VMEM((width, span), BF16),
            pltpu.VMEM((span, width), BF16),
            pltpu.SemaphoreType.DMA((2,)),
            pltpu.VMEM((width, width), F32),
            pltpu.VMEM((width, width), F32),
            pltpu.VMEM((width, BLK), F32),
            pltpu.VMEM((width, BLK), F32),
            pltpu.VMEM((lines, 4, width, tokens), BF16),
            pltpu.VMEM((lines, 2, width, tokens), BF16),
            pltpu.VMEM((lines, width, tokens), BF16),
            pltpu.VMEM((lines - 1, width, tokens), BF16),
            pltpu.VMEM((stages, 16, width), F32),
            pltpu.VMEM((5 * 16, width), F32),
        ]
        + bufs
        + [pltpu.SemaphoreType.DMA((copies,)), pltpu.SemaphoreType.DMA((copies,))],
        compiler_params=pltpu.CompilerParams(
            collective_id=cid, has_side_effects=True, vmem_limit_bytes=63 * 2**20
        ),
        cost_estimate=pl.CostEstimate(flops=10**10, bytes_accessed=30 * 2**20, transcendentals=0),
        name="finish",
    )(mine, come, dk, dv, unit_all, dpk, table, weights, dq, x, vectors, total, vec, bias, hidden)


def unpack_kernel(
    shards, rows_f, rows_l, sums_ref, vsum_ref, total_ref, grad_ref,
    grad_out, q_out, k_out, v_out, o_out, p_out, u_out, d_out, g1_out, b1_out, cb_out, pb_out, g2_out, b2_out, bd_out, bu_out,
    loss_out,
    low, wide, up, in_sem, out_sem,
):
    width = vsum_ref.shape[1]
    rows_out, rows_up = q_out.shape[0], d_out.shape[0]
    parts = u_out.shape[1] // width
    w = lax.axis_index("wsh")
    pieces = [(rows_up, d_out), (2 * rows_up, o_out), (rows_f, q_out), (rows_f + rows_out, p_out),
              (rows_f + rows_l, k_out), (rows_f + rows_l + rows_out, v_out)]
    ins = [pltpu.make_async_copy(sums_ref.at[0:rows_up], low.at[0:rows_up], in_sem.at[0])]
    for index, (begin, out) in enumerate(pieces):
        size = out.shape[0]
        ins.append(pltpu.make_async_copy(sums_ref.at[begin : begin + size], low.at[begin : begin + size], in_sem.at[1 + index]))
    for copy in ins:
        copy.start()
    outs = [pltpu.make_async_copy(grad_ref, grad_out, out_sem.at[0])]
    outs[0].start()
    ins[0].wait()
    for c in range(parts):
        up[:, c * width : (c + 1) * width] = low[c * rows_out : (c + 1) * rows_out].astype(F32)
    outs.append(pltpu.make_async_copy(up, u_out, out_sem.at[1]))
    outs[1].start()
    for index, (begin, out) in enumerate(pieces):
        size = out.shape[0]
        ins[1 + index].wait()
        wide[begin : begin + size] = low[begin : begin + size].astype(F32)
        copy = pltpu.make_async_copy(wide.at[begin : begin + size], out, out_sem.at[2 + index])
        copy.start()
        outs.append(copy)

    def share(row):
        part = vsum_ref[row : row + 1, 0:rows_out]
        for s in range(1, shards):
            part = jnp.where(w == s, vsum_ref[row : row + 1, s * rows_out : (s + 1) * rows_out], part)
        return part.reshape(rows_out)

    for row, ref in enumerate((g1_out, b1_out, cb_out, pb_out, g2_out, b2_out, bd_out)):
        ref[...] = share(row)
    per = rows_up // rows_out
    for q in range(per):
        part = None
        for s in range(shards):
            group = s * per + q
            row, place = 7 + group // shards, group % shards
            piece = vsum_ref[row : row + 1, place * rows_out : (place + 1) * rows_out]
            part = piece if part is None else jnp.where(w == s, piece, part)
        bu_out[q * rows_out : (q + 1) * rows_out] = part.reshape(rows_out)
    loss_out[0, 0] = vsum_ref[7 + parts, 0] / (total_ref[0, 0] * width)
    for copy in outs:
        copy.wait()


def unpack(shards, rows_f, rows_l, hidden, sums, vsum, total, grad):
    tokens, width = grad.shape
    rows_out, rows_up = width // shards, hidden // shards
    vmem = pl.BlockSpec(memory_space=pltpu.VMEM)
    hbm = pl.BlockSpec(memory_space=pl.ANY)
    square = jax.ShapeDtypeStruct((rows_out, width), F32)
    vector = jax.ShapeDtypeStruct((rows_out,), F32)
    return pl.pallas_call(
        functools.partial(unpack_kernel, shards, rows_f, rows_l),
        out_shape=(
            jax.ShapeDtypeStruct((tokens, width), F32), square, square, square, square, square,
            jax.ShapeDtypeStruct((rows_out, hidden), F32), jax.ShapeDtypeStruct((rows_up, width), F32),
            vector, vector, vector, vector, vector, vector, vector, jax.ShapeDtypeStruct((rows_up,), F32),
            jax.ShapeDtypeStruct((1, 1), F32),
        ),
        in_specs=[hbm, vmem, vmem, hbm],
        out_specs=(hbm,) * 8 + (vmem,) * 8 + (pl.BlockSpec(memory_space=pltpu.SMEM),),
        scratch_shapes=[
            pltpu.VMEM(sums.shape, BF16),
            pltpu.VMEM(sums.shape, F32),
            pltpu.VMEM((rows_out, hidden), F32),
            pltpu.SemaphoreType.DMA((7,)),
            pltpu.SemaphoreType.DMA((8,)),
        ],
        compiler_params=pltpu.CompilerParams(vmem_limit_bytes=40 * 2**20),
        cost_estimate=pl.CostEstimate(flops=10**6, bytes_accessed=12 * 2**20, transcendentals=0),
        name="unpack",
    )(sums, vsum, total, grad)


PARTS = 2


def start_kernel(
    lines, shards, x_ref, wk_ref, wv_ref, wp_ref, wq_ref, wo_ref, wu_ref, wd_ref,
    g1_ref, b1_ref, cb_ref, pb_ref, g2_ref, b2_ref, bd_ref, bu_ref, mask_ref, far_ref, near_ref,
    k_ref, v_ref, unit_ref, pk_ref, table_ref, qc_ref, qp_ref, weights_ref, wo_out, wu_out, wd_out, vectors_ref, total_ref,
    x_all, k_buf, v_buf, u_buf, pk_buf, t_buf, vec_src, vec_buf, cnt_buf, cnt_acc,
    up_send, up_recv, down_send, down_recv, b_send, b_recv, c_send, c_recv,
    y_send, y_recv, yc_send, yc_recv, d_send, d_recv, s_send, s_recv, out_sem, pos_sem, own_sem,
):
    tokens, width = x_ref.shape
    piece = tokens // PARTS
    half = width // 2
    chunks = pk_buf.shape[0] // BLK
    ctx = lax.axis_index("ctx")
    w = lax.axis_index("wsh")
    core = lax.rem(ctx, 2)
    b = lax.rem(ctx // 2, 2)
    a = ctx // 4

    def at(a_to, b_to, core_to):
        return (a_to * 2 + b_to) * 2 + core_to

    def shard_peer(s):
        return (ctx, lax.rem(w + s, shards))

    def line_peer(s):
        return (at(lax.rem(a + s, lines), b, core), w)

    core_peer = (at(a, b, 1 - core), w)
    b_peer = (at(a, 1 - b, core), w)
    peers = [core_peer, b_peer] + [line_peer(s) for s in range(1, lines)] + [shard_peer(s) for s in range(1, shards)]
    barrier = pltpu.get_barrier_semaphore()
    for peer in peers:
        pl.semaphore_signal(barrier, inc=1, device_id=peer, device_id_type=MESH)

    def remote(src, dst, send, recv, peer):
        return pltpu.make_async_remote_copy(
            src_ref=src, dst_ref=dst, send_sem=send, recv_sem=recv, device_id=peer, device_id_type=MESH
        )

    def block(slot):
        return aligned(slot * tokens, tokens)

    x_all[block(ctx)] = x_ref[...]
    rows_out = wq_ref.shape[0]
    quarter = rows_out // 2
    rows_up = wd_ref.shape[0]
    part_up = rows_up // 4
    weight_in = (wk_ref, wv_ref, wp_ref, wq_ref, wo_ref, wu_ref)
    weight_to = tuple(weights_ref.at[m] for m in range(4)) + (wo_out, wu_out)
    own_copies = [
        pltpu.make_async_copy(ref, to.at[aligned(w * rows_out, rows_out)], own_sem.at[m])
        for m, (ref, to) in enumerate(zip(weight_in, weight_to))
    ]
    own_copies.append(pltpu.make_async_copy(wd_ref, wd_out.at[aligned(w * rows_up, rows_up)], own_sem.at[6]))
    for copy in own_copies:
        copy.start()
    vec_src[...] = jnp.zeros_like(vec_src)
    for row, ref in enumerate((g1_ref, b1_ref, cb_ref, pb_ref, g2_ref, b2_ref, bd_ref)):
        vec_src[row : row + 1] = ref[...].astype(F32).reshape(1, rows_out)
    bias_rows = rows_up // rows_out
    for q in range(bias_rows):
        vec_src[7 + q : 8 + q] = bu_ref[q * rows_out : (q + 1) * rows_out].astype(F32).reshape(1, rows_out)
    cnt_acc[0:8] = jnp.broadcast_to(jnp.sum(mask_ref[...].astype(F32), axis=1, keepdims=True), (8, BLK))
    pl.semaphore_wait(barrier, len(peers))

    def x_copy(slot, h, send, recv, peer):
        rows = aligned(slot * tokens + h * piece, piece)
        return remote(x_all.at[rows], x_all.at[rows], send, recv, peer)

    def up_copy(p, h):
        peer = (at(jnp.minimum(a + 1, lines - 1), b, core), w)
        return x_copy(at(p, b, core), h, up_send.at[p, h], up_recv.at[p, h], peer)

    def down_copy(p, h):
        peer = (at(jnp.maximum(a - 1, 0), b, core), w)
        return x_copy(at(p, b, core), h, down_send.at[p, h], down_recv.at[p, h], peer)

    def b_copy(p, h, b_from):
        return x_copy(at(p, b_from, core), h, b_send.at[p, h], b_recv.at[p, h], b_peer)

    def c_copy(p, far, b_from, core_from):
        rows = block(at(p, b_from, core_from))
        return remote(x_all.at[rows], x_all.at[rows], c_send.at[far, p], c_recv.at[far, p], core_peer)

    def weight_copy(m, s):
        rows = aligned(w * rows_out + core * quarter, quarter)
        src = weight_in[m].at[aligned(core * quarter, quarter)]
        return remote(src, weight_to[m].at[rows], y_send.at[m, s - 1], y_recv.at[m, s - 1], shard_peer(s))

    def weight_pass(m, s):
        rows = aligned(lax.rem(w + shards - s, shards) * rows_out + core * quarter, quarter)
        return remote(
            weight_to[m].at[rows], weight_to[m].at[rows], yc_send.at[m, s - 1], yc_recv.at[m, s - 1], core_peer
        )

    def down_rows(s, b_of, core_of):
        owner = lax.rem(w + shards - s, shards)
        return aligned(owner * rows_up + (b_of * 2 + core_of) * part_up, part_up)

    def down_weight(s):
        src = wd_ref.at[aligned((b * 2 + core) * part_up, part_up)]
        return remote(src, wd_out.at[down_rows(0, b, core)], d_send.at[0, s - 1], d_recv.at[0, s - 1], shard_peer(s))

    def down_pass(kind, s):
        rows = down_rows(s, 1 - b if kind == 3 else b, core)
        peer = b_peer if kind == 1 else core_peer
        return remote(wd_out.at[rows], wd_out.at[rows], d_send.at[kind, s - 1], d_recv.at[kind, s - 1], peer)

    def vec_copy(s):
        return remote(vec_src, vec_buf.at[s - 1], s_send.at[s - 1], s_recv.at[s - 1], shard_peer(s))

    for s in range(1, shards):
        vec_copy(s).start()
    for h in range(PARTS):

        @pl.when(a + 1 < lines)
        def _():
            up_copy(a, h).start()

        @pl.when(a >= 1)
        def _():
            down_copy(a, h).start()

        b_copy(a, h, b).start()
    c_copy(a, 0, b, core).start()
    for m in range(len(weight_in)):
        for s in range(1, shards):
            weight_copy(m, s).start()
    for s in range(1, shards):
        down_weight(s).start()

    stages = [[core_peer], [b_peer], [line_peer(s) for s in range(1, lines)], [shard_peer(s) for s in range(1, shards)]]
    slots = []
    place = 0
    for stage in stages:
        slots.append(place)
        place += len(stage)

    def cnt_copy(stage, index):
        slot = slots[stage] + index
        sem = shards - 1 + slot
        return remote(cnt_acc.at[pl.ds(stage * 8, 8)], cnt_buf.at[slot], s_send.at[sem], s_recv.at[sem], stages[stage][index])

    def cnt_start(stage):
        for index in range(len(stages[stage])):
            cnt_copy(stage, index).start()

    def cnt_finish(stage):
        total = cnt_acc[stage * 8 : stage * 8 + 8]
        for index in range(len(stages[stage])):
            cnt_copy(stage, index).wait()
            total = total + cnt_buf[slots[stage] + index]
        cnt_acc[(stage + 1) * 8 : (stage + 2) * 8] = total

    cnt_start(0)

    def table_step(d, _):
        sin_far, cos_far = far_ref[0, pl.ds(d, 1)], far_ref[1, pl.ds(d, 1)]
        sin_near, cos_near = near_ref[0], near_ref[1]
        rows = aligned(d * BLK, BLK)
        t_buf[rows, :half] = (sin_far * cos_near - cos_far * sin_near).astype(BF16)
        t_buf[rows, half:] = (cos_far * cos_near + sin_far * sin_near).astype(BF16)
        return 0

    lax.fori_loop(0, chunks, table_step, 0)
    table_out = pltpu.make_async_copy(t_buf, table_ref, pos_sem.at[0])
    table_out.start()
    cnt_finish(0)
    cnt_start(1)
    lane_to = lax.broadcasted_iota(jnp.int32, (rows_out, width), 1)
    lane_from = lax.broadcasted_iota(jnp.int32, (rows_out, width), 0)
    row_at = lax.broadcasted_iota(jnp.int32, (16, width), 0)

    def spread(values, place):
        return dot_nn(values.astype(BF16), (lane_to == lane_from + place * rows_out).astype(BF16))

    def placed(values, owner):
        full = jnp.where(row_at < 7, spread(values, owner), 0.0)
        for q in range(bias_rows):
            group = owner * bias_rows + q
            row = jnp.broadcast_to(values[7 + q : 8 + q], values.shape)
            full = full + jnp.where(row_at == 7 + group // shards, spread(row, lax.rem(group, shards)), 0.0)
        return full

    vectors = placed(vec_src[...], w)
    for s in range(1, shards):
        vec_copy(s).wait()
        vectors = vectors + placed(vec_buf[s - 1], lax.rem(w + shards - s, shards))
    vectors_ref[...] = vectors
    gain, offset = vectors_ref[0:1], vectors_ref[1:2]
    cnt_finish(1)
    cnt_start(2)
    for copy in own_copies[:4]:
        copy.wait()
    for m in range(2):
        for s in range(1, shards):
            weight_copy(m, s).wait()
            weight_pass(m, s).start()
    for m in range(2):
        for s in range(1, shards):
            weight_pass(m, s).wait()

    def unit_of(rows):
        values = rows.astype(F32)
        center = values - jnp.mean(values, axis=1, keepdims=True)
        return center * lax.rsqrt(jnp.mean(center * center, axis=1, keepdims=True) + epsilon)

    def out_copies(slot):
        rows = block(slot)
        return (
            pltpu.make_async_copy(k_buf.at[rows], k_ref.at[rows], out_sem.at[0, slot]),
            pltpu.make_async_copy(v_buf.at[rows], v_ref.at[rows], out_sem.at[1, slot]),
            pltpu.make_async_copy(u_buf.at[rows], unit_ref.at[rows], out_sem.at[2, slot]),
        )

    def project(p):
        def one(q, _):
            other_b = lax.rem(q, 2)
            other_core = q // 2

            @pl.when(q == 1)
            def _():
                for h in range(PARTS):
                    b_copy(p, h, b).wait()
                c_copy(p, 1, 1 - b, core).start()

            @pl.when(q == 2)
            def _():
                c_copy(p, 0, b, core).wait()

            @pl.when(q == 3)
            def _():
                c_copy(p, 1, 1 - b, core).wait()

            slot = at(p, b + other_b - 2 * b * other_b, core + other_core - 2 * core * other_core)
            rows = block(slot)
            unit = unit_of(x_all[rows])
            u_buf[rows] = unit.astype(BF16)
            normed = (unit * gain + offset).astype(BF16)
            k_buf[rows] = dot_nn(normed, weights_ref[0]).astype(BF16)
            v_buf[rows] = dot_nn(normed, weights_ref[1]).astype(BF16)
            for copy in out_copies(slot):
                copy.start()
            return 0

        lax.fori_loop(0, 4, one, 0)

    def pos_step(d, _):
        rows = aligned(d * BLK, BLK)
        pk_buf[rows] = dot_nn(t_buf[rows], weights_ref[2]).astype(BF16)
        return 0

    def line_step(s, _):
        low, high = a - 1 - s, a + 1 + s

        for h in range(PARTS):

            @pl.when((s < lines - 1) & (low >= 0))
            def _():
                p = jnp.maximum(low, 0)
                up_copy(p, h).wait_recv()

                @pl.when(a + 1 < lines)
                def _():
                    up_copy(p, h).start()

                b_copy(p, h, b).start()
                if h == PARTS - 1:
                    c_copy(p, 0, b, core).start()

            @pl.when((s < lines - 1) & (high < lines))
            def _():
                p = jnp.minimum(high, lines - 1)
                down_copy(p, h).wait_recv()

                @pl.when(a >= 1)
                def _():
                    down_copy(p, h).start()

                b_copy(p, h, b).start()
                if h == PARTS - 1:
                    c_copy(p, 0, b, core).start()

        @pl.when(s == 0)
        def _():
            for m in range(2, 4):
                for t in range(1, shards):
                    weight_copy(m, t).wait()
                    weight_pass(m, t).start()

        @pl.when(s == 1)
        def _():
            for m in range(2, 4):
                for t in range(1, shards):
                    weight_pass(m, t).wait()

        @pl.when(s == lines - 1)
        def _():
            for m in range(4, 6):
                for t in range(1, shards):
                    weight_copy(m, t).wait()
                    weight_pass(m, t).start()

        @pl.when(a - s >= 0)
        def _():
            project(jnp.maximum(a - s, 0))

        @pl.when((s >= 1) & (a + s < lines))
        def _():
            project(jnp.minimum(a + s, lines - 1))

        @pl.when(s >= 1)
        def _():
            lax.fori_loop(chunks * (s - 1) // (lines - 1), chunks * s // (lines - 1), pos_step, 0)

        return 0

    lax.fori_loop(0, lines, line_step, 0)
    pos_out = pltpu.make_async_copy(pk_buf, pk_ref, pos_sem.at[1])
    pos_out.start()
    normed = (unit_of(x_ref[...]) * gain + offset).astype(BF16)
    queries = dot_nn(normed, weights_ref[3]).astype(BF16).astype(F32)
    qc_ref[...] = ((queries + vectors_ref[2:3]) * 0.125).astype(BF16)
    qp_ref[...] = ((queries + vectors_ref[3:4]) * 0.125).astype(BF16)
    cnt_finish(2)
    cnt_start(3)

    for s in range(1, shards):
        down_weight(s).wait()
        down_pass(1, s).start()
        down_pass(2, s).start()

    def sends_done(p, _):
        for h in range(PARTS):

            @pl.when((a + 1 < lines) & (p <= a))
            def _():
                up_copy(p, h).wait_send()

            @pl.when((a >= 1) & (p >= a))
            def _():
                down_copy(p, h).wait_send()

        return 0

    lax.fori_loop(0, lines, sends_done, 0)

    def outs_done(slot, _):
        for copy in out_copies(slot):
            copy.wait()
        return 0

    lax.fori_loop(0, 4 * lines, outs_done, 0)
    for m in range(4, 6):
        for s in range(1, shards):
            weight_pass(m, s).wait()
    for s in range(1, shards):
        down_pass(1, s).wait()
        down_pass(3, s).start()
    for s in range(1, shards):
        down_pass(2, s).wait()
        down_pass(3, s).wait()
    for copy in own_copies[4:]:
        copy.wait()
    table_out.wait()
    pos_out.wait()
    cnt_finish(3)
    total_ref[...] = cnt_acc[4 * 8 : 5 * 8]


def start(lines, shards, cid, limit, x, weights, vectors, mask, far, near):
    tokens, width = x.shape
    hidden = weights[5].shape[1]
    rows_out = weights[0].shape[0]
    members = 4 * lines
    keys = members * tokens
    span = limit * BLK
    vmem = pl.BlockSpec(memory_space=pltpu.VMEM)
    hbm = pl.BlockSpec(memory_space=pl.ANY)
    small = 2 * (shards - 1) + 1 + 1 + lines - 1
    dma = pltpu.SemaphoreType.DMA
    other = shards - 1
    return pl.pallas_call(
        functools.partial(start_kernel, lines, shards),
        out_shape=(
            jax.ShapeDtypeStruct((keys, width), BF16),
            jax.ShapeDtypeStruct((keys, width), BF16),
            jax.ShapeDtypeStruct((keys, width), BF16),
            jax.ShapeDtypeStruct((span, width), BF16),
            jax.ShapeDtypeStruct((span, width), BF16),
            jax.ShapeDtypeStruct((tokens, width), BF16),
            jax.ShapeDtypeStruct((tokens, width), BF16),
            jax.ShapeDtypeStruct((4, width, width), BF16),
            jax.ShapeDtypeStruct((width, width), BF16),
            jax.ShapeDtypeStruct((width, hidden), BF16),
            jax.ShapeDtypeStruct((hidden, width), BF16),
            jax.ShapeDtypeStruct((16, width), F32),
            jax.ShapeDtypeStruct((8, BLK), F32),
        ),
        in_specs=[vmem] + [hbm] * 7 + [vmem] * 11,
        out_specs=(hbm,) * 5 + (vmem,) * 3 + (hbm,) * 3 + (vmem,) * 2,
        scratch_shapes=[
            pltpu.VMEM((keys, width), BF16),
            pltpu.VMEM((keys, width), BF16),
            pltpu.VMEM((keys, width), BF16),
            pltpu.VMEM((keys, width), BF16),
            pltpu.VMEM((span, width), BF16),
            pltpu.VMEM((span, width), BF16),
            pltpu.VMEM((16, rows_out), F32),
            pltpu.VMEM((other, 16, rows_out), F32),
            pltpu.VMEM((lines + shards, 8, BLK), F32),
            pltpu.VMEM((5 * 8, BLK), F32),
        ]
        + [dma((lines, PARTS))] * 6
        + [dma((2, lines))] * 2
        + [dma((6, other))] * 4
        + [dma((4, other))] * 2
        + [dma((small,))] * 2
        + [dma((3, members)), dma((2,)), dma((7,))],
        compiler_params=pltpu.CompilerParams(collective_id=cid, has_side_effects=True, vmem_limit_bytes=60 * 2**20),
        cost_estimate=pl.CostEstimate(flops=6 * 10**9, bytes_accessed=20 * 2**20, transcendentals=0),
        name="start",
    )(x, *weights, *vectors, mask, far, near)


GELU_SCALE = math.sqrt(2.0 / math.pi)


def middle_kernel(
    shards, rows_f, mask_ref, x_ref, mixed_ref, teacher_ref, out_grad_ref, vectors_ref, total_ref, wo_ref, wu_ref, wd_ref,
    out_ref, hidden_ref, gm_ref, mine_ref, theirs_ref, vec_ref,
    wo, wu, wd, slope, act, gf_ref, landed, sem, send_sem, recv_sem,
):
    tokens, width = x_ref.shape
    parts = wu.shape[1] // width
    ctx = lax.axis_index("ctx")
    core = lax.rem(ctx, 2)
    b = lax.rem(ctx // 2, 2)
    core_peer = (ctx + 1 - 2 * core, lax.axis_index("wsh"))
    barrier = pltpu.get_barrier_semaphore()
    pl.semaphore_signal(barrier, inc=1, device_id=core_peer, device_id_type=MESH)
    copies = [
        pltpu.make_async_copy(src, dst, sem.at[m])
        for m, (src, dst) in enumerate(((wo_ref, wo), (wu_ref, wu), (wd_ref, wd)))
    ]
    for copy in copies:
        copy.start()
    half, quarter = rows_f // 2, rows_f // 4

    def give(begin, size, index):
        rows = aligned((1 - core) * half + begin, size)
        return pltpu.make_async_remote_copy(
            src_ref=gf_ref.at[:, rows], dst_ref=landed.at[:, begin : begin + size],
            send_sem=send_sem.at[index], recv_sem=recv_sem.at[index], device_id=core_peer, device_id_type=MESH,
        )

    gain, offset, down_bias = vectors_ref[4:5], vectors_ref[5:6], vectors_ref[6:7]
    mixed = mixed_ref[...].astype(BF16)
    copies[0].wait()
    hidden = x_ref[...].astype(F32) + dot_nn(mixed, wo[...])
    center = hidden - jnp.mean(hidden, axis=1, keepdims=True)
    inverse = lax.rsqrt(jnp.mean(center * center, axis=1, keepdims=True) + epsilon)
    unit = center * inverse
    normed = (unit * gain + offset).astype(BF16)
    result = hidden + down_bias
    copies[1].wait()
    copies[2].wait()
    for c in range(parts):
        cols = slice(c * width, (c + 1) * width)
        v = dot_nn(normed, wu[:, cols]) + vectors_ref[7 + c : 8 + c]
        square = v * v
        t = jnp.tanh(GELU_SCALE * (v + 0.044715 * (square * v)))
        act[:, cols] = (0.5 * v * (1.0 + t)).astype(BF16)
        slope[:, cols] = 0.5 * (1.0 + t) + 0.5 * v * (1.0 - t * t) * (GELU_SCALE * (1.0 + 3.0 * 0.044715 * square))
        result = result + dot_nn(act[:, cols], wd[cols])
    out_ref[...] = result.astype(BF16)
    mask = jnp.broadcast_to(mask_ref[...].astype(F32), (8, tokens)).T[:, 0:1]
    error = result - teacher_ref[...].astype(F32)
    masked = mask * error
    count = jnp.sum(total_ref[0:1, 0:1], axis=1, keepdims=True)
    grad_result = out_grad_ref[...].astype(F32) + (2.0 / (count * width)) * masked
    branch = grad_result.astype(BF16)
    vec_ref[...] = jnp.zeros_like(vec_ref)
    vec_ref[7 + parts : 8 + parts] = jnp.broadcast_to(
        jnp.sum(jnp.sum(masked * error, axis=1, keepdims=True), axis=0, keepdims=True), (1, width)
    )
    vec_ref[6:7] = jnp.sum(branch.astype(F32), axis=0, keepdims=True)
    rows_up = wd.shape[0] // shards
    rows_out = width // shards
    used = 2 * rows_up + rows_out
    if used < rows_f:
        gf_ref[:, used:] = jnp.zeros((shards, rows_f - used, width), BF16)
    grad_normed = jnp.zeros((tokens, width), F32)
    for c in range(parts):
        cols = slice(c * width, (c + 1) * width)
        grad_pre = (dot_nt(branch, wd[cols]) * slope[:, cols]).astype(BF16)
        vec_ref[7 + c : 8 + c] = jnp.sum(grad_pre.astype(F32), axis=0, keepdims=True)
        grad_normed = grad_normed + dot_nt(grad_pre, wu[:, cols])
        up = dot_tn(normed, grad_pre).astype(BF16)
        down = dot_tn(act[:, cols], branch).astype(BF16)
        for s in range(shards):
            gf_ref[s, c * rows_out : (c + 1) * rows_out] = up[s * rows_out : (s + 1) * rows_out]
        step = min(rows_up, width)
        for begin in range(0, width, step):
            row = c * width + begin
            place = rows_up + row % rows_up
            gf_ref[row // rows_up, place : place + step] = down[begin : begin + step]
    pl.semaphore_wait(barrier, 1)
    early = max(0, 2 * rows_up - half)
    if early:
        give(0, early, 0).start()
    vec_ref[4:5] = jnp.sum(grad_normed * unit, axis=0, keepdims=True)
    vec_ref[5:6] = jnp.sum(grad_normed, axis=0, keepdims=True)
    scaled = grad_normed * gain
    grad_hidden = grad_result + inverse * (
        scaled - jnp.mean(scaled, axis=1, keepdims=True) - unit * jnp.mean(scaled * unit, axis=1, keepdims=True)
    )
    hidden_ref[...] = grad_hidden
    attn = grad_hidden.astype(BF16)
    gm_ref[...] = dot_nt(attn, wo[...]).astype(BF16)
    outer = dot_tn(mixed, attn).astype(BF16)
    for s in range(shards):
        gf_ref[s, 2 * rows_up : used] = outer[s * rows_out : (s + 1) * rows_out]
    give(early, half - early, 1).start()
    if early:
        give(0, early, 0).wait()
    give(early, half - early, 1).wait()
    for ref, place in ((theirs_ref, 1 - b), (mine_ref, b)):
        own = gf_ref[:, aligned(core * half + place * quarter, quarter)].astype(F32)
        ref[...] = (own + landed[:, aligned(place * quarter, quarter)].astype(F32)).astype(BF16)


def middle(shards, rows_f, cid, mask, x, mixed, teacher, out_grad, vectors, total, wo, wu, wd):
    tokens, width = x.shape
    hidden = wu.shape[1]
    vmem = pl.BlockSpec(memory_space=pltpu.VMEM)
    hbm = pl.BlockSpec(memory_space=pl.ANY)
    return pl.pallas_call(
        functools.partial(middle_kernel, shards, rows_f),
        out_shape=(
            jax.ShapeDtypeStruct((tokens, width), BF16),
            jax.ShapeDtypeStruct((tokens, width), F32),
            jax.ShapeDtypeStruct((tokens, width), BF16),
            jax.ShapeDtypeStruct((shards, rows_f // 4, width), BF16),
            jax.ShapeDtypeStruct((shards, rows_f // 4, width), BF16),
            jax.ShapeDtypeStruct((16, width), F32),
        ),
        in_specs=[vmem] * 7 + [hbm] * 3,
        out_specs=(vmem,) * 6,
        scratch_shapes=[
            pltpu.VMEM((width, width), BF16),
            pltpu.VMEM((width, hidden), BF16),
            pltpu.VMEM((hidden, width), BF16),
            pltpu.VMEM((tokens, hidden), F32),
            pltpu.VMEM((tokens, hidden), BF16),
            pltpu.VMEM((shards, rows_f, width), BF16),
            pltpu.VMEM((shards, rows_f // 2, width), BF16),
            pltpu.SemaphoreType.DMA((3,)),
            pltpu.SemaphoreType.DMA((2,)),
            pltpu.SemaphoreType.DMA((2,)),
        ],
        compiler_params=pltpu.CompilerParams(collective_id=cid, has_side_effects=True, vmem_limit_bytes=56 * 2**20),
        cost_estimate=pl.CostEstimate(flops=4 * 10**9, bytes_accessed=20 * 2**20, transcendentals=10**6),
        name="middle",
    )(mask, x, mixed, teacher, out_grad, vectors, total, wo, wu, wd)


def body(
    inputs, block_perm, seq_lengths, loss_mask, teacher, out_grad, gain_one, bias_one, w_query, w_key, w_value,
    w_output, w_pos, content_bias, position_bias, gain_two, bias_two, w_up, bias_up, w_down, bias_down,
):
    width = inputs.shape[2]
    shards = lax.axis_size("wsh")
    members = lax.axis_size("ctx")
    lines = members // 4
    hidden = bias_up.shape[0] * shards
    blocks = block_perm.shape[1]
    limit = blocks // 2 + 1
    rows_up, rows_out = hidden // shards, width // shards

    frequency = np.exp(np.arange(width // 2) * (-2.0 * math.log(10000.0) / width))
    far_angle = (np.arange(-(-limit // 8) * 8) * BLK + (BLK - 1))[:, None] * frequency[None]
    near_angle = np.arange(BLK)[:, None] * frequency[None]
    far = jnp.asarray(np.stack([np.sin(far_angle), np.cos(far_angle)]), F32)
    near = jnp.asarray(np.stack([np.sin(near_angle), np.cos(near_angle)]), F32)

    keys, values, unit_all, pos_keys, table, qc, qp, weights, wo, wu, wd, vectors, total = start(
        lines, shards, 0, limit, inputs[0], (w_key, w_value, w_pos, w_query, w_output, w_up, w_down),
        (gain_one, bias_one, content_bias, position_bias, gain_two, bias_two, bias_down, bias_up), loss_mask, far, near,
    )
    mixed, linv, probs = attn_fwd(block_perm, seq_lengths, qc, qp, keys, values, pos_keys, blocks, limit)

    step = 16 * lines
    pieces = -(-(2 * rows_up + rows_out) // (4 * step))
    split = min(3, pieces)
    chunks_f = tuple((pieces * (i + 1) // split - pieces * i // split) * step for i in range(split))
    rows_f = 4 * step * pieces
    rows_l = -(-2 * rows_out // (4 * step)) * 4 * step
    output, grad_hidden, grad_mixed, mine, theirs, vec = middle(
        shards, rows_f, 2, loss_mask, inputs[0], mixed, teacher[0], out_grad[0], vectors, total, wo, wu, wd
    )
    come = lax.ppermute(theirs, "ctx", [(i, i ^ 2) for i in range(members)])
    grad_query, bias_grads, dk_t, dv_t, dpk_t = attn_bwd(
        block_perm, seq_lengths, qc, qp, keys, values, pos_keys, probs, linv, grad_mixed, mixed, blocks, limit
    )
    grad_input, sums, vsum = finish(
        lines, shards, chunks_f, rows_l, 1, mine, come, dk_t, dv_t, unit_all, dpk_t, table, weights, grad_query,
        inputs[0], vectors, total, vec, bias_grads, grad_hidden,
    )
    (
        grad_input, g_query, g_key, g_value, g_output, g_pos, g_up, g_down,
        v_g1, v_b1, v_cb, v_pb, v_g2, v_b2, v_bd, v_bu, loss,
    ) = unpack(shards, rows_f, rows_l, hidden, sums, vsum, total, grad_input)
    return (
        output[None], loss.reshape(()), grad_input[None], v_g1, v_b1, g_query, g_key, g_value, g_output, g_pos,
        v_cb, v_pb, v_g2, v_b2, g_up, v_bu, g_down, v_bd,
    )


def solution(mesh):
    rows = P("wsh", "ctx", None)
    vector = P("wsh")
    matrix = P("wsh", None)
    placed = (
        rows, matrix, matrix, P("wsh", "ctx"), rows, rows, vector, vector, matrix, matrix, matrix, matrix, matrix,
        vector, vector, vector, vector, matrix, vector, matrix, vector,
    )
    out = (
        rows, P(), rows, vector, vector, matrix, matrix, matrix, matrix, matrix, vector, vector, vector, vector,
        matrix, vector, matrix, vector,
    )
    return jax.shard_map(body, mesh=mesh, in_specs=placed, out_specs=out, check_vma=False)
```

```python
import functools
import math

import jax
import jax.numpy as jnp
import numpy as np
from jax import lax
from jax.experimental import pallas as pl
from jax.experimental.pallas import tpu as pltpu
from jax.sharding import PartitionSpec as P

HEADS = 8
HEAD = 64
PAIRS = HEADS // 2
BLK = 128
ROWS = HEADS * BLK
NEG = -1e30
epsilon = 1e-05
F32 = jnp.float32
BF16 = jnp.bfloat16


def dot_nt(a, b):
    return lax.dot_general(a, b, (((1,), (1,)), ((), ())), preferred_element_type=F32)


def dot_nn(a, b):
    return lax.dot_general(a, b, (((1,), (0,)), ((), ())), preferred_element_type=F32)


def dot_tn(a, b):
    return lax.dot_general(a, b, (((0,), (0,)), ((), ())), preferred_element_type=F32)


def iotas():
    row = lax.broadcasted_iota(jnp.int32, (BLK, BLK), 0)
    col = lax.broadcasted_iota(jnp.int32, (BLK, BLK), 1)
    return row, col


def read_places(perm_ref, lengths_ref, meta, blocks, count):
    device = lax.axis_index("ctx")
    meta[0] = perm_ref[0, 2 * device]
    meta[1] = perm_ref[0, 2 * device + 1]

    def place(slot, _):
        meta[2 + perm_ref[0, slot]] = slot
        return 0

    lax.fori_loop(0, blocks, place, 0)
    end = jnp.int32(0)
    for e in range(count):
        end = end + lengths_ref[0, e]
        meta[2 + blocks + e] = end


def block_range(meta, a, blocks, limit):
    qb = meta[a]
    first = qb * BLK
    low = jnp.int32(0)
    for e in range(meta.shape[0] - 2 - blocks):
        end = meta[2 + blocks + e]
        low = jnp.where(first >= end, jnp.maximum(low, end), low)
    lowest = low // BLK
    return qb, lowest, jnp.minimum(qb - lowest + 1, limit)


def stack_heads(pair):
    lane = lax.broadcasted_iota(jnp.int32, pair.shape, 1)
    zero = jnp.zeros_like(pair)
    return jnp.concatenate([jnp.where(lane < HEAD, pair, zero), jnp.where(lane >= HEAD, pair, zero)], axis=0)


def flip_rows(x):
    index = 7 - lax.broadcasted_iota(jnp.int32, (8, BLK), 0)
    slabs = [jnp.take_along_axis(x[8 * g : 8 * g + 8], index, axis=0) for g in reversed(range(BLK // 8))]
    return jnp.concatenate(slabs, axis=0)


def flip_two(x):
    return jnp.concatenate([flip_rows(x[:BLK]), flip_rows(x[BLK:])], axis=0)


def attn_fwd_kernel(
    blocks, limit, perm_ref, lengths_ref, qc_ref, qp_ref, k_ref, v_ref, pk_ref, mixed_ref, linv_ref, p_ref,
    meta, q2c, q2p, prev, top, total, acc, s_scr, p_buf, p_sem,
):
    read_places(perm_ref, lengths_ref, meta, blocks, lengths_ref.shape[1])
    row, col = iotas()
    tri = col <= row

    def p_copy(slot, index):
        return pltpu.make_async_copy(p_buf.at[slot], p_ref.at[index], p_sem.at[slot])

    def one_query_block(a, _):
        qb, lowest, count = block_range(meta, a, blocks, limit)
        rows_a = pl.ds(pl.multiple_of(a * BLK, BLK), BLK)
        pos = qb * BLK + row
        start = jnp.zeros((BLK, BLK), jnp.int32)
        for e in range(meta.shape[0] - 2 - blocks):
            end = meta[2 + blocks + e]
            start = jnp.where(pos >= end, jnp.maximum(start, end), start)
        for hp in range(PAIRS):
            lanes = slice(hp * BLK, (hp + 1) * BLK)
            q2c[hp] = stack_heads(qc_ref[rows_a, lanes].astype(F32)).astype(BF16)
            q2p[hp] = stack_heads(qp_ref[rows_a, lanes].astype(F32)).astype(BF16)
        prev[...] = jnp.zeros_like(prev)
        top[...] = jnp.full_like(top, NEG)
        total[...] = jnp.zeros_like(total)
        acc[...] = jnp.zeros_like(acc)

        def score_step(d, _):
            kb = qb - d
            off = pl.multiple_of(meta[2 + kb] * BLK, BLK)
            place = kb * BLK + col
            bias = jnp.where((place >= start) & (place <= pos), 0.0, NEG).astype(F32)
            drow = pl.multiple_of(d * BLK, BLK)
            for hp in range(PAIRS):
                lanes = slice(hp * BLK, (hp + 1) * BLK)
                s = dot_nt(q2c[hp], k_ref[pl.ds(off, BLK), lanes])
                r = dot_nt(q2p[hp], pk_ref[pl.ds(drow, BLK), lanes])
                for half in range(2):
                    part = slice(half * BLK, (half + 1) * BLK)
                    rows = slice((2 * hp + half) * BLK, (2 * hp + half + 1) * BLK)
                    rot = pltpu.roll(r[part], 1, 1, stride=1, stride_axis=0)
                    score = s[part] + jnp.where(tri, rot, prev[rows]) + bias
                    prev[rows] = rot
                    s_scr[d, rows] = score
                    top[rows] = jnp.maximum(top[rows], score)
            return 0

        lax.fori_loop(0, count, score_step, 0)
        for h in range(HEADS):
            rows = slice(h * BLK, (h + 1) * BLK)
            top[rows] = jnp.broadcast_to(jnp.max(top[rows], axis=1, keepdims=True), (BLK, BLK))

        def mix_step(d, _):
            kb = qb - d
            off = pl.multiple_of(meta[2 + kb] * BLK, BLK)
            slot = lax.rem(d, 2)

            @pl.when(d >= 2)
            def _():
                p_copy(slot, 0).wait()

            for hp in range(PAIRS):
                lanes = slice(hp * BLK, (hp + 1) * BLK)
                rows = slice(2 * hp * BLK, 2 * (hp + 1) * BLK)
                p = jnp.exp(s_scr[d, rows] - top[rows])
                total[rows] += p
                p_buf[slot, rows] = flip_two(p).astype(BF16)
                acc[hp] += dot_nn(p.astype(BF16), v_ref[pl.ds(off, BLK), lanes])
            p_copy(slot, a * limit + d).start()
            return 0

        lax.fori_loop(0, count, mix_step, 0)
        p_copy(lax.rem(count - 1, 2), 0).wait()

        @pl.when(count >= 2)
        def _():
            p_copy(lax.rem(count, 2), 0).wait()

        lane = lax.broadcasted_iota(jnp.int32, (BLK, BLK), 1)
        for hp in range(PAIRS):
            lanes = slice(hp * BLK, (hp + 1) * BLK)
            parts = []
            for half in range(2):
                h = 2 * hp + half
                rows = slice(h * BLK, (h + 1) * BLK)
                inv = 1.0 / jnp.sum(total[rows], axis=1, keepdims=True)
                inv = jnp.broadcast_to(inv, (BLK, BLK))
                linv_ref[a, rows] = inv
                parts.append(acc[hp, half * BLK : (half + 1) * BLK] * inv)
            mixed_ref[rows_a, lanes] = jnp.where(lane < HEAD, parts[0], parts[1])
        return 0

    lax.fori_loop(0, 2, one_query_block, 0)


def attn_fwd(perm, lengths, qc, qp, k, v, pk, blocks, limit):
    tokens, width = qc.shape
    vmem = pl.BlockSpec(memory_space=pltpu.VMEM)
    return pl.pallas_call(
        functools.partial(attn_fwd_kernel, blocks, limit),
        out_shape=(
            jax.ShapeDtypeStruct((tokens, width), F32),
            jax.ShapeDtypeStruct((2, ROWS, BLK), F32),
            jax.ShapeDtypeStruct((2 * limit, ROWS, BLK), BF16),
        ),
        in_specs=[pl.BlockSpec(memory_space=pltpu.SMEM)] * 2 + [vmem] * 5,
        out_specs=(vmem, vmem, pl.BlockSpec(memory_space=pl.ANY)),
        scratch_shapes=[
            pltpu.SMEM((2 + blocks + lengths.shape[1],), jnp.int32),
            pltpu.VMEM((PAIRS, 2 * BLK, BLK), BF16),
            pltpu.VMEM((PAIRS, 2 * BLK, BLK), BF16),
            pltpu.VMEM((ROWS, BLK), F32),
            pltpu.VMEM((ROWS, BLK), F32),
            pltpu.VMEM((ROWS, BLK), F32),
            pltpu.VMEM((PAIRS, 2 * BLK, BLK), F32),
            pltpu.VMEM((limit, ROWS, BLK), F32),
            pltpu.VMEM((2, ROWS, BLK), BF16),
            pltpu.SemaphoreType.DMA((2,)),
        ],
        compiler_params=pltpu.CompilerParams(vmem_limit_bytes=56 * 2**20),
        cost_estimate=pl.CostEstimate(flops=3 * 10**9, bytes_accessed=20 * 2**20, transcendentals=4 * 10**6),
        name="attn_fwd",
    )(perm, lengths, qc, qp, k, v, pk)


def attn_bwd_kernel(
    blocks, limit, perm_ref, lengths_ref, qc_ref, qp_ref, k_ref, v_ref, pk_ref, p_ref, linv_ref, gm_ref, mixed_ref,
    dq_ref, bias_ref, dk_ref, dv_ref, dpk_ref,
    meta, q2c_t, q2p_t, gm2, gm2_t, dd, carry, dqk, dqp, dpk, p_buf, p_sem,
):
    read_places(perm_ref, lengths_ref, meta, blocks, lengths_ref.shape[1])
    row, col = iotas()
    tri = col <= BLK - 1 - row
    dk_ref[...] = jnp.zeros_like(dk_ref)
    dv_ref[...] = jnp.zeros_like(dv_ref)
    dpk[...] = jnp.zeros_like(dpk)
    bias_ref[...] = jnp.zeros_like(bias_ref)

    def p_copy(slot, index):
        return pltpu.make_async_copy(p_ref.at[index], p_buf.at[slot], p_sem.at[slot])

    def one_query_block(a, _):
        qb, lowest, count = block_range(meta, a, blocks, limit)
        rows_a = pl.ds(pl.multiple_of(a * BLK, BLK), BLK)
        p_copy(0, a * limit + count - 1).start()
        for hp in range(PAIRS):
            lanes = slice(hp * BLK, (hp + 1) * BLK)
            rows = slice(2 * hp * BLK, 2 * (hp + 1) * BLK)
            q2c_t[hp] = stack_heads(flip_rows(qc_ref[rows_a, lanes].astype(F32))).T.astype(BF16)
            q2p_t[hp] = stack_heads(flip_rows(qp_ref[rows_a, lanes].astype(F32))).T.astype(BF16)
            g = stack_heads(gm_ref[rows_a, lanes].astype(F32))
            scaled = flip_two(g * linv_ref[a, rows])
            gm2[hp] = scaled.astype(BF16)
            gm2_t[hp] = scaled.T.astype(BF16)
            pair = flip_rows(mixed_ref[rows_a, lanes])
            dd[rows] = jnp.broadcast_to(
                jnp.sum(scaled * jnp.concatenate([pair, pair], axis=0), axis=1, keepdims=True), (2 * BLK, BLK)
            )
        carry[...] = jnp.zeros_like(carry)
        dqk[...] = jnp.zeros_like(dqk)
        dqp[...] = jnp.zeros_like(dqp)

        def step(t, _):
            d = count - 1 - t
            kb = qb - d
            off = pl.multiple_of(meta[2 + kb] * BLK, BLK)
            keys = pl.ds(off, BLK)
            drow = pl.ds(pl.multiple_of(d * BLK, BLK), BLK)
            slot = lax.rem(t, 2)
            p_copy(slot, 0).wait()

            @pl.when(d >= 1)
            def _():
                p_copy(1 - slot, a * limit + d - 1).start()

            for hp in range(PAIRS):
                lanes = slice(hp * BLK, (hp + 1) * BLK)
                rows = slice(2 * hp * BLK, 2 * (hp + 1) * BLK)
                p = p_buf[slot, rows]
                g = dot_nt(gm2[hp], v_ref[keys, lanes])
                gs = p.astype(F32) * (g - dd[rows])
                gs_low = gs.astype(BF16)
                gs = gs_low.astype(F32)
                rots = []
                for half in range(2):
                    part = slice(half * BLK, (half + 1) * BLK)
                    crow = slice((2 * hp + half) * BLK, (2 * hp + half + 1) * BLK)
                    both = jnp.where(tri, gs[part], carry[crow])
                    carry[crow] = gs[part]
                    rots.append(pltpu.roll(both, 0, 1, stride=1, stride_axis=0))
                rot = jnp.concatenate(rots, axis=0).astype(BF16)
                dqk[hp] += dot_nn(gs_low, k_ref[keys, lanes])
                dqp[hp] += dot_nn(rot, pk_ref[drow, lanes])
                dk_ref[lanes, keys] = (dk_ref[lanes, keys].astype(F32) + dot_nn(q2c_t[hp], gs_low)).astype(BF16)
                dv_ref[lanes, keys] = (dv_ref[lanes, keys].astype(F32) + dot_nn(gm2_t[hp], p)).astype(BF16)
                dpk[lanes, drow] += dot_nn(q2p_t[hp], rot)
            return 0

        lax.fori_loop(0, count, step, 0)
        lane = lax.broadcasted_iota(jnp.int32, (BLK, BLK), 1)
        for hp in range(PAIRS):
            lanes = slice(hp * BLK, (hp + 1) * BLK)
            ck = jnp.where(lane < HEAD, dqk[hp, :BLK], dqk[hp, BLK:]) * 0.125
            cp = jnp.where(lane < HEAD, dqp[hp, :BLK], dqp[hp, BLK:]) * 0.125
            dq_ref[rows_a, lanes] = flip_rows(ck + cp).astype(BF16)
            bias_ref[0:1, lanes] += jnp.sum(ck, axis=0, keepdims=True)
            bias_ref[1:2, lanes] += jnp.sum(cp, axis=0, keepdims=True)
        return 0

    lax.fori_loop(0, 2, one_query_block, 0)
    dpk_ref[...] = dpk[...].astype(BF16)


def attn_bwd(perm, lengths, qc, qp, k, v, pk, p, linv, gm, mixed, blocks, limit):
    tokens, width = qc.shape
    keys = k.shape[0]
    span = pk.shape[0]
    vmem = pl.BlockSpec(memory_space=pltpu.VMEM)
    return pl.pallas_call(
        functools.partial(attn_bwd_kernel, blocks, limit),
        out_shape=(
            jax.ShapeDtypeStruct((tokens, width), BF16),
            jax.ShapeDtypeStruct((8, width), F32),
            jax.ShapeDtypeStruct((width, keys), BF16),
            jax.ShapeDtypeStruct((width, keys), BF16),
            jax.ShapeDtypeStruct((width, span), BF16),
        ),
        in_specs=[pl.BlockSpec(memory_space=pltpu.SMEM)] * 2
        + [vmem] * 5
        + [pl.BlockSpec(memory_space=pl.ANY)]
        + [vmem] * 3,
        out_specs=(vmem,) * 5,
        scratch_shapes=[
            pltpu.SMEM((2 + blocks + lengths.shape[1],), jnp.int32),
            pltpu.VMEM((PAIRS, BLK, 2 * BLK), BF16),
            pltpu.VMEM((PAIRS, BLK, 2 * BLK), BF16),
            pltpu.VMEM((PAIRS, 2 * BLK, BLK), BF16),
            pltpu.VMEM((PAIRS, BLK, 2 * BLK), BF16),
            pltpu.VMEM((ROWS, BLK), F32),
            pltpu.VMEM((ROWS, BLK), F32),
            pltpu.VMEM((PAIRS, 2 * BLK, BLK), F32),
            pltpu.VMEM((PAIRS, 2 * BLK, BLK), F32),
            pltpu.VMEM((width, span), F32),
            pltpu.VMEM((2, ROWS, BLK), BF16),
            pltpu.SemaphoreType.DMA((2,)),
        ],
        compiler_params=pltpu.CompilerParams(vmem_limit_bytes=60 * 2**20),
        cost_estimate=pl.CostEstimate(flops=6 * 10**9, bytes_accessed=30 * 2**20, transcendentals=0),
        name="attn_bwd",
    )(perm, lengths, qc, qp, k, v, pk, p, linv, gm, mixed)


MESH = pl.DeviceIdType.MESH


def fold_rows(x):
    return jnp.broadcast_to(x, (x.shape[0], BLK)).T[0:1]


def aligned(begin, size):
    return pl.ds(pl.multiple_of(begin, math.gcd(size, 16)), size)


def finish_kernel(
    lines, shards, chunks_f, sets, rows_l,
    come_ref, dk_ref, dv_ref, unit_all_ref, dpk_ref, table_ref, weights_ref, dq_ref, x_ref,
    vectors_ref, total_ref, vec_ref, bias_ref, hidden_ref,
    grad_ref, sums_ref, vsum_ref,
    dk_buf, dv_buf, un_buf, in_sem, dpk_buf, table_buf, pos_sem, m_q, mt_k, mt_v, cs_q, cs_k, cs_v, dxp, bx0, bx1, bx2, vbuf, vacc,
    *rest,
):
    wk_ref, wv_ref, wq_ref = weights_ref.at[0], weights_ref.at[1], weights_ref.at[3]
    tokens, width = dq_ref.shape
    bufs_f = rest[: 2 * len(chunks_f)]
    bufs_l = rest[2 * len(chunks_f) : -2]
    send_sem, recv_sem = rest[-2:]
    ctx = lax.axis_index("ctx")
    w = lax.axis_index("wsh")
    core = lax.rem(ctx, 2)
    b = lax.rem(ctx // 2, 2)
    a = ctx // 4

    def at(a_to, b_to, core_to):
        return (a_to * 2 + b_to) * 2 + core_to

    def line_peer(s):
        return (at(lax.rem(a + s, lines), b, core), w)

    def shard_peer(s):
        return (ctx, lax.rem(w + s, shards))

    core_peer = (at(a, b, 1 - core), w)
    b_peer = (at(a, 1 - b, core), w)
    peers = [core_peer, b_peer] + [line_peer(s) for s in range(1, lines)] + [shard_peer(s) for s in range(1, shards)]
    barrier = pltpu.get_barrier_semaphore()
    for peer in peers:
        pl.semaphore_signal(barrier, inc=1, device_id=peer, device_id_type=MESH)

    counter = [0]

    def take(number):
        begin = counter[0]
        counter[0] += number
        return begin

    def remote(src, dst, index, peer):
        return pltpu.make_async_remote_copy(
            src_ref=src, dst_ref=dst, send_sem=send_sem.at[index], recv_sem=recv_sem.at[index],
            device_id=peer, device_id_type=MESH,
        )

    bits = lines.bit_length() - 1
    order = []
    for bit in range(bits):
        order += [m for m in reversed(range(lines)) if m & ((1 << (bit + 1)) - 1) == 1 << bit]
    order.append(0)

    def other(mask):
        place = 0
        for bit in range(bits):
            own = lax.rem(a // (1 << bit), 2)
            place = place + (1 << bit) * ((1 - own) if mask >> bit & 1 else own)
        return place

    def line_place(j):
        place = jnp.int32(0)
        for index, mask in enumerate(order):
            place = place + jnp.where(j == index, other(mask), 0)
        return place

    def line_at(mask):
        return (at(other(mask), b, core), w)

    group = 4 * tokens

    def fetch(j, slot):
        begin = pl.multiple_of(line_place(j) * group, group)
        return (
            pltpu.make_async_copy(dk_ref.at[:, pl.ds(begin, group)], dk_buf.at[slot], in_sem.at[slot, 0]),
            pltpu.make_async_copy(dv_ref.at[:, pl.ds(begin, group)], dv_buf.at[slot], in_sem.at[slot, 1]),
            pltpu.make_async_copy(unit_all_ref.at[pl.ds(begin, group)], un_buf.at[slot], in_sem.at[slot, 2]),
        )

    pos_copies = [
        pltpu.make_async_copy(dpk_ref, dpk_buf, pos_sem.at[0]),
        pltpu.make_async_copy(table_ref, table_buf, pos_sem.at[1]),
    ]
    for copy in pos_copies:
        copy.start()
    for copy in fetch(0, 0):
        copy.start()

    def start_all(copies):
        for copy in copies:
            copy.start()

    def wait_all(copies):
        for copy in copies:
            copy.wait()

    class Feed:
        def __init__(self, begin, share, total_rows, bufs):
            self.begin, self.share = begin, share
            self.base = core * (total_rows // 2) + begin * 2 * lines
            self.b0, self.b1 = bufs
            self.iy, self.iag, self.ix, self.ic = take(shards - 1), take(lines - 1), take(1), take(1)

        def y_copies(self):
            return [
                remote(
                    come_ref.at[lax.rem(w + s, shards), pl.ds(self.begin, self.share)],
                    self.b1.at[s - 1], self.iy + s - 1, shard_peer(s),
                )
                for s in range(1, shards)
            ]

        def ag_copies(self):
            own = aligned(self.base + (b * lines + a) * self.share, self.share)
            return [remote(sums_ref.at[own], sums_ref.at[own], self.iag + s - 1, line_peer(s)) for s in range(1, lines)]

        def x_copies(self):
            own = aligned(self.base + b * lines * self.share, lines * self.share)
            return [remote(sums_ref.at[own], sums_ref.at[own], self.ix, b_peer)]

        def c_copies(self):
            own = aligned(self.base, 2 * lines * self.share)
            return [remote(sums_ref.at[own], sums_ref.at[own], self.ic, core_peer)]

        def y(self):
            start_all(self.y_copies())

        def ag(self):
            wait_all(self.y_copies())
            total = come_ref[w, pl.ds(self.begin, self.share)].astype(F32)
            for s in range(shards - 1):
                total = total + self.b1[s].astype(F32)
            sums_ref[aligned(self.base + (b * lines + a) * self.share, self.share)] = total.astype(BF16)
            start_all(self.ag_copies())

        def x(self):
            wait_all(self.ag_copies())
            start_all(self.x_copies())

        def c(self):
            wait_all(self.x_copies())
            start_all(self.c_copies())

        def done(self):
            wait_all(self.c_copies())

    class Late:
        def __init__(self, out, rows, names, bufs):
            self.out, self.rows, self.names, self.begun = out, rows, names, set()
            self.src, self.b0, self.b1, self.b2, self.b3 = bufs
            self.rc, self.rb, self.share = rows // 2, rows // 4, rows // 4 // lines
            self.i0, self.iy, self.i2 = take(1), take(shards - 1), take(1)
            self.irs, self.iag, self.ix, self.ic = take(lines - 1), take(lines - 1), take(1), take(1)

        def c0_copies(self):
            return [remote(self.src.at[:, aligned((1 - core) * self.rc, self.rc)], self.b0, self.i0, core_peer)]

        def y_copies(self):
            return [
                remote(self.b0.at[lax.rem(w + s, shards)], self.b1.at[s - 1], self.iy + s - 1, shard_peer(s))
                for s in range(1, shards)
            ]

        def x0_copies(self):
            return [remote(self.b1.at[0, aligned((1 - b) * self.rb, self.rb)], self.b2, self.i2, b_peer)]

        def rs_copies(self):
            return [
                remote(
                    self.b2.at[aligned(lax.rem(a + s, lines) * self.share, self.share)],
                    self.b3.at[s - 1], self.irs + s - 1, line_peer(s),
                )
                for s in range(1, lines)
            ]

        def ag_copies(self):
            own = aligned(self.out + core * self.rc + b * self.rb + a * self.share, self.share)
            return [remote(sums_ref.at[own], sums_ref.at[own], self.iag + s - 1, line_peer(s)) for s in range(1, lines)]

        def x_copies(self):
            own = aligned(self.out + core * self.rc + b * self.rb, self.rb)
            return [remote(sums_ref.at[own], sums_ref.at[own], self.ix, b_peer)]

        def c_copies(self):
            own = aligned(self.out + core * self.rc, self.rc)
            return [remote(sums_ref.at[own], sums_ref.at[own], self.ic, core_peer)]

        def c0(self):
            for m, name in enumerate(self.names):
                grad = gradient(name)
                for s in range(shards):
                    self.src[s, m * rows_out : (m + 1) * rows_out] = grad[s * rows_out : (s + 1) * rows_out].astype(BF16)
            used = len(self.names) * rows_out
            if used < rows_l:
                self.src[:, used:] = jnp.zeros((shards, rows_l - used, width), BF16)
            start_all(self.c0_copies())

        def y(self):
            wait_all(self.c0_copies())
            own = self.src[:, aligned(core * self.rc, self.rc)]
            self.b0[...] = (self.b0[...].astype(F32) + own.astype(F32)).astype(BF16)
            start_all(self.y_copies())

        def x0(self):
            wait_all(self.y_copies())
            total = self.b0[w].astype(F32)
            for s in range(shards - 1):
                total = total + self.b1[s].astype(F32)
            self.b1[0] = total.astype(BF16)
            start_all(self.x0_copies())

        def rs(self):
            wait_all(self.x0_copies())
            own = self.b1[0, aligned(b * self.rb, self.rb)]
            self.b2[...] = (self.b2[...].astype(F32) + own.astype(F32)).astype(BF16)
            start_all(self.rs_copies())

        def ag(self):
            wait_all(self.rs_copies())
            total = self.b2[aligned(a * self.share, self.share)].astype(F32)
            for s in range(lines - 1):
                total = total + self.b3[s].astype(F32)
            own = aligned(self.out + core * self.rc + b * self.rb + a * self.share, self.share)
            sums_ref[own] = total.astype(BF16)
            start_all(self.ag_copies())

        def x(self):
            wait_all(self.ag_copies())
            start_all(self.x_copies())

        def c(self):
            wait_all(self.x_copies())
            start_all(self.c_copies())

        def done(self):
            wait_all(self.c_copies())

    rows_f = 4 * lines * sum(chunks_f)
    rows_out = width // shards
    feeds = []
    begin = 0
    for index, share in enumerate(chunks_f):
        feeds.append(Feed(begin, share, rows_f, bufs_f[2 * index : 2 * index + 2]))
        begin += share
    lates = {}
    for index, names in enumerate(sets):
        late = Late(rows_f + index * rows_l, rows_l, names, bufs_l[5 * index : 5 * index + 5])
        for name in names:
            lates[name] = late

    def late_step(name, step):
        late = lates[name]
        if step not in late.begun:
            late.begun.add(step)
            getattr(late, step)()

    values = x_ref[...].astype(F32)
    center = values - jnp.mean(values, axis=1, keepdims=True)
    inverse = lax.rsqrt(jnp.mean(center * center, axis=1, keepdims=True) + epsilon)
    unit = center * inverse

    def gradient(name):
        cols = vectors_ref[0:8].T
        gain_col, bias_col = cols[:, 0:1], cols[:, 1:2]
        if name == "q":
            m_q[...] = dot_tn(unit.astype(BF16), dq_ref[...])
            cs_q[...] = jnp.broadcast_to(jnp.sum(dq_ref[...].astype(F32), axis=0, keepdims=True), cs_q.shape)
            return gain_col * m_q[...] + bias_col * cs_q[0:1]
        if name == "p":
            wait_all(pos_copies)
            return dot_nn(dpk_buf[...], table_buf[...]).T
        m, cs = (mt_k, cs_k) if name == "k" else (mt_v, cs_v)
        return gain_col * m[...] + bias_col * fold_rows(cs[:, 0:1])

    mt_k[...] = jnp.zeros_like(mt_k)
    mt_v[...] = jnp.zeros_like(mt_v)
    cs_k[...] = jnp.zeros_like(cs_k)
    cs_v[...] = jnp.zeros_like(cs_v)
    pl.semaphore_wait(barrier, len(peers))
    for feed in feeds:
        feed.y()

    i_x0, i_x1, i_x2 = take(lines), take(lines), take(lines)

    def copy_x0(j):
        return remote(dxp.at[j, 1 - core], bx0.at[j], i_x0 + j, core_peer)

    def copy_x1(j):
        return remote(bx0.at[j, 1 - b], bx1.at[j], i_x1 + j, b_peer)

    def copy_x2(mask):
        return remote(bx1.at[order.index(mask)], bx2.at[mask - 1], i_x2 + mask, line_at(mask & -mask))

    def after_x0(j):
        copy_x0(j).wait()
        bx0[j] = (bx0[j].astype(F32) + dxp[j, core].astype(F32)).astype(BF16)
        copy_x1(j).start()

    def after_x1(j):
        mask = order[j]
        copy_x1(j).wait()
        total = bx1[j].astype(F32) + bx0[j, b].astype(F32)
        for bit in range(bits):
            if mask and 1 << bit >= (mask & -mask):
                break
            source = mask | 1 << bit
            copy_x2(source).wait()
            total = total + bx2[source - 1].astype(F32)
        if mask:
            bx1[j] = total.astype(BF16)
            copy_x2(mask).start()
        return total

    last = lines - 1
    events = {}

    def plan(j, after, work, *args):
        events.setdefault((min(j, last), after), []).append((work, args))

    plan(0, "blocks", late_step, "q", "c0")
    plan(0, "blocks", late_step, "p", "c0")
    for j in range(lines):
        if j == 0 or j == last:
            plan(j, "blocks" if j == 0 else "all", after_x0, j)
        else:
            plan(j + 1, "blocks", after_x0, j)
    plan(0, "all", late_step, "q", "y")
    plan(0, "all", feeds[0].ag)
    plan(0, "all", late_step, "p", "y")
    plan(3, "first", after_x1, 0)
    plan(3, "blocks", late_step, "p", "x0")

    def happen(j, after):
        for (when, place), works in sorted(events.items()):
            if place == after:

                @pl.when(j == when)
                def _():
                    for work, args in works:
                        work(*args)

    def line_step(j, _):
        slot = lax.rem(j, 2)

        @pl.when(j < last)
        def _():
            start_all(fetch(j + 1, 1 - slot))

        wait_all(fetch(j, slot))

        def make_block(core_of, b_of):
            keys = pl.ds(pl.multiple_of((2 * b_of + core_of) * tokens, tokens), tokens)
            part = dot_nn(wk_ref[...], dk_buf[slot, :, keys]) + dot_nn(wv_ref[...], dv_buf[slot, :, keys])
            dxp[j, core_of, b_of] = part.astype(BF16)

        make_block(1 - core, 0)
        make_block(1 - core, 1)
        copy_x0(j).start()
        happen(j, "first")
        make_block(core, 0)
        make_block(core, 1)
        happen(j, "blocks")
        mt_k[...] += dot_nn(dk_buf[slot], un_buf[slot])
        mt_v[...] += dot_nn(dv_buf[slot], un_buf[slot])
        for cs, buf in ((cs_k, dk_buf), (cs_v, dv_buf)):
            total = cs[...]
            for piece in range(group // BLK):
                total = total + buf[slot, :, piece * BLK : (piece + 1) * BLK].astype(F32)
            cs[...] = total
        happen(j, "all")
        return 0

    lax.fori_loop(0, lines, line_step, 0)
    for m, cs in ((mt_k, cs_k), (mt_v, cs_v)):
        m[...] = m[...].T
        cs[...] = jnp.broadcast_to(jnp.sum(cs[...], axis=1, keepdims=True), cs.shape)

    vstages = [[core_peer], [b_peer], [line_peer(s) for s in range(1, lines)], [shard_peer(s) for s in range(1, shards)]]
    vslots = []
    place = 0
    for stage in vstages:
        vslots.append(place)
        place += len(stage)
    vbegin = take(place)

    def v_copy(stage, index):
        slot = vslots[stage] + index
        return remote(vacc.at[pl.ds(stage * 16, 16)], vbuf.at[slot], vbegin + slot, vstages[stage][index])

    def v_start(stage):
        for index in range(len(vstages[stage])):
            v_copy(stage, index).start()

    def v_finish(stage):
        total = vacc[stage * 16 : stage * 16 + 16]
        for index in range(len(vstages[stage])):
            v_copy(stage, index).wait()
            total = total + vbuf[vslots[stage] + index]
        vacc[(stage + 1) * 16 : (stage + 2) * 16] = total

    def vectors_begin():
        vacc[0:16] = vec_ref[...]
        vacc[2:4] = bias_ref[0:2]
        gain_grad = m_q[...] * wq_ref[...].astype(F32)
        gain_grad = gain_grad + mt_k[...] * wk_ref[...].astype(F32) + mt_v[...] * wv_ref[...].astype(F32)
        vacc[0:1] = fold_rows(jnp.sum(gain_grad, axis=1, keepdims=True))
        total = dot_nt(cs_q[...].astype(BF16), wq_ref[...])
        for cs, weight in ((cs_k, wk_ref), (cs_v, wv_ref)):
            row = jnp.broadcast_to(fold_rows(cs[:, 0:1]), (8, width))
            total = total + dot_nt(row.astype(BF16), weight[...])
        vacc[1:2] = total[0:1]
        v_start(0)

    late_step("v", "c0")
    feeds[0].x()
    vectors_begin()
    if lines > 2:
        after_x1(1)
    late_step("q", "x0")
    late_step("v", "y")
    late_step("k", "c0")
    late_step("p", "rs")
    v_finish(0)
    v_start(1)
    for feed in feeds[1:]:
        feed.ag()
    late_step("k", "y")
    late_step("v", "x0")
    for j in range(2, lines - 1):
        after_x1(j)
    late_step("k", "x0")
    late_step("p", "ag")
    own = after_x1(lines - 1)
    for feed in feeds[1:]:
        feed.x()
    feeds[0].c()
    late_step("q", "rs")
    v_finish(1)
    v_start(2)
    scaled = (own.T + dot_nt(dq_ref[...], wq_ref[...])) * vectors_ref[0:1]
    grad_ref[...] = hidden_ref[...] + inverse * (
        scaled - jnp.mean(scaled, axis=1, keepdims=True) - unit * jnp.mean(scaled * unit, axis=1, keepdims=True)
    )
    late_step("v", "rs")
    late_step("p", "x")
    late_step("k", "rs")
    late_step("q", "ag")
    v_finish(2)
    v_start(3)
    late_step("v", "ag")
    late_step("k", "ag")
    v_finish(3)
    vsum_ref[...] = vacc[4 * 16 : 5 * 16]
    late_step("q", "x")
    for feed in feeds[1:]:
        feed.c()
    late_step("v", "x")
    late_step("p", "c")
    late_step("k", "x")
    late_step("q", "c")
    late_step("v", "c")
    late_step("k", "c")
    for feed in feeds:
        feed.done()
    for name in "qpvk":
        late_step(name, "done")


def finish(lines, shards, chunks_f, sets, rows_l, cid, come, dk, dv, unit_all, dpk, table, weights, dq, x, vectors, total, vec, bias, hidden):
    tokens, width = dq.shape
    vmem = pl.BlockSpec(memory_space=pltpu.VMEM)
    hbm = pl.BlockSpec(memory_space=pl.ANY)
    bufs = []
    for share in chunks_f:
        bufs += [pltpu.VMEM((16, width), BF16), pltpu.VMEM((shards - 1, share, width), BF16)]
    for names in sets:
        bufs += [
            pltpu.VMEM((shards, rows_l, width), BF16),
            pltpu.VMEM((shards, rows_l // 2, width), BF16),
            pltpu.VMEM((shards - 1, rows_l // 2, width), BF16),
            pltpu.VMEM((rows_l // 4, width), BF16),
            pltpu.VMEM((lines - 1, rows_l // 4 // lines, width), BF16),
        ]
    hops = shards - 1 + 2 * (lines - 1)
    copies = len(chunks_f) * (shards + lines) + len(sets) * (hops + 4) + 3 * lines + 2 + lines - 1 + shards - 1
    total_rows = 4 * lines * sum(chunks_f) + len(sets) * rows_l
    stages = 1 + 1 + (lines - 1) + (shards - 1)
    span = dpk.shape[1]
    return pl.pallas_call(
        functools.partial(finish_kernel, lines, shards, tuple(chunks_f), sets, rows_l),
        out_shape=(
            jax.ShapeDtypeStruct((tokens, width), F32),
            jax.ShapeDtypeStruct((total_rows, width), BF16),
            jax.ShapeDtypeStruct((16, width), F32),
        ),
        in_specs=[vmem] + [hbm] * 5 + [vmem] * 8,
        out_specs=(vmem,) * 3,
        scratch_shapes=[
            pltpu.VMEM((2, width, 4 * tokens), BF16),
            pltpu.VMEM((2, width, 4 * tokens), BF16),
            pltpu.VMEM((2, 4 * tokens, width), BF16),
            pltpu.SemaphoreType.DMA((2, 3)),
            pltpu.VMEM((width, span), BF16),
            pltpu.VMEM((span, width), BF16),
            pltpu.SemaphoreType.DMA((2,)),
            pltpu.VMEM((width, width), F32),
            pltpu.VMEM((width, width), F32),
            pltpu.VMEM((width, width), F32),
            pltpu.VMEM((8, width), F32),
            pltpu.VMEM((width, BLK), F32),
            pltpu.VMEM((width, BLK), F32),
            pltpu.VMEM((lines, 2, 2, width, tokens), BF16),
            pltpu.VMEM((lines, 2, width, tokens), BF16),
            pltpu.VMEM((lines, width, tokens), BF16),
            pltpu.VMEM((lines - 1, width, tokens), BF16),
            pltpu.VMEM((stages, 16, width), F32),
            pltpu.VMEM((5 * 16, width), F32),
        ]
        + bufs
        + [pltpu.SemaphoreType.DMA((copies,)), pltpu.SemaphoreType.DMA((copies,))],
        compiler_params=pltpu.CompilerParams(
            collective_id=cid, has_side_effects=True, vmem_limit_bytes=63 * 2**20
        ),
        cost_estimate=pl.CostEstimate(flops=10**10, bytes_accessed=30 * 2**20, transcendentals=0),
        name="finish",
    )(come, dk, dv, unit_all, dpk, table, weights, dq, x, vectors, total, vec, bias, hidden)


def unpack_kernel(
    shards, rows_f, sets, rows_l, sums_ref, vsum_ref, total_ref, grad_ref,
    grad_out, q_out, k_out, v_out, o_out, p_out, u_out, d_out, g1_out, b1_out, cb_out, pb_out, g2_out, b2_out, bd_out, bu_out,
    loss_out,
    low, wide, up, in_sem, out_sem,
):
    width = vsum_ref.shape[1]
    rows_out, rows_up = q_out.shape[0], d_out.shape[0]
    parts = u_out.shape[1] // width
    w = lax.axis_index("wsh")
    pieces = [(rows_up, d_out), (2 * rows_up, o_out)]
    to = {"q": q_out, "p": p_out, "k": k_out, "v": v_out}
    for index, names in enumerate(sets):
        pieces += [(rows_f + index * rows_l + m * rows_out, to[name]) for m, name in enumerate(names)]
    ins = [pltpu.make_async_copy(sums_ref.at[0:rows_up], low.at[0:rows_up], in_sem.at[0])]
    for index, (begin, out) in enumerate(pieces):
        size = out.shape[0]
        ins.append(pltpu.make_async_copy(sums_ref.at[begin : begin + size], low.at[begin : begin + size], in_sem.at[1 + index]))
    for copy in ins:
        copy.start()
    outs = [pltpu.make_async_copy(grad_ref, grad_out, out_sem.at[0])]
    outs[0].start()
    ins[0].wait()
    for c in range(parts):
        up[:, c * width : (c + 1) * width] = low[c * rows_out : (c + 1) * rows_out].astype(F32)
    outs.append(pltpu.make_async_copy(up, u_out, out_sem.at[1]))
    outs[1].start()
    for index, (begin, out) in enumerate(pieces):
        size = out.shape[0]
        ins[1 + index].wait()
        wide[begin : begin + size] = low[begin : begin + size].astype(F32)
        copy = pltpu.make_async_copy(wide.at[begin : begin + size], out, out_sem.at[2 + index])
        copy.start()
        outs.append(copy)

    def share(row):
        part = vsum_ref[row : row + 1, 0:rows_out]
        for s in range(1, shards):
            part = jnp.where(w == s, vsum_ref[row : row + 1, s * rows_out : (s + 1) * rows_out], part)
        return part.reshape(rows_out)

    for row, ref in enumerate((g1_out, b1_out, cb_out, pb_out, g2_out, b2_out, bd_out)):
        ref[...] = share(row)
    per = rows_up // rows_out
    for q in range(per):
        part = None
        for s in range(shards):
            group = s * per + q
            row, place = 7 + group // shards, group % shards
            piece = vsum_ref[row : row + 1, place * rows_out : (place + 1) * rows_out]
            part = piece if part is None else jnp.where(w == s, piece, part)
        bu_out[q * rows_out : (q + 1) * rows_out] = part.reshape(rows_out)
    loss_out[0, 0] = vsum_ref[7 + parts, 0] / (total_ref[0, 0] * width)
    for copy in outs:
        copy.wait()


def unpack(shards, rows_f, sets, rows_l, hidden, sums, vsum, total, grad):
    tokens, width = grad.shape
    rows_out, rows_up = width // shards, hidden // shards
    vmem = pl.BlockSpec(memory_space=pltpu.VMEM)
    hbm = pl.BlockSpec(memory_space=pl.ANY)
    square = jax.ShapeDtypeStruct((rows_out, width), F32)
    vector = jax.ShapeDtypeStruct((rows_out,), F32)
    return pl.pallas_call(
        functools.partial(unpack_kernel, shards, rows_f, sets, rows_l),
        out_shape=(
            jax.ShapeDtypeStruct((tokens, width), F32), square, square, square, square, square,
            jax.ShapeDtypeStruct((rows_out, hidden), F32), jax.ShapeDtypeStruct((rows_up, width), F32),
            vector, vector, vector, vector, vector, vector, vector, jax.ShapeDtypeStruct((rows_up,), F32),
            jax.ShapeDtypeStruct((1, 1), F32),
        ),
        in_specs=[hbm, vmem, vmem, hbm],
        out_specs=(hbm,) * 8 + (vmem,) * 8 + (pl.BlockSpec(memory_space=pltpu.SMEM),),
        scratch_shapes=[
            pltpu.VMEM(sums.shape, BF16),
            pltpu.VMEM(sums.shape, F32),
            pltpu.VMEM((rows_out, hidden), F32),
            pltpu.SemaphoreType.DMA((7,)),
            pltpu.SemaphoreType.DMA((8,)),
        ],
        compiler_params=pltpu.CompilerParams(vmem_limit_bytes=40 * 2**20),
        cost_estimate=pl.CostEstimate(flops=10**6, bytes_accessed=12 * 2**20, transcendentals=0),
        name="unpack",
    )(sums, vsum, total, grad)


PARTS = 2


def start_kernel(
    lines, shards, x_ref, wk_ref, wv_ref, wp_ref, wq_ref, wo_ref, wu_ref, wd_ref,
    g1_ref, b1_ref, cb_ref, pb_ref, g2_ref, b2_ref, bd_ref, bu_ref, mask_ref, far_ref, near_ref,
    k_ref, v_ref, unit_ref, pk_ref, table_ref, qc_ref, qp_ref, weights_ref, wo_out, wu_out, wd_out, vectors_ref, total_ref,
    x_all, k_buf, v_buf, u_buf, pk_buf, t_buf, wo_buf, wu_buf, wd_buf, vec_src, vec_buf, cnt_buf, cnt_acc,
    up_send, up_recv, down_send, down_recv, b_send, b_recv, c_send, c_recv,
    y_send, y_recv, yc_send, yc_recv, d_send, d_recv, s_send, s_recv, out_sem, pos_sem, own_sem,
):
    tokens, width = x_ref.shape
    piece = tokens // PARTS
    half = width // 2
    chunks = pk_buf.shape[0] // BLK
    ctx = lax.axis_index("ctx")
    w = lax.axis_index("wsh")
    core = lax.rem(ctx, 2)
    b = lax.rem(ctx // 2, 2)
    a = ctx // 4

    def at(a_to, b_to, core_to):
        return (a_to * 2 + b_to) * 2 + core_to

    def shard_peer(s):
        return (ctx, lax.rem(w + s, shards))

    def line_peer(s):
        return (at(lax.rem(a + s, lines), b, core), w)

    core_peer = (at(a, b, 1 - core), w)
    b_peer = (at(a, 1 - b, core), w)
    peers = [core_peer, b_peer] + [line_peer(s) for s in range(1, lines)] + [shard_peer(s) for s in range(1, shards)]
    barrier = pltpu.get_barrier_semaphore()
    for peer in peers:
        pl.semaphore_signal(barrier, inc=1, device_id=peer, device_id_type=MESH)

    def remote(src, dst, send, recv, peer):
        return pltpu.make_async_remote_copy(
            src_ref=src, dst_ref=dst, send_sem=send, recv_sem=recv, device_id=peer, device_id_type=MESH
        )

    def block(slot):
        return aligned(slot * tokens, tokens)

    x_all[block(ctx)] = x_ref[...]
    rows_out = wq_ref.shape[0]
    quarter = rows_out // 2
    rows_up = wd_ref.shape[0]
    weight_in = (wk_ref, wv_ref, wp_ref, wq_ref, wo_ref)
    weight_to = tuple(weights_ref.at[m] for m in range(4)) + (wo_buf,)
    own_copies = [
        pltpu.make_async_copy(ref, to.at[aligned(w * rows_out, rows_out)], own_sem.at[m])
        for m, (ref, to) in enumerate(zip(weight_in[:4], weight_to))
    ]
    for copy in own_copies:
        copy.start()
    vec_src[...] = jnp.zeros_like(vec_src)
    for row, ref in enumerate((g1_ref, b1_ref, cb_ref, pb_ref, g2_ref, b2_ref, bd_ref)):
        vec_src[row : row + 1] = ref[...].astype(F32).reshape(1, rows_out)
    bias_rows = rows_up // rows_out
    for q in range(bias_rows):
        vec_src[7 + q : 8 + q] = bu_ref[q * rows_out : (q + 1) * rows_out].astype(F32).reshape(1, rows_out)
    cnt_acc[0:8] = jnp.broadcast_to(jnp.sum(mask_ref[...].astype(F32), axis=1, keepdims=True), (8, BLK))
    pl.semaphore_wait(barrier, len(peers))

    def x_copy(slot, h, send, recv, peer):
        rows = aligned(slot * tokens + h * piece, piece)
        return remote(x_all.at[rows], x_all.at[rows], send, recv, peer)

    def up_copy(p, h):
        peer = (at(jnp.minimum(a + 1, lines - 1), b, core), w)
        return x_copy(at(p, b, core), h, up_send.at[p, h], up_recv.at[p, h], peer)

    def down_copy(p, h):
        peer = (at(jnp.maximum(a - 1, 0), b, core), w)
        return x_copy(at(p, b, core), h, down_send.at[p, h], down_recv.at[p, h], peer)

    def b_copy(p, h, b_from):
        return x_copy(at(p, b_from, core), h, b_send.at[p, h], b_recv.at[p, h], b_peer)

    def c_copy(p, far, b_from, core_from):
        rows = block(at(p, b_from, core_from))
        return remote(x_all.at[rows], x_all.at[rows], c_send.at[far, p], c_recv.at[far, p], core_peer)

    def weight_copy(m, s):
        rows = aligned(w * rows_out + core * quarter, quarter)
        src = weight_in[m].at[aligned(core * quarter, quarter)]
        return remote(src, weight_to[m].at[rows], y_send.at[m, s - 1], y_recv.at[m, s - 1], shard_peer(s))

    def weight_pass(m, s):
        rows = aligned(lax.rem(w + shards - s, shards) * rows_out + core * quarter, quarter)
        return remote(
            weight_to[m].at[rows], weight_to[m].at[rows], yc_send.at[m, s - 1], yc_recv.at[m, s - 1], core_peer
        )

    low = lax.rem(a, 2)
    quarter_in, quarter_to = (wd_ref, wu_ref), (wd_buf, wu_buf)
    pair_peer = (at(a + 1 - 2 * low, b, core), w)

    def quarter_rows(m, s, low_of):
        size = quarter_in[m].shape[0]
        owner = lax.rem(w + shards - s, shards)
        return aligned(owner * size + (low_of * 2 + core) * (size // 4), size // 4)

    def quarter_copy(m, s):
        size = quarter_in[m].shape[0]
        src = quarter_in[m].at[aligned((low * 2 + core) * (size // 4), size // 4)]
        dst = quarter_to[m].at[quarter_rows(m, 0, low)]
        return remote(src, dst, d_send.at[m, 0, s - 1], d_recv.at[m, 0, s - 1], shard_peer(s))

    def quarter_pass(m, kind, s):
        rows = quarter_rows(m, s, 1 - low if kind == 3 else low)
        peer = pair_peer if kind == 1 else core_peer
        ref = quarter_to[m].at[rows]
        return remote(ref, ref, d_send.at[m, kind, s - 1], d_recv.at[m, kind, s - 1], peer)

    def quarter_on(m):
        for s in range(1, shards):
            quarter_copy(m, s).wait()
            quarter_pass(m, 1, s).start()
            quarter_pass(m, 2, s).start()

    def vec_copy(s):
        return remote(vec_src, vec_buf.at[s - 1], s_send.at[s - 1], s_recv.at[s - 1], shard_peer(s))

    stages = [[shard_peer(s) for s in range(1, shards)], [core_peer], [b_peer], [line_peer(s) for s in range(1, lines)]]
    slots = []
    place = 0
    for stage in stages:
        slots.append(place)
        place += len(stage)

    def cnt_copy(stage, index):
        slot = slots[stage] + index
        sem = shards - 1 + slot
        return remote(cnt_acc.at[pl.ds(stage * 8, 8)], cnt_buf.at[slot], s_send.at[sem], s_recv.at[sem], stages[stage][index])

    def cnt_start(stage):
        for index in range(len(stages[stage])):
            cnt_copy(stage, index).start()

    def cnt_finish(stage):
        total = cnt_acc[stage * 8 : stage * 8 + 8]
        for index in range(len(stages[stage])):
            cnt_copy(stage, index).wait()
            total = total + cnt_buf[slots[stage] + index]
        cnt_acc[(stage + 1) * 8 : (stage + 2) * 8] = total

    for s in range(1, shards):
        vec_copy(s).start()
    cnt_start(0)
    for h in range(PARTS):

        @pl.when(a + 1 < lines)
        def _():
            up_copy(a, h).start()

        @pl.when(a >= 1)
        def _():
            down_copy(a, h).start()

        b_copy(a, h, b).start()
    c_copy(a, 0, b, core).start()
    for kind, m in ((0, 0), (0, 1), (1, 0), (0, 2), (1, 1), (0, 3), (0, 4)):
        for s in range(1, shards):
            (quarter_copy if kind else weight_copy)(m, s).start()


    def table_step(d, _):
        sin_far, cos_far = far_ref[0, pl.ds(d, 1)], far_ref[1, pl.ds(d, 1)]
        sin_near, cos_near = near_ref[0], near_ref[1]
        rows = aligned(d * BLK, BLK)
        t_buf[rows, :half] = (sin_far * cos_near - cos_far * sin_near).astype(BF16)
        t_buf[rows, half:] = (cos_far * cos_near + sin_far * sin_near).astype(BF16)
        return 0

    lax.fori_loop(0, chunks, table_step, 0)
    table_out = pltpu.make_async_copy(t_buf, table_ref, pos_sem.at[0])
    table_out.start()
    lane_to = lax.broadcasted_iota(jnp.int32, (rows_out, width), 1)
    lane_from = lax.broadcasted_iota(jnp.int32, (rows_out, width), 0)
    row_at = lax.broadcasted_iota(jnp.int32, (16, width), 0)

    def spread(values, place):
        return dot_nn(values.astype(BF16), (lane_to == lane_from + place * rows_out).astype(BF16))

    def placed(values, owner):
        full = jnp.where(row_at < 7, spread(values, owner), 0.0)
        for q in range(bias_rows):
            group = owner * bias_rows + q
            row = jnp.broadcast_to(values[7 + q : 8 + q], values.shape)
            full = full + jnp.where(row_at == 7 + group // shards, spread(row, lax.rem(group, shards)), 0.0)
        return full

    vectors = placed(vec_src[...], w)
    for s in range(1, shards):
        vec_copy(s).wait()
        vectors = vectors + placed(vec_buf[s - 1], lax.rem(w + shards - s, shards))
    vectors_ref[...] = vectors
    cnt_finish(0)
    cnt_start(1)

    def unit_of(rows):
        values = rows.astype(F32)
        center = values - jnp.mean(values, axis=1, keepdims=True)
        return center * lax.rsqrt(jnp.mean(center * center, axis=1, keepdims=True) + epsilon)

    def out_copies(slot):
        rows = block(slot)
        return (
            pltpu.make_async_copy(k_buf.at[rows], k_ref.at[rows], out_sem.at[0, slot]),
            pltpu.make_async_copy(v_buf.at[rows], v_ref.at[rows], out_sem.at[1, slot]),
            pltpu.make_async_copy(u_buf.at[rows], unit_ref.at[rows], out_sem.at[2, slot]),
        )

    def project(p):
        def one(q, _):
            other_b = lax.rem(q, 2)
            other_core = q // 2

            @pl.when(q == 1)
            def _():
                for h in range(PARTS):
                    b_copy(p, h, b).wait()
                c_copy(p, 1, 1 - b, core).start()

            @pl.when(q == 2)
            def _():
                c_copy(p, 0, b, core).wait()

            @pl.when(q == 3)
            def _():
                c_copy(p, 1, 1 - b, core).wait()

            slot = at(p, b + other_b - 2 * b * other_b, core + other_core - 2 * core * other_core)
            rows = block(slot)
            unit = unit_of(x_all[rows])
            u_buf[rows] = unit.astype(BF16)
            normed = (unit * vectors_ref[0:1] + vectors_ref[1:2]).astype(BF16)
            k_buf[rows] = dot_nn(normed, weights_ref[0]).astype(BF16)
            v_buf[rows] = dot_nn(normed, weights_ref[1]).astype(BF16)
            for copy in out_copies(slot):
                copy.start()
            return 0

        lax.fori_loop(0, 4, one, 0)

    def pos_step(d, _):
        rows = aligned(d * BLK, BLK)
        pk_buf[rows] = dot_nn(t_buf[rows], weights_ref[2]).astype(BF16)
        return 0

    last = lines - 1

    def line_step(s, _):
        below, high = a - 1 - s, a + 1 + s

        for h in range(PARTS):

            @pl.when((s < lines - 1) & (below >= 0))
            def _():
                p = jnp.maximum(below, 0)
                up_copy(p, h).wait_recv()

                @pl.when(a + 1 < lines)
                def _():
                    up_copy(p, h).start()

                b_copy(p, h, b).start()
                if h == PARTS - 1:
                    c_copy(p, 0, b, core).start()

            @pl.when((s < lines - 1) & (high < lines))
            def _():
                p = jnp.minimum(high, lines - 1)
                down_copy(p, h).wait_recv()

                @pl.when(a >= 1)
                def _():
                    down_copy(p, h).start()

                b_copy(p, h, b).start()
                if h == PARTS - 1:
                    c_copy(p, 0, b, core).start()

        @pl.when(s == 0)
        def _():
            cnt_finish(1)
            cnt_start(2)
            for copy in own_copies:
                copy.wait()
            for m in range(2):
                for t in range(1, shards):
                    weight_copy(m, t).wait()
                    weight_pass(m, t).start()
            for m in range(2):
                for t in range(1, shards):
                    weight_pass(m, t).wait()

        @pl.when(s == min(1, last))
        def _():
            cnt_finish(2)
            cnt_start(3)

        @pl.when(s == min(2, last))
        def _():
            for t in range(1, shards):
                weight_copy(2, t).wait()
                weight_pass(2, t).start()
            for t in range(1, shards):
                weight_pass(2, t).wait()

        @pl.when(s == last)
        def _():
            for m in range(3, 5):
                for t in range(1, shards):
                    weight_copy(m, t).wait()
                    weight_pass(m, t).start()
            for t in range(1, shards):
                weight_pass(3, t).wait()

        @pl.when(a - s >= 0)
        def _():
            project(jnp.maximum(a - s, 0))

        @pl.when((s >= 1) & (a + s < lines))
        def _():
            project(jnp.minimum(a + s, lines - 1))

        @pl.when(s == min(1, last))
        def _():
            quarter_on(0)

        @pl.when(s == min(2, last))
        def _():
            lax.fori_loop(0, chunks // 2, pos_step, 0)
            quarter_on(1)

        @pl.when(s == last)
        def _():
            lax.fori_loop(chunks // 2, chunks, pos_step, 0)

        return 0

    lax.fori_loop(0, lines, line_step, 0)
    pos_out = pltpu.make_async_copy(pk_buf, pk_ref, pos_sem.at[1])
    pos_out.start()
    normed = (unit_of(x_ref[...]) * vectors_ref[0:1] + vectors_ref[1:2]).astype(BF16)
    queries = dot_nn(normed, weights_ref[3]).astype(BF16).astype(F32)
    qc_ref[...] = ((queries + vectors_ref[2:3]) * 0.125).astype(BF16)
    qp_ref[...] = ((queries + vectors_ref[3:4]) * 0.125).astype(BF16)
    cnt_finish(3)
    total_ref[...] = cnt_acc[4 * 8 : 5 * 8]

    def sends_done(p, _):
        for h in range(PARTS):

            @pl.when((a + 1 < lines) & (p <= a))
            def _():
                up_copy(p, h).wait_send()

            @pl.when((a >= 1) & (p >= a))
            def _():
                down_copy(p, h).wait_send()

        return 0

    lax.fori_loop(0, lines, sends_done, 0)

    def outs_done(slot, _):
        for copy in out_copies(slot):
            copy.wait()
        return 0

    lax.fori_loop(0, 4 * lines, outs_done, 0)
    for s in range(1, shards):
        weight_pass(4, s).wait()
        for m in range(2):
            quarter_pass(m, 1, s).wait()
            quarter_pass(m, 3, s).start()
    for s in range(1, shards):
        for m in range(2):
            quarter_pass(m, 2, s).wait()
            quarter_pass(m, 3, s).wait()
    far_copies = []
    for m, (buf, to) in enumerate(((wo_buf, wo_out), (wu_buf, wu_out), (wd_buf, wd_out))):
        size = buf.shape[0] // shards
        for s in range(1, shards):
            rows = aligned(lax.rem(w + s, shards) * size, size)
            far_copies.append(pltpu.make_async_copy(buf.at[rows], to.at[rows], own_sem.at[4 + m * (shards - 1) + s - 1]))
    for copy in far_copies:
        copy.start()
    for copy in far_copies:
        copy.wait()
    table_out.wait()
    pos_out.wait()


def start(lines, shards, cid, limit, x, weights, vectors, mask, far, near):
    tokens, width = x.shape
    hidden = weights[5].shape[1]
    rows_out = weights[0].shape[0]
    members = 4 * lines
    keys = members * tokens
    span = limit * BLK
    vmem = pl.BlockSpec(memory_space=pltpu.VMEM)
    hbm = pl.BlockSpec(memory_space=pl.ANY)
    small = 2 * (shards - 1) + 1 + 1 + lines - 1
    dma = pltpu.SemaphoreType.DMA
    other = shards - 1
    return pl.pallas_call(
        functools.partial(start_kernel, lines, shards),
        out_shape=(
            jax.ShapeDtypeStruct((keys, width), BF16),
            jax.ShapeDtypeStruct((keys, width), BF16),
            jax.ShapeDtypeStruct((keys, width), BF16),
            jax.ShapeDtypeStruct((span, width), BF16),
            jax.ShapeDtypeStruct((span, width), BF16),
            jax.ShapeDtypeStruct((tokens, width), BF16),
            jax.ShapeDtypeStruct((tokens, width), BF16),
            jax.ShapeDtypeStruct((4, width, width), BF16),
            jax.ShapeDtypeStruct((width, width), BF16),
            jax.ShapeDtypeStruct((width, hidden), BF16),
            jax.ShapeDtypeStruct((hidden, width), BF16),
            jax.ShapeDtypeStruct((16, width), F32),
            jax.ShapeDtypeStruct((8, BLK), F32),
        ),
        in_specs=[vmem] + [hbm] * 7 + [vmem] * 11,
        out_specs=(hbm,) * 5 + (vmem,) * 3 + (hbm,) * 3 + (vmem,) * 2,
        scratch_shapes=[
            pltpu.VMEM((keys, width), BF16),
            pltpu.VMEM((keys, width), BF16),
            pltpu.VMEM((keys, width), BF16),
            pltpu.VMEM((keys, width), BF16),
            pltpu.VMEM((span, width), BF16),
            pltpu.VMEM((span, width), BF16),
            pltpu.VMEM((width, width), BF16),
            pltpu.VMEM((width, hidden), BF16),
            pltpu.VMEM((hidden, width), BF16),
            pltpu.VMEM((16, rows_out), F32),
            pltpu.VMEM((other, 16, rows_out), F32),
            pltpu.VMEM((lines + shards, 8, BLK), F32),
            pltpu.VMEM((5 * 8, BLK), F32),
        ]
        + [dma((lines, PARTS))] * 6
        + [dma((2, lines))] * 2
        + [dma((5, other))] * 4
        + [dma((2, 4, other))] * 2
        + [dma((small,))] * 2
        + [dma((3, members)), dma((2,)), dma((4 + 3 * other,))],
        compiler_params=pltpu.CompilerParams(collective_id=cid, has_side_effects=True, vmem_limit_bytes=60 * 2**20),
        cost_estimate=pl.CostEstimate(flops=6 * 10**9, bytes_accessed=20 * 2**20, transcendentals=0),
        name="start",
    )(x, *weights, *vectors, mask, far, near)


GELU_SCALE = math.sqrt(2.0 / math.pi)


def middle_kernel(
    shards, chunks_f, mask_ref, x_ref, mixed_ref, teacher_ref, out_grad_ref, vectors_ref, total_ref,
    wo_own, wu_own, wd_own, wo_ref, wu_ref, wd_ref,
    out_ref, hidden_ref, gm_ref, share_ref, vec_ref,
    wo, wu, wd, slope, act, gf_ref, landed, sem, send_sem, recv_sem,
):
    tokens, width = x_ref.shape
    parts = wu.shape[1] // width
    ctx = lax.axis_index("ctx")
    core = lax.rem(ctx, 2)
    core_peer = (ctx + 1 - 2 * core, lax.axis_index("wsh"))
    barrier = pltpu.get_barrier_semaphore()
    pl.semaphore_signal(barrier, inc=1, device_id=core_peer, device_id_type=MESH)
    w = lax.axis_index("wsh")
    copies = []
    for k, (own, gathered, full) in enumerate(((wo_own, wo_ref, wo), (wu_own, wu_ref, wu), (wd_own, wd_ref, wd))):
        size = own.shape[0]
        part = [pltpu.make_async_copy(own, full.at[aligned(w * size, size)], sem.at[k, 0])]
        for s in range(1, shards):
            rows = aligned(lax.rem(w + s, shards) * size, size)
            part.append(pltpu.make_async_copy(gathered.at[rows], full.at[rows], sem.at[k, s]))
        for copy in part:
            copy.start()
        copies.append(part)

    def arrive(k):
        for copy in copies[k]:
            copy.wait()

    members = share_ref.shape[0]
    lines = members // 2
    rows_f = 2 * members * sum(chunks_f)
    half = rows_f // 2

    def give(begin, size, index):
        rows = aligned((1 - core) * half + begin, size)
        return pltpu.make_async_remote_copy(
            src_ref=gf_ref.at[:, rows], dst_ref=landed.at[:, begin : begin + size],
            send_sem=send_sem.at[index], recv_sem=recv_sem.at[index], device_id=core_peer, device_id_type=MESH,
        )

    gain, offset, down_bias = vectors_ref[4:5], vectors_ref[5:6], vectors_ref[6:7]
    mixed = mixed_ref[...].astype(BF16)
    arrive(0)
    hidden = x_ref[...].astype(F32) + dot_nn(mixed, wo[...])
    center = hidden - jnp.mean(hidden, axis=1, keepdims=True)
    inverse = lax.rsqrt(jnp.mean(center * center, axis=1, keepdims=True) + epsilon)
    unit = center * inverse
    normed = (unit * gain + offset).astype(BF16)
    result = hidden + down_bias
    arrive(1)
    arrive(2)
    for c in range(parts):
        cols = slice(c * width, (c + 1) * width)
        v = dot_nn(normed, wu[:, cols]) + vectors_ref[7 + c : 8 + c]
        square = v * v
        t = jnp.tanh(GELU_SCALE * (v + 0.044715 * (square * v)))
        act[:, cols] = (0.5 * v * (1.0 + t)).astype(BF16)
        slope[:, cols] = 0.5 * (1.0 + t) + 0.5 * v * (1.0 - t * t) * (GELU_SCALE * (1.0 + 3.0 * 0.044715 * square))
        result = result + dot_nn(act[:, cols], wd[cols])
    out_ref[...] = result.astype(BF16)
    mask = jnp.broadcast_to(mask_ref[...].astype(F32), (8, tokens)).T[:, 0:1]
    error = result - teacher_ref[...].astype(F32)
    masked = mask * error
    count = jnp.sum(total_ref[0:1, 0:1], axis=1, keepdims=True)
    grad_result = out_grad_ref[...].astype(F32) + (2.0 / (count * width)) * masked
    branch = grad_result.astype(BF16)
    vec_ref[...] = jnp.zeros_like(vec_ref)
    vec_ref[7 + parts : 8 + parts] = jnp.broadcast_to(
        jnp.sum(jnp.sum(masked * error, axis=1, keepdims=True), axis=0, keepdims=True), (1, width)
    )
    vec_ref[6:7] = jnp.sum(branch.astype(F32), axis=0, keepdims=True)
    rows_up = wd.shape[0] // shards
    rows_out = width // shards
    used = 2 * rows_up + rows_out
    if used < rows_f:
        gf_ref[:, used:] = jnp.zeros((shards, rows_f - used, width), BF16)
    grad_normed = jnp.zeros((tokens, width), F32)
    for c in range(parts):
        cols = slice(c * width, (c + 1) * width)
        grad_pre = (dot_nt(branch, wd[cols]) * slope[:, cols]).astype(BF16)
        vec_ref[7 + c : 8 + c] = jnp.sum(grad_pre.astype(F32), axis=0, keepdims=True)
        grad_normed = grad_normed + dot_nt(grad_pre, wu[:, cols])
        up = dot_tn(normed, grad_pre).astype(BF16)
        down = dot_tn(act[:, cols], branch).astype(BF16)
        for s in range(shards):
            gf_ref[s, c * rows_out : (c + 1) * rows_out] = up[s * rows_out : (s + 1) * rows_out]
        step = min(rows_up, width)
        for begin in range(0, width, step):
            row = c * width + begin
            place = rows_up + row % rows_up
            gf_ref[row // rows_up, place : place + step] = down[begin : begin + step]
    pl.semaphore_wait(barrier, 1)
    early = max(0, 2 * rows_up - half)
    if early:
        give(0, early, 0).start()
    vec_ref[4:5] = jnp.sum(grad_normed * unit, axis=0, keepdims=True)
    vec_ref[5:6] = jnp.sum(grad_normed, axis=0, keepdims=True)
    scaled = grad_normed * gain
    grad_hidden = grad_result + inverse * (
        scaled - jnp.mean(scaled, axis=1, keepdims=True) - unit * jnp.mean(scaled * unit, axis=1, keepdims=True)
    )
    hidden_ref[...] = grad_hidden
    attn = grad_hidden.astype(BF16)
    gm_ref[...] = dot_nt(attn, wo[...]).astype(BF16)
    outer = dot_tn(mixed, attn).astype(BF16)
    for s in range(shards):
        gf_ref[s, 2 * rows_up : used] = outer[s * rows_out : (s + 1) * rows_out]
    give(early, half - early, 1).start()
    if early:
        give(0, early, 0).wait()
    give(early, half - early, 1).wait()
    for index in range(members):
        place = index % 2 * lines + index // 2
        begin = 0
        for size in chunks_f:
            rows = begin * members + place * size
            own = gf_ref[:, aligned(core * half + rows, size)].astype(F32)
            share_ref[index, :, begin : begin + size] = (own + landed[:, rows : rows + size].astype(F32)).astype(BF16)
            begin += size


def middle(shards, lines, chunks_f, cid, mask, x, mixed, teacher, out_grad, vectors, total, own, gathered):
    tokens, width = x.shape
    hidden = own[1].shape[1]
    rows_f = 4 * lines * sum(chunks_f)
    vmem = pl.BlockSpec(memory_space=pltpu.VMEM)
    hbm = pl.BlockSpec(memory_space=pl.ANY)
    return pl.pallas_call(
        functools.partial(middle_kernel, shards, tuple(chunks_f)),
        out_shape=(
            jax.ShapeDtypeStruct((tokens, width), BF16),
            jax.ShapeDtypeStruct((tokens, width), F32),
            jax.ShapeDtypeStruct((tokens, width), BF16),
            jax.ShapeDtypeStruct((2 * lines, shards, sum(chunks_f), width), BF16),
            jax.ShapeDtypeStruct((16, width), F32),
        ),
        in_specs=[vmem] * 7 + [hbm] * 6,
        out_specs=(vmem,) * 5,
        scratch_shapes=[
            pltpu.VMEM((width, width), BF16),
            pltpu.VMEM((width, hidden), BF16),
            pltpu.VMEM((hidden, width), BF16),
            pltpu.VMEM((tokens, hidden), F32),
            pltpu.VMEM((tokens, hidden), BF16),
            pltpu.VMEM((shards, rows_f, width), BF16),
            pltpu.VMEM((shards, rows_f // 2, width), BF16),
            pltpu.SemaphoreType.DMA((3, shards)),
            pltpu.SemaphoreType.DMA((2,)),
            pltpu.SemaphoreType.DMA((2,)),
        ],
        compiler_params=pltpu.CompilerParams(collective_id=cid, has_side_effects=True, vmem_limit_bytes=56 * 2**20),
        cost_estimate=pl.CostEstimate(flops=4 * 10**9, bytes_accessed=20 * 2**20, transcendentals=10**6),
        name="middle",
    )(mask, x, mixed, teacher, out_grad, vectors, total, *own, *gathered)


def body(
    inputs, block_perm, seq_lengths, loss_mask, teacher, out_grad, gain_one, bias_one, w_query, w_key, w_value,
    w_output, w_pos, content_bias, position_bias, gain_two, bias_two, w_up, bias_up, w_down, bias_down,
):
    width = inputs.shape[2]
    shards = lax.axis_size("wsh")
    members = lax.axis_size("ctx")
    lines = members // 4
    hidden = bias_up.shape[0] * shards
    blocks = block_perm.shape[1]
    limit = blocks // 2 + 1
    rows_up, rows_out = hidden // shards, width // shards

    frequency = np.exp(np.arange(width // 2) * (-2.0 * math.log(10000.0) / width))
    far_angle = (np.arange(-(-limit // 8) * 8) * BLK + (BLK - 1))[:, None] * frequency[None]
    near_angle = np.arange(BLK)[:, None] * frequency[None]
    far = jnp.asarray(np.stack([np.sin(far_angle), np.cos(far_angle)]), F32)
    near = jnp.asarray(np.stack([np.sin(near_angle), np.cos(near_angle)]), F32)

    keys, values, unit_all, pos_keys, table, qc, qp, weights, wo, wu, wd, vectors, total = start(
        lines, shards, 0, limit, inputs[0], (w_key, w_value, w_pos, w_query, w_output, w_up, w_down),
        (gain_one, bias_one, content_bias, position_bias, gain_two, bias_two, bias_down, bias_up), loss_mask, far, near,
    )
    mixed, linv, probs = attn_fwd(block_perm, seq_lengths, qc, qp, keys, values, pos_keys, blocks, limit)

    step = 4 * lines
    need = -(-(2 * rows_up + rows_out) // step)
    pieces = -(-need // 16)
    chunks_f = ((pieces + 1) // 2 * 16, pieces // 2 * 16) if pieces > 1 else (16,)
    rows_f = step * sum(chunks_f)
    if rows_out % (64 * lines):
        sets, rows_l = (("q", "p"), ("k", "v")), -(-2 * rows_out // (64 * lines)) * 64 * lines
    else:
        sets, rows_l = (("q",), ("p",), ("k",), ("v",)), rows_out
    output, grad_hidden, grad_mixed, early, vec = middle(
        shards, lines, chunks_f, 2, loss_mask, inputs[0], mixed, teacher[0], out_grad[0], vectors, total,
        (w_output, w_up, w_down), (wo, wu, wd),
    )
    same_core = [[i for i in range(members) if i % 2 == c] for c in range(2)]
    come = lax.psum_scatter(early, "ctx", scatter_dimension=0, axis_index_groups=same_core, tiled=True)[0]
    grad_query, bias_grads, dk_t, dv_t, dpk_t = attn_bwd(
        block_perm, seq_lengths, qc, qp, keys, values, pos_keys, probs, linv, grad_mixed, mixed, blocks, limit
    )
    grad_input, sums, vsum = finish(
        lines, shards, chunks_f, sets, rows_l, 1, come, dk_t, dv_t, unit_all, dpk_t, table, weights, grad_query,
        inputs[0], vectors, total, vec, bias_grads, grad_hidden,
    )
    (
        grad_input, g_query, g_key, g_value, g_output, g_pos, g_up, g_down,
        v_g1, v_b1, v_cb, v_pb, v_g2, v_b2, v_bd, v_bu, loss,
    ) = unpack(shards, rows_f, sets, rows_l, hidden, sums, vsum, total, grad_input)
    return (
        output[None], loss.reshape(()), grad_input[None], v_g1, v_b1, g_query, g_key, g_value, g_output, g_pos,
        v_cb, v_pb, v_g2, v_b2, g_up, v_bu, g_down, v_bd,
    )


def solution(mesh):
    rows = P("wsh", "ctx", None)
    vector = P("wsh")
    matrix = P("wsh", None)
    placed = (
        rows, matrix, matrix, P("wsh", "ctx"), rows, rows, vector, vector, matrix, matrix, matrix, matrix, matrix,
        vector, vector, vector, vector, matrix, vector, matrix, vector,
    )
    out = (
        rows, P(), rows, vector, vector, matrix, matrix, matrix, matrix, matrix, vector, vector, vector, vector,
        matrix, vector, matrix, vector,
    )
    return jax.shard_map(body, mesh=mesh, in_specs=placed, out_specs=out, check_vma=False)
```

```python
import functools
import math

import jax
import jax.numpy as jnp
import numpy as np
from jax import lax
from jax.experimental import pallas as pl
from jax.experimental.pallas import tpu as pltpu
from jax.sharding import PartitionSpec as P

HEADS = 8
HEAD = 64
PAIRS = HEADS // 2
BLK = 128
ROWS = HEADS * BLK
NEG = -1e30
epsilon = 1e-05
F32 = jnp.float32
BF16 = jnp.bfloat16


def dot_nt(a, b):
    return lax.dot_general(a, b, (((1,), (1,)), ((), ())), preferred_element_type=F32)


def dot_nn(a, b):
    return lax.dot_general(a, b, (((1,), (0,)), ((), ())), preferred_element_type=F32)


def dot_tn(a, b):
    return lax.dot_general(a, b, (((0,), (0,)), ((), ())), preferred_element_type=F32)


def iotas():
    row = lax.broadcasted_iota(jnp.int32, (BLK, BLK), 0)
    col = lax.broadcasted_iota(jnp.int32, (BLK, BLK), 1)
    return row, col


def read_places(perm_ref, lengths_ref, meta, blocks, count):
    device = lax.axis_index("ctx")
    meta[0] = perm_ref[0, 2 * device]
    meta[1] = perm_ref[0, 2 * device + 1]

    def place(slot, _):
        meta[2 + perm_ref[0, slot]] = slot
        return 0

    lax.fori_loop(0, blocks, place, 0)
    end = jnp.int32(0)
    for e in range(count):
        end = end + lengths_ref[0, e]
        meta[2 + blocks + e] = end


def block_range(meta, a, blocks, limit):
    qb = meta[a]
    first = qb * BLK
    low = jnp.int32(0)
    for e in range(meta.shape[0] - 2 - blocks):
        end = meta[2 + blocks + e]
        low = jnp.where(first >= end, jnp.maximum(low, end), low)
    lowest = low // BLK
    return qb, lowest, jnp.minimum(qb - lowest + 1, limit)


def stack_heads(pair):
    lane = lax.broadcasted_iota(jnp.int32, pair.shape, 1)
    zero = jnp.zeros_like(pair)
    return jnp.concatenate([jnp.where(lane < HEAD, pair, zero), jnp.where(lane >= HEAD, pair, zero)], axis=0)


def flip_rows(x):
    index = 7 - lax.broadcasted_iota(jnp.int32, (8, BLK), 0)
    slabs = [jnp.take_along_axis(x[8 * g : 8 * g + 8], index, axis=0) for g in reversed(range(BLK // 8))]
    return jnp.concatenate(slabs, axis=0)


def flip_two(x):
    return jnp.concatenate([flip_rows(x[:BLK]), flip_rows(x[BLK:])], axis=0)


def attn_fwd_kernel(
    blocks, limit, perm_ref, lengths_ref, qc_ref, qp_ref, k_ref, v_ref, pk_ref, mixed_ref, linv_ref, p_ref,
    meta, q2c, q2p, prev, top, total, acc, s_scr, p_buf, p_sem,
):
    read_places(perm_ref, lengths_ref, meta, blocks, lengths_ref.shape[1])
    row, col = iotas()
    tri = col <= row

    def p_copy(slot, index):
        return pltpu.make_async_copy(p_buf.at[slot], p_ref.at[index], p_sem.at[slot])

    def one_query_block(a, _):
        qb, lowest, count = block_range(meta, a, blocks, limit)
        rows_a = pl.ds(pl.multiple_of(a * BLK, BLK), BLK)
        pos = qb * BLK + row
        start = jnp.zeros((BLK, BLK), jnp.int32)
        for e in range(meta.shape[0] - 2 - blocks):
            end = meta[2 + blocks + e]
            start = jnp.where(pos >= end, jnp.maximum(start, end), start)
        for hp in range(PAIRS):
            lanes = slice(hp * BLK, (hp + 1) * BLK)
            q2c[hp] = stack_heads(qc_ref[rows_a, lanes].astype(F32)).astype(BF16)
            q2p[hp] = stack_heads(qp_ref[rows_a, lanes].astype(F32)).astype(BF16)
        prev[...] = jnp.zeros_like(prev)
        top[...] = jnp.full_like(top, NEG)
        total[...] = jnp.zeros_like(total)
        acc[...] = jnp.zeros_like(acc)

        def score_step(d, _):
            kb = qb - d
            off = pl.multiple_of(meta[2 + kb] * BLK, BLK)
            place = kb * BLK + col
            bias = jnp.where((place >= start) & (place <= pos), 0.0, NEG).astype(F32)
            drow = pl.multiple_of(d * BLK, BLK)
            for hp in range(PAIRS):
                lanes = slice(hp * BLK, (hp + 1) * BLK)
                s = dot_nt(q2c[hp], k_ref[pl.ds(off, BLK), lanes])
                r = dot_nt(q2p[hp], pk_ref[pl.ds(drow, BLK), lanes])
                for half in range(2):
                    part = slice(half * BLK, (half + 1) * BLK)
                    rows = slice((2 * hp + half) * BLK, (2 * hp + half + 1) * BLK)
                    rot = pltpu.roll(r[part], 1, 1, stride=1, stride_axis=0)
                    score = s[part] + jnp.where(tri, rot, prev[rows]) + bias
                    prev[rows] = rot
                    s_scr[d, rows] = score
                    top[rows] = jnp.maximum(top[rows], score)
            return 0

        lax.fori_loop(0, count, score_step, 0)
        for h in range(HEADS):
            rows = slice(h * BLK, (h + 1) * BLK)
            top[rows] = jnp.broadcast_to(jnp.max(top[rows], axis=1, keepdims=True), (BLK, BLK))

        def mix_step(d, _):
            kb = qb - d
            off = pl.multiple_of(meta[2 + kb] * BLK, BLK)
            slot = lax.rem(d, 2)

            @pl.when(d >= 2)
            def _():
                p_copy(slot, 0).wait()

            for hp in range(PAIRS):
                lanes = slice(hp * BLK, (hp + 1) * BLK)
                rows = slice(2 * hp * BLK, 2 * (hp + 1) * BLK)
                p = jnp.exp(s_scr[d, rows] - top[rows])
                total[rows] += p
                p_buf[slot, rows] = flip_two(p).astype(BF16)
                acc[hp] += dot_nn(p.astype(BF16), v_ref[pl.ds(off, BLK), lanes])
            p_copy(slot, a * limit + d).start()
            return 0

        lax.fori_loop(0, count, mix_step, 0)
        p_copy(lax.rem(count - 1, 2), 0).wait()

        @pl.when(count >= 2)
        def _():
            p_copy(lax.rem(count, 2), 0).wait()

        lane = lax.broadcasted_iota(jnp.int32, (BLK, BLK), 1)
        for hp in range(PAIRS):
            lanes = slice(hp * BLK, (hp + 1) * BLK)
            parts = []
            for half in range(2):
                h = 2 * hp + half
                rows = slice(h * BLK, (h + 1) * BLK)
                inv = 1.0 / jnp.sum(total[rows], axis=1, keepdims=True)
                inv = jnp.broadcast_to(inv, (BLK, BLK))
                linv_ref[a, rows] = inv
                parts.append(acc[hp, half * BLK : (half + 1) * BLK] * inv)
            mixed_ref[rows_a, lanes] = jnp.where(lane < HEAD, parts[0], parts[1])
        return 0

    lax.fori_loop(0, 2, one_query_block, 0)


def attn_fwd(perm, lengths, qc, qp, k, v, pk, blocks, limit):
    tokens, width = qc.shape
    vmem = pl.BlockSpec(memory_space=pltpu.VMEM)
    return pl.pallas_call(
        functools.partial(attn_fwd_kernel, blocks, limit),
        out_shape=(
            jax.ShapeDtypeStruct((tokens, width), F32),
            jax.ShapeDtypeStruct((2, ROWS, BLK), F32),
            jax.ShapeDtypeStruct((2 * limit, ROWS, BLK), BF16),
        ),
        in_specs=[pl.BlockSpec(memory_space=pltpu.SMEM)] * 2 + [vmem] * 5,
        out_specs=(vmem, vmem, pl.BlockSpec(memory_space=pl.ANY)),
        scratch_shapes=[
            pltpu.SMEM((2 + blocks + lengths.shape[1],), jnp.int32),
            pltpu.VMEM((PAIRS, 2 * BLK, BLK), BF16),
            pltpu.VMEM((PAIRS, 2 * BLK, BLK), BF16),
            pltpu.VMEM((ROWS, BLK), F32),
            pltpu.VMEM((ROWS, BLK), F32),
            pltpu.VMEM((ROWS, BLK), F32),
            pltpu.VMEM((PAIRS, 2 * BLK, BLK), F32),
            pltpu.VMEM((limit, ROWS, BLK), F32),
            pltpu.VMEM((2, ROWS, BLK), BF16),
            pltpu.SemaphoreType.DMA((2,)),
        ],
        compiler_params=pltpu.CompilerParams(vmem_limit_bytes=56 * 2**20),
        cost_estimate=pl.CostEstimate(flops=3 * 10**9, bytes_accessed=20 * 2**20, transcendentals=4 * 10**6),
        name="attn_fwd",
    )(perm, lengths, qc, qp, k, v, pk)


def attn_bwd_kernel(
    blocks, limit, perm_ref, lengths_ref, qc_ref, qp_ref, k_ref, v_ref, pk_ref, p_ref, linv_ref, gm_ref, mixed_ref,
    dq_ref, bias_ref, dk_ref, dv_ref, dpk_ref,
    meta, q2c_t, q2p_t, gm2, gm2_t, dd, carry, dqk, dqp, dpk, p_buf, p_sem,
):
    read_places(perm_ref, lengths_ref, meta, blocks, lengths_ref.shape[1])
    row, col = iotas()
    tri = col <= BLK - 1 - row
    dk_ref[...] = jnp.zeros_like(dk_ref)
    dv_ref[...] = jnp.zeros_like(dv_ref)
    dpk[...] = jnp.zeros_like(dpk)
    bias_ref[...] = jnp.zeros_like(bias_ref)

    def p_copy(slot, index):
        return pltpu.make_async_copy(p_ref.at[index], p_buf.at[slot], p_sem.at[slot])

    def one_query_block(a, _):
        qb, lowest, count = block_range(meta, a, blocks, limit)
        rows_a = pl.ds(pl.multiple_of(a * BLK, BLK), BLK)
        p_copy(0, a * limit + count - 1).start()
        for hp in range(PAIRS):
            lanes = slice(hp * BLK, (hp + 1) * BLK)
            rows = slice(2 * hp * BLK, 2 * (hp + 1) * BLK)
            q2c_t[hp] = stack_heads(flip_rows(qc_ref[rows_a, lanes].astype(F32))).T.astype(BF16)
            q2p_t[hp] = stack_heads(flip_rows(qp_ref[rows_a, lanes].astype(F32))).T.astype(BF16)
            g = stack_heads(gm_ref[rows_a, lanes].astype(F32))
            scaled = flip_two(g * linv_ref[a, rows])
            gm2[hp] = scaled.astype(BF16)
            gm2_t[hp] = scaled.T.astype(BF16)
            pair = flip_rows(mixed_ref[rows_a, lanes])
            dd[rows] = jnp.broadcast_to(
                jnp.sum(scaled * jnp.concatenate([pair, pair], axis=0), axis=1, keepdims=True), (2 * BLK, BLK)
            )
        carry[...] = jnp.zeros_like(carry)
        dqk[...] = jnp.zeros_like(dqk)
        dqp[...] = jnp.zeros_like(dqp)

        def step(t, _):
            d = count - 1 - t
            kb = qb - d
            off = pl.multiple_of(meta[2 + kb] * BLK, BLK)
            keys = pl.ds(off, BLK)
            drow = pl.ds(pl.multiple_of(d * BLK, BLK), BLK)
            slot = lax.rem(t, 2)
            p_copy(slot, 0).wait()

            @pl.when(d >= 1)
            def _():
                p_copy(1 - slot, a * limit + d - 1).start()

            for hp in range(PAIRS):
                lanes = slice(hp * BLK, (hp + 1) * BLK)
                rows = slice(2 * hp * BLK, 2 * (hp + 1) * BLK)
                p = p_buf[slot, rows]
                g = dot_nt(gm2[hp], v_ref[keys, lanes])
                gs = p.astype(F32) * (g - dd[rows])
                gs_low = gs.astype(BF16)
                gs = gs_low.astype(F32)
                rots = []
                for half in range(2):
                    part = slice(half * BLK, (half + 1) * BLK)
                    crow = slice((2 * hp + half) * BLK, (2 * hp + half + 1) * BLK)
                    both = jnp.where(tri, gs[part], carry[crow])
                    carry[crow] = gs[part]
                    rots.append(pltpu.roll(both, 0, 1, stride=1, stride_axis=0))
                rot = jnp.concatenate(rots, axis=0).astype(BF16)
                dqk[hp] += dot_nn(gs_low, k_ref[keys, lanes])
                dqp[hp] += dot_nn(rot, pk_ref[drow, lanes])
                dk_ref[lanes, keys] = (dk_ref[lanes, keys].astype(F32) + dot_nn(q2c_t[hp], gs_low)).astype(BF16)
                dv_ref[lanes, keys] = (dv_ref[lanes, keys].astype(F32) + dot_nn(gm2_t[hp], p)).astype(BF16)
                dpk[lanes, drow] += dot_nn(q2p_t[hp], rot)
            return 0

        lax.fori_loop(0, count, step, 0)
        lane = lax.broadcasted_iota(jnp.int32, (BLK, BLK), 1)
        for hp in range(PAIRS):
            lanes = slice(hp * BLK, (hp + 1) * BLK)
            ck = jnp.where(lane < HEAD, dqk[hp, :BLK], dqk[hp, BLK:]) * 0.125
            cp = jnp.where(lane < HEAD, dqp[hp, :BLK], dqp[hp, BLK:]) * 0.125
            dq_ref[rows_a, lanes] = flip_rows(ck + cp).astype(BF16)
            bias_ref[0:1, lanes] += jnp.sum(ck, axis=0, keepdims=True)
            bias_ref[1:2, lanes] += jnp.sum(cp, axis=0, keepdims=True)
        return 0

    lax.fori_loop(0, 2, one_query_block, 0)
    dpk_ref[...] = dpk[...].astype(BF16)


def attn_bwd(perm, lengths, qc, qp, k, v, pk, p, linv, gm, mixed, blocks, limit):
    tokens, width = qc.shape
    keys = k.shape[0]
    span = pk.shape[0]
    vmem = pl.BlockSpec(memory_space=pltpu.VMEM)
    return pl.pallas_call(
        functools.partial(attn_bwd_kernel, blocks, limit),
        out_shape=(
            jax.ShapeDtypeStruct((tokens, width), BF16),
            jax.ShapeDtypeStruct((8, width), F32),
            jax.ShapeDtypeStruct((width, keys), BF16),
            jax.ShapeDtypeStruct((width, keys), BF16),
            jax.ShapeDtypeStruct((width, span), BF16),
        ),
        in_specs=[pl.BlockSpec(memory_space=pltpu.SMEM)] * 2
        + [vmem] * 5
        + [pl.BlockSpec(memory_space=pl.ANY)]
        + [vmem] * 3,
        out_specs=(vmem,) * 5,
        scratch_shapes=[
            pltpu.SMEM((2 + blocks + lengths.shape[1],), jnp.int32),
            pltpu.VMEM((PAIRS, BLK, 2 * BLK), BF16),
            pltpu.VMEM((PAIRS, BLK, 2 * BLK), BF16),
            pltpu.VMEM((PAIRS, 2 * BLK, BLK), BF16),
            pltpu.VMEM((PAIRS, BLK, 2 * BLK), BF16),
            pltpu.VMEM((ROWS, BLK), F32),
            pltpu.VMEM((ROWS, BLK), F32),
            pltpu.VMEM((PAIRS, 2 * BLK, BLK), F32),
            pltpu.VMEM((PAIRS, 2 * BLK, BLK), F32),
            pltpu.VMEM((width, span), F32),
            pltpu.VMEM((2, ROWS, BLK), BF16),
            pltpu.SemaphoreType.DMA((2,)),
        ],
        compiler_params=pltpu.CompilerParams(vmem_limit_bytes=60 * 2**20),
        cost_estimate=pl.CostEstimate(flops=6 * 10**9, bytes_accessed=30 * 2**20, transcendentals=0),
        name="attn_bwd",
    )(perm, lengths, qc, qp, k, v, pk, p, linv, gm, mixed)


MESH = pl.DeviceIdType.MESH


def fold_rows(x):
    return jnp.broadcast_to(x, (x.shape[0], BLK)).T[0:1]


def aligned(begin, size):
    return pl.ds(pl.multiple_of(begin, math.gcd(size, 16)), size)


def finish_kernel(
    lines, shards, chunks_f, sets, rows_l,
    mine_ref, come_ref, dk_ref, dv_ref, unit_all_ref, dpk_ref, table_ref, weights_in, dq_ref, x_ref,
    vectors_ref, total_ref, vec_ref, bias_ref, hidden_in,
    grad_ref, sums_ref, vsum_ref,
    dk_buf, dv_buf, un_buf, in_sem, dpk_buf, table_buf, weights_ref, hidden_ref, pos_sem, m_q, mt_k, mt_v, cs_q, cs_k, cs_v, dxp, bx0, bx1, bx2, vbuf, vacc,
    *rest,
):
    wk_ref, wv_ref, wq_ref = weights_ref.at[0], weights_ref.at[1], weights_ref.at[3]
    tokens, width = dq_ref.shape
    bufs_f = rest[: 3 * len(chunks_f)]
    bufs_l = rest[3 * len(chunks_f) : -2]
    send_sem, recv_sem = rest[-2:]
    ctx = lax.axis_index("ctx")
    w = lax.axis_index("wsh")
    core = lax.rem(ctx, 2)
    b = lax.rem(ctx // 2, 2)
    a = ctx // 4

    def at(a_to, b_to, core_to):
        return (a_to * 2 + b_to) * 2 + core_to

    def line_peer(s):
        return (at(lax.rem(a + s, lines), b, core), w)

    def shard_peer(s):
        return (ctx, lax.rem(w + s, shards))

    core_peer = (at(a, b, 1 - core), w)
    b_peer = (at(a, 1 - b, core), w)
    peers = [core_peer, b_peer] + [line_peer(s) for s in range(1, lines)] + [shard_peer(s) for s in range(1, shards)]
    barrier = pltpu.get_barrier_semaphore()
    for peer in peers:
        pl.semaphore_signal(barrier, inc=1, device_id=peer, device_id_type=MESH)

    counter = [0]

    def take(number):
        begin = counter[0]
        counter[0] += number
        return begin

    def remote(src, dst, index, peer):
        return pltpu.make_async_remote_copy(
            src_ref=src, dst_ref=dst, send_sem=send_sem.at[index], recv_sem=recv_sem.at[index],
            device_id=peer, device_id_type=MESH,
        )

    bits = lines.bit_length() - 1
    order = []
    for bit in range(bits):
        order += [m for m in reversed(range(lines)) if m & ((1 << (bit + 1)) - 1) == 1 << bit]
    order.append(0)

    def other(mask):
        place = 0
        for bit in range(bits):
            own = lax.rem(a // (1 << bit), 2)
            place = place + (1 << bit) * ((1 - own) if mask >> bit & 1 else own)
        return place

    def line_place(j):
        place = jnp.int32(0)
        for index, mask in enumerate(order):
            place = place + jnp.where(j == index, other(mask), 0)
        return place

    def line_at(mask):
        return (at(other(mask), b, core), w)

    group = 4 * tokens

    def fetch(j, slot):
        begin = pl.multiple_of(line_place(j) * group, group)
        return (
            pltpu.make_async_copy(dk_ref.at[:, pl.ds(begin, group)], dk_buf.at[slot], in_sem.at[slot, 0]),
            pltpu.make_async_copy(dv_ref.at[:, pl.ds(begin, group)], dv_buf.at[slot], in_sem.at[slot, 1]),
            pltpu.make_async_copy(unit_all_ref.at[pl.ds(begin, group)], un_buf.at[slot], in_sem.at[slot, 2]),
        )

    span, hold = table_ref.shape[0], table_buf.shape[0]
    pos_parts = [(begin, min(hold, span - begin)) for begin in range(0, span, hold)]

    def pos_copies(begin, size):
        rows = pl.ds(begin, size)
        return [
            pltpu.make_async_copy(dpk_ref.at[:, rows], dpk_buf.at[:, 0:size], pos_sem.at[0]),
            pltpu.make_async_copy(table_ref.at[rows], table_buf.at[0:size], pos_sem.at[1]),
        ]

    weights_copy = pltpu.make_async_copy(weights_in, weights_ref, pos_sem.at[2])
    hidden_copy = pltpu.make_async_copy(hidden_in, hidden_ref, pos_sem.at[3])
    weights_copy.start()
    for copy in fetch(0, 0):
        copy.start()
    for copy in pos_copies(*pos_parts[0]):
        copy.start()
    hidden_copy.start()

    def start_all(copies):
        for copy in copies:
            copy.start()

    def wait_all(copies):
        for copy in copies:
            copy.wait()

    def own_bit(bit):
        return lax.rem(a // (1 << bit), 2)

    def bit_peer(bit):
        return line_at(1 << bit)

    class Feed:
        def __init__(self, begin, rows, total_rows, bufs):
            self.begin, self.rows = begin, rows
            self.rc, self.rb = total_rows // 2, total_rows // 4
            self.b0, self.b1, self.b2 = bufs
            self.iy, self.irs, self.iag, self.ix, self.ic = take(shards - 1), take(bits), take(bits), take(1), take(2)

        def region(self, bit):
            start = 0
            for k in range(bit):
                start = start + own_bit(k) * (self.rows >> (k + 1))
            return start, self.rows >> bit

        def y_copies(self):
            return [
                remote(self.b0.at[lax.rem(w + s, shards)], self.b1.at[s - 1], self.iy + s - 1, shard_peer(s))
                for s in range(1, shards)
            ]

        def rs_copies(self, bit):
            start, size = self.region(bit)
            size = size // 2
            give = aligned(start + (1 - own_bit(bit)) * size, size)
            begin = sum(self.rows >> (k + 1) for k in range(bit))
            return [remote(self.b1.at[0, give], self.b2.at[begin : begin + size], self.irs + bit, bit_peer(bit))]

        def place(self, b_of, begin, size):
            return aligned(core * self.rc + b_of * self.rb + self.begin + begin, size)

        def ag_copies(self, bit):
            own = self.place(b, *self.region(bit + 1))
            return [remote(sums_ref.at[own], sums_ref.at[own], self.iag + bit, bit_peer(bit))]

        def x_copies(self):
            own = self.place(b, 0, self.rows)
            return [remote(sums_ref.at[own], sums_ref.at[own], self.ix, b_peer)]

        def c_copies(self):
            return [
                remote(sums_ref.at[rows], sums_ref.at[rows], self.ic + k, core_peer)
                for k, rows in enumerate((self.place(b, 0, self.rows), self.place(1 - b, 0, self.rows)))
            ]

        def y(self):
            rows = pl.ds(self.begin, self.rows)
            self.b0[...] = (mine_ref[:, rows].astype(F32) + come_ref[:, rows].astype(F32)).astype(BF16)
            start_all(self.y_copies())

        def rs(self, bit):
            if bit == 0:
                wait_all(self.y_copies())
                total = self.b0[w].astype(F32)
                for s in range(shards - 1):
                    total = total + self.b1[s].astype(F32)
                self.b1[0] = total.astype(BF16)
            else:
                self.add(bit - 1)
            start_all(self.rs_copies(bit))

        def add(self, bit):
            wait_all(self.rs_copies(bit))
            start, size = self.region(bit + 1)
            begin = sum(self.rows >> (k + 1) for k in range(bit))
            rows = aligned(start, size)
            self.b1[0, rows] = (self.b1[0, rows].astype(F32) + self.b2[begin : begin + size].astype(F32)).astype(BF16)

        def ag(self, bit):
            if bit == bits - 1:
                self.add(bit)
                start, size = self.region(bits)
                sums_ref[self.place(b, start, size)] = self.b1[0, aligned(start, size)]
            else:
                wait_all(self.ag_copies(bit + 1))
            start_all(self.ag_copies(bit))

        def x(self):
            wait_all(self.ag_copies(0))
            start_all(self.x_copies())

        def c(self):
            wait_all(self.x_copies())
            start_all(self.c_copies())

        def done(self):
            wait_all(self.c_copies())

    class Late:
        def __init__(self, out, rows, names, bufs):
            self.out, self.rows, self.names, self.begun = out, rows, names, set()
            self.src, self.b0, self.b1, self.b2, self.b3 = bufs
            self.rc, self.rb, self.share = rows // 2, rows // 4, rows // 4 // lines
            self.i0, self.iy, self.i2 = take(1), take(shards - 1), take(1)
            self.irs, self.iag, self.ix, self.ic = take(lines - 1), take(lines - 1), take(1), take(1)

        def c0_copies(self):
            return [remote(self.src.at[:, aligned((1 - core) * self.rc, self.rc)], self.b0, self.i0, core_peer)]

        def y_copies(self):
            return [
                remote(self.b0.at[lax.rem(w + s, shards)], self.b1.at[s - 1], self.iy + s - 1, shard_peer(s))
                for s in range(1, shards)
            ]

        def x0_copies(self):
            return [remote(self.b1.at[0, aligned((1 - b) * self.rb, self.rb)], self.b2, self.i2, b_peer)]

        def rs_copies(self):
            return [
                remote(
                    self.b2.at[aligned(lax.rem(a + s, lines) * self.share, self.share)],
                    self.b3.at[s - 1], self.irs + s - 1, line_peer(s),
                )
                for s in range(1, lines)
            ]

        def ag_copies(self):
            own = aligned(self.out + core * self.rc + b * self.rb + a * self.share, self.share)
            return [remote(sums_ref.at[own], sums_ref.at[own], self.iag + s - 1, line_peer(s)) for s in range(1, lines)]

        def x_copies(self):
            own = aligned(self.out + core * self.rc + b * self.rb, self.rb)
            return [remote(sums_ref.at[own], sums_ref.at[own], self.ix, b_peer)]

        def c_copies(self):
            own = aligned(self.out + core * self.rc, self.rc)
            return [remote(sums_ref.at[own], sums_ref.at[own], self.ic, core_peer)]

        def c0(self):
            for m, name in enumerate(self.names):
                grad = gradient(name)
                for s in range(shards):
                    self.src[s, m * rows_out : (m + 1) * rows_out] = grad[s * rows_out : (s + 1) * rows_out].astype(BF16)
            used = len(self.names) * rows_out
            if used < rows_l:
                self.src[:, used:] = jnp.zeros((shards, rows_l - used, width), BF16)
            start_all(self.c0_copies())

        def y(self):
            wait_all(self.c0_copies())
            own = self.src[:, aligned(core * self.rc, self.rc)]
            self.b0[...] = (self.b0[...].astype(F32) + own.astype(F32)).astype(BF16)
            start_all(self.y_copies())

        def x0(self):
            wait_all(self.y_copies())
            total = self.b0[w].astype(F32)
            for s in range(shards - 1):
                total = total + self.b1[s].astype(F32)
            self.b1[0] = total.astype(BF16)
            start_all(self.x0_copies())

        def rs(self):
            wait_all(self.x0_copies())
            own = self.b1[0, aligned(b * self.rb, self.rb)]
            self.b2[...] = (self.b2[...].astype(F32) + own.astype(F32)).astype(BF16)
            start_all(self.rs_copies())

        def ag(self):
            wait_all(self.rs_copies())
            total = self.b2[aligned(a * self.share, self.share)].astype(F32)
            for s in range(lines - 1):
                total = total + self.b3[s].astype(F32)
            own = aligned(self.out + core * self.rc + b * self.rb + a * self.share, self.share)
            sums_ref[own] = total.astype(BF16)
            start_all(self.ag_copies())

        def x(self):
            wait_all(self.ag_copies())
            start_all(self.x_copies())

        def c(self):
            wait_all(self.x_copies())
            start_all(self.c_copies())

        def done(self):
            wait_all(self.c_copies())

    rows_f = 4 * sum(chunks_f)
    rows_out = width // shards
    feeds = []
    begin = 0
    for index, rows in enumerate(chunks_f):
        feeds.append(Feed(begin, rows, rows_f, bufs_f[3 * index : 3 * index + 3]))
        begin += rows
    lates = {}
    for index, names in enumerate(sets):
        late = Late(rows_f + index * rows_l, rows_l, names, bufs_l[5 * index : 5 * index + 5])
        for name in names:
            lates[name] = late

    def late_step(name, step):
        late = lates[name]
        if step not in late.begun:
            late.begun.add(step)
            getattr(late, step)()

    values = x_ref[...].astype(F32)
    center = values - jnp.mean(values, axis=1, keepdims=True)
    inverse = lax.rsqrt(jnp.mean(center * center, axis=1, keepdims=True) + epsilon)
    unit = center * inverse

    def gradient(name):
        cols = vectors_ref[0:8].T
        gain_col, bias_col = cols[:, 0:1], cols[:, 1:2]
        if name == "q":
            m_q[...] = dot_tn(unit.astype(BF16), dq_ref[...])
            cs_q[...] = jnp.broadcast_to(jnp.sum(dq_ref[...].astype(F32), axis=0, keepdims=True), cs_q.shape)
            return gain_col * m_q[...] + bias_col * cs_q[0:1]
        if name == "p":
            total = jnp.zeros((width, width), F32)
            for index, (begin, size) in enumerate(pos_parts):
                if index:
                    start_all(pos_copies(begin, size))
                wait_all(pos_copies(begin, size))
                total = total + dot_nn(dpk_buf[:, 0:size], table_buf[0:size])
            return total.T
        m, cs = (mt_k, cs_k) if name == "k" else (mt_v, cs_v)
        return gain_col * m[...] + bias_col * fold_rows(cs[:, 0:1])

    mt_k[...] = jnp.zeros_like(mt_k)
    mt_v[...] = jnp.zeros_like(mt_v)
    cs_k[...] = jnp.zeros_like(cs_k)
    cs_v[...] = jnp.zeros_like(cs_v)
    pl.semaphore_wait(barrier, len(peers))
    for feed in feeds:
        feed.y()
    weights_copy.wait()

    i_x0, i_x1, i_x2 = take(lines), take(lines), take(lines)

    def copy_x0(j):
        return remote(dxp.at[j, 1 - core], bx0.at[j], i_x0 + j, core_peer)

    def copy_x1(j):
        return remote(bx0.at[j, 1 - b], bx1.at[j], i_x1 + j, b_peer)

    def copy_x2(mask):
        return remote(bx1.at[order.index(mask)], bx2.at[mask - 1], i_x2 + mask, line_at(mask & -mask))

    def after_x0(j):
        copy_x0(j).wait()
        bx0[j] = (bx0[j].astype(F32) + dxp[j, core].astype(F32)).astype(BF16)
        copy_x1(j).start()

    def after_x1(j):
        mask = order[j]
        copy_x1(j).wait()
        total = bx1[j].astype(F32) + bx0[j, b].astype(F32)
        for bit in range(bits):
            if mask and 1 << bit >= (mask & -mask):
                break
            source = mask | 1 << bit
            copy_x2(source).wait()
            total = total + bx2[source - 1].astype(F32)
        if mask:
            bx1[j] = total.astype(BF16)
            copy_x2(mask).start()
        return total

    last = lines - 1
    events = {}

    def plan(j, after, work, *args):
        events.setdefault((min(j, last), after), []).append((work, args))

    plan(0, "blocks", late_step, "p", "c0")
    plan(0, "blocks", after_x0, 0)
    plan(0, "blocks", late_step, "q", "c0")
    plan(1, "all", feeds[0].rs, 0)
    plan(1, "all", late_step, "q", "y")
    if last > 1:
        plan(1, "all", after_x0, 1)
    for j in range(2, last):
        plan(j + 1, "first", after_x0, j)
    plan(2, "blocks", after_x1, 0)
    for feed in feeds[1:]:
        plan(3, "blocks", feed.rs, 0)

    def happen(j, after):
        for (when, place), works in sorted(events.items()):
            if place == after:

                @pl.when(j == when)
                def _():
                    for work, args in works:
                        work(*args)

    def line_step(j, _):
        slot = lax.rem(j, 2)

        @pl.when(j < last)
        def _():
            start_all(fetch(j + 1, 1 - slot))

        wait_all(fetch(j, slot))

        def make_block(core_of, b_of):
            keys = pl.ds(pl.multiple_of((2 * b_of + core_of) * tokens, tokens), tokens)
            part = dot_nn(wk_ref[...], dk_buf[slot, :, keys]) + dot_nn(wv_ref[...], dv_buf[slot, :, keys])
            dxp[j, core_of, b_of] = part.astype(BF16)

        make_block(1 - core, 0)
        make_block(1 - core, 1)
        copy_x0(j).start()
        happen(j, "first")
        make_block(core, 0)
        make_block(core, 1)
        happen(j, "blocks")
        mt_k[...] += dot_nn(dk_buf[slot], un_buf[slot])
        mt_v[...] += dot_nn(dv_buf[slot], un_buf[slot])
        for cs, buf in ((cs_k, dk_buf), (cs_v, dv_buf)):
            total = cs[...]
            for piece in range(group // BLK):
                total = total + buf[slot, :, piece * BLK : (piece + 1) * BLK].astype(F32)
            cs[...] = total
        happen(j, "all")
        return 0

    lax.fori_loop(0, lines, line_step, 0)
    for m, cs in ((mt_k, cs_k), (mt_v, cs_v)):
        m[...] = m[...].T
        cs[...] = jnp.broadcast_to(jnp.sum(cs[...], axis=1, keepdims=True), cs.shape)

    vstages = [[core_peer], [b_peer], [line_peer(s) for s in range(1, lines)], [shard_peer(s) for s in range(1, shards)]]
    vslots = []
    place = 0
    for stage in vstages:
        vslots.append(place)
        place += len(stage)
    vbegin = take(place)

    def v_copy(stage, index):
        slot = vslots[stage] + index
        return remote(vacc.at[pl.ds(stage * 16, 16)], vbuf.at[slot], vbegin + slot, vstages[stage][index])

    def v_start(stage):
        for index in range(len(vstages[stage])):
            v_copy(stage, index).start()

    def v_finish(stage):
        total = vacc[stage * 16 : stage * 16 + 16]
        for index in range(len(vstages[stage])):
            v_copy(stage, index).wait()
            total = total + vbuf[vslots[stage] + index]
        vacc[(stage + 1) * 16 : (stage + 2) * 16] = total

    def vectors_begin():
        vacc[0:16] = vec_ref[...]
        vacc[2:4] = bias_ref[0:2]
        gain_grad = m_q[...] * wq_ref[...].astype(F32)
        gain_grad = gain_grad + mt_k[...] * wk_ref[...].astype(F32) + mt_v[...] * wv_ref[...].astype(F32)
        vacc[0:1] = fold_rows(jnp.sum(gain_grad, axis=1, keepdims=True))
        total = dot_nt(cs_q[...].astype(BF16), wq_ref[...])
        for cs, weight in ((cs_k, wk_ref), (cs_v, wv_ref)):
            row = jnp.broadcast_to(fold_rows(cs[:, 0:1]), (8, width))
            total = total + dot_nt(row.astype(BF16), weight[...])
        vacc[1:2] = total[0:1]
        v_start(0)

    def rest(feed, step):
        if step < bits:
            feed.rs(step)
        else:
            feed.ag(2 * bits - 1 - step)

    one, two = feeds[0], feeds[-1]
    pair = len(feeds) > 1
    late_step("v", "c0")
    vectors_begin()
    for step in range(1, bits):
        rest(one, step)
    if last > 1:
        after_x1(1)
    late_step("v", "y")
    after_x0(last)
    v_finish(0)
    v_start(1)
    late_step("p", "y")
    late_step("q", "x0")
    late_step("k", "c0")
    if pair:
        for step in range(1, bits):
            rest(two, step)
    rest(one, bits)
    late_step("k", "y")
    late_step("v", "x0")
    late_step("p", "x0")
    v_finish(1)
    v_start(2)
    if pair:
        rest(two, bits)
    late_step("k", "x0")
    for step in range(bits + 1, 2 * bits):
        rest(one, step)
    v_finish(2)
    v_start(3)
    for j in range(2, last):
        after_x1(j)
    if pair:
        for step in range(bits + 1, 2 * bits):
            rest(two, step)
    late_step("q", "rs")
    late_step("v", "rs")
    v_finish(3)
    vsum_ref[...] = vacc[4 * 16 : 5 * 16]
    late_step("p", "rs")
    one.x()
    late_step("k", "rs")
    own = after_x1(last)
    scaled = (own.T + dot_nt(dq_ref[...], wq_ref[...])) * vectors_ref[0:1]
    hidden_copy.wait()
    grad_ref[...] = hidden_ref[...] + inverse * (
        scaled - jnp.mean(scaled, axis=1, keepdims=True) - unit * jnp.mean(scaled * unit, axis=1, keepdims=True)
    )
    if pair:
        two.x()
    late_step("q", "ag")
    one.c()
    late_step("v", "ag")
    late_step("p", "ag")
    late_step("k", "ag")
    late_step("q", "x")
    late_step("v", "x")
    if pair:
        two.c()
    late_step("p", "x")
    late_step("k", "x")
    late_step("q", "c")
    late_step("v", "c")
    late_step("p", "c")
    late_step("k", "c")
    for feed in feeds:
        feed.done()
    for name in "qpvk":
        late_step(name, "done")


def finish(lines, shards, chunks_f, sets, rows_l, cid, mine, come, dk, dv, unit_all, dpk, table, weights, dq, x, vectors, total, vec, bias, hidden):
    tokens, width = dq.shape
    vmem = pl.BlockSpec(memory_space=pltpu.VMEM)
    hbm = pl.BlockSpec(memory_space=pl.ANY)
    bufs = []
    for rows in chunks_f:
        bufs += [
            pltpu.VMEM((shards, rows, width), BF16),
            pltpu.VMEM((shards - 1, rows, width), BF16),
            pltpu.VMEM((rows, width), BF16),
        ]
    for names in sets:
        bufs += [
            pltpu.VMEM((shards, rows_l, width), BF16),
            pltpu.VMEM((shards, rows_l // 2, width), BF16),
            pltpu.VMEM((shards - 1, rows_l // 2, width), BF16),
            pltpu.VMEM((rows_l // 4, width), BF16),
            pltpu.VMEM((lines - 1, rows_l // 4 // lines, width), BF16),
        ]
    hops = shards - 1 + 2 * (lines - 1)
    copies = len(chunks_f) * (shards + 2 + 2 * (lines.bit_length() - 1)) + len(sets) * (hops + 4) + 3 * lines + 2 + lines - 1 + shards - 1
    total_rows = 4 * sum(chunks_f) + len(sets) * rows_l
    stages = 1 + 1 + (lines - 1) + (shards - 1)
    hold = min(dpk.shape[1], 17 * BLK)
    return pl.pallas_call(
        functools.partial(finish_kernel, lines, shards, tuple(chunks_f), sets, rows_l),
        out_shape=(
            jax.ShapeDtypeStruct((tokens, width), F32),
            jax.ShapeDtypeStruct((total_rows, width), BF16),
            jax.ShapeDtypeStruct((16, width), F32),
        ),
        in_specs=[vmem] * 2 + [hbm] * 6 + [vmem] * 6 + [hbm],
        out_specs=(vmem,) * 3,
        scratch_shapes=[
            pltpu.VMEM((2, width, 4 * tokens), BF16),
            pltpu.VMEM((2, width, 4 * tokens), BF16),
            pltpu.VMEM((2, 4 * tokens, width), BF16),
            pltpu.SemaphoreType.DMA((2, 3)),
            pltpu.VMEM((width, hold), BF16),
            pltpu.VMEM((hold, width), BF16),
            pltpu.VMEM((4, width, width), BF16),
            pltpu.VMEM((tokens, width), F32),
            pltpu.SemaphoreType.DMA((4,)),
            pltpu.VMEM((width, width), F32),
            pltpu.VMEM((width, width), F32),
            pltpu.VMEM((width, width), F32),
            pltpu.VMEM((8, width), F32),
            pltpu.VMEM((width, BLK), F32),
            pltpu.VMEM((width, BLK), F32),
            pltpu.VMEM((lines, 2, 2, width, tokens), BF16),
            pltpu.VMEM((lines, 2, width, tokens), BF16),
            pltpu.VMEM((lines, width, tokens), BF16),
            pltpu.VMEM((lines - 1, width, tokens), BF16),
            pltpu.VMEM((stages, 16, width), F32),
            pltpu.VMEM((5 * 16, width), F32),
        ]
        + bufs
        + [pltpu.SemaphoreType.DMA((copies,)), pltpu.SemaphoreType.DMA((copies,))],
        compiler_params=pltpu.CompilerParams(
            collective_id=cid, has_side_effects=True, vmem_limit_bytes=63 * 2**20
        ),
        cost_estimate=pl.CostEstimate(flops=10**10, bytes_accessed=30 * 2**20, transcendentals=0),
        name="finish",
    )(mine, come, dk, dv, unit_all, dpk, table, weights, dq, x, vectors, total, vec, bias, hidden)


def unpack_kernel(
    shards, rows_f, sets, rows_l, sums_ref, vsum_ref, total_ref, grad_ref, result_ref,
    grad_out, result_out, q_out, k_out, v_out, o_out, p_out, u_out, d_out, g1_out, b1_out, cb_out, pb_out, g2_out, b2_out, bd_out, bu_out,
    loss_out,
    low, wide, up, in_sem, out_sem,
):
    width = vsum_ref.shape[1]
    rows_out, rows_up = q_out.shape[0], d_out.shape[0]
    parts = u_out.shape[1] // width
    w = lax.axis_index("wsh")
    pieces = [(rows_up, d_out), (2 * rows_up, o_out)]
    to = {"q": q_out, "p": p_out, "k": k_out, "v": v_out}
    for index, names in enumerate(sets):
        pieces += [(rows_f + index * rows_l + m * rows_out, to[name]) for m, name in enumerate(names)]
    ins = [pltpu.make_async_copy(sums_ref.at[0:rows_up], low.at[0:rows_up], in_sem.at[0])]
    for index, (begin, out) in enumerate(pieces):
        size = out.shape[0]
        ins.append(pltpu.make_async_copy(sums_ref.at[begin : begin + size], low.at[begin : begin + size], in_sem.at[1 + index]))
    for copy in ins:
        copy.start()
    outs = []
    grad_out[...] = grad_ref[...]
    result_out[...] = result_ref[...]
    ins[0].wait()
    for c in range(parts):
        up[:, c * width : (c + 1) * width] = low[c * rows_out : (c + 1) * rows_out].astype(F32)
    outs.append(pltpu.make_async_copy(up, u_out, out_sem.at[0]))
    outs[0].start()
    for index, (begin, out) in enumerate(pieces):
        size = out.shape[0]
        ins[1 + index].wait()
        wide[begin : begin + size] = low[begin : begin + size].astype(F32)
        copy = pltpu.make_async_copy(wide.at[begin : begin + size], out, out_sem.at[1 + index])
        copy.start()
        outs.append(copy)

    def share(row):
        part = vsum_ref[row : row + 1, 0:rows_out]
        for s in range(1, shards):
            part = jnp.where(w == s, vsum_ref[row : row + 1, s * rows_out : (s + 1) * rows_out], part)
        return part.reshape(rows_out)

    for row, ref in enumerate((g1_out, b1_out, cb_out, pb_out, g2_out, b2_out, bd_out)):
        ref[...] = share(row)
    per = rows_up // rows_out
    for q in range(per):
        part = None
        for s in range(shards):
            group = s * per + q
            row, place = 7 + group // shards, group % shards
            piece = vsum_ref[row : row + 1, place * rows_out : (place + 1) * rows_out]
            part = piece if part is None else jnp.where(w == s, piece, part)
        bu_out[q * rows_out : (q + 1) * rows_out] = part.reshape(rows_out)
    loss_out[0, 0] = vsum_ref[7 + parts, 0] / (total_ref[0, 0] * width)
    for copy in outs:
        copy.wait()


def unpack(shards, rows_f, sets, rows_l, hidden, sums, vsum, total, grad, result):
    tokens, width = grad.shape
    rows_out, rows_up = width // shards, hidden // shards
    vmem = pl.BlockSpec(memory_space=pltpu.VMEM)
    hbm = pl.BlockSpec(memory_space=pl.ANY)
    square = jax.ShapeDtypeStruct((rows_out, width), F32)
    vector = jax.ShapeDtypeStruct((rows_out,), F32)
    return pl.pallas_call(
        functools.partial(unpack_kernel, shards, rows_f, sets, rows_l),
        out_shape=(
            jax.ShapeDtypeStruct((tokens, width), F32), jax.ShapeDtypeStruct((tokens, width), BF16), square, square, square, square, square,
            jax.ShapeDtypeStruct((rows_out, hidden), F32), jax.ShapeDtypeStruct((rows_up, width), F32),
            vector, vector, vector, vector, vector, vector, vector, jax.ShapeDtypeStruct((rows_up,), F32),
            jax.ShapeDtypeStruct((1, 1), F32),
        ),
        in_specs=[hbm, vmem, vmem, vmem, vmem],
        out_specs=(vmem,) * 2 + (hbm,) * 7 + (vmem,) * 8 + (pl.BlockSpec(memory_space=pltpu.SMEM),),
        scratch_shapes=[
            pltpu.VMEM(sums.shape, BF16),
            pltpu.VMEM(sums.shape, F32),
            pltpu.VMEM((rows_out, hidden), F32),
            pltpu.SemaphoreType.DMA((7,)),
            pltpu.SemaphoreType.DMA((8,)),
        ],
        compiler_params=pltpu.CompilerParams(vmem_limit_bytes=62 * 2**20),
        cost_estimate=pl.CostEstimate(flops=10**6, bytes_accessed=12 * 2**20, transcendentals=0),
        name="unpack",
    )(sums, vsum, total, grad, result)


PARTS = 2


def start_kernel(
    lines, shards, x_ref, wk_ref, wv_ref, wp_ref, wq_ref, wo_ref, wu_ref, wd_ref,
    g1_ref, b1_ref, cb_ref, pb_ref, g2_ref, b2_ref, bd_ref, bu_ref, mask_ref, far_ref, near_ref,
    k_ref, v_ref, unit_ref, pk_ref, table_ref, qc_ref, qp_ref, weights_ref, wo_out, wu_out, wd_out, vectors_ref, total_ref,
    x_all, k_buf, v_buf, u_buf, pk_buf, t_buf, wo_buf, wu_buf, wd_buf, vec_src, vec_buf, cnt_buf, cnt_acc,
    up_send, up_recv, down_send, down_recv, b_send, b_recv, c_send, c_recv,
    y_send, y_recv, yc_send, yc_recv, d_send, d_recv, s_send, s_recv, out_sem, pos_sem, own_sem,
):
    tokens, width = x_ref.shape
    piece = tokens // PARTS
    half = width // 2
    chunks = pk_buf.shape[0] // BLK
    ctx = lax.axis_index("ctx")
    w = lax.axis_index("wsh")
    core = lax.rem(ctx, 2)
    b = lax.rem(ctx // 2, 2)
    a = ctx // 4

    def at(a_to, b_to, core_to):
        return (a_to * 2 + b_to) * 2 + core_to

    def shard_peer(s):
        return (ctx, lax.rem(w + s, shards))

    def line_peer(s):
        return (at(lax.rem(a + s, lines), b, core), w)

    core_peer = (at(a, b, 1 - core), w)
    b_peer = (at(a, 1 - b, core), w)
    peers = [core_peer, b_peer] + [line_peer(s) for s in range(1, lines)] + [shard_peer(s) for s in range(1, shards)]
    barrier = pltpu.get_barrier_semaphore()
    for peer in peers:
        pl.semaphore_signal(barrier, inc=1, device_id=peer, device_id_type=MESH)

    def remote(src, dst, send, recv, peer):
        return pltpu.make_async_remote_copy(
            src_ref=src, dst_ref=dst, send_sem=send, recv_sem=recv, device_id=peer, device_id_type=MESH
        )

    def block(slot):
        return aligned(slot * tokens, tokens)

    x_all[block(ctx)] = x_ref[...]
    rows_out = wq_ref.shape[0]
    quarter = rows_out // 2
    rows_up = wd_ref.shape[0]
    weight_in = (wk_ref, wv_ref, wp_ref, wq_ref, wo_ref)
    weight_to = tuple(weights_ref.at[m] for m in range(4)) + (wo_buf,)
    own_copies = [
        pltpu.make_async_copy(ref, to.at[aligned(w * rows_out, rows_out)], own_sem.at[m])
        for m, (ref, to) in enumerate(zip(weight_in[:4], weight_to))
    ]
    for copy in own_copies:
        copy.start()
    vec_src[...] = jnp.zeros_like(vec_src)
    for row, ref in enumerate((g1_ref, b1_ref, cb_ref, pb_ref, g2_ref, b2_ref, bd_ref)):
        vec_src[row : row + 1] = ref[...].astype(F32).reshape(1, rows_out)
    bias_rows = rows_up // rows_out
    for q in range(bias_rows):
        vec_src[7 + q : 8 + q] = bu_ref[q * rows_out : (q + 1) * rows_out].astype(F32).reshape(1, rows_out)
    cnt_acc[0:8] = jnp.broadcast_to(jnp.sum(mask_ref[...].astype(F32), axis=1, keepdims=True), (8, BLK))
    pl.semaphore_wait(barrier, len(peers))

    def x_copy(slot, h, send, recv, peer):
        rows = aligned(slot * tokens + h * piece, piece)
        return remote(x_all.at[rows], x_all.at[rows], send, recv, peer)

    def up_copy(p, h):
        peer = (at(jnp.minimum(a + 1, lines - 1), b, core), w)
        return x_copy(at(p, b, core), h, up_send.at[p, h], up_recv.at[p, h], peer)

    def down_copy(p, h):
        peer = (at(jnp.maximum(a - 1, 0), b, core), w)
        return x_copy(at(p, b, core), h, down_send.at[p, h], down_recv.at[p, h], peer)

    def b_copy(p, h, b_from):
        return x_copy(at(p, b_from, core), h, b_send.at[p, h], b_recv.at[p, h], b_peer)

    def c_copy(p, far, b_from, core_from):
        rows = block(at(p, b_from, core_from))
        return remote(x_all.at[rows], x_all.at[rows], c_send.at[far, p], c_recv.at[far, p], core_peer)

    def weight_copy(m, s):
        rows = aligned(w * rows_out + core * quarter, quarter)
        src = weight_in[m].at[aligned(core * quarter, quarter)]
        return remote(src, weight_to[m].at[rows], y_send.at[m, s - 1], y_recv.at[m, s - 1], shard_peer(s))

    def weight_pass(m, s):
        rows = aligned(lax.rem(w + shards - s, shards) * rows_out + core * quarter, quarter)
        return remote(
            weight_to[m].at[rows], weight_to[m].at[rows], yc_send.at[m, s - 1], yc_recv.at[m, s - 1], core_peer
        )

    low = lax.rem(a, 2)
    quarter_in, quarter_to = (wd_ref, wu_ref), (wd_buf, wu_buf)
    pair_peer = (at(a + 1 - 2 * low, b, core), w)

    def quarter_rows(m, s, low_of):
        size = quarter_in[m].shape[0]
        owner = lax.rem(w + shards - s, shards)
        return aligned(owner * size + (low_of * 2 + core) * (size // 4), size // 4)

    def quarter_copy(m, s):
        size = quarter_in[m].shape[0]
        src = quarter_in[m].at[aligned((low * 2 + core) * (size // 4), size // 4)]
        dst = quarter_to[m].at[quarter_rows(m, 0, low)]
        return remote(src, dst, d_send.at[m, 0, s - 1], d_recv.at[m, 0, s - 1], shard_peer(s))

    def quarter_pass(m, kind, s):
        rows = quarter_rows(m, s, 1 - low if kind == 3 else low)
        peer = pair_peer if kind == 1 else core_peer
        ref = quarter_to[m].at[rows]
        return remote(ref, ref, d_send.at[m, kind, s - 1], d_recv.at[m, kind, s - 1], peer)

    def quarter_on(m):
        for s in range(1, shards):
            quarter_copy(m, s).wait()
            quarter_pass(m, 1, s).start()
            quarter_pass(m, 2, s).start()

    def vec_copy(s):
        return remote(vec_src, vec_buf.at[s - 1], s_send.at[s - 1], s_recv.at[s - 1], shard_peer(s))

    stages = [[shard_peer(s) for s in range(1, shards)], [core_peer], [b_peer], [line_peer(s) for s in range(1, lines)]]
    slots = []
    place = 0
    for stage in stages:
        slots.append(place)
        place += len(stage)

    def cnt_copy(stage, index):
        slot = slots[stage] + index
        sem = shards - 1 + slot
        return remote(cnt_acc.at[pl.ds(stage * 8, 8)], cnt_buf.at[slot], s_send.at[sem], s_recv.at[sem], stages[stage][index])

    def cnt_start(stage):
        for index in range(len(stages[stage])):
            cnt_copy(stage, index).start()

    def cnt_finish(stage):
        total = cnt_acc[stage * 8 : stage * 8 + 8]
        for index in range(len(stages[stage])):
            cnt_copy(stage, index).wait()
            total = total + cnt_buf[slots[stage] + index]
        cnt_acc[(stage + 1) * 8 : (stage + 2) * 8] = total

    for s in range(1, shards):
        vec_copy(s).start()
    cnt_start(0)
    for h in range(PARTS):

        @pl.when(a + 1 < lines)
        def _():
            up_copy(a, h).start()

        @pl.when(a >= 1)
        def _():
            down_copy(a, h).start()

        b_copy(a, h, b).start()
    c_copy(a, 0, b, core).start()
    for kind, m in ((0, 0), (0, 1), (1, 0), (0, 2), (1, 1), (0, 3), (0, 4)):
        for s in range(1, shards):
            (quarter_copy if kind else weight_copy)(m, s).start()


    def table_step(d, _):
        sin_far, cos_far = far_ref[0, pl.ds(d, 1)], far_ref[1, pl.ds(d, 1)]
        sin_near, cos_near = near_ref[0], near_ref[1]
        rows = aligned(d * BLK, BLK)
        t_buf[rows, :half] = (sin_far * cos_near - cos_far * sin_near).astype(BF16)
        t_buf[rows, half:] = (cos_far * cos_near + sin_far * sin_near).astype(BF16)
        return 0

    lax.fori_loop(0, chunks, table_step, 0)
    table_out = pltpu.make_async_copy(t_buf, table_ref, pos_sem.at[0])
    table_out.start()
    lane_to = lax.broadcasted_iota(jnp.int32, (rows_out, width), 1)
    lane_from = lax.broadcasted_iota(jnp.int32, (rows_out, width), 0)
    row_at = lax.broadcasted_iota(jnp.int32, (16, width), 0)

    def spread(values, place):
        return dot_nn(values.astype(BF16), (lane_to == lane_from + place * rows_out).astype(BF16))

    def placed(values, owner):
        full = jnp.where(row_at < 7, spread(values, owner), 0.0)
        for q in range(bias_rows):
            group = owner * bias_rows + q
            row = jnp.broadcast_to(values[7 + q : 8 + q], values.shape)
            full = full + jnp.where(row_at == 7 + group // shards, spread(row, lax.rem(group, shards)), 0.0)
        return full

    vectors = placed(vec_src[...], w)
    for s in range(1, shards):
        vec_copy(s).wait()
        vectors = vectors + placed(vec_buf[s - 1], lax.rem(w + shards - s, shards))
    vectors_ref[...] = vectors
    cnt_finish(0)
    cnt_start(1)

    def unit_of(rows):
        values = rows.astype(F32)
        center = values - jnp.mean(values, axis=1, keepdims=True)
        return center * lax.rsqrt(jnp.mean(center * center, axis=1, keepdims=True) + epsilon)

    def out_copies(slot):
        rows = block(slot)
        return (
            pltpu.make_async_copy(k_buf.at[rows], k_ref.at[rows], out_sem.at[0, slot]),
            pltpu.make_async_copy(v_buf.at[rows], v_ref.at[rows], out_sem.at[1, slot]),
            pltpu.make_async_copy(u_buf.at[rows], unit_ref.at[rows], out_sem.at[2, slot]),
        )

    def project(p):
        def one(q, _):
            other_b = lax.rem(q, 2)
            other_core = q // 2

            @pl.when(q == 1)
            def _():
                for h in range(PARTS):
                    b_copy(p, h, b).wait()
                c_copy(p, 1, 1 - b, core).start()

            @pl.when(q == 2)
            def _():
                c_copy(p, 0, b, core).wait()

            @pl.when(q == 3)
            def _():
                c_copy(p, 1, 1 - b, core).wait()

            slot = at(p, b + other_b - 2 * b * other_b, core + other_core - 2 * core * other_core)
            rows = block(slot)
            unit = unit_of(x_all[rows])
            u_buf[rows] = unit.astype(BF16)
            normed = (unit * vectors_ref[0:1] + vectors_ref[1:2]).astype(BF16)
            k_buf[rows] = dot_nn(normed, weights_ref[0]).astype(BF16)
            v_buf[rows] = dot_nn(normed, weights_ref[1]).astype(BF16)
            for copy in out_copies(slot):
                copy.start()
            return 0

        lax.fori_loop(0, 4, one, 0)

    def pos_step(d, _):
        rows = aligned(d * BLK, BLK)
        pk_buf[rows] = dot_nn(t_buf[rows], weights_ref[2]).astype(BF16)
        return 0

    last = lines - 1

    def line_step(s, _):
        below, high = a - 1 - s, a + 1 + s

        for h in range(PARTS):

            @pl.when((s < lines - 1) & (below >= 0))
            def _():
                p = jnp.maximum(below, 0)
                up_copy(p, h).wait_recv()

                @pl.when(a + 1 < lines)
                def _():
                    up_copy(p, h).start()

                b_copy(p, h, b).start()
                if h == PARTS - 1:
                    c_copy(p, 0, b, core).start()

            @pl.when((s < lines - 1) & (high < lines))
            def _():
                p = jnp.minimum(high, lines - 1)
                down_copy(p, h).wait_recv()

                @pl.when(a >= 1)
                def _():
                    down_copy(p, h).start()

                b_copy(p, h, b).start()
                if h == PARTS - 1:
                    c_copy(p, 0, b, core).start()

        @pl.when(s == 0)
        def _():
            cnt_finish(1)
            cnt_start(2)
            for copy in own_copies:
                copy.wait()
            for m in range(2):
                for t in range(1, shards):
                    weight_copy(m, t).wait()
                    weight_pass(m, t).start()
            for m in range(2):
                for t in range(1, shards):
                    weight_pass(m, t).wait()

        @pl.when(s == min(1, last))
        def _():
            cnt_finish(2)
            cnt_start(3)

        @pl.when(s == min(2, last))
        def _():
            for t in range(1, shards):
                weight_copy(2, t).wait()
                weight_pass(2, t).start()
            for t in range(1, shards):
                weight_pass(2, t).wait()

        @pl.when(s == last)
        def _():
            for m in range(3, 5):
                for t in range(1, shards):
                    weight_copy(m, t).wait()
                    weight_pass(m, t).start()
            for t in range(1, shards):
                weight_pass(3, t).wait()

        @pl.when(a - s >= 0)
        def _():
            project(jnp.maximum(a - s, 0))

        @pl.when((s >= 1) & (a + s < lines))
        def _():
            project(jnp.minimum(a + s, lines - 1))

        @pl.when(s == min(1, last))
        def _():
            quarter_on(0)

        @pl.when(s == min(2, last))
        def _():
            lax.fori_loop(0, chunks // 2, pos_step, 0)
            quarter_on(1)

        @pl.when(s == last)
        def _():
            lax.fori_loop(chunks // 2, chunks, pos_step, 0)

        return 0

    lax.fori_loop(0, lines, line_step, 0)
    pos_out = pltpu.make_async_copy(pk_buf, pk_ref, pos_sem.at[1])
    pos_out.start()
    normed = (unit_of(x_ref[...]) * vectors_ref[0:1] + vectors_ref[1:2]).astype(BF16)
    queries = dot_nn(normed, weights_ref[3]).astype(BF16).astype(F32)
    qc_ref[...] = ((queries + vectors_ref[2:3]) * 0.125).astype(BF16)
    qp_ref[...] = ((queries + vectors_ref[3:4]) * 0.125).astype(BF16)
    cnt_finish(3)
    total_ref[...] = cnt_acc[4 * 8 : 5 * 8]

    def sends_done(p, _):
        for h in range(PARTS):

            @pl.when((a + 1 < lines) & (p <= a))
            def _():
                up_copy(p, h).wait_send()

            @pl.when((a >= 1) & (p >= a))
            def _():
                down_copy(p, h).wait_send()

        return 0

    lax.fori_loop(0, lines, sends_done, 0)

    def outs_done(slot, _):
        for copy in out_copies(slot):
            copy.wait()
        return 0

    lax.fori_loop(0, 4 * lines, outs_done, 0)
    for s in range(1, shards):
        weight_pass(4, s).wait()
        for m in range(2):
            quarter_pass(m, 1, s).wait()
            quarter_pass(m, 3, s).start()
    for s in range(1, shards):
        for m in range(2):
            quarter_pass(m, 2, s).wait()
            quarter_pass(m, 3, s).wait()
    far_copies = []
    for m, (buf, to) in enumerate(((wo_buf, wo_out), (wu_buf, wu_out), (wd_buf, wd_out))):
        size = buf.shape[0] // shards
        for s in range(1, shards):
            rows = aligned(lax.rem(w + s, shards) * size, size)
            far_copies.append(pltpu.make_async_copy(buf.at[rows], to.at[rows], own_sem.at[4 + m * (shards - 1) + s - 1]))
    for copy in far_copies:
        copy.start()
    for copy in far_copies:
        copy.wait()
    table_out.wait()
    pos_out.wait()


def start(lines, shards, cid, limit, x, weights, vectors, mask, far, near):
    tokens, width = x.shape
    hidden = weights[5].shape[1]
    rows_out = weights[0].shape[0]
    members = 4 * lines
    keys = members * tokens
    span = limit * BLK
    vmem = pl.BlockSpec(memory_space=pltpu.VMEM)
    hbm = pl.BlockSpec(memory_space=pl.ANY)
    small = 2 * (shards - 1) + 1 + 1 + lines - 1
    dma = pltpu.SemaphoreType.DMA
    other = shards - 1
    return pl.pallas_call(
        functools.partial(start_kernel, lines, shards),
        out_shape=(
            jax.ShapeDtypeStruct((keys, width), BF16),
            jax.ShapeDtypeStruct((keys, width), BF16),
            jax.ShapeDtypeStruct((keys, width), BF16),
            jax.ShapeDtypeStruct((span, width), BF16),
            jax.ShapeDtypeStruct((span, width), BF16),
            jax.ShapeDtypeStruct((tokens, width), BF16),
            jax.ShapeDtypeStruct((tokens, width), BF16),
            jax.ShapeDtypeStruct((4, width, width), BF16),
            jax.ShapeDtypeStruct((width, width), BF16),
            jax.ShapeDtypeStruct((width, hidden), BF16),
            jax.ShapeDtypeStruct((hidden, width), BF16),
            jax.ShapeDtypeStruct((16, width), F32),
            jax.ShapeDtypeStruct((8, BLK), F32),
        ),
        in_specs=[vmem] + [hbm] * 7 + [vmem] * 11,
        out_specs=(hbm,) * 5 + (vmem,) * 3 + (hbm,) * 3 + (vmem,) * 2,
        scratch_shapes=[
            pltpu.VMEM((keys, width), BF16),
            pltpu.VMEM((keys, width), BF16),
            pltpu.VMEM((keys, width), BF16),
            pltpu.VMEM((keys, width), BF16),
            pltpu.VMEM((span, width), BF16),
            pltpu.VMEM((span, width), BF16),
            pltpu.VMEM((width, width), BF16),
            pltpu.VMEM((width, hidden), BF16),
            pltpu.VMEM((hidden, width), BF16),
            pltpu.VMEM((16, rows_out), F32),
            pltpu.VMEM((other, 16, rows_out), F32),
            pltpu.VMEM((lines + shards, 8, BLK), F32),
            pltpu.VMEM((5 * 8, BLK), F32),
        ]
        + [dma((lines, PARTS))] * 6
        + [dma((2, lines))] * 2
        + [dma((5, other))] * 4
        + [dma((2, 4, other))] * 2
        + [dma((small,))] * 2
        + [dma((3, members)), dma((2,)), dma((4 + 3 * other,))],
        compiler_params=pltpu.CompilerParams(collective_id=cid, has_side_effects=True, vmem_limit_bytes=60 * 2**20),
        cost_estimate=pl.CostEstimate(flops=6 * 10**9, bytes_accessed=20 * 2**20, transcendentals=0),
        name="start",
    )(x, *weights, *vectors, mask, far, near)


GELU_SCALE = math.sqrt(2.0 / math.pi)


def middle_kernel(
    shards, rows_f, mask_ref, x_ref, mixed_ref, teacher_ref, out_grad_ref, vectors_ref, total_ref,
    wo_own, wu_own, wd_own, wo_ref, wu_ref, wd_ref,
    out_ref, hidden_ref, gm_ref, mine_ref, theirs_ref, vec_ref,
    wo, wu, wd, slope, act, gf_ref, landed, sem, send_sem, recv_sem,
):
    tokens, width = x_ref.shape
    parts = wu.shape[1] // width
    ctx = lax.axis_index("ctx")
    core = lax.rem(ctx, 2)
    core_peer = (ctx + 1 - 2 * core, lax.axis_index("wsh"))
    barrier = pltpu.get_barrier_semaphore()
    pl.semaphore_signal(barrier, inc=1, device_id=core_peer, device_id_type=MESH)
    w = lax.axis_index("wsh")
    copies = []
    for k, (own, gathered, full) in enumerate(((wo_own, wo_ref, wo), (wu_own, wu_ref, wu), (wd_own, wd_ref, wd))):
        size = own.shape[0]
        part = [pltpu.make_async_copy(own, full.at[aligned(w * size, size)], sem.at[k, 0])]
        for s in range(1, shards):
            rows = aligned(lax.rem(w + s, shards) * size, size)
            part.append(pltpu.make_async_copy(gathered.at[rows], full.at[rows], sem.at[k, s]))
        for copy in part:
            copy.start()
        copies.append(part)

    def arrive(k):
        for copy in copies[k]:
            copy.wait()

    b = lax.rem(ctx // 2, 2)
    half, quarter = rows_f // 2, rows_f // 4

    def give(begin, size, index):
        rows = aligned((1 - core) * half + begin, size)
        return pltpu.make_async_remote_copy(
            src_ref=gf_ref.at[:, rows], dst_ref=landed.at[:, begin : begin + size],
            send_sem=send_sem.at[index], recv_sem=recv_sem.at[index], device_id=core_peer, device_id_type=MESH,
        )

    gain, offset, down_bias = vectors_ref[4:5], vectors_ref[5:6], vectors_ref[6:7]
    mixed = mixed_ref[...].astype(BF16)
    arrive(0)
    hidden = x_ref[...].astype(F32) + dot_nn(mixed, wo[...])
    center = hidden - jnp.mean(hidden, axis=1, keepdims=True)
    inverse = lax.rsqrt(jnp.mean(center * center, axis=1, keepdims=True) + epsilon)
    unit = center * inverse
    normed = (unit * gain + offset).astype(BF16)
    result = hidden + down_bias
    arrive(1)
    arrive(2)
    for c in range(parts):
        cols = slice(c * width, (c + 1) * width)
        v = dot_nn(normed, wu[:, cols]) + vectors_ref[7 + c : 8 + c]
        square = v * v
        t = jnp.tanh(GELU_SCALE * (v + 0.044715 * (square * v)))
        act[:, cols] = (0.5 * v * (1.0 + t)).astype(BF16)
        slope[:, cols] = 0.5 * (1.0 + t) + 0.5 * v * (1.0 - t * t) * (GELU_SCALE * (1.0 + 3.0 * 0.044715 * square))
        result = result + dot_nn(act[:, cols], wd[cols])
    out_ref[...] = result.astype(BF16)
    mask = jnp.broadcast_to(mask_ref[...].astype(F32), (8, tokens)).T[:, 0:1]
    error = result - teacher_ref[...].astype(F32)
    masked = mask * error
    count = jnp.sum(total_ref[0:1, 0:1], axis=1, keepdims=True)
    grad_result = out_grad_ref[...].astype(F32) + (2.0 / (count * width)) * masked
    branch = grad_result.astype(BF16)
    vec_ref[...] = jnp.zeros_like(vec_ref)
    vec_ref[7 + parts : 8 + parts] = jnp.broadcast_to(
        jnp.sum(jnp.sum(masked * error, axis=1, keepdims=True), axis=0, keepdims=True), (1, width)
    )
    vec_ref[6:7] = jnp.sum(branch.astype(F32), axis=0, keepdims=True)
    rows_up = wd.shape[0] // shards
    rows_out = width // shards
    used = 2 * rows_up + rows_out
    if used < rows_f:
        gf_ref[:, used:] = jnp.zeros((shards, rows_f - used, width), BF16)
    grad_normed = jnp.zeros((tokens, width), F32)
    for c in range(parts):
        cols = slice(c * width, (c + 1) * width)
        grad_pre = (dot_nt(branch, wd[cols]) * slope[:, cols]).astype(BF16)
        vec_ref[7 + c : 8 + c] = jnp.sum(grad_pre.astype(F32), axis=0, keepdims=True)
        grad_normed = grad_normed + dot_nt(grad_pre, wu[:, cols])
        up = dot_tn(normed, grad_pre).astype(BF16)
        down = dot_tn(act[:, cols], branch).astype(BF16)
        for s in range(shards):
            gf_ref[s, c * rows_out : (c + 1) * rows_out] = up[s * rows_out : (s + 1) * rows_out]
        step = min(rows_up, width)
        for begin in range(0, width, step):
            row = c * width + begin
            place = rows_up + row % rows_up
            gf_ref[row // rows_up, place : place + step] = down[begin : begin + step]
    pl.semaphore_wait(barrier, 1)
    early = max(0, 2 * rows_up - half)
    if early:
        give(0, early, 0).start()
    vec_ref[4:5] = jnp.sum(grad_normed * unit, axis=0, keepdims=True)
    vec_ref[5:6] = jnp.sum(grad_normed, axis=0, keepdims=True)
    scaled = grad_normed * gain
    grad_hidden = grad_result + inverse * (
        scaled - jnp.mean(scaled, axis=1, keepdims=True) - unit * jnp.mean(scaled * unit, axis=1, keepdims=True)
    )
    hidden_ref[...] = grad_hidden
    attn = grad_hidden.astype(BF16)
    gm_ref[...] = dot_nt(attn, wo[...]).astype(BF16)
    outer = dot_tn(mixed, attn).astype(BF16)
    for s in range(shards):
        gf_ref[s, 2 * rows_up : used] = outer[s * rows_out : (s + 1) * rows_out]
    give(early, half - early, 1).start()
    if early:
        give(0, early, 0).wait()
    give(early, half - early, 1).wait()
    for ref, place in ((theirs_ref, 1 - b), (mine_ref, b)):
        own = gf_ref[:, aligned(core * half + place * quarter, quarter)].astype(F32)
        ref[...] = (own + landed[:, aligned(place * quarter, quarter)].astype(F32)).astype(BF16)


def middle(shards, rows_f, cid, mask, x, mixed, teacher, out_grad, vectors, total, own, gathered):
    tokens, width = x.shape
    hidden = own[1].shape[1]
    vmem = pl.BlockSpec(memory_space=pltpu.VMEM)
    hbm = pl.BlockSpec(memory_space=pl.ANY)
    return pl.pallas_call(
        functools.partial(middle_kernel, shards, rows_f),
        out_shape=(
            jax.ShapeDtypeStruct((tokens, width), BF16),
            jax.ShapeDtypeStruct((tokens, width), F32),
            jax.ShapeDtypeStruct((tokens, width), BF16),
            jax.ShapeDtypeStruct((shards, rows_f // 4, width), BF16),
            jax.ShapeDtypeStruct((shards, rows_f // 4, width), BF16),
            jax.ShapeDtypeStruct((16, width), F32),
        ),
        in_specs=[vmem] * 7 + [hbm] * 6,
        out_specs=(vmem,) * 6,
        scratch_shapes=[
            pltpu.VMEM((width, width), BF16),
            pltpu.VMEM((width, hidden), BF16),
            pltpu.VMEM((hidden, width), BF16),
            pltpu.VMEM((tokens, hidden), F32),
            pltpu.VMEM((tokens, hidden), BF16),
            pltpu.VMEM((shards, rows_f, width), BF16),
            pltpu.VMEM((shards, rows_f // 2, width), BF16),
            pltpu.SemaphoreType.DMA((3, shards)),
            pltpu.SemaphoreType.DMA((2,)),
            pltpu.SemaphoreType.DMA((2,)),
        ],
        compiler_params=pltpu.CompilerParams(collective_id=cid, has_side_effects=True, vmem_limit_bytes=56 * 2**20),
        cost_estimate=pl.CostEstimate(flops=4 * 10**9, bytes_accessed=20 * 2**20, transcendentals=10**6),
        name="middle",
    )(mask, x, mixed, teacher, out_grad, vectors, total, *own, *gathered)


def body(
    inputs, block_perm, seq_lengths, loss_mask, teacher, out_grad, gain_one, bias_one, w_query, w_key, w_value,
    w_output, w_pos, content_bias, position_bias, gain_two, bias_two, w_up, bias_up, w_down, bias_down,
):
    width = inputs.shape[2]
    shards = lax.axis_size("wsh")
    members = lax.axis_size("ctx")
    lines = members // 4
    hidden = bias_up.shape[0] * shards
    blocks = block_perm.shape[1]
    limit = blocks // 2 + 1
    rows_up, rows_out = hidden // shards, width // shards

    frequency = np.exp(np.arange(width // 2) * (-2.0 * math.log(10000.0) / width))
    far_angle = (np.arange(-(-limit // 8) * 8) * BLK + (BLK - 1))[:, None] * frequency[None]
    near_angle = np.arange(BLK)[:, None] * frequency[None]
    far = jnp.asarray(np.stack([np.sin(far_angle), np.cos(far_angle)]), F32)
    near = jnp.asarray(np.stack([np.sin(near_angle), np.cos(near_angle)]), F32)

    keys, values, unit_all, pos_keys, table, qc, qp, weights, wo, wu, wd, vectors, total = start(
        lines, shards, 0, limit, inputs[0], (w_key, w_value, w_pos, w_query, w_output, w_up, w_down),
        (gain_one, bias_one, content_bias, position_bias, gain_two, bias_two, bias_down, bias_up), loss_mask, far, near,
    )
    mixed, linv, probs = attn_fwd(block_perm, seq_lengths, qc, qp, keys, values, pos_keys, blocks, limit)

    step = 16 * lines
    pieces = -(-(2 * rows_up + rows_out) // (4 * step))
    split = min(2, pieces)
    chunks_f = tuple((pieces * (i + 1) // split - pieces * i // split) * step for i in range(split))
    rows_f = 4 * step * pieces
    if rows_out % (32 * lines):
        sets, rows_l = (("q", "p"), ("k", "v")), -(-2 * rows_out // (32 * lines)) * 32 * lines
    else:
        sets, rows_l = (("q",), ("p",), ("k",), ("v",)), rows_out
    output, grad_hidden, grad_mixed, mine, theirs, vec = middle(
        shards, rows_f, 2, loss_mask, inputs[0], mixed, teacher[0], out_grad[0], vectors, total,
        (w_output, w_up, w_down), (wo, wu, wd),
    )
    come = lax.ppermute(theirs, "ctx", [(i, i ^ 2) for i in range(members)])
    grad_query, bias_grads, dk_t, dv_t, dpk_t = attn_bwd(
        block_perm, seq_lengths, qc, qp, keys, values, pos_keys, probs, linv, grad_mixed, mixed, blocks, limit
    )
    grad_input, sums, vsum = finish(
        lines, shards, chunks_f, sets, rows_l, 1, mine, come, dk_t, dv_t, unit_all, dpk_t, table, weights, grad_query,
        inputs[0], vectors, total, vec, bias_grads, grad_hidden,
    )
    (
        grad_input, output, g_query, g_key, g_value, g_output, g_pos, g_up, g_down,
        v_g1, v_b1, v_cb, v_pb, v_g2, v_b2, v_bd, v_bu, loss,
    ) = unpack(shards, rows_f, sets, rows_l, hidden, sums, vsum, total, grad_input, output)
    return (
        output[None], loss.reshape(()), grad_input[None], v_g1, v_b1, g_query, g_key, g_value, g_output, g_pos,
        v_cb, v_pb, v_g2, v_b2, g_up, v_bu, g_down, v_bd,
    )


def solution(mesh):
    rows = P("wsh", "ctx", None)
    vector = P("wsh")
    matrix = P("wsh", None)
    placed = (
        rows, matrix, matrix, P("wsh", "ctx"), rows, rows, vector, vector, matrix, matrix, matrix, matrix, matrix,
        vector, vector, vector, vector, matrix, vector, matrix, vector,
    )
    out = (
        rows, P(), rows, vector, vector, matrix, matrix, matrix, matrix, matrix, vector, vector, vector, vector,
        matrix, vector, matrix, vector,
    )
    return jax.shard_map(body, mesh=mesh, in_specs=placed, out_specs=out, check_vma=False)
```

```python
import functools
import math

import jax
import jax.numpy as jnp
import numpy as np
from jax import lax
from jax.experimental import pallas as pl
from jax.experimental.pallas import tpu as pltpu
from jax.sharding import PartitionSpec as P

HEADS = 8
HEAD = 64
PAIRS = HEADS // 2
BLK = 128
ROWS = HEADS * BLK
NEG = -1e30
epsilon = 1e-05
F32 = jnp.float32
BF16 = jnp.bfloat16


def dot_nt(a, b):
    return lax.dot_general(a, b, (((1,), (1,)), ((), ())), preferred_element_type=F32)


def dot_nn(a, b):
    return lax.dot_general(a, b, (((1,), (0,)), ((), ())), preferred_element_type=F32)


def dot_tn(a, b):
    return lax.dot_general(a, b, (((0,), (0,)), ((), ())), preferred_element_type=F32)


def iotas():
    row = lax.broadcasted_iota(jnp.int32, (BLK, BLK), 0)
    col = lax.broadcasted_iota(jnp.int32, (BLK, BLK), 1)
    return row, col


def read_places(perm_ref, lengths_ref, meta, blocks, count):
    device = lax.axis_index("ctx")
    meta[0] = perm_ref[0, 2 * device]
    meta[1] = perm_ref[0, 2 * device + 1]

    def place(slot, _):
        meta[2 + perm_ref[0, slot]] = slot
        return 0

    lax.fori_loop(0, blocks, place, 0)
    end = jnp.int32(0)
    for e in range(count):
        end = end + lengths_ref[0, e]
        meta[2 + blocks + e] = end


def block_range(meta, a, blocks, limit):
    qb = meta[a]
    first = qb * BLK
    low = jnp.int32(0)
    for e in range(meta.shape[0] - 2 - blocks):
        end = meta[2 + blocks + e]
        low = jnp.where(first >= end, jnp.maximum(low, end), low)
    lowest = low // BLK
    return qb, lowest, jnp.minimum(qb - lowest + 1, limit)


def stack_heads(pair):
    lane = lax.broadcasted_iota(jnp.int32, pair.shape, 1)
    zero = jnp.zeros_like(pair)
    return jnp.concatenate([jnp.where(lane < HEAD, pair, zero), jnp.where(lane >= HEAD, pair, zero)], axis=0)


def flip_rows(x):
    index = 7 - lax.broadcasted_iota(jnp.int32, (8, BLK), 0)
    slabs = [jnp.take_along_axis(x[8 * g : 8 * g + 8], index, axis=0) for g in reversed(range(BLK // 8))]
    return jnp.concatenate(slabs, axis=0)


def flip_two(x):
    return jnp.concatenate([flip_rows(x[:BLK]), flip_rows(x[BLK:])], axis=0)


def needed_blocks(meta, blocks, limit):
    ranges = []
    for a in range(2):
        qb, lowest, count = block_range(meta, a, blocks, limit)
        ranges.append((qb + 1 - 2 * ((count + 1) // 2), qb))
    return ranges


def load_keys(meta, blocks, limit, pairs, sem):
    (low0, high0), (low1, high1) = needed_blocks(meta, blocks, limit)
    for hbm, ref in pairs:
        ref[0:BLK] = jnp.zeros((BLK, ref.shape[1]), ref.dtype)

    def copies(kb):
        slot = pl.ds(pl.multiple_of(meta[2 + kb] * BLK, BLK), BLK)
        place = pl.ds(pl.multiple_of((kb + 1) * BLK, BLK), BLK)
        return [
            pltpu.make_async_copy(hbm.at[slot], ref.at[place], sem.at[index, kb]) for index, (hbm, ref) in enumerate(pairs)
        ]

    def begin(kb, _):
        @pl.when(((kb >= low0) & (kb <= high0)) | ((kb >= low1) & (kb <= high1)))
        def _():
            for copy in copies(kb):
                copy.start()

        return 0

    lax.fori_loop(0, blocks, begin, 0)

    def arrive(a):
        low, high = (jnp.where(a == 0, x, y) for x, y in ((low0, low1), (high0, high1)))

        def one(kb, _):
            @pl.when((a == 0) | (kb < low0) | (kb > high0))
            def _():
                for copy in copies(kb):
                    copy.wait()

            return 0

        lax.fori_loop(jnp.maximum(low, 0), high + 1, one, 0)

    return arrive


def wide_iotas():
    row = lax.broadcasted_iota(jnp.int32, (BLK, 2 * BLK), 0)
    col = lax.broadcasted_iota(jnp.int32, (BLK, 2 * BLK), 1)
    return row, col


def attn_fwd_kernel(
    blocks, limit, perm_ref, lengths_ref, qc_ref, qp_ref, k_in, v_in, pk_in, mixed_ref, linv_ref, p_ref,
    meta, k_ref, v_ref, pk_ref, q2c, q2p, prev, top, total, acc, s_scr, p_buf, kv_sem, pk_sem, p_sem,
):
    read_places(perm_ref, lengths_ref, meta, blocks, lengths_ref.shape[1])
    span = pk_in.shape[0]
    pk_copy = pltpu.make_async_copy(pk_in, pk_ref.at[0:span], pk_sem)
    pk_copy.start()
    arrive = load_keys(meta, blocks, limit, ((k_in, k_ref), (v_in, v_ref)), kv_sem)
    pk_ref[span:] = jnp.zeros((BLK, pk_ref.shape[1]), BF16)
    row, col = iotas()
    tri = col <= row
    wide_row, wide_col = wide_iotas()
    tiles = s_scr.shape[0]

    def p_copy(slot, index):
        return pltpu.make_async_copy(p_buf.at[slot], p_ref.at[index], p_sem.at[slot])

    def one_query_block(a, _):
        qb, lowest, count = block_range(meta, a, blocks, limit)
        pairs = (count + 1) // 2
        rows_a = pl.ds(pl.multiple_of(a * BLK, BLK), BLK)
        pos = qb * BLK + wide_row
        start = jnp.zeros((BLK, 2 * BLK), jnp.int32)
        for e in range(meta.shape[0] - 2 - blocks):
            end = meta[2 + blocks + e]
            start = jnp.where(pos >= end, jnp.maximum(start, end), start)
        for hp in range(PAIRS):
            lanes = slice(hp * BLK, (hp + 1) * BLK)
            q2c[hp] = stack_heads(qc_ref[rows_a, lanes].astype(F32)).astype(BF16)
            q2p[hp] = stack_heads(qp_ref[rows_a, lanes].astype(F32)).astype(BF16)
        prev[...] = jnp.zeros_like(prev)
        top[...] = jnp.full_like(top, NEG)
        total[...] = jnp.zeros_like(total)
        acc[...] = jnp.zeros_like(acc)
        arrive(a)

        @pl.when(a == 0)
        def _():
            pk_copy.wait()

        def score_step(t, _):
            kb = qb - 2 * t
            keys = pl.ds(pl.multiple_of(kb * BLK, BLK), 2 * BLK)
            place = (kb - 1) * BLK + wide_col
            bias = jnp.where((place >= start) & (place <= pos), 0.0, NEG).astype(F32)
            drows = pl.ds(pl.multiple_of(2 * t * BLK, BLK), 2 * BLK)
            for hp in range(PAIRS):
                lanes = slice(hp * BLK, (hp + 1) * BLK)
                s = dot_nt(q2c[hp], k_ref[keys, lanes])
                r = dot_nt(q2p[hp], pk_ref[drows, lanes])
                for half in range(2):
                    part = slice(half * BLK, (half + 1) * BLK)
                    rows = slice((2 * hp + half) * BLK, (2 * hp + half + 1) * BLK)
                    near = pltpu.roll(r[part, :BLK], 1, 1, stride=1, stride_axis=0)
                    far = pltpu.roll(r[part, BLK:], 1, 1, stride=1, stride_axis=0)
                    late = s[part, BLK:] + jnp.where(tri, near, prev[rows]) + bias[:, BLK:]
                    early = s[part, :BLK] + jnp.where(tri, far, near) + bias[:, :BLK]
                    prev[rows] = far
                    s_scr[t, rows, :BLK] = early
                    s_scr[t, rows, BLK:] = late
                    top[rows] = jnp.maximum(top[rows], jnp.maximum(early, late))
            return 0

        lax.fori_loop(0, pairs, score_step, 0)
        for h in range(HEADS):
            rows = slice(h * BLK, (h + 1) * BLK)
            top[rows] = jnp.broadcast_to(jnp.max(top[rows], axis=1, keepdims=True), (BLK, BLK))

        def mix_step(t, _):
            kb = qb - 2 * t
            keys = pl.ds(pl.multiple_of(kb * BLK, BLK), 2 * BLK)
            slot = lax.rem(t, 2)

            @pl.when(t >= 2)
            def _():
                p_copy(slot, 0).wait()

            for hp in range(PAIRS):
                lanes = slice(hp * BLK, (hp + 1) * BLK)
                rows = slice(2 * hp * BLK, 2 * (hp + 1) * BLK)
                early = jnp.exp(s_scr[t, rows, :BLK] - top[rows])
                late = jnp.exp(s_scr[t, rows, BLK:] - top[rows])
                total[rows] += early + late
                p_buf[slot, rows, :BLK] = flip_two(early).astype(BF16)
                p_buf[slot, rows, BLK:] = flip_two(late).astype(BF16)
                low = jnp.concatenate([early.astype(BF16), late.astype(BF16)], axis=1)
                acc[hp] += dot_nn(low, v_ref[keys, lanes])
            p_copy(slot, a * tiles + t).start()
            return 0

        lax.fori_loop(0, pairs, mix_step, 0)
        p_copy(lax.rem(pairs - 1, 2), 0).wait()

        @pl.when(pairs >= 2)
        def _():
            p_copy(lax.rem(pairs, 2), 0).wait()

        lane = lax.broadcasted_iota(jnp.int32, (BLK, BLK), 1)
        for hp in range(PAIRS):
            lanes = slice(hp * BLK, (hp + 1) * BLK)
            parts = []
            for half in range(2):
                h = 2 * hp + half
                rows = slice(h * BLK, (h + 1) * BLK)
                inv = 1.0 / jnp.sum(total[rows], axis=1, keepdims=True)
                inv = jnp.broadcast_to(inv, (BLK, BLK))
                linv_ref[a, rows] = inv
                parts.append(acc[hp, half * BLK : (half + 1) * BLK] * inv)
            mixed_ref[rows_a, lanes] = jnp.where(lane < HEAD, parts[0], parts[1])
        return 0

    lax.fori_loop(0, 2, one_query_block, 0)


def attn_fwd(perm, lengths, qc, qp, k, v, pk, blocks, limit):
    tokens, width = qc.shape
    keys, span = k.shape[0], pk.shape[0]
    tiles = (limit + 1) // 2
    vmem = pl.BlockSpec(memory_space=pltpu.VMEM)
    hbm = pl.BlockSpec(memory_space=pl.ANY)
    return pl.pallas_call(
        functools.partial(attn_fwd_kernel, blocks, limit),
        out_shape=(
            jax.ShapeDtypeStruct((tokens, width), F32),
            jax.ShapeDtypeStruct((2, ROWS, BLK), F32),
            jax.ShapeDtypeStruct((2 * tiles, ROWS, 2 * BLK), BF16),
        ),
        in_specs=[pl.BlockSpec(memory_space=pltpu.SMEM)] * 2 + [vmem] * 2 + [hbm] * 3,
        out_specs=(vmem, vmem, hbm),
        scratch_shapes=[
            pltpu.SMEM((2 + blocks + lengths.shape[1],), jnp.int32),
            pltpu.VMEM((keys + BLK, width), BF16),
            pltpu.VMEM((keys + BLK, width), BF16),
            pltpu.VMEM((span + BLK, width), BF16),
            pltpu.VMEM((PAIRS, 2 * BLK, BLK), BF16),
            pltpu.VMEM((PAIRS, 2 * BLK, BLK), BF16),
            pltpu.VMEM((ROWS, BLK), F32),
            pltpu.VMEM((ROWS, BLK), F32),
            pltpu.VMEM((ROWS, BLK), F32),
            pltpu.VMEM((PAIRS, 2 * BLK, BLK), F32),
            pltpu.VMEM((tiles, ROWS, 2 * BLK), F32),
            pltpu.VMEM((2, ROWS, 2 * BLK), BF16),
            pltpu.SemaphoreType.DMA((2, blocks)),
            pltpu.SemaphoreType.DMA,
            pltpu.SemaphoreType.DMA((2,)),
        ],
        compiler_params=pltpu.CompilerParams(vmem_limit_bytes=60 * 2**20),
        cost_estimate=pl.CostEstimate(flops=3 * 10**9, bytes_accessed=20 * 2**20, transcendentals=4 * 10**6),
        name="attn_fwd",
    )(perm, lengths, qc, qp, k, v, pk)


def attn_bwd_kernel(
    blocks, limit, perm_ref, lengths_ref, qc_ref, qp_ref, k_in, v_in, pk_in, p_ref, linv_ref, gm_ref, mixed_ref,
    dq_ref, bias_ref, dk_out, dv_out, dpk_ref,
    meta, k_ref, v_ref, pk_ref, dk_ref, dv_ref, q2c_t, q2p_t, gm2, gm2_t, dd, carry, dqk, dqp, dpk, p_buf,
    empty, kv_sem, pk_sem, p_sem, out_sem,
):
    read_places(perm_ref, lengths_ref, meta, blocks, lengths_ref.shape[1])
    span = pk_in.shape[0]
    pk_copy = pltpu.make_async_copy(pk_in, pk_ref.at[0:span], pk_sem)
    pk_copy.start()
    arrive = load_keys(meta, blocks, limit, ((k_in, k_ref), (v_in, v_ref)), kv_sem)
    pk_ref[span:] = jnp.zeros((BLK, pk_ref.shape[1]), BF16)
    row, col = iotas()
    tri = col <= BLK - 1 - row
    tiles = p_ref.shape[0] // 2
    (low0, high0), (low1, high1) = needed_blocks(meta, blocks, limit)

    def out_copies(kb, nothing=False):
        slot = pl.ds(pl.multiple_of(meta[2 + kb] * BLK, BLK), BLK)
        place = pl.ds(pl.multiple_of((kb + 1) * BLK, BLK), BLK)
        return [
            pltpu.make_async_copy(empty if nothing else ref.at[:, place], out.at[:, slot], out_sem.at[index, kb])
            for index, (ref, out) in enumerate(((dk_ref, dk_out), (dv_ref, dv_out)))
        ]

    empty[...] = jnp.zeros_like(empty)
    for ref in (dk_ref, dv_ref):
        ref[:, 0:BLK] = jnp.zeros((ref.shape[0], BLK), BF16)

    def prepare(kb, _):
        used = ((kb >= low0) & (kb <= high0)) | ((kb >= low1) & (kb <= high1))

        @pl.when(used)
        def _():
            place = pl.ds(pl.multiple_of((kb + 1) * BLK, BLK), BLK)
            for ref in (dk_ref, dv_ref):
                ref[:, place] = jnp.zeros((ref.shape[0], BLK), BF16)

        @pl.when(jnp.logical_not(used))
        def _():
            for copy in out_copies(kb, True):
                copy.start()

        return 0

    lax.fori_loop(0, blocks, prepare, 0)
    dpk[...] = jnp.zeros_like(dpk)
    bias_ref[...] = jnp.zeros_like(bias_ref)

    def p_copy(slot, index):
        return pltpu.make_async_copy(p_ref.at[index], p_buf.at[slot], p_sem.at[slot])

    def one_query_block(a, _):
        qb, lowest, count = block_range(meta, a, blocks, limit)
        pairs = (count + 1) // 2
        rows_a = pl.ds(pl.multiple_of(a * BLK, BLK), BLK)
        p_copy(0, a * tiles + pairs - 1).start()
        for hp in range(PAIRS):
            lanes = slice(hp * BLK, (hp + 1) * BLK)
            rows = slice(2 * hp * BLK, 2 * (hp + 1) * BLK)
            q2c_t[hp] = stack_heads(flip_rows(qc_ref[rows_a, lanes].astype(F32))).T.astype(BF16)
            q2p_t[hp] = stack_heads(flip_rows(qp_ref[rows_a, lanes].astype(F32))).T.astype(BF16)
            g = stack_heads(gm_ref[rows_a, lanes].astype(F32))
            scaled = flip_two(g * linv_ref[a, rows])
            gm2[hp] = scaled.astype(BF16)
            gm2_t[hp] = scaled.T.astype(BF16)
            pair = flip_rows(mixed_ref[rows_a, lanes])
            dd[rows] = jnp.broadcast_to(
                jnp.sum(scaled * jnp.concatenate([pair, pair], axis=0), axis=1, keepdims=True), (2 * BLK, BLK)
            )
        carry[...] = jnp.zeros_like(carry)
        dqk[...] = jnp.zeros_like(dqk)
        dqp[...] = jnp.zeros_like(dqp)
        arrive(a)

        @pl.when(a == 0)
        def _():
            pk_copy.wait()

        def step(t, _):
            tile = pairs - 1 - t
            kb = qb - 2 * tile
            keys = pl.ds(pl.multiple_of(kb * BLK, BLK), 2 * BLK)
            drows = pl.ds(pl.multiple_of(2 * tile * BLK, BLK), 2 * BLK)
            slot = lax.rem(t, 2)
            p_copy(slot, 0).wait()

            @pl.when(tile >= 1)
            def _():
                p_copy(1 - slot, a * tiles + tile - 1).start()

            for hp in range(PAIRS):
                lanes = slice(hp * BLK, (hp + 1) * BLK)
                rows = slice(2 * hp * BLK, 2 * (hp + 1) * BLK)
                p = p_buf[slot, rows]
                g = dot_nt(gm2[hp], v_ref[keys, lanes])
                early = (p[:, :BLK].astype(F32) * (g[:, :BLK] - dd[rows])).astype(BF16)
                late = (p[:, BLK:].astype(F32) * (g[:, BLK:] - dd[rows])).astype(BF16)
                gs = jnp.concatenate([early, late], axis=1)
                early, late = early.astype(F32), late.astype(F32)
                rots = []
                for half in range(2):
                    part = slice(half * BLK, (half + 1) * BLK)
                    crow = slice((2 * hp + half) * BLK, (2 * hp + half + 1) * BLK)
                    far = jnp.where(tri, early[part], carry[crow])
                    near = jnp.where(tri, late[part], early[part])
                    carry[crow] = late[part]
                    rots.append(
                        jnp.concatenate(
                            [
                                pltpu.roll(near, 0, 1, stride=1, stride_axis=0).astype(BF16),
                                pltpu.roll(far, 0, 1, stride=1, stride_axis=0).astype(BF16),
                            ],
                            axis=1,
                        )
                    )
                rot = jnp.concatenate(rots, axis=0)
                dqk[hp] += dot_nn(gs, k_ref[keys, lanes])
                dqp[hp] += dot_nn(rot, pk_ref[drows, lanes])
                dk_ref[lanes, keys] = (dk_ref[lanes, keys].astype(F32) + dot_nn(q2c_t[hp], gs)).astype(BF16)
                dv_ref[lanes, keys] = (dv_ref[lanes, keys].astype(F32) + dot_nn(gm2_t[hp], p)).astype(BF16)
                dpk[lanes, drows] += dot_nn(q2p_t[hp], rot)
            return 0

        lax.fori_loop(0, pairs, step, 0)
        lane = lax.broadcasted_iota(jnp.int32, (BLK, BLK), 1)
        for hp in range(PAIRS):
            lanes = slice(hp * BLK, (hp + 1) * BLK)
            ck = jnp.where(lane < HEAD, dqk[hp, :BLK], dqk[hp, BLK:]) * 0.125
            cp = jnp.where(lane < HEAD, dqp[hp, :BLK], dqp[hp, BLK:]) * 0.125
            dq_ref[rows_a, lanes] = flip_rows(ck + cp).astype(BF16)
            bias_ref[0:1, lanes] += jnp.sum(ck, axis=0, keepdims=True)
            bias_ref[1:2, lanes] += jnp.sum(cp, axis=0, keepdims=True)

        def give(kb, _):
            @pl.when((a == 1) | (kb < low1) | (kb > high1))
            def _():
                for copy in out_copies(kb):
                    copy.start()

            return 0

        low, high = (jnp.where(a == 0, x, y) for x, y in ((low0, low1), (high0, high1)))
        lax.fori_loop(jnp.maximum(low, 0), high + 1, give, 0)
        return 0

    lax.fori_loop(0, 2, one_query_block, 0)

    def given(kb, _):
        for copy in out_copies(kb):
            copy.wait()
        return 0

    dpk_ref[...] = dpk[:, 0:span].astype(BF16)
    lax.fori_loop(0, blocks, given, 0)


def attn_bwd(perm, lengths, qc, qp, k, v, pk, p, linv, gm, mixed, blocks, limit):
    tokens, width = qc.shape
    keys, span = k.shape[0], pk.shape[0]
    vmem = pl.BlockSpec(memory_space=pltpu.VMEM)
    hbm = pl.BlockSpec(memory_space=pl.ANY)
    return pl.pallas_call(
        functools.partial(attn_bwd_kernel, blocks, limit),
        out_shape=(
            jax.ShapeDtypeStruct((tokens, width), BF16),
            jax.ShapeDtypeStruct((8, width), F32),
            jax.ShapeDtypeStruct((width, keys), BF16),
            jax.ShapeDtypeStruct((width, keys), BF16),
            jax.ShapeDtypeStruct((width, span), BF16),
        ),
        in_specs=[pl.BlockSpec(memory_space=pltpu.SMEM)] * 2 + [vmem] * 2 + [hbm] * 4 + [vmem] * 3,
        out_specs=(vmem, vmem, hbm, hbm, vmem),
        scratch_shapes=[
            pltpu.SMEM((2 + blocks + lengths.shape[1],), jnp.int32),
            pltpu.VMEM((keys + BLK, width), BF16),
            pltpu.VMEM((keys + BLK, width), BF16),
            pltpu.VMEM((span + BLK, width), BF16),
            pltpu.VMEM((width, keys + BLK), BF16),
            pltpu.VMEM((width, keys + BLK), BF16),
            pltpu.VMEM((PAIRS, BLK, 2 * BLK), BF16),
            pltpu.VMEM((PAIRS, BLK, 2 * BLK), BF16),
            pltpu.VMEM((PAIRS, 2 * BLK, BLK), BF16),
            pltpu.VMEM((PAIRS, BLK, 2 * BLK), BF16),
            pltpu.VMEM((ROWS, BLK), F32),
            pltpu.VMEM((ROWS, BLK), F32),
            pltpu.VMEM((PAIRS, 2 * BLK, BLK), F32),
            pltpu.VMEM((PAIRS, 2 * BLK, BLK), F32),
            pltpu.VMEM((width, span + BLK), F32),
            pltpu.VMEM((2, ROWS, 2 * BLK), BF16),
            pltpu.VMEM((width, BLK), BF16),
            pltpu.SemaphoreType.DMA((2, blocks)),
            pltpu.SemaphoreType.DMA,
            pltpu.SemaphoreType.DMA((2,)),
            pltpu.SemaphoreType.DMA((2, blocks)),
        ],
        compiler_params=pltpu.CompilerParams(vmem_limit_bytes=62 * 2**20),
        cost_estimate=pl.CostEstimate(flops=6 * 10**9, bytes_accessed=30 * 2**20, transcendentals=0),
        name="attn_bwd",
    )(perm, lengths, qc, qp, k, v, pk, p, linv, gm, mixed)


MESH = pl.DeviceIdType.MESH


def fold_rows(x):
    return jnp.broadcast_to(x, (x.shape[0], BLK)).T[0:1]


def aligned(begin, size):
    return pl.ds(pl.multiple_of(begin, math.gcd(size, 16)), size)


def finish_kernel(
    lines, shards, chunks_f, sets, rows_l,
    mine_ref, come_ref, dk_ref, dv_ref, unit_all_ref, dpk_ref, table_ref, weights_in, dq_ref, x_ref,
    vectors_ref, total_ref, vec_ref, bias_ref, hidden_in,
    grad_ref, sums_ref, vsum_ref,
    dk_buf, dv_buf, un_buf, in_sem, dpk_buf, table_buf, weights_ref, hidden_ref, pos_sem, m_q, mt_k, mt_v, cs_q, cs_k, cs_v, dxp, bx0, bx1, bx2, vbuf, vacc,
    *rest,
):
    wk_ref, wv_ref, wq_ref = weights_ref.at[0], weights_ref.at[1], weights_ref.at[3]
    tokens, width = dq_ref.shape
    bufs_f = rest[: 3 * len(chunks_f)]
    bufs_l = rest[3 * len(chunks_f) : -2]
    send_sem, recv_sem = rest[-2:]
    ctx = lax.axis_index("ctx")
    w = lax.axis_index("wsh")
    core = lax.rem(ctx, 2)
    b = lax.rem(ctx // 2, 2)
    a = ctx // 4

    def at(a_to, b_to, core_to):
        return (a_to * 2 + b_to) * 2 + core_to

    def line_peer(s):
        return (at(lax.rem(a + s, lines), b, core), w)

    def shard_peer(s):
        return (ctx, lax.rem(w + s, shards))

    core_peer = (at(a, b, 1 - core), w)
    b_peer = (at(a, 1 - b, core), w)
    peers = [core_peer, b_peer] + [line_peer(s) for s in range(1, lines)] + [shard_peer(s) for s in range(1, shards)]
    barrier = pltpu.get_barrier_semaphore()
    for peer in peers:
        pl.semaphore_signal(barrier, inc=1, device_id=peer, device_id_type=MESH)

    counter = [0]

    def take(number):
        begin = counter[0]
        counter[0] += number
        return begin

    def remote(src, dst, index, peer):
        return pltpu.make_async_remote_copy(
            src_ref=src, dst_ref=dst, send_sem=send_sem.at[index], recv_sem=recv_sem.at[index],
            device_id=peer, device_id_type=MESH,
        )

    bits = lines.bit_length() - 1
    order = []
    for bit in range(bits):
        order += [m for m in reversed(range(lines)) if m & ((1 << (bit + 1)) - 1) == 1 << bit]
    order.append(0)

    def other(mask):
        place = 0
        for bit in range(bits):
            own = lax.rem(a // (1 << bit), 2)
            place = place + (1 << bit) * ((1 - own) if mask >> bit & 1 else own)
        return place

    def line_place(j):
        place = jnp.int32(0)
        for index, mask in enumerate(order):
            place = place + jnp.where(j == index, other(mask), 0)
        return place

    def line_at(mask):
        return (at(other(mask), b, core), w)

    group = 4 * tokens

    def fetch(j, slot):
        begin = pl.multiple_of(line_place(j) * group, group)
        return (
            pltpu.make_async_copy(dk_ref.at[:, pl.ds(begin, group)], dk_buf.at[slot], in_sem.at[slot, 0]),
            pltpu.make_async_copy(dv_ref.at[:, pl.ds(begin, group)], dv_buf.at[slot], in_sem.at[slot, 1]),
            pltpu.make_async_copy(unit_all_ref.at[pl.ds(begin, group)], un_buf.at[slot], in_sem.at[slot, 2]),
        )

    span, hold = table_ref.shape[0], table_buf.shape[0]
    pos_parts = [(begin, min(hold, span - begin)) for begin in range(0, span, hold)]

    def pos_copies(begin, size):
        rows = pl.ds(begin, size)
        return [
            pltpu.make_async_copy(dpk_ref.at[:, rows], dpk_buf.at[:, 0:size], pos_sem.at[0]),
            pltpu.make_async_copy(table_ref.at[rows], table_buf.at[0:size], pos_sem.at[1]),
        ]

    weights_copy = pltpu.make_async_copy(weights_in, weights_ref, pos_sem.at[2])
    hidden_copy = pltpu.make_async_copy(hidden_in, hidden_ref, pos_sem.at[3])
    weights_copy.start()
    for copy in fetch(0, 0):
        copy.start()
    for copy in pos_copies(*pos_parts[0]):
        copy.start()
    hidden_copy.start()

    def start_all(copies):
        for copy in copies:
            copy.start()

    def wait_all(copies):
        for copy in copies:
            copy.wait()

    def own_bit(bit):
        return lax.rem(a // (1 << bit), 2)

    def bit_peer(bit):
        return line_at(1 << bit)

    class Feed:
        def __init__(self, begin, rows, total_rows, bufs):
            self.begin, self.rows = begin, rows
            self.rc, self.rb = total_rows // 2, total_rows // 4
            self.b0, self.b1, self.b2 = bufs
            self.iy, self.irs, self.iag, self.ix, self.ic = take(shards - 1), take(bits), take(bits), take(1), take(2)

        def region(self, bit):
            start = 0
            for k in range(bit):
                start = start + own_bit(k) * (self.rows >> (k + 1))
            return start, self.rows >> bit

        def y_copies(self):
            return [
                remote(self.b0.at[lax.rem(w + s, shards)], self.b1.at[s - 1], self.iy + s - 1, shard_peer(s))
                for s in range(1, shards)
            ]

        def rs_copies(self, bit):
            start, size = self.region(bit)
            size = size // 2
            give = aligned(start + (1 - own_bit(bit)) * size, size)
            begin = sum(self.rows >> (k + 1) for k in range(bit))
            return [remote(self.b1.at[0, give], self.b2.at[begin : begin + size], self.irs + bit, bit_peer(bit))]

        def place(self, b_of, begin, size):
            return aligned(core * self.rc + b_of * self.rb + self.begin + begin, size)

        def ag_copies(self, bit):
            own = self.place(b, *self.region(bit + 1))
            return [remote(sums_ref.at[own], sums_ref.at[own], self.iag + bit, bit_peer(bit))]

        def x_copies(self):
            own = self.place(b, 0, self.rows)
            return [remote(sums_ref.at[own], sums_ref.at[own], self.ix, b_peer)]

        def c_copies(self):
            return [
                remote(sums_ref.at[rows], sums_ref.at[rows], self.ic + k, core_peer)
                for k, rows in enumerate((self.place(b, 0, self.rows), self.place(1 - b, 0, self.rows)))
            ]

        def y(self):
            rows = pl.ds(self.begin, self.rows)
            self.b0[...] = (mine_ref[:, rows].astype(F32) + come_ref[:, rows].astype(F32)).astype(BF16)
            start_all(self.y_copies())

        def rs(self, bit):
            if bit == 0:
                wait_all(self.y_copies())
                total = self.b0[w].astype(F32)
                for s in range(shards - 1):
                    total = total + self.b1[s].astype(F32)
                self.b1[0] = total.astype(BF16)
            else:
                self.add(bit - 1)
            start_all(self.rs_copies(bit))

        def add(self, bit):
            wait_all(self.rs_copies(bit))
            start, size = self.region(bit + 1)
            begin = sum(self.rows >> (k + 1) for k in range(bit))
            rows = aligned(start, size)
            self.b1[0, rows] = (self.b1[0, rows].astype(F32) + self.b2[begin : begin + size].astype(F32)).astype(BF16)

        def ag(self, bit):
            if bit == bits - 1:
                self.add(bit)
                start, size = self.region(bits)
                sums_ref[self.place(b, start, size)] = self.b1[0, aligned(start, size)]
            else:
                wait_all(self.ag_copies(bit + 1))
            start_all(self.ag_copies(bit))

        def x(self):
            wait_all(self.ag_copies(0))
            start_all(self.x_copies())

        def c(self):
            wait_all(self.x_copies())
            start_all(self.c_copies())

        def done(self):
            wait_all(self.c_copies())

    class Late:
        def __init__(self, out, rows, names, bufs):
            self.out, self.rows, self.names, self.begun = out, rows, names, set()
            self.src, self.b0, self.b1, self.b2, self.b3 = bufs
            self.rc, self.rb, self.share = rows // 2, rows // 4, rows // 4 // lines
            self.i0, self.iy, self.i2 = take(1), take(shards - 1), take(1)
            self.irs, self.iag, self.ix, self.ic = take(lines - 1), take(lines - 1), take(1), take(1)

        def c0_copies(self):
            return [remote(self.src.at[:, aligned((1 - core) * self.rc, self.rc)], self.b0, self.i0, core_peer)]

        def y_copies(self):
            return [
                remote(self.b0.at[lax.rem(w + s, shards)], self.b1.at[s - 1], self.iy + s - 1, shard_peer(s))
                for s in range(1, shards)
            ]

        def x0_copies(self):
            return [remote(self.b1.at[0, aligned((1 - b) * self.rb, self.rb)], self.b2, self.i2, b_peer)]

        def rs_copies(self):
            return [
                remote(
                    self.b2.at[aligned(lax.rem(a + s, lines) * self.share, self.share)],
                    self.b3.at[s - 1], self.irs + s - 1, line_peer(s),
                )
                for s in range(1, lines)
            ]

        def ag_copies(self):
            own = aligned(self.out + core * self.rc + b * self.rb + a * self.share, self.share)
            return [remote(sums_ref.at[own], sums_ref.at[own], self.iag + s - 1, line_peer(s)) for s in range(1, lines)]

        def x_copies(self):
            own = aligned(self.out + core * self.rc + b * self.rb, self.rb)
            return [remote(sums_ref.at[own], sums_ref.at[own], self.ix, b_peer)]

        def c_copies(self):
            own = aligned(self.out + core * self.rc, self.rc)
            return [remote(sums_ref.at[own], sums_ref.at[own], self.ic, core_peer)]

        def c0(self):
            for m, name in enumerate(self.names):
                grad = gradient(name)
                for s in range(shards):
                    self.src[s, m * rows_out : (m + 1) * rows_out] = grad[s * rows_out : (s + 1) * rows_out].astype(BF16)
            used = len(self.names) * rows_out
            if used < rows_l:
                self.src[:, used:] = jnp.zeros((shards, rows_l - used, width), BF16)
            start_all(self.c0_copies())

        def y(self):
            wait_all(self.c0_copies())
            own = self.src[:, aligned(core * self.rc, self.rc)]
            self.b0[...] = (self.b0[...].astype(F32) + own.astype(F32)).astype(BF16)
            start_all(self.y_copies())

        def x0(self):
            wait_all(self.y_copies())
            total = self.b0[w].astype(F32)
            for s in range(shards - 1):
                total = total + self.b1[s].astype(F32)
            self.b1[0] = total.astype(BF16)
            start_all(self.x0_copies())

        def rs(self):
            wait_all(self.x0_copies())
            own = self.b1[0, aligned(b * self.rb, self.rb)]
            self.b2[...] = (self.b2[...].astype(F32) + own.astype(F32)).astype(BF16)
            start_all(self.rs_copies())

        def ag(self):
            wait_all(self.rs_copies())
            total = self.b2[aligned(a * self.share, self.share)].astype(F32)
            for s in range(lines - 1):
                total = total + self.b3[s].astype(F32)
            own = aligned(self.out + core * self.rc + b * self.rb + a * self.share, self.share)
            sums_ref[own] = total.astype(BF16)
            start_all(self.ag_copies())

        def x(self):
            wait_all(self.ag_copies())
            start_all(self.x_copies())

        def c(self):
            wait_all(self.x_copies())
            start_all(self.c_copies())

        def done(self):
            wait_all(self.c_copies())

    rows_f = 4 * sum(chunks_f)
    rows_out = width // shards
    feeds = []
    begin = 0
    for index, rows in enumerate(chunks_f):
        feeds.append(Feed(begin, rows, rows_f, bufs_f[3 * index : 3 * index + 3]))
        begin += rows
    lates = {}
    for index, names in enumerate(sets):
        late = Late(rows_f + index * rows_l, rows_l, names, bufs_l[5 * index : 5 * index + 5])
        for name in names:
            lates[name] = late

    def late_step(name, step):
        late = lates[name]
        if step not in late.begun:
            late.begun.add(step)
            getattr(late, step)()

    values = x_ref[...].astype(F32)
    center = values - jnp.mean(values, axis=1, keepdims=True)
    inverse = lax.rsqrt(jnp.mean(center * center, axis=1, keepdims=True) + epsilon)
    unit = center * inverse

    def gradient(name):
        cols = vectors_ref[0:8].T
        gain_col, bias_col = cols[:, 0:1], cols[:, 1:2]
        if name == "q":
            m_q[...] = dot_tn(unit.astype(BF16), dq_ref[...])
            cs_q[...] = jnp.broadcast_to(jnp.sum(dq_ref[...].astype(F32), axis=0, keepdims=True), cs_q.shape)
            return gain_col * m_q[...] + bias_col * cs_q[0:1]
        if name == "p":
            total = jnp.zeros((width, width), F32)
            for index, (begin, size) in enumerate(pos_parts):
                if index:
                    start_all(pos_copies(begin, size))
                wait_all(pos_copies(begin, size))
                total = total + dot_nn(dpk_buf[:, 0:size], table_buf[0:size])
            return total.T
        m, cs = (mt_k, cs_k) if name == "k" else (mt_v, cs_v)
        return gain_col * m[...] + bias_col * fold_rows(cs[:, 0:1])

    mt_k[...] = jnp.zeros_like(mt_k)
    mt_v[...] = jnp.zeros_like(mt_v)
    cs_k[...] = jnp.zeros_like(cs_k)
    cs_v[...] = jnp.zeros_like(cs_v)
    pl.semaphore_wait(barrier, len(peers))
    for feed in feeds:
        feed.y()
    weights_copy.wait()

    i_x0, i_x1, i_x2 = take(lines), take(lines), take(lines)

    def copy_x0(j):
        return remote(dxp.at[j, 1 - core], bx0.at[j], i_x0 + j, core_peer)

    def copy_x1(j):
        return remote(bx0.at[j, 1 - b], bx1.at[j], i_x1 + j, b_peer)

    def copy_x2(mask):
        return remote(bx1.at[order.index(mask)], bx2.at[mask - 1], i_x2 + mask, line_at(mask & -mask))

    def after_x0(j):
        copy_x0(j).wait()
        bx0[j] = (bx0[j].astype(F32) + dxp[j, core].astype(F32)).astype(BF16)
        copy_x1(j).start()

    def after_x1(j):
        mask = order[j]
        copy_x1(j).wait()
        total = bx1[j].astype(F32) + bx0[j, b].astype(F32)
        for bit in range(bits):
            if mask and 1 << bit >= (mask & -mask):
                break
            source = mask | 1 << bit
            copy_x2(source).wait()
            total = total + bx2[source - 1].astype(F32)
        if mask:
            bx1[j] = total.astype(BF16)
            copy_x2(mask).start()
        return total

    last = lines - 1
    events = {}

    def plan(j, after, work, *args):
        events.setdefault((min(j, last), after), []).append((work, args))

    plan(0, "blocks", late_step, "p", "c0")
    plan(0, "blocks", after_x0, 0)
    plan(0, "blocks", late_step, "q", "c0")
    plan(1, "all", feeds[0].rs, 0)
    plan(1, "all", late_step, "q", "y")
    if last > 1:
        plan(1, "all", after_x0, 1)
    for j in range(2, last):
        plan(j + 1, "first", after_x0, j)
    plan(2, "blocks", after_x1, 0)
    for feed in feeds[1:]:
        plan(3, "blocks", feed.rs, 0)

    def happen(j, after):
        for (when, place), works in sorted(events.items()):
            if place == after:

                @pl.when(j == when)
                def _():
                    for work, args in works:
                        work(*args)

    def line_step(j, _):
        slot = lax.rem(j, 2)

        @pl.when(j < last)
        def _():
            start_all(fetch(j + 1, 1 - slot))

        wait_all(fetch(j, slot))

        def make_block(core_of, b_of):
            keys = pl.ds(pl.multiple_of((2 * b_of + core_of) * tokens, tokens), tokens)
            part = dot_nn(wk_ref[...], dk_buf[slot, :, keys]) + dot_nn(wv_ref[...], dv_buf[slot, :, keys])
            dxp[j, core_of, b_of] = part.astype(BF16)

        make_block(1 - core, 0)
        make_block(1 - core, 1)
        copy_x0(j).start()
        happen(j, "first")
        make_block(core, 0)
        make_block(core, 1)
        happen(j, "blocks")
        mt_k[...] += dot_nn(dk_buf[slot], un_buf[slot])
        mt_v[...] += dot_nn(dv_buf[slot], un_buf[slot])
        for cs, buf in ((cs_k, dk_buf), (cs_v, dv_buf)):
            total = cs[...]
            for piece in range(group // BLK):
                total = total + buf[slot, :, piece * BLK : (piece + 1) * BLK].astype(F32)
            cs[...] = total
        happen(j, "all")
        return 0

    lax.fori_loop(0, lines, line_step, 0)
    for m, cs in ((mt_k, cs_k), (mt_v, cs_v)):
        m[...] = m[...].T
        cs[...] = jnp.broadcast_to(jnp.sum(cs[...], axis=1, keepdims=True), cs.shape)

    vstages = [[core_peer], [b_peer], [line_peer(s) for s in range(1, lines)], [shard_peer(s) for s in range(1, shards)]]
    vslots = []
    place = 0
    for stage in vstages:
        vslots.append(place)
        place += len(stage)
    vbegin = take(place)

    def v_copy(stage, index):
        slot = vslots[stage] + index
        return remote(vacc.at[pl.ds(stage * 16, 16)], vbuf.at[slot], vbegin + slot, vstages[stage][index])

    def v_start(stage):
        for index in range(len(vstages[stage])):
            v_copy(stage, index).start()

    def v_finish(stage):
        total = vacc[stage * 16 : stage * 16 + 16]
        for index in range(len(vstages[stage])):
            v_copy(stage, index).wait()
            total = total + vbuf[vslots[stage] + index]
        vacc[(stage + 1) * 16 : (stage + 2) * 16] = total

    def vectors_begin():
        vacc[0:16] = vec_ref[...]
        vacc[2:4] = bias_ref[0:2]
        gain_grad = m_q[...] * wq_ref[...].astype(F32)
        gain_grad = gain_grad + mt_k[...] * wk_ref[...].astype(F32) + mt_v[...] * wv_ref[...].astype(F32)
        vacc[0:1] = fold_rows(jnp.sum(gain_grad, axis=1, keepdims=True))
        total = dot_nt(cs_q[...].astype(BF16), wq_ref[...])
        for cs, weight in ((cs_k, wk_ref), (cs_v, wv_ref)):
            row = jnp.broadcast_to(fold_rows(cs[:, 0:1]), (8, width))
            total = total + dot_nt(row.astype(BF16), weight[...])
        vacc[1:2] = total[0:1]
        v_start(0)

    def rest(feed, step):
        if step < bits:
            feed.rs(step)
        else:
            feed.ag(2 * bits - 1 - step)

    one, two = feeds[0], feeds[-1]
    pair = len(feeds) > 1
    late_step("v", "c0")
    vectors_begin()
    for step in range(1, bits):
        rest(one, step)
    if last > 1:
        after_x1(1)
    late_step("v", "y")
    after_x0(last)
    v_finish(0)
    v_start(1)
    late_step("p", "y")
    late_step("q", "x0")
    late_step("k", "c0")
    if pair:
        for step in range(1, bits):
            rest(two, step)
    rest(one, bits)
    late_step("k", "y")
    late_step("v", "x0")
    late_step("p", "x0")
    v_finish(1)
    v_start(2)
    if pair:
        rest(two, bits)
    late_step("k", "x0")
    for step in range(bits + 1, 2 * bits):
        rest(one, step)
    v_finish(2)
    v_start(3)
    for j in range(2, last):
        after_x1(j)
    if pair:
        for step in range(bits + 1, 2 * bits):
            rest(two, step)
    late_step("q", "rs")
    late_step("v", "rs")
    v_finish(3)
    vsum_ref[...] = vacc[4 * 16 : 5 * 16]
    late_step("p", "rs")
    one.x()
    late_step("k", "rs")
    own = after_x1(last)
    scaled = (own.T + dot_nt(dq_ref[...], wq_ref[...])) * vectors_ref[0:1]
    hidden_copy.wait()
    grad_ref[...] = hidden_ref[...] + inverse * (
        scaled - jnp.mean(scaled, axis=1, keepdims=True) - unit * jnp.mean(scaled * unit, axis=1, keepdims=True)
    )
    if pair:
        two.x()
    late_step("q", "ag")
    one.c()
    late_step("v", "ag")
    late_step("p", "ag")
    late_step("k", "ag")
    late_step("q", "x")
    late_step("v", "x")
    if pair:
        two.c()
    late_step("p", "x")
    late_step("k", "x")
    late_step("q", "c")
    late_step("v", "c")
    late_step("p", "c")
    late_step("k", "c")
    for feed in feeds:
        feed.done()
    for name in "qpvk":
        late_step(name, "done")


def finish(lines, shards, chunks_f, sets, rows_l, cid, mine, come, dk, dv, unit_all, dpk, table, weights, dq, x, vectors, total, vec, bias, hidden):
    tokens, width = dq.shape
    vmem = pl.BlockSpec(memory_space=pltpu.VMEM)
    hbm = pl.BlockSpec(memory_space=pl.ANY)
    bufs = []
    for rows in chunks_f:
        bufs += [
            pltpu.VMEM((shards, rows, width), BF16),
            pltpu.VMEM((shards - 1, rows, width), BF16),
            pltpu.VMEM((rows, width), BF16),
        ]
    for names in sets:
        bufs += [
            pltpu.VMEM((shards, rows_l, width), BF16),
            pltpu.VMEM((shards, rows_l // 2, width), BF16),
            pltpu.VMEM((shards - 1, rows_l // 2, width), BF16),
            pltpu.VMEM((rows_l // 4, width), BF16),
            pltpu.VMEM((lines - 1, rows_l // 4 // lines, width), BF16),
        ]
    hops = shards - 1 + 2 * (lines - 1)
    copies = len(chunks_f) * (shards + 2 + 2 * (lines.bit_length() - 1)) + len(sets) * (hops + 4) + 3 * lines + 2 + lines - 1 + shards - 1
    total_rows = 4 * sum(chunks_f) + len(sets) * rows_l
    stages = 1 + 1 + (lines - 1) + (shards - 1)
    hold = min(dpk.shape[1], 17 * BLK)
    return pl.pallas_call(
        functools.partial(finish_kernel, lines, shards, tuple(chunks_f), sets, rows_l),
        out_shape=(
            jax.ShapeDtypeStruct((tokens, width), F32),
            jax.ShapeDtypeStruct((total_rows, width), BF16),
            jax.ShapeDtypeStruct((16, width), F32),
        ),
        in_specs=[vmem] * 2 + [hbm] * 6 + [vmem] * 6 + [hbm],
        out_specs=(vmem,) * 3,
        scratch_shapes=[
            pltpu.VMEM((2, width, 4 * tokens), BF16),
            pltpu.VMEM((2, width, 4 * tokens), BF16),
            pltpu.VMEM((2, 4 * tokens, width), BF16),
            pltpu.SemaphoreType.DMA((2, 3)),
            pltpu.VMEM((width, hold), BF16),
            pltpu.VMEM((hold, width), BF16),
            pltpu.VMEM((4, width, width), BF16),
            pltpu.VMEM((tokens, width), F32),
            pltpu.SemaphoreType.DMA((4,)),
            pltpu.VMEM((width, width), F32),
            pltpu.VMEM((width, width), F32),
            pltpu.VMEM((width, width), F32),
            pltpu.VMEM((8, width), F32),
            pltpu.VMEM((width, BLK), F32),
            pltpu.VMEM((width, BLK), F32),
            pltpu.VMEM((lines, 2, 2, width, tokens), BF16),
            pltpu.VMEM((lines, 2, width, tokens), BF16),
            pltpu.VMEM((lines, width, tokens), BF16),
            pltpu.VMEM((lines - 1, width, tokens), BF16),
            pltpu.VMEM((stages, 16, width), F32),
            pltpu.VMEM((5 * 16, width), F32),
        ]
        + bufs
        + [pltpu.SemaphoreType.DMA((copies,)), pltpu.SemaphoreType.DMA((copies,))],
        compiler_params=pltpu.CompilerParams(
            collective_id=cid, has_side_effects=True, vmem_limit_bytes=63 * 2**20
        ),
        cost_estimate=pl.CostEstimate(flops=10**10, bytes_accessed=30 * 2**20, transcendentals=0),
        name="finish",
    )(mine, come, dk, dv, unit_all, dpk, table, weights, dq, x, vectors, total, vec, bias, hidden)


def unpack_kernel(
    shards, rows_f, sets, rows_l, sums_ref, vsum_ref, total_ref, grad_ref, result_ref,
    grad_out, result_out, q_out, k_out, v_out, o_out, p_out, u_out, d_out, g1_out, b1_out, cb_out, pb_out, g2_out, b2_out, bd_out, bu_out,
    loss_out,
    low, wide, up, in_sem, out_sem,
):
    width = vsum_ref.shape[1]
    rows_out, rows_up = q_out.shape[0], d_out.shape[0]
    parts = u_out.shape[1] // width
    w = lax.axis_index("wsh")
    pieces = [(rows_up, d_out), (2 * rows_up, o_out)]
    to = {"q": q_out, "p": p_out, "k": k_out, "v": v_out}
    for index, names in enumerate(sets):
        pieces += [(rows_f + index * rows_l + m * rows_out, to[name]) for m, name in enumerate(names)]
    ins = [pltpu.make_async_copy(sums_ref.at[0:rows_up], low.at[0:rows_up], in_sem.at[0])]
    for index, (begin, out) in enumerate(pieces):
        size = out.shape[0]
        ins.append(pltpu.make_async_copy(sums_ref.at[begin : begin + size], low.at[begin : begin + size], in_sem.at[1 + index]))
    for copy in ins:
        copy.start()
    outs = []
    grad_out[...] = grad_ref[...]
    result_out[...] = result_ref[...]
    ins[0].wait()
    for c in range(parts):
        up[:, c * width : (c + 1) * width] = low[c * rows_out : (c + 1) * rows_out].astype(F32)
    outs.append(pltpu.make_async_copy(up, u_out, out_sem.at[0]))
    outs[0].start()
    for index, (begin, out) in enumerate(pieces):
        size = out.shape[0]
        ins[1 + index].wait()
        wide[begin : begin + size] = low[begin : begin + size].astype(F32)
        copy = pltpu.make_async_copy(wide.at[begin : begin + size], out, out_sem.at[1 + index])
        copy.start()
        outs.append(copy)

    def share(row):
        part = vsum_ref[row : row + 1, 0:rows_out]
        for s in range(1, shards):
            part = jnp.where(w == s, vsum_ref[row : row + 1, s * rows_out : (s + 1) * rows_out], part)
        return part.reshape(rows_out)

    for row, ref in enumerate((g1_out, b1_out, cb_out, pb_out, g2_out, b2_out, bd_out)):
        ref[...] = share(row)
    per = rows_up // rows_out
    for q in range(per):
        part = None
        for s in range(shards):
            group = s * per + q
            row, place = 7 + group // shards, group % shards
            piece = vsum_ref[row : row + 1, place * rows_out : (place + 1) * rows_out]
            part = piece if part is None else jnp.where(w == s, piece, part)
        bu_out[q * rows_out : (q + 1) * rows_out] = part.reshape(rows_out)
    loss_out[0, 0] = vsum_ref[7 + parts, 0] / (total_ref[0, 0] * width)
    for copy in outs:
        copy.wait()


def unpack(shards, rows_f, sets, rows_l, hidden, sums, vsum, total, grad, result):
    tokens, width = grad.shape
    rows_out, rows_up = width // shards, hidden // shards
    vmem = pl.BlockSpec(memory_space=pltpu.VMEM)
    hbm = pl.BlockSpec(memory_space=pl.ANY)
    square = jax.ShapeDtypeStruct((rows_out, width), F32)
    vector = jax.ShapeDtypeStruct((rows_out,), F32)
    return pl.pallas_call(
        functools.partial(unpack_kernel, shards, rows_f, sets, rows_l),
        out_shape=(
            jax.ShapeDtypeStruct((tokens, width), F32), jax.ShapeDtypeStruct((tokens, width), BF16), square, square, square, square, square,
            jax.ShapeDtypeStruct((rows_out, hidden), F32), jax.ShapeDtypeStruct((rows_up, width), F32),
            vector, vector, vector, vector, vector, vector, vector, jax.ShapeDtypeStruct((rows_up,), F32),
            jax.ShapeDtypeStruct((1, 1), F32),
        ),
        in_specs=[hbm, vmem, vmem, vmem, vmem],
        out_specs=(vmem,) * 2 + (hbm,) * 7 + (vmem,) * 8 + (pl.BlockSpec(memory_space=pltpu.SMEM),),
        scratch_shapes=[
            pltpu.VMEM(sums.shape, BF16),
            pltpu.VMEM(sums.shape, F32),
            pltpu.VMEM((rows_out, hidden), F32),
            pltpu.SemaphoreType.DMA((7,)),
            pltpu.SemaphoreType.DMA((8,)),
        ],
        compiler_params=pltpu.CompilerParams(vmem_limit_bytes=62 * 2**20),
        cost_estimate=pl.CostEstimate(flops=10**6, bytes_accessed=12 * 2**20, transcendentals=0),
        name="unpack",
    )(sums, vsum, total, grad, result)


PARTS = 2


def start_kernel(
    lines, shards, x_ref, wk_ref, wv_ref, wp_ref, wq_ref, wo_ref, wu_ref, wd_ref,
    g1_ref, b1_ref, cb_ref, pb_ref, g2_ref, b2_ref, bd_ref, bu_ref, mask_ref, far_ref, near_ref,
    k_ref, v_ref, unit_ref, pk_ref, table_ref, qc_ref, qp_ref, weights_ref, wo_out, wu_out, wd_out, vectors_ref, total_ref,
    x_all, k_buf, v_buf, u_buf, pk_buf, t_buf, wo_buf, wu_buf, wd_buf, vec_src, vec_buf, cnt_buf, cnt_acc,
    up_send, up_recv, down_send, down_recv, b_send, b_recv, c_send, c_recv,
    y_send, y_recv, yc_send, yc_recv, d_send, d_recv, s_send, s_recv, out_sem, pos_sem, own_sem,
):
    tokens, width = x_ref.shape
    piece = tokens // PARTS
    half = width // 2
    chunks = pk_buf.shape[0] // BLK
    ctx = lax.axis_index("ctx")
    w = lax.axis_index("wsh")
    core = lax.rem(ctx, 2)
    b = lax.rem(ctx // 2, 2)
    a = ctx // 4

    def at(a_to, b_to, core_to):
        return (a_to * 2 + b_to) * 2 + core_to

    def shard_peer(s):
        return (ctx, lax.rem(w + s, shards))

    def line_peer(s):
        return (at(lax.rem(a + s, lines), b, core), w)

    core_peer = (at(a, b, 1 - core), w)
    b_peer = (at(a, 1 - b, core), w)
    peers = [core_peer, b_peer] + [line_peer(s) for s in range(1, lines)] + [shard_peer(s) for s in range(1, shards)]
    barrier = pltpu.get_barrier_semaphore()
    for peer in peers:
        pl.semaphore_signal(barrier, inc=1, device_id=peer, device_id_type=MESH)

    def remote(src, dst, send, recv, peer):
        return pltpu.make_async_remote_copy(
            src_ref=src, dst_ref=dst, send_sem=send, recv_sem=recv, device_id=peer, device_id_type=MESH
        )

    def block(slot):
        return aligned(slot * tokens, tokens)

    x_all[block(ctx)] = x_ref[...]
    rows_out = wq_ref.shape[0]
    quarter = rows_out // 2
    rows_up = wd_ref.shape[0]
    weight_in = (wk_ref, wv_ref, wp_ref, wq_ref, wo_ref)
    weight_to = tuple(weights_ref.at[m] for m in range(4)) + (wo_buf,)
    own_copies = [
        pltpu.make_async_copy(ref, to.at[aligned(w * rows_out, rows_out)], own_sem.at[m])
        for m, (ref, to) in enumerate(zip(weight_in[:4], weight_to))
    ]
    for copy in own_copies:
        copy.start()
    vec_src[...] = jnp.zeros_like(vec_src)
    for row, ref in enumerate((g1_ref, b1_ref, cb_ref, pb_ref, g2_ref, b2_ref, bd_ref)):
        vec_src[row : row + 1] = ref[...].astype(F32).reshape(1, rows_out)
    bias_rows = rows_up // rows_out
    for q in range(bias_rows):
        vec_src[7 + q : 8 + q] = bu_ref[q * rows_out : (q + 1) * rows_out].astype(F32).reshape(1, rows_out)
    cnt_acc[0:8] = jnp.broadcast_to(jnp.sum(mask_ref[...].astype(F32), axis=1, keepdims=True), (8, BLK))
    pl.semaphore_wait(barrier, len(peers))

    def x_copy(slot, h, send, recv, peer):
        rows = aligned(slot * tokens + h * piece, piece)
        return remote(x_all.at[rows], x_all.at[rows], send, recv, peer)

    def up_copy(p, h):
        peer = (at(jnp.minimum(a + 1, lines - 1), b, core), w)
        return x_copy(at(p, b, core), h, up_send.at[p, h], up_recv.at[p, h], peer)

    def down_copy(p, h):
        peer = (at(jnp.maximum(a - 1, 0), b, core), w)
        return x_copy(at(p, b, core), h, down_send.at[p, h], down_recv.at[p, h], peer)

    def b_copy(p, h, b_from):
        return x_copy(at(p, b_from, core), h, b_send.at[p, h], b_recv.at[p, h], b_peer)

    def c_copy(p, far, b_from, core_from):
        rows = block(at(p, b_from, core_from))
        return remote(x_all.at[rows], x_all.at[rows], c_send.at[far, p], c_recv.at[far, p], core_peer)

    def weight_copy(m, s):
        rows = aligned(w * rows_out + core * quarter, quarter)
        src = weight_in[m].at[aligned(core * quarter, quarter)]
        return remote(src, weight_to[m].at[rows], y_send.at[m, s - 1], y_recv.at[m, s - 1], shard_peer(s))

    def weight_pass(m, s):
        rows = aligned(lax.rem(w + shards - s, shards) * rows_out + core * quarter, quarter)
        return remote(
            weight_to[m].at[rows], weight_to[m].at[rows], yc_send.at[m, s - 1], yc_recv.at[m, s - 1], core_peer
        )

    low = lax.rem(a, 2)
    quarter_in, quarter_to = (wd_ref, wu_ref), (wd_buf, wu_buf)
    pair_peer = (at(a + 1 - 2 * low, b, core), w)

    def quarter_rows(m, s, low_of):
        size = quarter_in[m].shape[0]
        owner = lax.rem(w + shards - s, shards)
        return aligned(owner * size + (low_of * 2 + core) * (size // 4), size // 4)

    def quarter_copy(m, s):
        size = quarter_in[m].shape[0]
        src = quarter_in[m].at[aligned((low * 2 + core) * (size // 4), size // 4)]
        dst = quarter_to[m].at[quarter_rows(m, 0, low)]
        return remote(src, dst, d_send.at[m, 0, s - 1], d_recv.at[m, 0, s - 1], shard_peer(s))

    def quarter_pass(m, kind, s):
        rows = quarter_rows(m, s, 1 - low if kind == 3 else low)
        peer = pair_peer if kind == 1 else core_peer
        ref = quarter_to[m].at[rows]
        return remote(ref, ref, d_send.at[m, kind, s - 1], d_recv.at[m, kind, s - 1], peer)

    def quarter_on(m):
        for s in range(1, shards):
            quarter_copy(m, s).wait()
            quarter_pass(m, 1, s).start()
            quarter_pass(m, 2, s).start()

    def vec_copy(s):
        return remote(vec_src, vec_buf.at[s - 1], s_send.at[s - 1], s_recv.at[s - 1], shard_peer(s))

    stages = [[shard_peer(s) for s in range(1, shards)], [core_peer], [b_peer], [line_peer(s) for s in range(1, lines)]]
    slots = []
    place = 0
    for stage in stages:
        slots.append(place)
        place += len(stage)

    def cnt_copy(stage, index):
        slot = slots[stage] + index
        sem = shards - 1 + slot
        return remote(cnt_acc.at[pl.ds(stage * 8, 8)], cnt_buf.at[slot], s_send.at[sem], s_recv.at[sem], stages[stage][index])

    def cnt_start(stage):
        for index in range(len(stages[stage])):
            cnt_copy(stage, index).start()

    def cnt_finish(stage):
        total = cnt_acc[stage * 8 : stage * 8 + 8]
        for index in range(len(stages[stage])):
            cnt_copy(stage, index).wait()
            total = total + cnt_buf[slots[stage] + index]
        cnt_acc[(stage + 1) * 8 : (stage + 2) * 8] = total

    for s in range(1, shards):
        vec_copy(s).start()
    cnt_start(0)
    for h in range(PARTS):

        @pl.when(a + 1 < lines)
        def _():
            up_copy(a, h).start()

        @pl.when(a >= 1)
        def _():
            down_copy(a, h).start()

        b_copy(a, h, b).start()
    c_copy(a, 0, b, core).start()
    for kind, m in ((0, 0), (0, 1), (1, 0), (0, 2), (1, 1), (0, 3), (0, 4)):
        for s in range(1, shards):
            (quarter_copy if kind else weight_copy)(m, s).start()


    def table_step(d, _):
        sin_far, cos_far = far_ref[0, pl.ds(d, 1)], far_ref[1, pl.ds(d, 1)]
        sin_near, cos_near = near_ref[0], near_ref[1]
        rows = aligned(d * BLK, BLK)
        t_buf[rows, :half] = (sin_far * cos_near - cos_far * sin_near).astype(BF16)
        t_buf[rows, half:] = (cos_far * cos_near + sin_far * sin_near).astype(BF16)
        return 0

    lax.fori_loop(0, chunks, table_step, 0)
    table_out = pltpu.make_async_copy(t_buf, table_ref, pos_sem.at[0])
    table_out.start()
    lane_to = lax.broadcasted_iota(jnp.int32, (rows_out, width), 1)
    lane_from = lax.broadcasted_iota(jnp.int32, (rows_out, width), 0)
    row_at = lax.broadcasted_iota(jnp.int32, (16, width), 0)

    def spread(values, place):
        return dot_nn(values.astype(BF16), (lane_to == lane_from + place * rows_out).astype(BF16))

    def placed(values, owner):
        full = jnp.where(row_at < 7, spread(values, owner), 0.0)
        for q in range(bias_rows):
            group = owner * bias_rows + q
            row = jnp.broadcast_to(values[7 + q : 8 + q], values.shape)
            full = full + jnp.where(row_at == 7 + group // shards, spread(row, lax.rem(group, shards)), 0.0)
        return full

    vectors = placed(vec_src[...], w)
    for s in range(1, shards):
        vec_copy(s).wait()
        vectors = vectors + placed(vec_buf[s - 1], lax.rem(w + shards - s, shards))
    vectors_ref[...] = vectors
    cnt_finish(0)
    cnt_start(1)

    def unit_of(rows):
        values = rows.astype(F32)
        center = values - jnp.mean(values, axis=1, keepdims=True)
        return center * lax.rsqrt(jnp.mean(center * center, axis=1, keepdims=True) + epsilon)

    def out_copies(slot):
        rows = block(slot)
        return (
            pltpu.make_async_copy(k_buf.at[rows], k_ref.at[rows], out_sem.at[0, slot]),
            pltpu.make_async_copy(v_buf.at[rows], v_ref.at[rows], out_sem.at[1, slot]),
            pltpu.make_async_copy(u_buf.at[rows], unit_ref.at[rows], out_sem.at[2, slot]),
        )

    def project(p):
        def one(q, _):
            other_b = lax.rem(q, 2)
            other_core = q // 2

            @pl.when(q == 1)
            def _():
                for h in range(PARTS):
                    b_copy(p, h, b).wait()
                c_copy(p, 1, 1 - b, core).start()

            @pl.when(q == 2)
            def _():
                c_copy(p, 0, b, core).wait()

            @pl.when(q == 3)
            def _():
                c_copy(p, 1, 1 - b, core).wait()

            slot = at(p, b + other_b - 2 * b * other_b, core + other_core - 2 * core * other_core)
            rows = block(slot)
            unit = unit_of(x_all[rows])
            u_buf[rows] = unit.astype(BF16)
            normed = (unit * vectors_ref[0:1] + vectors_ref[1:2]).astype(BF16)
            k_buf[rows] = dot_nn(normed, weights_ref[0]).astype(BF16)
            v_buf[rows] = dot_nn(normed, weights_ref[1]).astype(BF16)
            for copy in out_copies(slot):
                copy.start()
            return 0

        lax.fori_loop(0, 4, one, 0)

    def pos_step(d, _):
        rows = aligned(d * BLK, BLK)
        pk_buf[rows] = dot_nn(t_buf[rows], weights_ref[2]).astype(BF16)
        return 0

    last = lines - 1

    def line_step(s, _):
        below, high = a - 1 - s, a + 1 + s

        for h in range(PARTS):

            @pl.when((s < lines - 1) & (below >= 0))
            def _():
                p = jnp.maximum(below, 0)
                up_copy(p, h).wait_recv()

                @pl.when(a + 1 < lines)
                def _():
                    up_copy(p, h).start()

                b_copy(p, h, b).start()
                if h == PARTS - 1:
                    c_copy(p, 0, b, core).start()

            @pl.when((s < lines - 1) & (high < lines))
            def _():
                p = jnp.minimum(high, lines - 1)
                down_copy(p, h).wait_recv()

                @pl.when(a >= 1)
                def _():
                    down_copy(p, h).start()

                b_copy(p, h, b).start()
                if h == PARTS - 1:
                    c_copy(p, 0, b, core).start()

        @pl.when(s == 0)
        def _():
            cnt_finish(1)
            cnt_start(2)
            for copy in own_copies:
                copy.wait()
            for m in range(2):
                for t in range(1, shards):
                    weight_copy(m, t).wait()
                    weight_pass(m, t).start()
            for m in range(2):
                for t in range(1, shards):
                    weight_pass(m, t).wait()

        @pl.when(s == min(1, last))
        def _():
            cnt_finish(2)
            cnt_start(3)

        @pl.when(s == min(2, last))
        def _():
            for t in range(1, shards):
                weight_copy(2, t).wait()
                weight_pass(2, t).start()
            for t in range(1, shards):
                weight_pass(2, t).wait()

        @pl.when(s == last)
        def _():
            for m in range(3, 5):
                for t in range(1, shards):
                    weight_copy(m, t).wait()
                    weight_pass(m, t).start()
            for t in range(1, shards):
                weight_pass(3, t).wait()

        @pl.when(a - s >= 0)
        def _():
            project(jnp.maximum(a - s, 0))

        @pl.when((s >= 1) & (a + s < lines))
        def _():
            project(jnp.minimum(a + s, lines - 1))

        @pl.when(s == min(1, last))
        def _():
            quarter_on(0)

        @pl.when(s == min(2, last))
        def _():
            lax.fori_loop(0, chunks // 2, pos_step, 0)
            quarter_on(1)

        @pl.when(s == last)
        def _():
            lax.fori_loop(chunks // 2, chunks, pos_step, 0)

        return 0

    lax.fori_loop(0, lines, line_step, 0)
    pos_out = pltpu.make_async_copy(pk_buf, pk_ref, pos_sem.at[1])
    pos_out.start()
    normed = (unit_of(x_ref[...]) * vectors_ref[0:1] + vectors_ref[1:2]).astype(BF16)
    queries = dot_nn(normed, weights_ref[3]).astype(BF16).astype(F32)
    qc_ref[...] = ((queries + vectors_ref[2:3]) * 0.125).astype(BF16)
    qp_ref[...] = ((queries + vectors_ref[3:4]) * 0.125).astype(BF16)
    cnt_finish(3)
    total_ref[...] = cnt_acc[4 * 8 : 5 * 8]

    def sends_done(p, _):
        for h in range(PARTS):

            @pl.when((a + 1 < lines) & (p <= a))
            def _():
                up_copy(p, h).wait_send()

            @pl.when((a >= 1) & (p >= a))
            def _():
                down_copy(p, h).wait_send()

        return 0

    lax.fori_loop(0, lines, sends_done, 0)

    def outs_done(slot, _):
        for copy in out_copies(slot):
            copy.wait()
        return 0

    lax.fori_loop(0, 4 * lines, outs_done, 0)
    for s in range(1, shards):
        weight_pass(4, s).wait()
        for m in range(2):
            quarter_pass(m, 1, s).wait()
            quarter_pass(m, 3, s).start()
    for s in range(1, shards):
        for m in range(2):
            quarter_pass(m, 2, s).wait()
            quarter_pass(m, 3, s).wait()
    far_copies = []
    for m, (buf, to) in enumerate(((wo_buf, wo_out), (wu_buf, wu_out), (wd_buf, wd_out))):
        size = buf.shape[0] // shards
        for s in range(1, shards):
            rows = aligned(lax.rem(w + s, shards) * size, size)
            far_copies.append(pltpu.make_async_copy(buf.at[rows], to.at[rows], own_sem.at[4 + m * (shards - 1) + s - 1]))
    for copy in far_copies:
        copy.start()
    for copy in far_copies:
        copy.wait()
    table_out.wait()
    pos_out.wait()


def start(lines, shards, cid, limit, x, weights, vectors, mask, far, near):
    tokens, width = x.shape
    hidden = weights[5].shape[1]
    rows_out = weights[0].shape[0]
    members = 4 * lines
    keys = members * tokens
    span = limit * BLK
    vmem = pl.BlockSpec(memory_space=pltpu.VMEM)
    hbm = pl.BlockSpec(memory_space=pl.ANY)
    small = 2 * (shards - 1) + 1 + 1 + lines - 1
    dma = pltpu.SemaphoreType.DMA
    other = shards - 1
    return pl.pallas_call(
        functools.partial(start_kernel, lines, shards),
        out_shape=(
            jax.ShapeDtypeStruct((keys, width), BF16),
            jax.ShapeDtypeStruct((keys, width), BF16),
            jax.ShapeDtypeStruct((keys, width), BF16),
            jax.ShapeDtypeStruct((span, width), BF16),
            jax.ShapeDtypeStruct((span, width), BF16),
            jax.ShapeDtypeStruct((tokens, width), BF16),
            jax.ShapeDtypeStruct((tokens, width), BF16),
            jax.ShapeDtypeStruct((4, width, width), BF16),
            jax.ShapeDtypeStruct((width, width), BF16),
            jax.ShapeDtypeStruct((width, hidden), BF16),
            jax.ShapeDtypeStruct((hidden, width), BF16),
            jax.ShapeDtypeStruct((16, width), F32),
            jax.ShapeDtypeStruct((8, BLK), F32),
        ),
        in_specs=[vmem] + [hbm] * 7 + [vmem] * 11,
        out_specs=(hbm,) * 5 + (vmem,) * 3 + (hbm,) * 3 + (vmem,) * 2,
        scratch_shapes=[
            pltpu.VMEM((keys, width), BF16),
            pltpu.VMEM((keys, width), BF16),
            pltpu.VMEM((keys, width), BF16),
            pltpu.VMEM((keys, width), BF16),
            pltpu.VMEM((span, width), BF16),
            pltpu.VMEM((span, width), BF16),
            pltpu.VMEM((width, width), BF16),
            pltpu.VMEM((width, hidden), BF16),
            pltpu.VMEM((hidden, width), BF16),
            pltpu.VMEM((16, rows_out), F32),
            pltpu.VMEM((other, 16, rows_out), F32),
            pltpu.VMEM((lines + shards, 8, BLK), F32),
            pltpu.VMEM((5 * 8, BLK), F32),
        ]
        + [dma((lines, PARTS))] * 6
        + [dma((2, lines))] * 2
        + [dma((5, other))] * 4
        + [dma((2, 4, other))] * 2
        + [dma((small,))] * 2
        + [dma((3, members)), dma((2,)), dma((4 + 3 * other,))],
        compiler_params=pltpu.CompilerParams(collective_id=cid, has_side_effects=True, vmem_limit_bytes=60 * 2**20),
        cost_estimate=pl.CostEstimate(flops=6 * 10**9, bytes_accessed=20 * 2**20, transcendentals=0),
        name="start",
    )(x, *weights, *vectors, mask, far, near)


GELU_SCALE = math.sqrt(2.0 / math.pi)


def middle_kernel(
    shards, rows_f, mask_ref, x_ref, mixed_ref, teacher_ref, out_grad_ref, vectors_ref, total_ref,
    wo_own, wu_own, wd_own, wo_ref, wu_ref, wd_ref,
    out_ref, hidden_ref, gm_ref, mine_ref, theirs_ref, vec_ref,
    wo, wu, wd, slope, act, gf_ref, landed, sem, send_sem, recv_sem,
):
    tokens, width = x_ref.shape
    parts = wu.shape[1] // width
    ctx = lax.axis_index("ctx")
    core = lax.rem(ctx, 2)
    core_peer = (ctx + 1 - 2 * core, lax.axis_index("wsh"))
    barrier = pltpu.get_barrier_semaphore()
    pl.semaphore_signal(barrier, inc=1, device_id=core_peer, device_id_type=MESH)
    w = lax.axis_index("wsh")
    copies = []
    for k, (own, gathered, full) in enumerate(((wo_own, wo_ref, wo), (wu_own, wu_ref, wu), (wd_own, wd_ref, wd))):
        size = own.shape[0]
        part = [pltpu.make_async_copy(own, full.at[aligned(w * size, size)], sem.at[k, 0])]
        for s in range(1, shards):
            rows = aligned(lax.rem(w + s, shards) * size, size)
            part.append(pltpu.make_async_copy(gathered.at[rows], full.at[rows], sem.at[k, s]))
        for copy in part:
            copy.start()
        copies.append(part)

    def arrive(k):
        for copy in copies[k]:
            copy.wait()

    b = lax.rem(ctx // 2, 2)
    half, quarter = rows_f // 2, rows_f // 4

    def give(begin, size, index):
        rows = aligned((1 - core) * half + begin, size)
        return pltpu.make_async_remote_copy(
            src_ref=gf_ref.at[:, rows], dst_ref=landed.at[:, begin : begin + size],
            send_sem=send_sem.at[index], recv_sem=recv_sem.at[index], device_id=core_peer, device_id_type=MESH,
        )

    gain, offset, down_bias = vectors_ref[4:5], vectors_ref[5:6], vectors_ref[6:7]
    mixed = mixed_ref[...].astype(BF16)
    arrive(0)
    hidden = x_ref[...].astype(F32) + dot_nn(mixed, wo[...])
    center = hidden - jnp.mean(hidden, axis=1, keepdims=True)
    inverse = lax.rsqrt(jnp.mean(center * center, axis=1, keepdims=True) + epsilon)
    unit = center * inverse
    normed = (unit * gain + offset).astype(BF16)
    result = hidden + down_bias
    arrive(1)
    arrive(2)
    for c in range(parts):
        cols = slice(c * width, (c + 1) * width)
        v = dot_nn(normed, wu[:, cols]) + vectors_ref[7 + c : 8 + c]
        square = v * v
        t = jnp.tanh(GELU_SCALE * (v + 0.044715 * (square * v)))
        act[:, cols] = (0.5 * v * (1.0 + t)).astype(BF16)
        slope[:, cols] = 0.5 * (1.0 + t) + 0.5 * v * (1.0 - t * t) * (GELU_SCALE * (1.0 + 3.0 * 0.044715 * square))
        result = result + dot_nn(act[:, cols], wd[cols])
    out_ref[...] = result.astype(BF16)
    mask = jnp.broadcast_to(mask_ref[...].astype(F32), (8, tokens)).T[:, 0:1]
    error = result - teacher_ref[...].astype(F32)
    masked = mask * error
    count = jnp.sum(total_ref[0:1, 0:1], axis=1, keepdims=True)
    grad_result = out_grad_ref[...].astype(F32) + (2.0 / (count * width)) * masked
    branch = grad_result.astype(BF16)
    vec_ref[...] = jnp.zeros_like(vec_ref)
    vec_ref[7 + parts : 8 + parts] = jnp.broadcast_to(
        jnp.sum(jnp.sum(masked * error, axis=1, keepdims=True), axis=0, keepdims=True), (1, width)
    )
    vec_ref[6:7] = jnp.sum(branch.astype(F32), axis=0, keepdims=True)
    rows_up = wd.shape[0] // shards
    rows_out = width // shards
    used = 2 * rows_up + rows_out
    if used < rows_f:
        gf_ref[:, used:] = jnp.zeros((shards, rows_f - used, width), BF16)
    grad_normed = jnp.zeros((tokens, width), F32)
    for c in range(parts):
        cols = slice(c * width, (c + 1) * width)
        grad_pre = (dot_nt(branch, wd[cols]) * slope[:, cols]).astype(BF16)
        vec_ref[7 + c : 8 + c] = jnp.sum(grad_pre.astype(F32), axis=0, keepdims=True)
        grad_normed = grad_normed + dot_nt(grad_pre, wu[:, cols])
        up = dot_tn(normed, grad_pre).astype(BF16)
        down = dot_tn(act[:, cols], branch).astype(BF16)
        for s in range(shards):
            gf_ref[s, c * rows_out : (c + 1) * rows_out] = up[s * rows_out : (s + 1) * rows_out]
        step = min(rows_up, width)
        for begin in range(0, width, step):
            row = c * width + begin
            place = rows_up + row % rows_up
            gf_ref[row // rows_up, place : place + step] = down[begin : begin + step]
    pl.semaphore_wait(barrier, 1)
    early = max(0, 2 * rows_up - half)
    if early:
        give(0, early, 0).start()
    vec_ref[4:5] = jnp.sum(grad_normed * unit, axis=0, keepdims=True)
    vec_ref[5:6] = jnp.sum(grad_normed, axis=0, keepdims=True)
    scaled = grad_normed * gain
    grad_hidden = grad_result + inverse * (
        scaled - jnp.mean(scaled, axis=1, keepdims=True) - unit * jnp.mean(scaled * unit, axis=1, keepdims=True)
    )
    hidden_ref[...] = grad_hidden
    attn = grad_hidden.astype(BF16)
    gm_ref[...] = dot_nt(attn, wo[...]).astype(BF16)
    outer = dot_tn(mixed, attn).astype(BF16)
    for s in range(shards):
        gf_ref[s, 2 * rows_up : used] = outer[s * rows_out : (s + 1) * rows_out]
    give(early, half - early, 1).start()
    if early:
        give(0, early, 0).wait()
    give(early, half - early, 1).wait()
    for ref, place in ((theirs_ref, 1 - b), (mine_ref, b)):
        own = gf_ref[:, aligned(core * half + place * quarter, quarter)].astype(F32)
        ref[...] = (own + landed[:, aligned(place * quarter, quarter)].astype(F32)).astype(BF16)


def middle(shards, rows_f, cid, mask, x, mixed, teacher, out_grad, vectors, total, own, gathered):
    tokens, width = x.shape
    hidden = own[1].shape[1]
    vmem = pl.BlockSpec(memory_space=pltpu.VMEM)
    hbm = pl.BlockSpec(memory_space=pl.ANY)
    return pl.pallas_call(
        functools.partial(middle_kernel, shards, rows_f),
        out_shape=(
            jax.ShapeDtypeStruct((tokens, width), BF16),
            jax.ShapeDtypeStruct((tokens, width), F32),
            jax.ShapeDtypeStruct((tokens, width), BF16),
            jax.ShapeDtypeStruct((shards, rows_f // 4, width), BF16),
            jax.ShapeDtypeStruct((shards, rows_f // 4, width), BF16),
            jax.ShapeDtypeStruct((16, width), F32),
        ),
        in_specs=[vmem] * 7 + [hbm] * 6,
        out_specs=(vmem,) * 6,
        scratch_shapes=[
            pltpu.VMEM((width, width), BF16),
            pltpu.VMEM((width, hidden), BF16),
            pltpu.VMEM((hidden, width), BF16),
            pltpu.VMEM((tokens, hidden), F32),
            pltpu.VMEM((tokens, hidden), BF16),
            pltpu.VMEM((shards, rows_f, width), BF16),
            pltpu.VMEM((shards, rows_f // 2, width), BF16),
            pltpu.SemaphoreType.DMA((3, shards)),
            pltpu.SemaphoreType.DMA((2,)),
            pltpu.SemaphoreType.DMA((2,)),
        ],
        compiler_params=pltpu.CompilerParams(collective_id=cid, has_side_effects=True, vmem_limit_bytes=56 * 2**20),
        cost_estimate=pl.CostEstimate(flops=4 * 10**9, bytes_accessed=20 * 2**20, transcendentals=10**6),
        name="middle",
    )(mask, x, mixed, teacher, out_grad, vectors, total, *own, *gathered)


def body(
    inputs, block_perm, seq_lengths, loss_mask, teacher, out_grad, gain_one, bias_one, w_query, w_key, w_value,
    w_output, w_pos, content_bias, position_bias, gain_two, bias_two, w_up, bias_up, w_down, bias_down,
):
    width = inputs.shape[2]
    shards = lax.axis_size("wsh")
    members = lax.axis_size("ctx")
    lines = members // 4
    hidden = bias_up.shape[0] * shards
    blocks = block_perm.shape[1]
    limit = blocks // 2 + 1
    rows_up, rows_out = hidden // shards, width // shards

    frequency = np.exp(np.arange(width // 2) * (-2.0 * math.log(10000.0) / width))
    far_angle = (np.arange(-(-limit // 8) * 8) * BLK + (BLK - 1))[:, None] * frequency[None]
    near_angle = np.arange(BLK)[:, None] * frequency[None]
    far = jnp.asarray(np.stack([np.sin(far_angle), np.cos(far_angle)]), F32)
    near = jnp.asarray(np.stack([np.sin(near_angle), np.cos(near_angle)]), F32)

    keys, values, unit_all, pos_keys, table, qc, qp, weights, wo, wu, wd, vectors, total = start(
        lines, shards, 0, limit, inputs[0], (w_key, w_value, w_pos, w_query, w_output, w_up, w_down),
        (gain_one, bias_one, content_bias, position_bias, gain_two, bias_two, bias_down, bias_up), loss_mask, far, near,
    )
    mixed, linv, probs = attn_fwd(block_perm, seq_lengths, qc, qp, keys, values, pos_keys, blocks, limit)

    step = 16 * lines
    pieces = -(-(2 * rows_up + rows_out) // (4 * step))
    split = min(2, pieces)
    chunks_f = tuple((pieces * (i + 1) // split - pieces * i // split) * step for i in range(split))
    rows_f = 4 * step * pieces
    if rows_out % (32 * lines):
        sets, rows_l = (("q", "p"), ("k", "v")), -(-2 * rows_out // (32 * lines)) * 32 * lines
    else:
        sets, rows_l = (("q",), ("p",), ("k",), ("v",)), rows_out
    output, grad_hidden, grad_mixed, mine, theirs, vec = middle(
        shards, rows_f, 2, loss_mask, inputs[0], mixed, teacher[0], out_grad[0], vectors, total,
        (w_output, w_up, w_down), (wo, wu, wd),
    )
    come = lax.ppermute(theirs, "ctx", [(i, i ^ 2) for i in range(members)])
    grad_query, bias_grads, dk_t, dv_t, dpk_t = attn_bwd(
        block_perm, seq_lengths, qc, qp, keys, values, pos_keys, probs, linv, grad_mixed, mixed, blocks, limit
    )
    grad_input, sums, vsum = finish(
        lines, shards, chunks_f, sets, rows_l, 1, mine, come, dk_t, dv_t, unit_all, dpk_t, table, weights, grad_query,
        inputs[0], vectors, total, vec, bias_grads, grad_hidden,
    )
    (
        grad_input, output, g_query, g_key, g_value, g_output, g_pos, g_up, g_down,
        v_g1, v_b1, v_cb, v_pb, v_g2, v_b2, v_bd, v_bu, loss,
    ) = unpack(shards, rows_f, sets, rows_l, hidden, sums, vsum, total, grad_input, output)
    return (
        output[None], loss.reshape(()), grad_input[None], v_g1, v_b1, g_query, g_key, g_value, g_output, g_pos,
        v_cb, v_pb, v_g2, v_b2, g_up, v_bu, g_down, v_bd,
    )


def solution(mesh):
    rows = P("wsh", "ctx", None)
    vector = P("wsh")
    matrix = P("wsh", None)
    placed = (
        rows, matrix, matrix, P("wsh", "ctx"), rows, rows, vector, vector, matrix, matrix, matrix, matrix, matrix,
        vector, vector, vector, vector, matrix, vector, matrix, vector,
    )
    out = (
        rows, P(), rows, vector, vector, matrix, matrix, matrix, matrix, matrix, vector, vector, vector, vector,
        matrix, vector, matrix, vector,
    )
    return jax.shard_map(body, mesh=mesh, in_specs=placed, out_specs=out, check_vma=False)
```

```python
import functools
import math

import jax
import jax.numpy as jnp
import numpy as np
from jax import lax
from jax.experimental import pallas as pl
from jax.experimental.pallas import tpu as pltpu
from jax.sharding import PartitionSpec as P

HEADS = 8
HEAD = 64
PAIRS = HEADS // 2
BLK = 128
ROWS = HEADS * BLK
NEG = -1e30
epsilon = 1e-05
F32 = jnp.float32
BF16 = jnp.bfloat16


def dot_nt(a, b):
    return lax.dot_general(a, b, (((1,), (1,)), ((), ())), preferred_element_type=F32)


def dot_nn(a, b):
    return lax.dot_general(a, b, (((1,), (0,)), ((), ())), preferred_element_type=F32)


def dot_tn(a, b):
    return lax.dot_general(a, b, (((0,), (0,)), ((), ())), preferred_element_type=F32)


def iotas():
    row = lax.broadcasted_iota(jnp.int32, (BLK, BLK), 0)
    col = lax.broadcasted_iota(jnp.int32, (BLK, BLK), 1)
    return row, col


def read_places(perm_ref, lengths_ref, meta, blocks, count):
    device = lax.axis_index("ctx")
    meta[0] = perm_ref[0, 2 * device]
    meta[1] = perm_ref[0, 2 * device + 1]

    def place(slot, _):
        meta[2 + perm_ref[0, slot]] = slot
        return 0

    lax.fori_loop(0, blocks, place, 0)
    end = jnp.int32(0)
    for e in range(count):
        end = end + lengths_ref[0, e]
        meta[2 + blocks + e] = end


def block_range(meta, a, blocks, limit):
    qb = meta[a]
    first = qb * BLK
    low = jnp.int32(0)
    for e in range(meta.shape[0] - 2 - blocks):
        end = meta[2 + blocks + e]
        low = jnp.where(first >= end, jnp.maximum(low, end), low)
    lowest = low // BLK
    return qb, lowest, jnp.minimum(qb - lowest + 1, limit)


def stack_heads(pair):
    lane = lax.broadcasted_iota(jnp.int32, pair.shape, 1)
    zero = jnp.zeros_like(pair)
    return jnp.concatenate([jnp.where(lane < HEAD, pair, zero), jnp.where(lane >= HEAD, pair, zero)], axis=0)


def flip_rows(x):
    index = 7 - lax.broadcasted_iota(jnp.int32, (8, BLK), 0)
    slabs = [jnp.take_along_axis(x[8 * g : 8 * g + 8], index, axis=0) for g in reversed(range(BLK // 8))]
    return jnp.concatenate(slabs, axis=0)


def flip_two(x):
    return jnp.concatenate([flip_rows(x[:BLK]), flip_rows(x[BLK:])], axis=0)


def needed_blocks(meta, blocks, limit):
    ranges = []
    for a in range(2):
        qb, lowest, count = block_range(meta, a, blocks, limit)
        ranges.append((qb + 1 - 2 * ((count + 1) // 2), qb))
    return ranges


def load_keys(meta, blocks, limit, pairs, sem):
    (low0, high0), (low1, high1) = needed_blocks(meta, blocks, limit)
    for hbm, ref in pairs:
        ref[0:BLK] = jnp.zeros((BLK, ref.shape[1]), ref.dtype)

    def copies(kb):
        slot = pl.ds(pl.multiple_of(meta[2 + kb] * BLK, BLK), BLK)
        place = pl.ds(pl.multiple_of((kb + 1) * BLK, BLK), BLK)
        return [
            pltpu.make_async_copy(hbm.at[slot], ref.at[place], sem.at[index, kb]) for index, (hbm, ref) in enumerate(pairs)
        ]

    def begin(kb, _):
        @pl.when(((kb >= low0) & (kb <= high0)) | ((kb >= low1) & (kb <= high1)))
        def _():
            for copy in copies(kb):
                copy.start()

        return 0

    lax.fori_loop(0, blocks, begin, 0)

    def arrive(a):
        low, high = (jnp.where(a == 0, x, y) for x, y in ((low0, low1), (high0, high1)))

        def one(kb, _):
            @pl.when((a == 0) | (kb < low0) | (kb > high0))
            def _():
                for copy in copies(kb):
                    copy.wait()

            return 0

        lax.fori_loop(jnp.maximum(low, 0), high + 1, one, 0)

    return arrive


def wide_iotas():
    row = lax.broadcasted_iota(jnp.int32, (BLK, 2 * BLK), 0)
    col = lax.broadcasted_iota(jnp.int32, (BLK, 2 * BLK), 1)
    return row, col


def attn_fwd_kernel(
    blocks, limit, perm_ref, lengths_ref, qc_ref, qp_ref, k_in, v_in, pk_in, mixed_ref, linv_ref, p_ref,
    meta, k_ref, v_ref, pk_ref, q2c, q2p, prev, top, total, acc, s_scr, p_buf, kv_sem, pk_sem, p_sem,
):
    read_places(perm_ref, lengths_ref, meta, blocks, lengths_ref.shape[1])
    span = pk_in.shape[0]
    pk_copy = pltpu.make_async_copy(pk_in, pk_ref.at[0:span], pk_sem)
    pk_copy.start()
    arrive = load_keys(meta, blocks, limit, ((k_in, k_ref), (v_in, v_ref)), kv_sem)
    pk_ref[span:] = jnp.zeros((BLK, pk_ref.shape[1]), BF16)
    row, col = iotas()
    tri = col <= row
    wide_row, wide_col = wide_iotas()
    tiles = s_scr.shape[0]

    def p_copy(slot, index):
        return pltpu.make_async_copy(p_buf.at[slot], p_ref.at[index], p_sem.at[slot])

    def one_query_block(a, _):
        qb, lowest, count = block_range(meta, a, blocks, limit)
        pairs = (count + 1) // 2
        rows_a = pl.ds(pl.multiple_of(a * BLK, BLK), BLK)
        pos = qb * BLK + wide_row
        start = jnp.zeros((BLK, 2 * BLK), jnp.int32)
        for e in range(meta.shape[0] - 2 - blocks):
            end = meta[2 + blocks + e]
            start = jnp.where(pos >= end, jnp.maximum(start, end), start)
        for hp in range(PAIRS):
            lanes = slice(hp * BLK, (hp + 1) * BLK)
            q2c[hp] = stack_heads(qc_ref[rows_a, lanes].astype(F32)).astype(BF16)
            q2p[hp] = stack_heads(qp_ref[rows_a, lanes].astype(F32)).astype(BF16)
        prev[...] = jnp.zeros_like(prev)
        top[...] = jnp.full_like(top, NEG)
        total[...] = jnp.zeros_like(total)
        acc[...] = jnp.zeros_like(acc)
        arrive(a)

        @pl.when(a == 0)
        def _():
            pk_copy.wait()

        def score_step(t, _):
            kb = qb - 2 * t
            keys = pl.ds(pl.multiple_of(kb * BLK, BLK), 2 * BLK)
            place = (kb - 1) * BLK + wide_col
            bias = jnp.where((place >= start) & (place <= pos), 0.0, NEG).astype(F32)
            drows = pl.ds(pl.multiple_of(2 * t * BLK, BLK), 2 * BLK)
            for hp in range(PAIRS):
                lanes = slice(hp * BLK, (hp + 1) * BLK)
                s = dot_nt(q2c[hp], k_ref[keys, lanes])
                r = dot_nt(q2p[hp], pk_ref[drows, lanes])
                for half in range(2):
                    part = slice(half * BLK, (half + 1) * BLK)
                    rows = slice((2 * hp + half) * BLK, (2 * hp + half + 1) * BLK)
                    near = pltpu.roll(r[part, :BLK], 1, 1, stride=1, stride_axis=0)
                    far = pltpu.roll(r[part, BLK:], 1, 1, stride=1, stride_axis=0)
                    late = s[part, BLK:] + jnp.where(tri, near, prev[rows]) + bias[:, BLK:]
                    early = s[part, :BLK] + jnp.where(tri, far, near) + bias[:, :BLK]
                    prev[rows] = far
                    s_scr[t, rows, :BLK] = early
                    s_scr[t, rows, BLK:] = late
                    top[rows] = jnp.maximum(top[rows], jnp.maximum(early, late))
            return 0

        lax.fori_loop(0, pairs, score_step, 0)
        for h in range(HEADS):
            rows = slice(h * BLK, (h + 1) * BLK)
            top[rows] = jnp.broadcast_to(jnp.max(top[rows], axis=1, keepdims=True), (BLK, BLK))

        def mix_step(t, _):
            kb = qb - 2 * t
            keys = pl.ds(pl.multiple_of(kb * BLK, BLK), 2 * BLK)
            slot = lax.rem(t, 2)

            @pl.when(t >= 2)
            def _():
                p_copy(slot, 0).wait()

            for hp in range(PAIRS):
                lanes = slice(hp * BLK, (hp + 1) * BLK)
                rows = slice(2 * hp * BLK, 2 * (hp + 1) * BLK)
                early = jnp.exp(s_scr[t, rows, :BLK] - top[rows])
                late = jnp.exp(s_scr[t, rows, BLK:] - top[rows])
                total[rows] += early + late
                p_buf[slot, rows, :BLK] = flip_two(early).astype(BF16)
                p_buf[slot, rows, BLK:] = flip_two(late).astype(BF16)
                low = jnp.concatenate([early.astype(BF16), late.astype(BF16)], axis=1)
                acc[hp] += dot_nn(low, v_ref[keys, lanes])
            p_copy(slot, a * tiles + t).start()
            return 0

        lax.fori_loop(0, pairs, mix_step, 0)
        p_copy(lax.rem(pairs - 1, 2), 0).wait()

        @pl.when(pairs >= 2)
        def _():
            p_copy(lax.rem(pairs, 2), 0).wait()

        lane = lax.broadcasted_iota(jnp.int32, (BLK, BLK), 1)
        for hp in range(PAIRS):
            lanes = slice(hp * BLK, (hp + 1) * BLK)
            parts = []
            for half in range(2):
                h = 2 * hp + half
                rows = slice(h * BLK, (h + 1) * BLK)
                inv = 1.0 / jnp.sum(total[rows], axis=1, keepdims=True)
                inv = jnp.broadcast_to(inv, (BLK, BLK))
                linv_ref[a, rows] = inv
                parts.append(acc[hp, half * BLK : (half + 1) * BLK] * inv)
            mixed_ref[rows_a, lanes] = jnp.where(lane < HEAD, parts[0], parts[1])
        return 0

    lax.fori_loop(0, 2, one_query_block, 0)


def attn_fwd(perm, lengths, qc, qp, k, v, pk, blocks, limit):
    tokens, width = qc.shape
    keys, span = k.shape[0], pk.shape[0]
    tiles = (limit + 1) // 2
    vmem = pl.BlockSpec(memory_space=pltpu.VMEM)
    hbm = pl.BlockSpec(memory_space=pl.ANY)
    return pl.pallas_call(
        functools.partial(attn_fwd_kernel, blocks, limit),
        out_shape=(
            jax.ShapeDtypeStruct((tokens, width), F32),
            jax.ShapeDtypeStruct((2, ROWS, BLK), F32),
            jax.ShapeDtypeStruct((2 * tiles, ROWS, 2 * BLK), BF16),
        ),
        in_specs=[pl.BlockSpec(memory_space=pltpu.SMEM)] * 2 + [vmem] * 2 + [hbm] * 3,
        out_specs=(vmem, vmem, hbm),
        scratch_shapes=[
            pltpu.SMEM((2 + blocks + lengths.shape[1],), jnp.int32),
            pltpu.VMEM((keys + BLK, width), BF16),
            pltpu.VMEM((keys + BLK, width), BF16),
            pltpu.VMEM((span + BLK, width), BF16),
            pltpu.VMEM((PAIRS, 2 * BLK, BLK), BF16),
            pltpu.VMEM((PAIRS, 2 * BLK, BLK), BF16),
            pltpu.VMEM((ROWS, BLK), F32),
            pltpu.VMEM((ROWS, BLK), F32),
            pltpu.VMEM((ROWS, BLK), F32),
            pltpu.VMEM((PAIRS, 2 * BLK, BLK), F32),
            pltpu.VMEM((tiles, ROWS, 2 * BLK), F32),
            pltpu.VMEM((2, ROWS, 2 * BLK), BF16),
            pltpu.SemaphoreType.DMA((2, blocks)),
            pltpu.SemaphoreType.DMA,
            pltpu.SemaphoreType.DMA((2,)),
        ],
        compiler_params=pltpu.CompilerParams(vmem_limit_bytes=60 * 2**20),
        cost_estimate=pl.CostEstimate(flops=3 * 10**9, bytes_accessed=20 * 2**20, transcendentals=4 * 10**6),
        name="attn_fwd",
    )(perm, lengths, qc, qp, k, v, pk)


def attn_bwd_kernel(
    blocks, limit, perm_ref, lengths_ref, qc_ref, qp_ref, k_in, v_in, pk_in, p_ref, linv_ref, gm_ref, mixed_ref,
    dq_ref, bias_ref, dk_out, dv_out, dpk_ref,
    meta, k_ref, v_ref, pk_ref, dk_ref, dv_ref, q2c_t, q2p_t, gm2, gm2_t, dd, carry, dqk, dqp, dpk, p_buf,
    empty, kv_sem, pk_sem, p_sem, out_sem,
):
    read_places(perm_ref, lengths_ref, meta, blocks, lengths_ref.shape[1])
    span = pk_in.shape[0]
    pk_copy = pltpu.make_async_copy(pk_in, pk_ref.at[0:span], pk_sem)
    pk_copy.start()
    arrive = load_keys(meta, blocks, limit, ((k_in, k_ref), (v_in, v_ref)), kv_sem)
    pk_ref[span:] = jnp.zeros((BLK, pk_ref.shape[1]), BF16)
    row, col = iotas()
    tri = col <= BLK - 1 - row
    tiles = p_ref.shape[0] // 2
    (low0, high0), (low1, high1) = needed_blocks(meta, blocks, limit)

    def out_copies(kb, nothing=False):
        slot = pl.ds(pl.multiple_of(meta[2 + kb] * BLK, BLK), BLK)
        place = pl.ds(pl.multiple_of((kb + 1) * BLK, BLK), BLK)
        return [
            pltpu.make_async_copy(empty if nothing else ref.at[:, place], out.at[:, slot], out_sem.at[index, kb])
            for index, (ref, out) in enumerate(((dk_ref, dk_out), (dv_ref, dv_out)))
        ]

    empty[...] = jnp.zeros_like(empty)
    for ref in (dk_ref, dv_ref):
        ref[:, 0:BLK] = jnp.zeros((ref.shape[0], BLK), BF16)

    def prepare(kb, _):
        used = ((kb >= low0) & (kb <= high0)) | ((kb >= low1) & (kb <= high1))

        @pl.when(used)
        def _():
            place = pl.ds(pl.multiple_of((kb + 1) * BLK, BLK), BLK)
            for ref in (dk_ref, dv_ref):
                ref[:, place] = jnp.zeros((ref.shape[0], BLK), BF16)

        @pl.when(jnp.logical_not(used))
        def _():
            for copy in out_copies(kb, True):
                copy.start()

        return 0

    lax.fori_loop(0, blocks, prepare, 0)
    dpk[...] = jnp.zeros_like(dpk)
    bias_ref[...] = jnp.zeros_like(bias_ref)

    def p_copy(slot, index):
        return pltpu.make_async_copy(p_ref.at[index], p_buf.at[slot], p_sem.at[slot])

    def one_query_block(a, _):
        qb, lowest, count = block_range(meta, a, blocks, limit)
        pairs = (count + 1) // 2
        rows_a = pl.ds(pl.multiple_of(a * BLK, BLK), BLK)
        p_copy(0, a * tiles + pairs - 1).start()
        for hp in range(PAIRS):
            lanes = slice(hp * BLK, (hp + 1) * BLK)
            rows = slice(2 * hp * BLK, 2 * (hp + 1) * BLK)
            q2c_t[hp] = stack_heads(flip_rows(qc_ref[rows_a, lanes].astype(F32))).T.astype(BF16)
            q2p_t[hp] = stack_heads(flip_rows(qp_ref[rows_a, lanes].astype(F32))).T.astype(BF16)
            g = stack_heads(gm_ref[rows_a, lanes].astype(F32))
            scaled = flip_two(g * linv_ref[a, rows])
            gm2[hp] = scaled.astype(BF16)
            gm2_t[hp] = scaled.T.astype(BF16)
            pair = flip_rows(mixed_ref[rows_a, lanes])
            dd[rows] = jnp.broadcast_to(
                jnp.sum(scaled * jnp.concatenate([pair, pair], axis=0), axis=1, keepdims=True), (2 * BLK, BLK)
            )
        carry[...] = jnp.zeros_like(carry)
        dqk[...] = jnp.zeros_like(dqk)
        dqp[...] = jnp.zeros_like(dqp)
        arrive(a)

        @pl.when(a == 0)
        def _():
            pk_copy.wait()

        def step(t, _):
            tile = pairs - 1 - t
            kb = qb - 2 * tile
            keys = pl.ds(pl.multiple_of(kb * BLK, BLK), 2 * BLK)
            drows = pl.ds(pl.multiple_of(2 * tile * BLK, BLK), 2 * BLK)
            slot = lax.rem(t, 2)
            p_copy(slot, 0).wait()

            @pl.when(tile >= 1)
            def _():
                p_copy(1 - slot, a * tiles + tile - 1).start()

            for hp in range(PAIRS):
                lanes = slice(hp * BLK, (hp + 1) * BLK)
                rows = slice(2 * hp * BLK, 2 * (hp + 1) * BLK)
                p = p_buf[slot, rows]
                g = dot_nt(gm2[hp], v_ref[keys, lanes])
                early = (p[:, :BLK].astype(F32) * (g[:, :BLK] - dd[rows])).astype(BF16)
                late = (p[:, BLK:].astype(F32) * (g[:, BLK:] - dd[rows])).astype(BF16)
                gs = jnp.concatenate([early, late], axis=1)
                early, late = early.astype(F32), late.astype(F32)
                rots = []
                for half in range(2):
                    part = slice(half * BLK, (half + 1) * BLK)
                    crow = slice((2 * hp + half) * BLK, (2 * hp + half + 1) * BLK)
                    far = jnp.where(tri, early[part], carry[crow])
                    near = jnp.where(tri, late[part], early[part])
                    carry[crow] = late[part]
                    rots.append(
                        jnp.concatenate(
                            [
                                pltpu.roll(near, 0, 1, stride=1, stride_axis=0).astype(BF16),
                                pltpu.roll(far, 0, 1, stride=1, stride_axis=0).astype(BF16),
                            ],
                            axis=1,
                        )
                    )
                rot = jnp.concatenate(rots, axis=0)
                dqk[hp] += dot_nn(gs, k_ref[keys, lanes])
                dqp[hp] += dot_nn(rot, pk_ref[drows, lanes])
                dk_ref[lanes, keys] = (dk_ref[lanes, keys].astype(F32) + dot_nn(q2c_t[hp], gs)).astype(BF16)
                dv_ref[lanes, keys] = (dv_ref[lanes, keys].astype(F32) + dot_nn(gm2_t[hp], p)).astype(BF16)
                dpk[lanes, drows] += dot_nn(q2p_t[hp], rot)
            for block in (kb - 1, kb):

                @pl.when((block >= 0) & ((a == 1) | (block < low1) | (block > high1)))
                def _():
                    for copy in out_copies(jnp.maximum(block, 0)):
                        copy.start()

            return 0

        lax.fori_loop(0, pairs, step, 0)
        lane = lax.broadcasted_iota(jnp.int32, (BLK, BLK), 1)
        for hp in range(PAIRS):
            lanes = slice(hp * BLK, (hp + 1) * BLK)
            ck = jnp.where(lane < HEAD, dqk[hp, :BLK], dqk[hp, BLK:]) * 0.125
            cp = jnp.where(lane < HEAD, dqp[hp, :BLK], dqp[hp, BLK:]) * 0.125
            dq_ref[rows_a, lanes] = flip_rows(ck + cp).astype(BF16)
            bias_ref[0:1, lanes] += jnp.sum(ck, axis=0, keepdims=True)
            bias_ref[1:2, lanes] += jnp.sum(cp, axis=0, keepdims=True)
        return 0

    lax.fori_loop(0, 2, one_query_block, 0)

    def given(kb, _):
        for copy in out_copies(kb):
            copy.wait()
        return 0

    dpk_ref[...] = dpk[:, 0:span].astype(BF16)
    lax.fori_loop(0, blocks, given, 0)


def attn_bwd(perm, lengths, qc, qp, k, v, pk, p, linv, gm, mixed, blocks, limit):
    tokens, width = qc.shape
    keys, span = k.shape[0], pk.shape[0]
    vmem = pl.BlockSpec(memory_space=pltpu.VMEM)
    hbm = pl.BlockSpec(memory_space=pl.ANY)
    return pl.pallas_call(
        functools.partial(attn_bwd_kernel, blocks, limit),
        out_shape=(
            jax.ShapeDtypeStruct((tokens, width), BF16),
            jax.ShapeDtypeStruct((8, width), F32),
            jax.ShapeDtypeStruct((width, keys), BF16),
            jax.ShapeDtypeStruct((width, keys), BF16),
            jax.ShapeDtypeStruct((width, span), BF16),
        ),
        in_specs=[pl.BlockSpec(memory_space=pltpu.SMEM)] * 2 + [vmem] * 2 + [hbm] * 4 + [vmem] * 3,
        out_specs=(vmem, vmem, hbm, hbm, vmem),
        scratch_shapes=[
            pltpu.SMEM((2 + blocks + lengths.shape[1],), jnp.int32),
            pltpu.VMEM((keys + BLK, width), BF16),
            pltpu.VMEM((keys + BLK, width), BF16),
            pltpu.VMEM((span + BLK, width), BF16),
            pltpu.VMEM((width, keys + BLK), BF16),
            pltpu.VMEM((width, keys + BLK), BF16),
            pltpu.VMEM((PAIRS, BLK, 2 * BLK), BF16),
            pltpu.VMEM((PAIRS, BLK, 2 * BLK), BF16),
            pltpu.VMEM((PAIRS, 2 * BLK, BLK), BF16),
            pltpu.VMEM((PAIRS, BLK, 2 * BLK), BF16),
            pltpu.VMEM((ROWS, BLK), F32),
            pltpu.VMEM((ROWS, BLK), F32),
            pltpu.VMEM((PAIRS, 2 * BLK, BLK), F32),
            pltpu.VMEM((PAIRS, 2 * BLK, BLK), F32),
            pltpu.VMEM((width, span + BLK), F32),
            pltpu.VMEM((2, ROWS, 2 * BLK), BF16),
            pltpu.VMEM((width, BLK), BF16),
            pltpu.SemaphoreType.DMA((2, blocks)),
            pltpu.SemaphoreType.DMA,
            pltpu.SemaphoreType.DMA((2,)),
            pltpu.SemaphoreType.DMA((2, blocks)),
        ],
        compiler_params=pltpu.CompilerParams(vmem_limit_bytes=62 * 2**20),
        cost_estimate=pl.CostEstimate(flops=6 * 10**9, bytes_accessed=30 * 2**20, transcendentals=0),
        name="attn_bwd",
    )(perm, lengths, qc, qp, k, v, pk, p, linv, gm, mixed)


MESH = pl.DeviceIdType.MESH


def fold_rows(x):
    return jnp.broadcast_to(x, (x.shape[0], BLK)).T[0:1]


def aligned(begin, size):
    return pl.ds(pl.multiple_of(begin, math.gcd(size, 16)), size)


def finish_kernel(
    lines, shards, chunks_f, sets, rows_l,
    mine_ref, come_ref, dk_ref, dv_ref, unit_all_ref, dpk_ref, table_ref, weights_in, dq_ref, x_ref,
    vectors_ref, total_ref, vec_ref, bias_ref, hidden_in,
    grad_ref, sums_ref, vsum_ref,
    dk_buf, dv_buf, un_buf, in_sem, dpk_buf, table_buf, weights_ref, hidden_ref, pos_sem, m_q, mt_k, mt_v, cs_q, cs_k, cs_v, dxp, bx0, bx1, bx2, vbuf, vacc,
    *rest,
):
    wk_ref, wv_ref, wq_ref = weights_ref.at[0], weights_ref.at[1], weights_ref.at[3]
    tokens, width = dq_ref.shape
    bufs_f = rest[: 3 * len(chunks_f)]
    bufs_l = rest[3 * len(chunks_f) : -2]
    send_sem, recv_sem = rest[-2:]
    ctx = lax.axis_index("ctx")
    w = lax.axis_index("wsh")
    core = lax.rem(ctx, 2)
    b = lax.rem(ctx // 2, 2)
    a = ctx // 4

    def at(a_to, b_to, core_to):
        return (a_to * 2 + b_to) * 2 + core_to

    def line_peer(s):
        return (at(lax.rem(a + s, lines), b, core), w)

    def shard_peer(s):
        return (ctx, lax.rem(w + s, shards))

    core_peer = (at(a, b, 1 - core), w)
    b_peer = (at(a, 1 - b, core), w)
    peers = [core_peer, b_peer] + [line_peer(s) for s in range(1, lines)] + [shard_peer(s) for s in range(1, shards)]
    barrier = pltpu.get_barrier_semaphore()
    for peer in peers:
        pl.semaphore_signal(barrier, inc=1, device_id=peer, device_id_type=MESH)

    counter = [0]

    def take(number):
        begin = counter[0]
        counter[0] += number
        return begin

    def remote(src, dst, index, peer):
        return pltpu.make_async_remote_copy(
            src_ref=src, dst_ref=dst, send_sem=send_sem.at[index], recv_sem=recv_sem.at[index],
            device_id=peer, device_id_type=MESH,
        )

    bits = lines.bit_length() - 1
    order = []
    for bit in range(bits):
        order += [m for m in reversed(range(lines)) if m & ((1 << (bit + 1)) - 1) == 1 << bit]
    order.append(0)

    def other(mask):
        place = 0
        for bit in range(bits):
            own = lax.rem(a // (1 << bit), 2)
            place = place + (1 << bit) * ((1 - own) if mask >> bit & 1 else own)
        return place

    def line_place(j):
        place = jnp.int32(0)
        for index, mask in enumerate(order):
            place = place + jnp.where(j == index, other(mask), 0)
        return place

    def line_at(mask):
        return (at(other(mask), b, core), w)

    group = 4 * tokens

    def fetch(j, slot):
        begin = pl.multiple_of(line_place(j) * group, group)
        return (
            pltpu.make_async_copy(dk_ref.at[:, pl.ds(begin, group)], dk_buf.at[slot], in_sem.at[slot, 0]),
            pltpu.make_async_copy(dv_ref.at[:, pl.ds(begin, group)], dv_buf.at[slot], in_sem.at[slot, 1]),
            pltpu.make_async_copy(unit_all_ref.at[pl.ds(begin, group)], un_buf.at[slot], in_sem.at[slot, 2]),
        )

    span, hold = table_ref.shape[0], table_buf.shape[0]
    pos_parts = [(begin, min(hold, span - begin)) for begin in range(0, span, hold)]

    def pos_copies(begin, size):
        rows = pl.ds(begin, size)
        return [
            pltpu.make_async_copy(dpk_ref.at[:, rows], dpk_buf.at[:, 0:size], pos_sem.at[0]),
            pltpu.make_async_copy(table_ref.at[rows], table_buf.at[0:size], pos_sem.at[1]),
        ]

    weights_copy = pltpu.make_async_copy(weights_in, weights_ref, pos_sem.at[2])
    hidden_copy = pltpu.make_async_copy(hidden_in, hidden_ref, pos_sem.at[3])
    weights_copy.start()
    for copy in fetch(0, 0):
        copy.start()
    for copy in pos_copies(*pos_parts[0]):
        copy.start()
    hidden_copy.start()

    def start_all(copies):
        for copy in copies:
            copy.start()

    def wait_all(copies):
        for copy in copies:
            copy.wait()

    def own_bit(bit):
        return lax.rem(a // (1 << bit), 2)

    def bit_peer(bit):
        return line_at(1 << bit)

    class Feed:
        def __init__(self, begin, rows, total_rows, bufs):
            self.begin, self.rows = begin, rows
            self.rc, self.rb = total_rows // 2, total_rows // 4
            self.b0, self.b1, self.b2 = bufs
            self.iy, self.irs, self.iag, self.ix, self.ic = take(shards - 1), take(bits), take(bits), take(1), take(2)

        def region(self, bit):
            start = 0
            for k in range(bit):
                start = start + own_bit(k) * (self.rows >> (k + 1))
            return start, self.rows >> bit

        def y_copies(self):
            return [
                remote(self.b0.at[lax.rem(w + s, shards)], self.b1.at[s - 1], self.iy + s - 1, shard_peer(s))
                for s in range(1, shards)
            ]

        def rs_copies(self, bit):
            start, size = self.region(bit)
            size = size // 2
            give = aligned(start + (1 - own_bit(bit)) * size, size)
            begin = sum(self.rows >> (k + 1) for k in range(bit))
            return [remote(self.b1.at[0, give], self.b2.at[begin : begin + size], self.irs + bit, bit_peer(bit))]

        def place(self, b_of, begin, size):
            return aligned(core * self.rc + b_of * self.rb + self.begin + begin, size)

        def ag_copies(self, bit):
            own = self.place(b, *self.region(bit + 1))
            return [remote(sums_ref.at[own], sums_ref.at[own], self.iag + bit, bit_peer(bit))]

        def x_copies(self):
            own = self.place(b, 0, self.rows)
            return [remote(sums_ref.at[own], sums_ref.at[own], self.ix, b_peer)]

        def c_copies(self):
            return [
                remote(sums_ref.at[rows], sums_ref.at[rows], self.ic + k, core_peer)
                for k, rows in enumerate((self.place(b, 0, self.rows), self.place(1 - b, 0, self.rows)))
            ]

        def y(self):
            rows = pl.ds(self.begin, self.rows)
            self.b0[...] = (mine_ref[:, rows].astype(F32) + come_ref[:, rows].astype(F32)).astype(BF16)
            start_all(self.y_copies())

        def rs(self, bit):
            if bit == 0:
                wait_all(self.y_copies())
                total = self.b0[w].astype(F32)
                for s in range(shards - 1):
                    total = total + self.b1[s].astype(F32)
                self.b1[0] = total.astype(BF16)
            else:
                self.add(bit - 1)
            start_all(self.rs_copies(bit))

        def add(self, bit):
            wait_all(self.rs_copies(bit))
            start, size = self.region(bit + 1)
            begin = sum(self.rows >> (k + 1) for k in range(bit))
            rows = aligned(start, size)
            self.b1[0, rows] = (self.b1[0, rows].astype(F32) + self.b2[begin : begin + size].astype(F32)).astype(BF16)

        def ag(self, bit):
            if bit == bits - 1:
                self.add(bit)
                start, size = self.region(bits)
                sums_ref[self.place(b, start, size)] = self.b1[0, aligned(start, size)]
            else:
                wait_all(self.ag_copies(bit + 1))
            start_all(self.ag_copies(bit))

        def x(self):
            wait_all(self.ag_copies(0))
            start_all(self.x_copies())

        def c(self):
            wait_all(self.x_copies())
            start_all(self.c_copies())

        def done(self):
            wait_all(self.c_copies())

    class Late:
        def __init__(self, out, rows, names, bufs):
            self.out, self.rows, self.names, self.begun = out, rows, names, set()
            self.src, self.b0, self.b1, self.b2, self.b3 = bufs
            self.rc, self.rb, self.share = rows // 2, rows // 4, rows // 4 // lines
            self.i0, self.iy, self.i2 = take(1), take(shards - 1), take(1)
            self.irs, self.iag, self.ix, self.ic = take(lines - 1), take(lines - 1), take(1), take(1)

        def c0_copies(self):
            return [remote(self.src.at[:, aligned((1 - core) * self.rc, self.rc)], self.b0, self.i0, core_peer)]

        def y_copies(self):
            return [
                remote(self.b0.at[lax.rem(w + s, shards)], self.b1.at[s - 1], self.iy + s - 1, shard_peer(s))
                for s in range(1, shards)
            ]

        def x0_copies(self):
            return [remote(self.b1.at[0, aligned((1 - b) * self.rb, self.rb)], self.b2, self.i2, b_peer)]

        def rs_copies(self):
            return [
                remote(
                    self.b2.at[aligned(lax.rem(a + s, lines) * self.share, self.share)],
                    self.b3.at[s - 1], self.irs + s - 1, line_peer(s),
                )
                for s in range(1, lines)
            ]

        def ag_copies(self):
            own = aligned(self.out + core * self.rc + b * self.rb + a * self.share, self.share)
            return [remote(sums_ref.at[own], sums_ref.at[own], self.iag + s - 1, line_peer(s)) for s in range(1, lines)]

        def x_copies(self):
            own = aligned(self.out + core * self.rc + b * self.rb, self.rb)
            return [remote(sums_ref.at[own], sums_ref.at[own], self.ix, b_peer)]

        def c_copies(self):
            own = aligned(self.out + core * self.rc, self.rc)
            return [remote(sums_ref.at[own], sums_ref.at[own], self.ic, core_peer)]

        def c0(self):
            for m, name in enumerate(self.names):
                grad = gradient(name)
                for s in range(shards):
                    self.src[s, m * rows_out : (m + 1) * rows_out] = grad[s * rows_out : (s + 1) * rows_out].astype(BF16)
            used = len(self.names) * rows_out
            if used < rows_l:
                self.src[:, used:] = jnp.zeros((shards, rows_l - used, width), BF16)
            start_all(self.c0_copies())

        def y(self):
            wait_all(self.c0_copies())
            own = self.src[:, aligned(core * self.rc, self.rc)]
            self.b0[...] = (self.b0[...].astype(F32) + own.astype(F32)).astype(BF16)
            start_all(self.y_copies())

        def x0(self):
            wait_all(self.y_copies())
            total = self.b0[w].astype(F32)
            for s in range(shards - 1):
                total = total + self.b1[s].astype(F32)
            self.b1[0] = total.astype(BF16)
            start_all(self.x0_copies())

        def rs(self):
            wait_all(self.x0_copies())
            own = self.b1[0, aligned(b * self.rb, self.rb)]
            self.b2[...] = (self.b2[...].astype(F32) + own.astype(F32)).astype(BF16)
            start_all(self.rs_copies())

        def ag(self):
            wait_all(self.rs_copies())
            total = self.b2[aligned(a * self.share, self.share)].astype(F32)
            for s in range(lines - 1):
                total = total + self.b3[s].astype(F32)
            own = aligned(self.out + core * self.rc + b * self.rb + a * self.share, self.share)
            sums_ref[own] = total.astype(BF16)
            start_all(self.ag_copies())

        def x(self):
            wait_all(self.ag_copies())
            start_all(self.x_copies())

        def c(self):
            wait_all(self.x_copies())
            start_all(self.c_copies())

        def done(self):
            wait_all(self.c_copies())

    rows_f = 4 * sum(chunks_f)
    rows_out = width // shards
    feeds = []
    begin = 0
    for index, rows in enumerate(chunks_f):
        feeds.append(Feed(begin, rows, rows_f, bufs_f[3 * index : 3 * index + 3]))
        begin += rows
    lates = {}
    for index, names in enumerate(sets):
        late = Late(rows_f + index * rows_l, rows_l, names, bufs_l[5 * index : 5 * index + 5])
        for name in names:
            lates[name] = late

    def late_step(name, step):
        late = lates[name]
        if step not in late.begun:
            late.begun.add(step)
            getattr(late, step)()

    values = x_ref[...].astype(F32)
    center = values - jnp.mean(values, axis=1, keepdims=True)
    inverse = lax.rsqrt(jnp.mean(center * center, axis=1, keepdims=True) + epsilon)
    unit = center * inverse

    def gradient(name):
        cols = vectors_ref[0:8].T
        gain_col, bias_col = cols[:, 0:1], cols[:, 1:2]
        if name == "q":
            m_q[...] = dot_tn(unit.astype(BF16), dq_ref[...])
            cs_q[...] = jnp.broadcast_to(jnp.sum(dq_ref[...].astype(F32), axis=0, keepdims=True), cs_q.shape)
            return gain_col * m_q[...] + bias_col * cs_q[0:1]
        if name == "p":
            total = jnp.zeros((width, width), F32)
            for index, (begin, size) in enumerate(pos_parts):
                if index:
                    start_all(pos_copies(begin, size))
                wait_all(pos_copies(begin, size))
                total = total + dot_nn(dpk_buf[:, 0:size], table_buf[0:size])
            return total.T
        m, cs = (mt_k, cs_k) if name == "k" else (mt_v, cs_v)
        return gain_col * m[...] + bias_col * fold_rows(cs[:, 0:1])

    mt_k[...] = jnp.zeros_like(mt_k)
    mt_v[...] = jnp.zeros_like(mt_v)
    cs_k[...] = jnp.zeros_like(cs_k)
    cs_v[...] = jnp.zeros_like(cs_v)
    pl.semaphore_wait(barrier, len(peers))
    feeds[-1].y()
    weights_copy.wait()

    i_x0, i_x1, i_x2 = take(lines), take(lines), take(lines)

    def copy_x0(j):
        return remote(dxp.at[j, 1 - core], bx0.at[j], i_x0 + j, core_peer)

    def copy_x1(j):
        return remote(bx0.at[j, 1 - b], bx1.at[j], i_x1 + j, b_peer)

    def copy_x2(mask):
        return remote(bx1.at[order.index(mask)], bx2.at[mask - 1], i_x2 + mask, line_at(mask & -mask))

    def after_x0(j):
        copy_x0(j).wait()
        bx0[j] = (bx0[j].astype(F32) + dxp[j, core].astype(F32)).astype(BF16)
        copy_x1(j).start()

    def after_x1(j):
        mask = order[j]
        copy_x1(j).wait()
        total = bx1[j].astype(F32) + bx0[j, b].astype(F32)
        for bit in range(bits):
            if mask and 1 << bit >= (mask & -mask):
                break
            source = mask | 1 << bit
            copy_x2(source).wait()
            total = total + bx2[source - 1].astype(F32)
        if mask:
            bx1[j] = total.astype(BF16)
            copy_x2(mask).start()
        return total

    last = lines - 1
    events = {}

    def plan(j, after, work, *args):
        events.setdefault((min(j, last), after), []).append((work, args))

    one, two = feeds[0], feeds[-1]
    pair = len(feeds) > 1

    def along(feed, stage):
        begin, end = ((1, bits), (bits, bits + 1), (bits + 1, 2 * bits))[stage - 1]
        for step in range(begin, end):
            if step < bits:
                feed.rs(step)
            else:
                feed.ag(2 * bits - 1 - step)

    plan(0, "first", late_step, "q", "c0")
    plan(0, "blocks", after_x0, 0)
    plan(0, "blocks", late_step, "q", "y")
    plan(0, "blocks", late_step, "p", "c0")
    plan(1, "first", late_step, "p", "y")
    plan(1, "first", two.rs, 0)
    if pair:
        plan(1, "first", one.y)
    plan(1, "all", late_step, "q", "x0")
    if lines == 4:
        plan(1, "all", after_x1, 0)
        plan(1, "all", after_x0, 1)
    else:
        for j in range(1, last):
            plan(j + 1, "first", after_x0, j)
    plan(3, "first" if last >= 3 else "all", along, two, 1)
    plan(3, "blocks" if last >= 3 else "all", late_step, "p", "x0")
    plan(3, "blocks" if last >= 3 else "all", late_step, "q", "rs")

    def happen(j, after):
        for (when, place), works in sorted(events.items()):
            if place == after:

                @pl.when(j == when)
                def _():
                    for work, args in works:
                        work(*args)

    def line_step(j, _):
        slot = lax.rem(j, 2)

        @pl.when(j < last)
        def _():
            start_all(fetch(j + 1, 1 - slot))

        wait_all(fetch(j, slot))

        def make_block(core_of, b_of):
            keys = pl.ds(pl.multiple_of((2 * b_of + core_of) * tokens, tokens), tokens)
            part = dot_nn(wk_ref[...], dk_buf[slot, :, keys]) + dot_nn(wv_ref[...], dv_buf[slot, :, keys])
            dxp[j, core_of, b_of] = part.astype(BF16)

        make_block(1 - core, 0)
        make_block(1 - core, 1)
        copy_x0(j).start()
        happen(j, "first")
        make_block(core, 0)
        make_block(core, 1)
        happen(j, "blocks")
        mt_k[...] += dot_nn(dk_buf[slot], un_buf[slot])
        mt_v[...] += dot_nn(dv_buf[slot], un_buf[slot])
        for cs, buf in ((cs_k, dk_buf), (cs_v, dv_buf)):
            total = cs[...]
            for piece in range(group // BLK):
                total = total + buf[slot, :, piece * BLK : (piece + 1) * BLK].astype(F32)
            cs[...] = total
        happen(j, "all")
        return 0

    lax.fori_loop(0, lines, line_step, 0)
    for m, cs in ((mt_k, cs_k), (mt_v, cs_v)):
        m[...] = m[...].T
        cs[...] = jnp.broadcast_to(jnp.sum(cs[...], axis=1, keepdims=True), cs.shape)

    vstages = [[core_peer], [b_peer], [line_peer(s) for s in range(1, lines)], [shard_peer(s) for s in range(1, shards)]]
    vslots = []
    place = 0
    for stage in vstages:
        vslots.append(place)
        place += len(stage)
    vbegin = take(place)

    def v_copy(stage, index):
        slot = vslots[stage] + index
        return remote(vacc.at[pl.ds(stage * 16, 16)], vbuf.at[slot], vbegin + slot, vstages[stage][index])

    def v_start(stage):
        for index in range(len(vstages[stage])):
            v_copy(stage, index).start()

    def v_finish(stage):
        total = vacc[stage * 16 : stage * 16 + 16]
        for index in range(len(vstages[stage])):
            v_copy(stage, index).wait()
            total = total + vbuf[vslots[stage] + index]
        vacc[(stage + 1) * 16 : (stage + 2) * 16] = total

    def vectors_begin():
        vacc[0:16] = vec_ref[...]
        vacc[2:4] = bias_ref[0:2]
        gain_grad = m_q[...] * wq_ref[...].astype(F32)
        gain_grad = gain_grad + mt_k[...] * wk_ref[...].astype(F32) + mt_v[...] * wv_ref[...].astype(F32)
        vacc[0:1] = fold_rows(jnp.sum(gain_grad, axis=1, keepdims=True))
        total = dot_nt(cs_q[...].astype(BF16), wq_ref[...])
        for cs, weight in ((cs_k, wk_ref), (cs_v, wv_ref)):
            row = jnp.broadcast_to(fold_rows(cs[:, 0:1]), (8, width))
            total = total + dot_nt(row.astype(BF16), weight[...])
        vacc[1:2] = total[0:1]
        v_start(0)

    if pair:
        one.rs(0)
    after_x0(last)
    late_step("k", "c0")
    if lines == 4:
        after_x0(2)
    else:
        after_x1(0)
    along(two, 2)
    late_step("p", "rs")
    late_step("v", "c0")
    late_step("k", "y")
    late_step("q", "ag")
    vectors_begin()
    late_step("v", "y")
    if pair:
        along(one, 1)
    along(two, 3)
    late_step("p", "ag")
    v_finish(0)
    v_start(1)
    late_step("k", "x0")
    if pair:
        along(one, 2)
    late_step("v", "x0")
    v_finish(1)
    v_start(2)
    two.x()
    late_step("k", "rs")
    late_step("p", "x")
    late_step("v", "rs")
    if pair:
        along(one, 3)
    late_step("k", "ag")
    late_step("q", "x")
    late_step("v", "ag")
    for j in reversed(range(1, last)) if lines == 4 else range(1, last):
        after_x1(j)
    if pair:
        one.x()
    two.c()
    late_step("k", "x")
    late_step("p", "c")
    v_finish(2)
    v_start(3)
    late_step("v", "x")
    late_step("q", "c")
    if pair:
        one.c()
    own = after_x1(last)
    scaled = (own.T + dot_nt(dq_ref[...], wq_ref[...])) * vectors_ref[0:1]
    hidden_copy.wait()
    grad_ref[...] = hidden_ref[...] + inverse * (
        scaled - jnp.mean(scaled, axis=1, keepdims=True) - unit * jnp.mean(scaled * unit, axis=1, keepdims=True)
    )
    late_step("k", "c")
    late_step("v", "c")
    v_finish(3)
    vsum_ref[...] = vacc[4 * 16 : 5 * 16]
    for feed in feeds:
        feed.done()
    for name in "qpkv":
        late_step(name, "done")


def finish(lines, shards, chunks_f, sets, rows_l, cid, mine, come, dk, dv, unit_all, dpk, table, weights, dq, x, vectors, total, vec, bias, hidden):
    tokens, width = dq.shape
    vmem = pl.BlockSpec(memory_space=pltpu.VMEM)
    hbm = pl.BlockSpec(memory_space=pl.ANY)
    bufs = []
    for rows in chunks_f:
        bufs += [
            pltpu.VMEM((shards, rows, width), BF16),
            pltpu.VMEM((shards - 1, rows, width), BF16),
            pltpu.VMEM((rows, width), BF16),
        ]
    for names in sets:
        bufs += [
            pltpu.VMEM((shards, rows_l, width), BF16),
            pltpu.VMEM((shards, rows_l // 2, width), BF16),
            pltpu.VMEM((shards - 1, rows_l // 2, width), BF16),
            pltpu.VMEM((rows_l // 4, width), BF16),
            pltpu.VMEM((lines - 1, rows_l // 4 // lines, width), BF16),
        ]
    hops = shards - 1 + 2 * (lines - 1)
    copies = len(chunks_f) * (shards + 2 + 2 * (lines.bit_length() - 1)) + len(sets) * (hops + 4) + 3 * lines + 2 + lines - 1 + shards - 1
    total_rows = 4 * sum(chunks_f) + len(sets) * rows_l
    stages = 1 + 1 + (lines - 1) + (shards - 1)
    hold = min(dpk.shape[1], 17 * BLK)
    return pl.pallas_call(
        functools.partial(finish_kernel, lines, shards, tuple(chunks_f), sets, rows_l),
        out_shape=(
            jax.ShapeDtypeStruct((tokens, width), F32),
            jax.ShapeDtypeStruct((total_rows, width), BF16),
            jax.ShapeDtypeStruct((16, width), F32),
        ),
        in_specs=[vmem] * 2 + [hbm] * 6 + [vmem] * 6 + [hbm],
        out_specs=(vmem,) * 3,
        scratch_shapes=[
            pltpu.VMEM((2, width, 4 * tokens), BF16),
            pltpu.VMEM((2, width, 4 * tokens), BF16),
            pltpu.VMEM((2, 4 * tokens, width), BF16),
            pltpu.SemaphoreType.DMA((2, 3)),
            pltpu.VMEM((width, hold), BF16),
            pltpu.VMEM((hold, width), BF16),
            pltpu.VMEM((4, width, width), BF16),
            pltpu.VMEM((tokens, width), F32),
            pltpu.SemaphoreType.DMA((4,)),
            pltpu.VMEM((width, width), F32),
            pltpu.VMEM((width, width), F32),
            pltpu.VMEM((width, width), F32),
            pltpu.VMEM((8, width), F32),
            pltpu.VMEM((width, BLK), F32),
            pltpu.VMEM((width, BLK), F32),
            pltpu.VMEM((lines, 2, 2, width, tokens), BF16),
            pltpu.VMEM((lines, 2, width, tokens), BF16),
            pltpu.VMEM((lines, width, tokens), BF16),
            pltpu.VMEM((lines - 1, width, tokens), BF16),
            pltpu.VMEM((stages, 16, width), F32),
            pltpu.VMEM((5 * 16, width), F32),
        ]
        + bufs
        + [pltpu.SemaphoreType.DMA((copies,)), pltpu.SemaphoreType.DMA((copies,))],
        compiler_params=pltpu.CompilerParams(
            collective_id=cid, has_side_effects=True, vmem_limit_bytes=63 * 2**20
        ),
        cost_estimate=pl.CostEstimate(flops=10**10, bytes_accessed=30 * 2**20, transcendentals=0),
        name="finish",
    )(mine, come, dk, dv, unit_all, dpk, table, weights, dq, x, vectors, total, vec, bias, hidden)


def unpack_kernel(
    shards, rows_f, sets, rows_l, sums_ref, vsum_ref, total_ref, grad_ref, result_ref,
    grad_out, result_out, q_out, k_out, v_out, o_out, p_out, u_out, d_out, g1_out, b1_out, cb_out, pb_out, g2_out, b2_out, bd_out, bu_out,
    loss_out,
    low, wide, up, in_sem, out_sem,
):
    width = vsum_ref.shape[1]
    rows_out, rows_up = q_out.shape[0], d_out.shape[0]
    parts = u_out.shape[1] // width
    w = lax.axis_index("wsh")
    pieces = [(rows_up, d_out), (2 * rows_up, o_out)]
    to = {"q": q_out, "p": p_out, "k": k_out, "v": v_out}
    for index, names in enumerate(sets):
        pieces += [(rows_f + index * rows_l + m * rows_out, to[name]) for m, name in enumerate(names)]
    ins = [pltpu.make_async_copy(sums_ref.at[0:rows_up], low.at[0:rows_up], in_sem.at[0])]
    for index, (begin, out) in enumerate(pieces):
        size = out.shape[0]
        ins.append(pltpu.make_async_copy(sums_ref.at[begin : begin + size], low.at[begin : begin + size], in_sem.at[1 + index]))
    for copy in ins:
        copy.start()
    outs = []
    grad_out[...] = grad_ref[...]
    result_out[...] = result_ref[...]
    ins[0].wait()
    for c in range(parts):
        up[:, c * width : (c + 1) * width] = low[c * rows_out : (c + 1) * rows_out].astype(F32)
    outs.append(pltpu.make_async_copy(up, u_out, out_sem.at[0]))
    outs[0].start()
    for index, (begin, out) in enumerate(pieces):
        size = out.shape[0]
        ins[1 + index].wait()
        wide[begin : begin + size] = low[begin : begin + size].astype(F32)
        copy = pltpu.make_async_copy(wide.at[begin : begin + size], out, out_sem.at[1 + index])
        copy.start()
        outs.append(copy)

    def share(row):
        part = vsum_ref[row : row + 1, 0:rows_out]
        for s in range(1, shards):
            part = jnp.where(w == s, vsum_ref[row : row + 1, s * rows_out : (s + 1) * rows_out], part)
        return part.reshape(rows_out)

    for row, ref in enumerate((g1_out, b1_out, cb_out, pb_out, g2_out, b2_out, bd_out)):
        ref[...] = share(row)
    per = rows_up // rows_out
    for q in range(per):
        part = None
        for s in range(shards):
            group = s * per + q
            row, place = 7 + group // shards, group % shards
            piece = vsum_ref[row : row + 1, place * rows_out : (place + 1) * rows_out]
            part = piece if part is None else jnp.where(w == s, piece, part)
        bu_out[q * rows_out : (q + 1) * rows_out] = part.reshape(rows_out)
    loss_out[0, 0] = vsum_ref[7 + parts, 0] / (total_ref[0, 0] * width)
    for copy in outs:
        copy.wait()


def unpack(shards, rows_f, sets, rows_l, hidden, sums, vsum, total, grad, result):
    tokens, width = grad.shape
    rows_out, rows_up = width // shards, hidden // shards
    vmem = pl.BlockSpec(memory_space=pltpu.VMEM)
    hbm = pl.BlockSpec(memory_space=pl.ANY)
    square = jax.ShapeDtypeStruct((rows_out, width), F32)
    vector = jax.ShapeDtypeStruct((rows_out,), F32)
    return pl.pallas_call(
        functools.partial(unpack_kernel, shards, rows_f, sets, rows_l),
        out_shape=(
            jax.ShapeDtypeStruct((tokens, width), F32), jax.ShapeDtypeStruct((tokens, width), BF16), square, square, square, square, square,
            jax.ShapeDtypeStruct((rows_out, hidden), F32), jax.ShapeDtypeStruct((rows_up, width), F32),
            vector, vector, vector, vector, vector, vector, vector, jax.ShapeDtypeStruct((rows_up,), F32),
            jax.ShapeDtypeStruct((1, 1), F32),
        ),
        in_specs=[hbm, vmem, vmem, vmem, vmem],
        out_specs=(vmem,) * 2 + (hbm,) * 7 + (vmem,) * 8 + (pl.BlockSpec(memory_space=pltpu.SMEM),),
        scratch_shapes=[
            pltpu.VMEM(sums.shape, BF16),
            pltpu.VMEM(sums.shape, F32),
            pltpu.VMEM((rows_out, hidden), F32),
            pltpu.SemaphoreType.DMA((7,)),
            pltpu.SemaphoreType.DMA((8,)),
        ],
        compiler_params=pltpu.CompilerParams(vmem_limit_bytes=62 * 2**20),
        cost_estimate=pl.CostEstimate(flops=10**6, bytes_accessed=12 * 2**20, transcendentals=0),
        name="unpack",
    )(sums, vsum, total, grad, result)


PARTS = 2


def start_kernel(
    lines, shards, x_ref, wk_ref, wv_ref, wp_ref, wq_ref, wo_ref, wu_ref, wd_ref,
    g1_ref, b1_ref, cb_ref, pb_ref, g2_ref, b2_ref, bd_ref, bu_ref, mask_ref, far_ref, near_ref,
    k_ref, v_ref, unit_ref, pk_ref, table_ref, qc_ref, qp_ref, weights_ref, wo_out, wu_out, wd_out, vectors_ref, total_ref,
    x_all, k_buf, v_buf, u_buf, pk_buf, t_buf, wo_buf, wu_buf, wd_buf, vec_src, vec_buf, cnt_buf, cnt_acc,
    up_send, up_recv, down_send, down_recv, b_send, b_recv, c_send, c_recv,
    y_send, y_recv, yc_send, yc_recv, d_send, d_recv, s_send, s_recv, out_sem, pos_sem, own_sem,
):
    tokens, width = x_ref.shape
    piece = tokens // PARTS
    half = width // 2
    chunks = pk_buf.shape[0] // BLK
    ctx = lax.axis_index("ctx")
    w = lax.axis_index("wsh")
    core = lax.rem(ctx, 2)
    b = lax.rem(ctx // 2, 2)
    a = ctx // 4

    def at(a_to, b_to, core_to):
        return (a_to * 2 + b_to) * 2 + core_to

    def shard_peer(s):
        return (ctx, lax.rem(w + s, shards))

    def line_peer(s):
        return (at(lax.rem(a + s, lines), b, core), w)

    core_peer = (at(a, b, 1 - core), w)
    b_peer = (at(a, 1 - b, core), w)
    peers = [core_peer, b_peer] + [line_peer(s) for s in range(1, lines)] + [shard_peer(s) for s in range(1, shards)]
    barrier = pltpu.get_barrier_semaphore()
    for peer in peers:
        pl.semaphore_signal(barrier, inc=1, device_id=peer, device_id_type=MESH)

    def remote(src, dst, send, recv, peer):
        return pltpu.make_async_remote_copy(
            src_ref=src, dst_ref=dst, send_sem=send, recv_sem=recv, device_id=peer, device_id_type=MESH
        )

    def block(slot):
        return aligned(slot * tokens, tokens)

    x_all[block(ctx)] = x_ref[...]
    rows_out = wq_ref.shape[0]
    quarter = rows_out // 2
    rows_up = wd_ref.shape[0]
    weight_in = (wk_ref, wv_ref, wp_ref, wq_ref, wo_ref, wu_ref)
    weight_to = tuple(weights_ref.at[m] for m in range(4)) + (wo_buf, wu_buf)
    own_copies = [
        pltpu.make_async_copy(ref, to.at[aligned(w * rows_out, rows_out)], own_sem.at[m])
        for m, (ref, to) in enumerate(zip(weight_in[:4], weight_to))
    ]
    for copy in own_copies:
        copy.start()
    vec_src[...] = jnp.zeros_like(vec_src)
    for row, ref in enumerate((g1_ref, b1_ref, cb_ref, pb_ref, g2_ref, b2_ref, bd_ref)):
        vec_src[row : row + 1] = ref[...].astype(F32).reshape(1, rows_out)
    bias_rows = rows_up // rows_out
    for q in range(bias_rows):
        vec_src[7 + q : 8 + q] = bu_ref[q * rows_out : (q + 1) * rows_out].astype(F32).reshape(1, rows_out)
    cnt_acc[0:8] = jnp.broadcast_to(jnp.sum(mask_ref[...].astype(F32), axis=1, keepdims=True), (8, BLK))
    pl.semaphore_wait(barrier, len(peers))

    def x_copy(slot, h, send, recv, peer):
        rows = aligned(slot * tokens + h * piece, piece)
        return remote(x_all.at[rows], x_all.at[rows], send, recv, peer)

    def up_copy(p, h):
        peer = (at(jnp.minimum(a + 1, lines - 1), b, core), w)
        return x_copy(at(p, b, core), h, up_send.at[p, h], up_recv.at[p, h], peer)

    def down_copy(p, h):
        peer = (at(jnp.maximum(a - 1, 0), b, core), w)
        return x_copy(at(p, b, core), h, down_send.at[p, h], down_recv.at[p, h], peer)

    def b_copy(p, h, b_from):
        return x_copy(at(p, b_from, core), h, b_send.at[p, h], b_recv.at[p, h], b_peer)

    def c_copy(p, far, b_from, core_from):
        rows = block(at(p, b_from, core_from))
        return remote(x_all.at[rows], x_all.at[rows], c_send.at[far, p], c_recv.at[far, p], core_peer)

    def weight_copy(m, s):
        rows = aligned(w * rows_out + core * quarter, quarter)
        src = weight_in[m].at[aligned(core * quarter, quarter)]
        return remote(src, weight_to[m].at[rows], y_send.at[m, s - 1], y_recv.at[m, s - 1], shard_peer(s))

    def weight_pass(m, s):
        rows = aligned(lax.rem(w + shards - s, shards) * rows_out + core * quarter, quarter)
        return remote(
            weight_to[m].at[rows], weight_to[m].at[rows], yc_send.at[m, s - 1], yc_recv.at[m, s - 1], core_peer
        )

    low = lax.rem(a, 2)
    quarter_in, quarter_to = (wd_ref,), (wd_buf,)
    pair_peer = (at(a + 1 - 2 * low, b, core), w)

    def quarter_rows(m, s, low_of):
        size = quarter_in[m].shape[0]
        owner = lax.rem(w + shards - s, shards)
        return aligned(owner * size + (low_of * 2 + core) * (size // 4), size // 4)

    def quarter_copy(m, s):
        size = quarter_in[m].shape[0]
        src = quarter_in[m].at[aligned((low * 2 + core) * (size // 4), size // 4)]
        dst = quarter_to[m].at[quarter_rows(m, 0, low)]
        return remote(src, dst, d_send.at[m, 0, s - 1], d_recv.at[m, 0, s - 1], shard_peer(s))

    def quarter_pass(m, kind, s):
        rows = quarter_rows(m, s, 1 - low if kind == 3 else low)
        peer = pair_peer if kind == 1 else core_peer
        ref = quarter_to[m].at[rows]
        return remote(ref, ref, d_send.at[m, kind, s - 1], d_recv.at[m, kind, s - 1], peer)

    def quarter_on(m):
        for s in range(1, shards):
            quarter_copy(m, s).wait()
            quarter_pass(m, 1, s).start()
            quarter_pass(m, 2, s).start()

    def vec_copy(s):
        return remote(vec_src, vec_buf.at[s - 1], s_send.at[s - 1], s_recv.at[s - 1], shard_peer(s))

    stages = [[shard_peer(s) for s in range(1, shards)], [core_peer], [b_peer], [line_peer(s) for s in range(1, lines)]]
    slots = []
    place = 0
    for stage in stages:
        slots.append(place)
        place += len(stage)

    def cnt_copy(stage, index):
        slot = slots[stage] + index
        sem = shards - 1 + slot
        return remote(cnt_acc.at[pl.ds(stage * 8, 8)], cnt_buf.at[slot], s_send.at[sem], s_recv.at[sem], stages[stage][index])

    def cnt_start(stage):
        for index in range(len(stages[stage])):
            cnt_copy(stage, index).start()

    def cnt_finish(stage):
        total = cnt_acc[stage * 8 : stage * 8 + 8]
        for index in range(len(stages[stage])):
            cnt_copy(stage, index).wait()
            total = total + cnt_buf[slots[stage] + index]
        cnt_acc[(stage + 1) * 8 : (stage + 2) * 8] = total

    for s in range(1, shards):
        vec_copy(s).start()
    cnt_start(0)
    for h in range(PARTS):

        @pl.when(a + 1 < lines)
        def _():
            up_copy(a, h).start()

        @pl.when(a >= 1)
        def _():
            down_copy(a, h).start()

        b_copy(a, h, b).start()
    c_copy(a, 0, b, core).start()
    for kind, m in ((0, 0), (0, 1), (1, 0), (0, 2), (0, 5), (0, 3), (0, 4)):
        for s in range(1, shards):
            (quarter_copy if kind else weight_copy)(m, s).start()


    def table_step(d, _):
        sin_far, cos_far = far_ref[0, pl.ds(d, 1)], far_ref[1, pl.ds(d, 1)]
        sin_near, cos_near = near_ref[0], near_ref[1]
        rows = aligned(d * BLK, BLK)
        t_buf[rows, :half] = (sin_far * cos_near - cos_far * sin_near).astype(BF16)
        t_buf[rows, half:] = (cos_far * cos_near + sin_far * sin_near).astype(BF16)
        return 0

    lax.fori_loop(0, chunks, table_step, 0)
    table_out = pltpu.make_async_copy(t_buf, table_ref, pos_sem.at[0])
    table_out.start()
    lane_to = lax.broadcasted_iota(jnp.int32, (rows_out, width), 1)
    lane_from = lax.broadcasted_iota(jnp.int32, (rows_out, width), 0)
    row_at = lax.broadcasted_iota(jnp.int32, (16, width), 0)

    def spread(values, place):
        return dot_nn(values.astype(BF16), (lane_to == lane_from + place * rows_out).astype(BF16))

    def placed(values, owner):
        full = jnp.where(row_at < 7, spread(values, owner), 0.0)
        for q in range(bias_rows):
            group = owner * bias_rows + q
            row = jnp.broadcast_to(values[7 + q : 8 + q], values.shape)
            full = full + jnp.where(row_at == 7 + group // shards, spread(row, lax.rem(group, shards)), 0.0)
        return full

    vectors = placed(vec_src[...], w)
    for s in range(1, shards):
        vec_copy(s).wait()
        vectors = vectors + placed(vec_buf[s - 1], lax.rem(w + shards - s, shards))
    vectors_ref[...] = vectors
    cnt_finish(0)
    cnt_start(1)

    def unit_of(rows):
        values = rows.astype(F32)
        center = values - jnp.mean(values, axis=1, keepdims=True)
        return center * lax.rsqrt(jnp.mean(center * center, axis=1, keepdims=True) + epsilon)

    def out_copies(slot):
        rows = block(slot)
        return (
            pltpu.make_async_copy(k_buf.at[rows], k_ref.at[rows], out_sem.at[0, slot]),
            pltpu.make_async_copy(v_buf.at[rows], v_ref.at[rows], out_sem.at[1, slot]),
            pltpu.make_async_copy(u_buf.at[rows], unit_ref.at[rows], out_sem.at[2, slot]),
        )

    def project(p):
        def one(q, _):
            other_b = lax.rem(q, 2)
            other_core = q // 2

            @pl.when(q == 1)
            def _():
                for h in range(PARTS):
                    b_copy(p, h, b).wait()
                c_copy(p, 1, 1 - b, core).start()

            @pl.when(q == 2)
            def _():
                c_copy(p, 0, b, core).wait()

            @pl.when(q == 3)
            def _():
                c_copy(p, 1, 1 - b, core).wait()

            slot = at(p, b + other_b - 2 * b * other_b, core + other_core - 2 * core * other_core)
            rows = block(slot)
            unit = unit_of(x_all[rows])
            u_buf[rows] = unit.astype(BF16)
            normed = (unit * vectors_ref[0:1] + vectors_ref[1:2]).astype(BF16)
            k_buf[rows] = dot_nn(normed, weights_ref[0]).astype(BF16)
            v_buf[rows] = dot_nn(normed, weights_ref[1]).astype(BF16)
            for copy in out_copies(slot):
                copy.start()
            return 0

        lax.fori_loop(0, 4, one, 0)

    def pos_step(d, _):
        rows = aligned(d * BLK, BLK)
        pk_buf[rows] = dot_nn(t_buf[rows], weights_ref[2]).astype(BF16)
        return 0

    last = lines - 1

    def line_step(s, _):
        below, high = a - 1 - s, a + 1 + s

        for h in range(PARTS):

            @pl.when((s < lines - 1) & (below >= 0))
            def _():
                p = jnp.maximum(below, 0)
                up_copy(p, h).wait_recv()

                @pl.when(a + 1 < lines)
                def _():
                    up_copy(p, h).start()

                b_copy(p, h, b).start()
                if h == PARTS - 1:
                    c_copy(p, 0, b, core).start()

            @pl.when((s < lines - 1) & (high < lines))
            def _():
                p = jnp.minimum(high, lines - 1)
                down_copy(p, h).wait_recv()

                @pl.when(a >= 1)
                def _():
                    down_copy(p, h).start()

                b_copy(p, h, b).start()
                if h == PARTS - 1:
                    c_copy(p, 0, b, core).start()

        @pl.when(s == 0)
        def _():
            cnt_finish(1)
            cnt_start(2)
            for copy in own_copies:
                copy.wait()
            for m in range(2):
                for t in range(1, shards):
                    weight_copy(m, t).wait()
                    weight_pass(m, t).start()
            for m in range(2):
                for t in range(1, shards):
                    weight_pass(m, t).wait()

        @pl.when(s == min(1, last))
        def _():
            cnt_finish(2)
            cnt_start(3)

        @pl.when(s == min(2, last))
        def _():
            for t in range(1, shards):
                weight_copy(2, t).wait()
                weight_pass(2, t).start()
            for t in range(1, shards):
                weight_pass(2, t).wait()

        @pl.when(s == last)
        def _():
            for m in range(3, 5):
                for t in range(1, shards):
                    weight_copy(m, t).wait()
                    weight_pass(m, t).start()
            for t in range(1, shards):
                weight_pass(3, t).wait()

        @pl.when(a - s >= 0)
        def _():
            project(jnp.maximum(a - s, 0))

        @pl.when((s >= 1) & (a + s < lines))
        def _():
            project(jnp.minimum(a + s, lines - 1))

        @pl.when(s == min(1, last))
        def _():
            quarter_on(0)

        @pl.when(s == min(2, last))
        def _():
            lax.fori_loop(0, chunks // 2, pos_step, 0)
            for t in range(1, shards):
                weight_copy(5, t).wait()
                weight_pass(5, t).start()

        @pl.when(s == last)
        def _():
            lax.fori_loop(chunks // 2, chunks, pos_step, 0)

        return 0

    lax.fori_loop(0, lines, line_step, 0)
    pos_out = pltpu.make_async_copy(pk_buf, pk_ref, pos_sem.at[1])
    pos_out.start()
    normed = (unit_of(x_ref[...]) * vectors_ref[0:1] + vectors_ref[1:2]).astype(BF16)
    queries = dot_nn(normed, weights_ref[3]).astype(BF16).astype(F32)
    qc_ref[...] = ((queries + vectors_ref[2:3]) * 0.125).astype(BF16)
    qp_ref[...] = ((queries + vectors_ref[3:4]) * 0.125).astype(BF16)
    cnt_finish(3)
    total_ref[...] = cnt_acc[4 * 8 : 5 * 8]

    def sends_done(p, _):
        for h in range(PARTS):

            @pl.when((a + 1 < lines) & (p <= a))
            def _():
                up_copy(p, h).wait_send()

            @pl.when((a >= 1) & (p >= a))
            def _():
                down_copy(p, h).wait_send()

        return 0

    lax.fori_loop(0, lines, sends_done, 0)

    def outs_done(slot, _):
        for copy in out_copies(slot):
            copy.wait()
        return 0

    lax.fori_loop(0, 4 * lines, outs_done, 0)
    for s in range(1, shards):
        weight_pass(4, s).wait()
        weight_pass(5, s).wait()
        quarter_pass(0, 1, s).wait()
        quarter_pass(0, 3, s).start()
    for s in range(1, shards):
        quarter_pass(0, 2, s).wait()
        quarter_pass(0, 3, s).wait()
    far_copies = []
    for m, (buf, to) in enumerate(((wo_buf, wo_out), (wu_buf, wu_out), (wd_buf, wd_out))):
        size = buf.shape[0] // shards
        for s in range(1, shards):
            rows = aligned(lax.rem(w + s, shards) * size, size)
            far_copies.append(pltpu.make_async_copy(buf.at[rows], to.at[rows], own_sem.at[4 + m * (shards - 1) + s - 1]))
    for copy in far_copies:
        copy.start()
    for copy in far_copies:
        copy.wait()
    table_out.wait()
    pos_out.wait()


def start(lines, shards, cid, limit, x, weights, vectors, mask, far, near):
    tokens, width = x.shape
    hidden = weights[5].shape[1]
    rows_out = weights[0].shape[0]
    members = 4 * lines
    keys = members * tokens
    span = limit * BLK
    vmem = pl.BlockSpec(memory_space=pltpu.VMEM)
    hbm = pl.BlockSpec(memory_space=pl.ANY)
    small = 2 * (shards - 1) + 1 + 1 + lines - 1
    dma = pltpu.SemaphoreType.DMA
    other = shards - 1
    return pl.pallas_call(
        functools.partial(start_kernel, lines, shards),
        out_shape=(
            jax.ShapeDtypeStruct((keys, width), BF16),
            jax.ShapeDtypeStruct((keys, width), BF16),
            jax.ShapeDtypeStruct((keys, width), BF16),
            jax.ShapeDtypeStruct((span, width), BF16),
            jax.ShapeDtypeStruct((span, width), BF16),
            jax.ShapeDtypeStruct((tokens, width), BF16),
            jax.ShapeDtypeStruct((tokens, width), BF16),
            jax.ShapeDtypeStruct((4, width, width), BF16),
            jax.ShapeDtypeStruct((width, width), BF16),
            jax.ShapeDtypeStruct((width, hidden), BF16),
            jax.ShapeDtypeStruct((hidden, width), BF16),
            jax.ShapeDtypeStruct((16, width), F32),
            jax.ShapeDtypeStruct((8, BLK), F32),
        ),
        in_specs=[vmem] + [hbm] * 7 + [vmem] * 11,
        out_specs=(hbm,) * 5 + (vmem,) * 3 + (hbm,) * 3 + (vmem,) * 2,
        scratch_shapes=[
            pltpu.VMEM((keys, width), BF16),
            pltpu.VMEM((keys, width), BF16),
            pltpu.VMEM((keys, width), BF16),
            pltpu.VMEM((keys, width), BF16),
            pltpu.VMEM((span, width), BF16),
            pltpu.VMEM((span, width), BF16),
            pltpu.VMEM((width, width), BF16),
            pltpu.VMEM((width, hidden), BF16),
            pltpu.VMEM((hidden, width), BF16),
            pltpu.VMEM((16, rows_out), F32),
            pltpu.VMEM((other, 16, rows_out), F32),
            pltpu.VMEM((lines + shards, 8, BLK), F32),
            pltpu.VMEM((5 * 8, BLK), F32),
        ]
        + [dma((lines, PARTS))] * 6
        + [dma((2, lines))] * 2
        + [dma((6, other))] * 4
        + [dma((1, 4, other))] * 2
        + [dma((small,))] * 2
        + [dma((3, members)), dma((2,)), dma((4 + 3 * other,))],
        compiler_params=pltpu.CompilerParams(collective_id=cid, has_side_effects=True, vmem_limit_bytes=60 * 2**20),
        cost_estimate=pl.CostEstimate(flops=6 * 10**9, bytes_accessed=20 * 2**20, transcendentals=0),
        name="start",
    )(x, *weights, *vectors, mask, far, near)


GELU_SCALE = math.sqrt(2.0 / math.pi)


def middle_kernel(
    shards, rows_f, mask_ref, x_ref, mixed_ref, teacher_ref, out_grad_ref, vectors_ref, total_ref,
    wo_own, wu_own, wd_own, wo_ref, wu_ref, wd_ref,
    out_ref, hidden_ref, gm_ref, mine_ref, theirs_ref, vec_ref,
    wo, wu, wd, slope, act, gf_ref, landed, sem, send_sem, recv_sem,
):
    tokens, width = x_ref.shape
    parts = wu.shape[1] // width
    ctx = lax.axis_index("ctx")
    core = lax.rem(ctx, 2)
    core_peer = (ctx + 1 - 2 * core, lax.axis_index("wsh"))
    barrier = pltpu.get_barrier_semaphore()
    pl.semaphore_signal(barrier, inc=1, device_id=core_peer, device_id_type=MESH)
    w = lax.axis_index("wsh")
    copies = []
    for k, (own, gathered, full) in enumerate(((wo_own, wo_ref, wo), (wu_own, wu_ref, wu), (wd_own, wd_ref, wd))):
        size = own.shape[0]
        part = [pltpu.make_async_copy(own, full.at[aligned(w * size, size)], sem.at[k, 0])]
        for s in range(1, shards):
            rows = aligned(lax.rem(w + s, shards) * size, size)
            part.append(pltpu.make_async_copy(gathered.at[rows], full.at[rows], sem.at[k, s]))
        for copy in part:
            copy.start()
        copies.append(part)

    def arrive(k):
        for copy in copies[k]:
            copy.wait()

    b = lax.rem(ctx // 2, 2)
    half, quarter = rows_f // 2, rows_f // 4

    def give(begin, size, index):
        rows = aligned((1 - core) * half + begin, size)
        return pltpu.make_async_remote_copy(
            src_ref=gf_ref.at[:, rows], dst_ref=landed.at[:, begin : begin + size],
            send_sem=send_sem.at[index], recv_sem=recv_sem.at[index], device_id=core_peer, device_id_type=MESH,
        )

    gain, offset, down_bias = vectors_ref[4:5], vectors_ref[5:6], vectors_ref[6:7]
    mixed = mixed_ref[...].astype(BF16)
    arrive(0)
    hidden = x_ref[...].astype(F32) + dot_nn(mixed, wo[...])
    center = hidden - jnp.mean(hidden, axis=1, keepdims=True)
    inverse = lax.rsqrt(jnp.mean(center * center, axis=1, keepdims=True) + epsilon)
    unit = center * inverse
    normed = (unit * gain + offset).astype(BF16)
    result = hidden + down_bias
    arrive(1)
    arrive(2)
    for c in range(parts):
        cols = slice(c * width, (c + 1) * width)
        v = dot_nn(normed, wu[:, cols]) + vectors_ref[7 + c : 8 + c]
        square = v * v
        t = jnp.tanh(GELU_SCALE * (v + 0.044715 * (square * v)))
        act[:, cols] = (0.5 * v * (1.0 + t)).astype(BF16)
        slope[:, cols] = 0.5 * (1.0 + t) + 0.5 * v * (1.0 - t * t) * (GELU_SCALE * (1.0 + 3.0 * 0.044715 * square))
        result = result + dot_nn(act[:, cols], wd[cols])
    out_ref[...] = result.astype(BF16)
    mask = jnp.broadcast_to(mask_ref[...].astype(F32), (8, tokens)).T[:, 0:1]
    error = result - teacher_ref[...].astype(F32)
    masked = mask * error
    count = jnp.sum(total_ref[0:1, 0:1], axis=1, keepdims=True)
    grad_result = out_grad_ref[...].astype(F32) + (2.0 / (count * width)) * masked
    branch = grad_result.astype(BF16)
    vec_ref[...] = jnp.zeros_like(vec_ref)
    vec_ref[7 + parts : 8 + parts] = jnp.broadcast_to(
        jnp.sum(jnp.sum(masked * error, axis=1, keepdims=True), axis=0, keepdims=True), (1, width)
    )
    vec_ref[6:7] = jnp.sum(branch.astype(F32), axis=0, keepdims=True)
    rows_up = wd.shape[0] // shards
    rows_out = width // shards
    used = 2 * rows_up + rows_out
    if used < rows_f:
        gf_ref[:, used:] = jnp.zeros((shards, rows_f - used, width), BF16)
    grad_normed = jnp.zeros((tokens, width), F32)
    for c in range(parts):
        cols = slice(c * width, (c + 1) * width)
        grad_pre = (dot_nt(branch, wd[cols]) * slope[:, cols]).astype(BF16)
        vec_ref[7 + c : 8 + c] = jnp.sum(grad_pre.astype(F32), axis=0, keepdims=True)
        grad_normed = grad_normed + dot_nt(grad_pre, wu[:, cols])
        up = dot_tn(normed, grad_pre).astype(BF16)
        down = dot_tn(act[:, cols], branch).astype(BF16)
        for s in range(shards):
            gf_ref[s, c * rows_out : (c + 1) * rows_out] = up[s * rows_out : (s + 1) * rows_out]
        step = min(rows_up, width)
        for begin in range(0, width, step):
            row = c * width + begin
            place = rows_up + row % rows_up
            gf_ref[row // rows_up, place : place + step] = down[begin : begin + step]
    pl.semaphore_wait(barrier, 1)
    early = max(0, 2 * rows_up - half)
    if early:
        give(0, early, 0).start()
    vec_ref[4:5] = jnp.sum(grad_normed * unit, axis=0, keepdims=True)
    vec_ref[5:6] = jnp.sum(grad_normed, axis=0, keepdims=True)
    scaled = grad_normed * gain
    grad_hidden = grad_result + inverse * (
        scaled - jnp.mean(scaled, axis=1, keepdims=True) - unit * jnp.mean(scaled * unit, axis=1, keepdims=True)
    )
    hidden_ref[...] = grad_hidden
    attn = grad_hidden.astype(BF16)
    gm_ref[...] = dot_nt(attn, wo[...]).astype(BF16)
    outer = dot_tn(mixed, attn).astype(BF16)
    for s in range(shards):
        gf_ref[s, 2 * rows_up : used] = outer[s * rows_out : (s + 1) * rows_out]
    give(early, half - early, 1).start()
    if early:
        give(0, early, 0).wait()
    give(early, half - early, 1).wait()
    for ref, place in ((theirs_ref, 1 - b), (mine_ref, b)):
        own = gf_ref[:, aligned(core * half + place * quarter, quarter)].astype(F32)
        ref[...] = (own + landed[:, aligned(place * quarter, quarter)].astype(F32)).astype(BF16)


def middle(shards, rows_f, cid, mask, x, mixed, teacher, out_grad, vectors, total, own, gathered):
    tokens, width = x.shape
    hidden = own[1].shape[1]
    vmem = pl.BlockSpec(memory_space=pltpu.VMEM)
    hbm = pl.BlockSpec(memory_space=pl.ANY)
    return pl.pallas_call(
        functools.partial(middle_kernel, shards, rows_f),
        out_shape=(
            jax.ShapeDtypeStruct((tokens, width), BF16),
            jax.ShapeDtypeStruct((tokens, width), F32),
            jax.ShapeDtypeStruct((tokens, width), BF16),
            jax.ShapeDtypeStruct((shards, rows_f // 4, width), BF16),
            jax.ShapeDtypeStruct((shards, rows_f // 4, width), BF16),
            jax.ShapeDtypeStruct((16, width), F32),
        ),
        in_specs=[vmem] * 7 + [hbm] * 6,
        out_specs=(vmem,) * 6,
        scratch_shapes=[
            pltpu.VMEM((width, width), BF16),
            pltpu.VMEM((width, hidden), BF16),
            pltpu.VMEM((hidden, width), BF16),
            pltpu.VMEM((tokens, hidden), F32),
            pltpu.VMEM((tokens, hidden), BF16),
            pltpu.VMEM((shards, rows_f, width), BF16),
            pltpu.VMEM((shards, rows_f // 2, width), BF16),
            pltpu.SemaphoreType.DMA((3, shards)),
            pltpu.SemaphoreType.DMA((2,)),
            pltpu.SemaphoreType.DMA((2,)),
        ],
        compiler_params=pltpu.CompilerParams(collective_id=cid, has_side_effects=True, vmem_limit_bytes=56 * 2**20),
        cost_estimate=pl.CostEstimate(flops=4 * 10**9, bytes_accessed=20 * 2**20, transcendentals=10**6),
        name="middle",
    )(mask, x, mixed, teacher, out_grad, vectors, total, *own, *gathered)


def body(
    inputs, block_perm, seq_lengths, loss_mask, teacher, out_grad, gain_one, bias_one, w_query, w_key, w_value,
    w_output, w_pos, content_bias, position_bias, gain_two, bias_two, w_up, bias_up, w_down, bias_down,
):
    width = inputs.shape[2]
    shards = lax.axis_size("wsh")
    members = lax.axis_size("ctx")
    lines = members // 4
    hidden = bias_up.shape[0] * shards
    blocks = block_perm.shape[1]
    limit = blocks // 2 + 1
    rows_up, rows_out = hidden // shards, width // shards

    frequency = np.exp(np.arange(width // 2) * (-2.0 * math.log(10000.0) / width))
    far_angle = (np.arange(-(-limit // 8) * 8) * BLK + (BLK - 1))[:, None] * frequency[None]
    near_angle = np.arange(BLK)[:, None] * frequency[None]
    far = jnp.asarray(np.stack([np.sin(far_angle), np.cos(far_angle)]), F32)
    near = jnp.asarray(np.stack([np.sin(near_angle), np.cos(near_angle)]), F32)

    keys, values, unit_all, pos_keys, table, qc, qp, weights, wo, wu, wd, vectors, total = start(
        lines, shards, 0, limit, inputs[0], (w_key, w_value, w_pos, w_query, w_output, w_up, w_down),
        (gain_one, bias_one, content_bias, position_bias, gain_two, bias_two, bias_down, bias_up), loss_mask, far, near,
    )
    mixed, linv, probs = attn_fwd(block_perm, seq_lengths, qc, qp, keys, values, pos_keys, blocks, limit)

    step = 16 * lines
    pieces = -(-(2 * rows_up + rows_out) // (4 * step))
    split = min(2, pieces)
    chunks_f = tuple((pieces * (i + 1) // split - pieces * i // split) * step for i in range(split))
    rows_f = 4 * step * pieces
    if rows_out % (32 * lines):
        sets, rows_l = (("q", "p"), ("k", "v")), -(-2 * rows_out // (32 * lines)) * 32 * lines
    else:
        sets, rows_l = (("q",), ("p",), ("k",), ("v",)), rows_out
    output, grad_hidden, grad_mixed, mine, theirs, vec = middle(
        shards, rows_f, 2, loss_mask, inputs[0], mixed, teacher[0], out_grad[0], vectors, total,
        (w_output, w_up, w_down), (wo, wu, wd),
    )
    come = lax.ppermute(theirs, "ctx", [(i, i ^ 2) for i in range(members)])
    grad_query, bias_grads, dk_t, dv_t, dpk_t = attn_bwd(
        block_perm, seq_lengths, qc, qp, keys, values, pos_keys, probs, linv, grad_mixed, mixed, blocks, limit
    )
    grad_input, sums, vsum = finish(
        lines, shards, chunks_f, sets, rows_l, 1, mine, come, dk_t, dv_t, unit_all, dpk_t, table, weights, grad_query,
        inputs[0], vectors, total, vec, bias_grads, grad_hidden,
    )
    (
        grad_input, output, g_query, g_key, g_value, g_output, g_pos, g_up, g_down,
        v_g1, v_b1, v_cb, v_pb, v_g2, v_b2, v_bd, v_bu, loss,
    ) = unpack(shards, rows_f, sets, rows_l, hidden, sums, vsum, total, grad_input, output)
    return (
        output[None], loss.reshape(()), grad_input[None], v_g1, v_b1, g_query, g_key, g_value, g_output, g_pos,
        v_cb, v_pb, v_g2, v_b2, g_up, v_bu, g_down, v_bd,
    )


def solution(mesh):
    rows = P("wsh", "ctx", None)
    vector = P("wsh")
    matrix = P("wsh", None)
    placed = (
        rows, matrix, matrix, P("wsh", "ctx"), rows, rows, vector, vector, matrix, matrix, matrix, matrix, matrix,
        vector, vector, vector, vector, matrix, vector, matrix, vector,
    )
    out = (
        rows, P(), rows, vector, vector, matrix, matrix, matrix, matrix, matrix, vector, vector, vector, vector,
        matrix, vector, matrix, vector,
    )
    return jax.shard_map(body, mesh=mesh, in_specs=placed, out_specs=out, check_vma=False)
```

```python
import functools
import math

import jax
import jax.numpy as jnp
import numpy as np
from jax import lax
from jax.experimental import pallas as pl
from jax.experimental.pallas import tpu as pltpu
from jax.sharding import PartitionSpec as P

HEADS = 8
HEAD = 64
PAIRS = HEADS // 2
BLK = 128
ROWS = HEADS * BLK
NEG = -1e30
epsilon = 1e-05
F32 = jnp.float32
BF16 = jnp.bfloat16


def dot_nt(a, b):
    return lax.dot_general(a, b, (((1,), (1,)), ((), ())), preferred_element_type=F32)


def dot_nn(a, b):
    return lax.dot_general(a, b, (((1,), (0,)), ((), ())), preferred_element_type=F32)


def dot_tn(a, b):
    return lax.dot_general(a, b, (((0,), (0,)), ((), ())), preferred_element_type=F32)


def iotas():
    row = lax.broadcasted_iota(jnp.int32, (BLK, BLK), 0)
    col = lax.broadcasted_iota(jnp.int32, (BLK, BLK), 1)
    return row, col


def read_places(perm_ref, lengths_ref, meta, blocks, count):
    device = lax.axis_index("ctx")
    meta[0] = perm_ref[0, 2 * device]
    meta[1] = perm_ref[0, 2 * device + 1]

    def place(slot, _):
        meta[2 + perm_ref[0, slot]] = slot
        return 0

    lax.fori_loop(0, blocks, place, 0, unroll=True)
    end = jnp.int32(0)
    for e in range(count):
        end = end + lengths_ref[0, e]
        meta[2 + blocks + e] = end


def block_range(meta, a, blocks, limit):
    qb = meta[a]
    first = qb * BLK
    low = jnp.int32(0)
    for e in range(meta.shape[0] - 2 - blocks):
        end = meta[2 + blocks + e]
        low = jnp.where(first >= end, jnp.maximum(low, end), low)
    lowest = low // BLK
    return qb, lowest, jnp.minimum(qb - lowest + 1, limit)


def stack_heads(pair):
    lane = lax.broadcasted_iota(jnp.int32, pair.shape, 1)
    zero = jnp.zeros_like(pair)
    return jnp.concatenate([jnp.where(lane < HEAD, pair, zero), jnp.where(lane >= HEAD, pair, zero)], axis=0)


def flip_rows(x):
    index = 7 - lax.broadcasted_iota(jnp.int32, (8, BLK), 0)
    slabs = [jnp.take_along_axis(x[8 * g : 8 * g + 8], index, axis=0) for g in reversed(range(BLK // 8))]
    return jnp.concatenate(slabs, axis=0)


def flip_two(x):
    return jnp.concatenate([flip_rows(x[:BLK]), flip_rows(x[BLK:])], axis=0)


def needed_blocks(meta, blocks, limit):
    ranges = []
    for a in range(2):
        qb, lowest, count = block_range(meta, a, blocks, limit)
        ranges.append((qb + 1 - 2 * ((count + 1) // 2), qb))
    return ranges


def load_keys(meta, blocks, limit, pairs, sem):
    (low0, high0), (low1, high1) = needed_blocks(meta, blocks, limit)
    for hbm, ref in pairs:
        ref[0:BLK] = jnp.zeros((BLK, ref.shape[1]), ref.dtype)

    def copies(kb):
        slot = pl.ds(pl.multiple_of(meta[2 + kb] * BLK, BLK), BLK)
        place = pl.ds(pl.multiple_of((kb + 1) * BLK, BLK), BLK)
        return [
            pltpu.make_async_copy(hbm.at[slot], ref.at[place], sem.at[index, kb]) for index, (hbm, ref) in enumerate(pairs)
        ]

    def begin(kb, _):
        @pl.when(((kb >= low0) & (kb <= high0)) | ((kb >= low1) & (kb <= high1)))
        def _():
            for copy in copies(kb):
                copy.start()

        return 0

    lax.fori_loop(0, blocks, begin, 0)

    def arrive(a):
        low, high = (jnp.where(a == 0, x, y) for x, y in ((low0, low1), (high0, high1)))

        def one(kb, _):
            @pl.when((a == 0) | (kb < low0) | (kb > high0))
            def _():
                for copy in copies(kb):
                    copy.wait()

            return 0

        lax.fori_loop(jnp.maximum(low, 0), high + 1, one, 0)

    return arrive


def wide_iotas():
    row = lax.broadcasted_iota(jnp.int32, (BLK, 2 * BLK), 0)
    col = lax.broadcasted_iota(jnp.int32, (BLK, 2 * BLK), 1)
    return row, col


def attn_fwd_kernel(
    blocks, limit, perm_ref, lengths_ref, qc_ref, qp_ref, k_in, v_in, pk_in, mixed_ref, linv_ref, p_ref,
    meta, k_ref, v_ref, pk_ref, q2c, q2p, prev, top, total, acc, s_scr, p_buf, kv_sem, pk_sem, p_sem,
):
    read_places(perm_ref, lengths_ref, meta, blocks, lengths_ref.shape[1])
    span = pk_in.shape[0]
    pk_copy = pltpu.make_async_copy(pk_in, pk_ref.at[0:span], pk_sem)
    pk_copy.start()
    arrive = load_keys(meta, blocks, limit, ((k_in, k_ref), (v_in, v_ref)), kv_sem)
    pk_ref[span:] = jnp.zeros((BLK, pk_ref.shape[1]), BF16)
    row, col = iotas()
    tri = col <= row
    wide_row, wide_col = wide_iotas()
    tiles = s_scr.shape[0]

    def p_copy(slot, index):
        return pltpu.make_async_copy(p_buf.at[slot], p_ref.at[index], p_sem.at[slot])

    def one_query_block(a, _):
        qb, lowest, count = block_range(meta, a, blocks, limit)
        pairs = (count + 1) // 2
        rows_a = pl.ds(pl.multiple_of(a * BLK, BLK), BLK)
        pos = qb * BLK + wide_row
        start = jnp.zeros((BLK, 2 * BLK), jnp.int32)
        for e in range(meta.shape[0] - 2 - blocks):
            end = meta[2 + blocks + e]
            start = jnp.where(pos >= end, jnp.maximum(start, end), start)
        for hp in range(PAIRS):
            lanes = slice(hp * BLK, (hp + 1) * BLK)
            q2c[hp] = stack_heads(qc_ref[rows_a, lanes].astype(F32)).astype(BF16)
            q2p[hp] = stack_heads(qp_ref[rows_a, lanes].astype(F32)).astype(BF16)
        prev[...] = jnp.zeros_like(prev)
        top[...] = jnp.full_like(top, NEG)
        total[...] = jnp.zeros_like(total)
        acc[...] = jnp.zeros_like(acc)
        arrive(a)

        @pl.when(a == 0)
        def _():
            pk_copy.wait()

        def score_step(t, _):
            kb = qb - 2 * t
            keys = pl.ds(pl.multiple_of(kb * BLK, BLK), 2 * BLK)
            place = (kb - 1) * BLK + wide_col
            bias = jnp.where((place >= start) & (place <= pos), 0.0, NEG).astype(F32)
            drows = pl.ds(pl.multiple_of(2 * t * BLK, BLK), 2 * BLK)
            for hp in range(PAIRS):
                lanes = slice(hp * BLK, (hp + 1) * BLK)
                s = dot_nt(q2c[hp], k_ref[keys, lanes])
                r = dot_nt(q2p[hp], pk_ref[drows, lanes])
                for half in range(2):
                    part = slice(half * BLK, (half + 1) * BLK)
                    rows = slice((2 * hp + half) * BLK, (2 * hp + half + 1) * BLK)
                    near = pltpu.roll(r[part, :BLK], 1, 1, stride=1, stride_axis=0)
                    far = pltpu.roll(r[part, BLK:], 1, 1, stride=1, stride_axis=0)
                    late = s[part, BLK:] + jnp.where(tri, near, prev[rows]) + bias[:, BLK:]
                    early = s[part, :BLK] + jnp.where(tri, far, near) + bias[:, :BLK]
                    prev[rows] = far
                    s_scr[t, rows, :BLK] = early
                    s_scr[t, rows, BLK:] = late
                    top[rows] = jnp.maximum(top[rows], jnp.maximum(early, late))
            return 0

        lax.fori_loop(0, pairs, score_step, 0)
        for h in range(HEADS):
            rows = slice(h * BLK, (h + 1) * BLK)
            top[rows] = jnp.broadcast_to(jnp.max(top[rows], axis=1, keepdims=True), (BLK, BLK))

        def mix_step(t, _):
            kb = qb - 2 * t
            keys = pl.ds(pl.multiple_of(kb * BLK, BLK), 2 * BLK)
            slot = lax.rem(t, 2)

            @pl.when(t >= 2)
            def _():
                p_copy(slot, 0).wait()

            for hp in range(PAIRS):
                lanes = slice(hp * BLK, (hp + 1) * BLK)
                rows = slice(2 * hp * BLK, 2 * (hp + 1) * BLK)
                early = jnp.exp(s_scr[t, rows, :BLK] - top[rows])
                late = jnp.exp(s_scr[t, rows, BLK:] - top[rows])
                total[rows] += early + late
                p_buf[slot, rows, :BLK] = flip_two(early).astype(BF16)
                p_buf[slot, rows, BLK:] = flip_two(late).astype(BF16)
                low = jnp.concatenate([early.astype(BF16), late.astype(BF16)], axis=1)
                acc[hp] += dot_nn(low, v_ref[keys, lanes])
            p_copy(slot, a * tiles + t).start()
            return 0

        lax.fori_loop(0, pairs, mix_step, 0)
        p_copy(lax.rem(pairs - 1, 2), 0).wait()

        @pl.when(pairs >= 2)
        def _():
            p_copy(lax.rem(pairs, 2), 0).wait()

        lane = lax.broadcasted_iota(jnp.int32, (BLK, BLK), 1)
        for hp in range(PAIRS):
            lanes = slice(hp * BLK, (hp + 1) * BLK)
            parts = []
            for half in range(2):
                h = 2 * hp + half
                rows = slice(h * BLK, (h + 1) * BLK)
                inv = 1.0 / jnp.sum(total[rows], axis=1, keepdims=True)
                inv = jnp.broadcast_to(inv, (BLK, BLK))
                linv_ref[a, rows] = inv
                parts.append(acc[hp, half * BLK : (half + 1) * BLK] * inv)
            mixed_ref[rows_a, lanes] = jnp.where(lane < HEAD, parts[0], parts[1])
        return 0

    lax.fori_loop(0, 2, one_query_block, 0)


def attn_fwd(perm, lengths, qc, qp, k, v, pk, blocks, limit):
    tokens, width = qc.shape
    keys, span = k.shape[0], pk.shape[0]
    tiles = (limit + 1) // 2
    vmem = pl.BlockSpec(memory_space=pltpu.VMEM)
    hbm = pl.BlockSpec(memory_space=pl.ANY)
    return pl.pallas_call(
        functools.partial(attn_fwd_kernel, blocks, limit),
        out_shape=(
            jax.ShapeDtypeStruct((tokens, width), F32),
            jax.ShapeDtypeStruct((2, ROWS, BLK), F32),
            jax.ShapeDtypeStruct((2 * tiles, ROWS, 2 * BLK), BF16),
        ),
        in_specs=[pl.BlockSpec(memory_space=pltpu.SMEM)] * 2 + [vmem] * 2 + [hbm] * 3,
        out_specs=(vmem, vmem, hbm),
        scratch_shapes=[
            pltpu.SMEM((2 + blocks + lengths.shape[1],), jnp.int32),
            pltpu.VMEM((keys + BLK, width), BF16),
            pltpu.VMEM((keys + BLK, width), BF16),
            pltpu.VMEM((span + BLK, width), BF16),
            pltpu.VMEM((PAIRS, 2 * BLK, BLK), BF16),
            pltpu.VMEM((PAIRS, 2 * BLK, BLK), BF16),
            pltpu.VMEM((ROWS, BLK), F32),
            pltpu.VMEM((ROWS, BLK), F32),
            pltpu.VMEM((ROWS, BLK), F32),
            pltpu.VMEM((PAIRS, 2 * BLK, BLK), F32),
            pltpu.VMEM((tiles, ROWS, 2 * BLK), F32),
            pltpu.VMEM((2, ROWS, 2 * BLK), BF16),
            pltpu.SemaphoreType.DMA((2, blocks)),
            pltpu.SemaphoreType.DMA,
            pltpu.SemaphoreType.DMA((2,)),
        ],
        compiler_params=pltpu.CompilerParams(vmem_limit_bytes=60 * 2**20),
        cost_estimate=pl.CostEstimate(flops=3 * 10**9, bytes_accessed=20 * 2**20, transcendentals=4 * 10**6),
        name="attn_fwd",
    )(perm, lengths, qc, qp, k, v, pk)


def attn_bwd_kernel(
    blocks, limit, perm_ref, lengths_ref, qc_ref, qp_ref, k_in, v_in, pk_in, p_ref, linv_ref, gm_ref, mixed_ref,
    dq_ref, bias_ref, dk_out, dv_out, dpk_ref,
    meta, k_ref, v_ref, pk_ref, dk_ref, dv_ref, q2c_t, q2p_t, gm2, gm2_t, dd, carry, dqk, dqp, dpk, p_buf,
    empty, kv_sem, pk_sem, p_sem, out_sem,
):
    read_places(perm_ref, lengths_ref, meta, blocks, lengths_ref.shape[1])
    span = pk_in.shape[0]
    pk_copy = pltpu.make_async_copy(pk_in, pk_ref.at[0:span], pk_sem)
    pk_copy.start()
    arrive = load_keys(meta, blocks, limit, ((k_in, k_ref), (v_in, v_ref)), kv_sem)
    pk_ref[span:] = jnp.zeros((BLK, pk_ref.shape[1]), BF16)
    row, col = iotas()
    tri = col <= BLK - 1 - row
    tiles = p_ref.shape[0] // 2
    (low0, high0), (low1, high1) = needed_blocks(meta, blocks, limit)

    def out_copies(kb, nothing=False):
        slot = pl.ds(pl.multiple_of(meta[2 + kb] * BLK, BLK), BLK)
        place = pl.ds(pl.multiple_of((kb + 1) * BLK, BLK), BLK)
        return [
            pltpu.make_async_copy(empty if nothing else ref.at[:, place], out.at[:, slot], out_sem.at[index, kb])
            for index, (ref, out) in enumerate(((dk_ref, dk_out), (dv_ref, dv_out)))
        ]

    empty[...] = jnp.zeros_like(empty)
    for ref in (dk_ref, dv_ref):
        ref[:, 0:BLK] = jnp.zeros((ref.shape[0], BLK), BF16)

    def prepare(kb, _):
        used = ((kb >= low0) & (kb <= high0)) | ((kb >= low1) & (kb <= high1))

        @pl.when(used)
        def _():
            place = pl.ds(pl.multiple_of((kb + 1) * BLK, BLK), BLK)
            for ref in (dk_ref, dv_ref):
                ref[:, place] = jnp.zeros((ref.shape[0], BLK), BF16)

        @pl.when(jnp.logical_not(used))
        def _():
            for copy in out_copies(kb, True):
                copy.start()

        return 0

    lax.fori_loop(0, blocks, prepare, 0)
    dpk[...] = jnp.zeros_like(dpk)
    bias_ref[...] = jnp.zeros_like(bias_ref)

    def p_copy(slot, index):
        return pltpu.make_async_copy(p_ref.at[index], p_buf.at[slot], p_sem.at[slot])

    def one_query_block(a, _):
        qb, lowest, count = block_range(meta, a, blocks, limit)
        pairs = (count + 1) // 2
        rows_a = pl.ds(pl.multiple_of(a * BLK, BLK), BLK)
        p_copy(0, a * tiles + pairs - 1).start()
        for hp in range(PAIRS):
            lanes = slice(hp * BLK, (hp + 1) * BLK)
            rows = slice(2 * hp * BLK, 2 * (hp + 1) * BLK)
            q2c_t[hp] = stack_heads(flip_rows(qc_ref[rows_a, lanes].astype(F32))).T.astype(BF16)
            q2p_t[hp] = stack_heads(flip_rows(qp_ref[rows_a, lanes].astype(F32))).T.astype(BF16)
            g = stack_heads(gm_ref[rows_a, lanes].astype(F32))
            scaled = flip_two(g * linv_ref[a, rows])
            gm2[hp] = scaled.astype(BF16)
            gm2_t[hp] = scaled.T.astype(BF16)
            pair = flip_rows(mixed_ref[rows_a, lanes])
            dd[rows] = jnp.broadcast_to(
                jnp.sum(scaled * jnp.concatenate([pair, pair], axis=0), axis=1, keepdims=True), (2 * BLK, BLK)
            )
        carry[...] = jnp.zeros_like(carry)
        dqk[...] = jnp.zeros_like(dqk)
        dqp[...] = jnp.zeros_like(dqp)
        arrive(a)

        @pl.when(a == 0)
        def _():
            pk_copy.wait()

        def step(t, _):
            tile = pairs - 1 - t
            kb = qb - 2 * tile
            keys = pl.ds(pl.multiple_of(kb * BLK, BLK), 2 * BLK)
            drows = pl.ds(pl.multiple_of(2 * tile * BLK, BLK), 2 * BLK)
            slot = lax.rem(t, 2)
            p_copy(slot, 0).wait()

            @pl.when(tile >= 1)
            def _():
                p_copy(1 - slot, a * tiles + tile - 1).start()

            for hp in range(PAIRS):
                lanes = slice(hp * BLK, (hp + 1) * BLK)
                rows = slice(2 * hp * BLK, 2 * (hp + 1) * BLK)
                p = p_buf[slot, rows]
                g = dot_nt(gm2[hp], v_ref[keys, lanes])
                early = (p[:, :BLK].astype(F32) * (g[:, :BLK] - dd[rows])).astype(BF16)
                late = (p[:, BLK:].astype(F32) * (g[:, BLK:] - dd[rows])).astype(BF16)
                gs = jnp.concatenate([early, late], axis=1)
                early, late = early.astype(F32), late.astype(F32)
                rots = []
                for half in range(2):
                    part = slice(half * BLK, (half + 1) * BLK)
                    crow = slice((2 * hp + half) * BLK, (2 * hp + half + 1) * BLK)
                    far = jnp.where(tri, early[part], carry[crow])
                    near = jnp.where(tri, late[part], early[part])
                    carry[crow] = late[part]
                    rots.append(
                        jnp.concatenate(
                            [
                                pltpu.roll(near, 0, 1, stride=1, stride_axis=0).astype(BF16),
                                pltpu.roll(far, 0, 1, stride=1, stride_axis=0).astype(BF16),
                            ],
                            axis=1,
                        )
                    )
                rot = jnp.concatenate(rots, axis=0)
                dqk[hp] += dot_nn(gs, k_ref[keys, lanes])
                dqp[hp] += dot_nn(rot, pk_ref[drows, lanes])
                dk_ref[lanes, keys] = (dk_ref[lanes, keys].astype(F32) + dot_nn(q2c_t[hp], gs)).astype(BF16)
                dv_ref[lanes, keys] = (dv_ref[lanes, keys].astype(F32) + dot_nn(gm2_t[hp], p)).astype(BF16)
                dpk[lanes, drows] += dot_nn(q2p_t[hp], rot)
            for block in (kb - 1, kb):

                @pl.when((block >= 0) & ((a == 1) | (block < low1) | (block > high1)))
                def _():
                    for copy in out_copies(jnp.maximum(block, 0)):
                        copy.start()

            return 0

        lax.fori_loop(0, pairs, step, 0)
        lane = lax.broadcasted_iota(jnp.int32, (BLK, BLK), 1)
        for hp in range(PAIRS):
            lanes = slice(hp * BLK, (hp + 1) * BLK)
            ck = jnp.where(lane < HEAD, dqk[hp, :BLK], dqk[hp, BLK:]) * 0.125
            cp = jnp.where(lane < HEAD, dqp[hp, :BLK], dqp[hp, BLK:]) * 0.125
            dq_ref[rows_a, lanes] = flip_rows(ck + cp).astype(BF16)
            bias_ref[0:1, lanes] += jnp.sum(ck, axis=0, keepdims=True)
            bias_ref[1:2, lanes] += jnp.sum(cp, axis=0, keepdims=True)
        return 0

    lax.fori_loop(0, 2, one_query_block, 0)

    def given(kb, _):
        for copy in out_copies(kb):
            copy.wait()
        return 0

    dpk_ref[...] = dpk[:, 0:span].astype(BF16)
    lax.fori_loop(0, blocks, given, 0)


def attn_bwd(perm, lengths, qc, qp, k, v, pk, p, linv, gm, mixed, blocks, limit):
    tokens, width = qc.shape
    keys, span = k.shape[0], pk.shape[0]
    vmem = pl.BlockSpec(memory_space=pltpu.VMEM)
    hbm = pl.BlockSpec(memory_space=pl.ANY)
    return pl.pallas_call(
        functools.partial(attn_bwd_kernel, blocks, limit),
        out_shape=(
            jax.ShapeDtypeStruct((tokens, width), BF16),
            jax.ShapeDtypeStruct((8, width), F32),
            jax.ShapeDtypeStruct((width, keys), BF16),
            jax.ShapeDtypeStruct((width, keys), BF16),
            jax.ShapeDtypeStruct((width, span), BF16),
        ),
        in_specs=[pl.BlockSpec(memory_space=pltpu.SMEM)] * 2 + [vmem] * 2 + [hbm] * 4 + [vmem] * 3,
        out_specs=(vmem, vmem, hbm, hbm, vmem),
        scratch_shapes=[
            pltpu.SMEM((2 + blocks + lengths.shape[1],), jnp.int32),
            pltpu.VMEM((keys + BLK, width), BF16),
            pltpu.VMEM((keys + BLK, width), BF16),
            pltpu.VMEM((span + BLK, width), BF16),
            pltpu.VMEM((width, keys + BLK), BF16),
            pltpu.VMEM((width, keys + BLK), BF16),
            pltpu.VMEM((PAIRS, BLK, 2 * BLK), BF16),
            pltpu.VMEM((PAIRS, BLK, 2 * BLK), BF16),
            pltpu.VMEM((PAIRS, 2 * BLK, BLK), BF16),
            pltpu.VMEM((PAIRS, BLK, 2 * BLK), BF16),
            pltpu.VMEM((ROWS, BLK), F32),
            pltpu.VMEM((ROWS, BLK), F32),
            pltpu.VMEM((PAIRS, 2 * BLK, BLK), F32),
            pltpu.VMEM((PAIRS, 2 * BLK, BLK), F32),
            pltpu.VMEM((width, span + BLK), F32),
            pltpu.VMEM((2, ROWS, 2 * BLK), BF16),
            pltpu.VMEM((width, BLK), BF16),
            pltpu.SemaphoreType.DMA((2, blocks)),
            pltpu.SemaphoreType.DMA,
            pltpu.SemaphoreType.DMA((2,)),
            pltpu.SemaphoreType.DMA((2, blocks)),
        ],
        compiler_params=pltpu.CompilerParams(vmem_limit_bytes=62 * 2**20),
        cost_estimate=pl.CostEstimate(flops=6 * 10**9, bytes_accessed=30 * 2**20, transcendentals=0),
        name="attn_bwd",
    )(perm, lengths, qc, qp, k, v, pk, p, linv, gm, mixed)


MESH = pl.DeviceIdType.MESH


def fold_rows(x):
    return jnp.broadcast_to(x, (x.shape[0], BLK)).T[0:1]


def aligned(begin, size):
    return pl.ds(pl.multiple_of(begin, math.gcd(size, 16)), size)


def finish_kernel(
    lines, shards, chunks_f, sets, rows_l,
    mine_ref, come_ref, dk_ref, dv_ref, unit_all_ref, dpk_ref, table_ref, weights_in, dq_ref, x_ref,
    vectors_ref, total_ref, vec_ref, bias_ref, hidden_in,
    grad_ref, sums_ref, vsum_ref,
    dk_buf, dv_buf, un_buf, in_sem, dpk_buf, table_buf, weights_ref, hidden_ref, pos_sem, m_q, mt_k, mt_v, cs_q, cs_k, cs_v, dxp, bx0, bx1, bx2, vbuf, vacc,
    *rest,
):
    wk_ref, wv_ref, wq_ref = weights_ref.at[0], weights_ref.at[1], weights_ref.at[3]
    tokens, width = dq_ref.shape
    bufs_f = rest[: 3 * len(chunks_f)]
    bufs_l = rest[3 * len(chunks_f) : -2]
    send_sem, recv_sem = rest[-2:]
    ctx = lax.axis_index("ctx")
    w = lax.axis_index("wsh")
    core = lax.rem(ctx, 2)
    b = lax.rem(ctx // 2, 2)
    a = ctx // 4

    def at(a_to, b_to, core_to):
        return (a_to * 2 + b_to) * 2 + core_to

    def line_peer(s):
        return (at(lax.rem(a + s, lines), b, core), w)

    def shard_peer(s):
        return (ctx, lax.rem(w + s, shards))

    core_peer = (at(a, b, 1 - core), w)
    b_peer = (at(a, 1 - b, core), w)
    peers = [core_peer, b_peer] + [line_peer(s) for s in range(1, lines)] + [shard_peer(s) for s in range(1, shards)]
    barrier = pltpu.get_barrier_semaphore()
    for peer in peers:
        pl.semaphore_signal(barrier, inc=1, device_id=peer, device_id_type=MESH)

    counter = [0]

    def take(number):
        begin = counter[0]
        counter[0] += number
        return begin

    def remote(src, dst, index, peer):
        return pltpu.make_async_remote_copy(
            src_ref=src, dst_ref=dst, send_sem=send_sem.at[index], recv_sem=recv_sem.at[index],
            device_id=peer, device_id_type=MESH,
        )

    bits = lines.bit_length() - 1
    order = []
    for bit in range(bits):
        order += [m for m in reversed(range(lines)) if m & ((1 << (bit + 1)) - 1) == 1 << bit]
    order.append(0)

    def other(mask):
        place = 0
        for bit in range(bits):
            own = lax.rem(a // (1 << bit), 2)
            place = place + (1 << bit) * ((1 - own) if mask >> bit & 1 else own)
        return place

    def line_place(j):
        place = jnp.int32(0)
        for index, mask in enumerate(order):
            place = place + jnp.where(j == index, other(mask), 0)
        return place

    def line_at(mask):
        return (at(other(mask), b, core), w)

    group = 4 * tokens

    def fetch(j, slot):
        begin = pl.multiple_of(line_place(j) * group, group)
        return (
            pltpu.make_async_copy(dk_ref.at[:, pl.ds(begin, group)], dk_buf.at[slot], in_sem.at[slot, 0]),
            pltpu.make_async_copy(dv_ref.at[:, pl.ds(begin, group)], dv_buf.at[slot], in_sem.at[slot, 1]),
            pltpu.make_async_copy(unit_all_ref.at[pl.ds(begin, group)], un_buf.at[slot], in_sem.at[slot, 2]),
        )

    span, hold = table_ref.shape[0], table_buf.shape[0]
    pos_parts = [(begin, min(hold, span - begin)) for begin in range(0, span, hold)]

    def pos_copies(begin, size):
        rows = pl.ds(begin, size)
        return [
            pltpu.make_async_copy(dpk_ref.at[:, rows], dpk_buf.at[:, 0:size], pos_sem.at[0]),
            pltpu.make_async_copy(table_ref.at[rows], table_buf.at[0:size], pos_sem.at[1]),
        ]

    weights_copy = pltpu.make_async_copy(weights_in, weights_ref, pos_sem.at[2])
    hidden_copy = pltpu.make_async_copy(hidden_in, hidden_ref, pos_sem.at[3])
    weights_copy.start()
    for copy in fetch(0, 0):
        copy.start()
    for copy in pos_copies(*pos_parts[0]):
        copy.start()
    hidden_copy.start()

    def start_all(copies):
        for copy in copies:
            copy.start()

    def wait_all(copies):
        for copy in copies:
            copy.wait()

    def own_bit(bit):
        return lax.rem(a // (1 << bit), 2)

    def bit_peer(bit):
        return line_at(1 << bit)

    class Feed:
        def __init__(self, begin, rows, total_rows, bufs):
            self.begin, self.rows = begin, rows
            self.rc, self.rb = total_rows // 2, total_rows // 4
            self.b0, self.b1, self.b2 = bufs
            self.iy, self.irs, self.iag, self.ix, self.ic = take(shards - 1), take(bits), take(bits), take(1), take(2)

        def region(self, bit):
            start = 0
            for k in range(bit):
                start = start + own_bit(k) * (self.rows >> (k + 1))
            return start, self.rows >> bit

        def y_copies(self):
            return [
                remote(self.b0.at[lax.rem(w + s, shards)], self.b1.at[s - 1], self.iy + s - 1, shard_peer(s))
                for s in range(1, shards)
            ]

        def rs_copies(self, bit):
            start, size = self.region(bit)
            size = size // 2
            give = aligned(start + (1 - own_bit(bit)) * size, size)
            begin = sum(self.rows >> (k + 1) for k in range(bit))
            return [remote(self.b1.at[0, give], self.b2.at[begin : begin + size], self.irs + bit, bit_peer(bit))]

        def place(self, b_of, begin, size):
            return aligned(core * self.rc + b_of * self.rb + self.begin + begin, size)

        def ag_copies(self, bit):
            own = self.place(b, *self.region(bit + 1))
            return [remote(sums_ref.at[own], sums_ref.at[own], self.iag + bit, bit_peer(bit))]

        def x_copies(self):
            own = self.place(b, 0, self.rows)
            return [remote(sums_ref.at[own], sums_ref.at[own], self.ix, b_peer)]

        def c_copies(self):
            return [
                remote(sums_ref.at[rows], sums_ref.at[rows], self.ic + k, core_peer)
                for k, rows in enumerate((self.place(b, 0, self.rows), self.place(1 - b, 0, self.rows)))
            ]

        def y(self):
            rows = pl.ds(self.begin, self.rows)
            self.b0[...] = (mine_ref[:, rows].astype(F32) + come_ref[:, rows].astype(F32)).astype(BF16)
            start_all(self.y_copies())

        def rs(self, bit):
            if bit == 0:
                wait_all(self.y_copies())
                total = self.b0[w].astype(F32)
                for s in range(shards - 1):
                    total = total + self.b1[s].astype(F32)
                self.b1[0] = total.astype(BF16)
            else:
                self.add(bit - 1)
            start_all(self.rs_copies(bit))

        def add(self, bit):
            wait_all(self.rs_copies(bit))
            start, size = self.region(bit + 1)
            begin = sum(self.rows >> (k + 1) for k in range(bit))
            rows = aligned(start, size)
            self.b1[0, rows] = (self.b1[0, rows].astype(F32) + self.b2[begin : begin + size].astype(F32)).astype(BF16)

        def ag(self, bit):
            if bit == bits - 1:
                self.add(bit)
                start, size = self.region(bits)
                sums_ref[self.place(b, start, size)] = self.b1[0, aligned(start, size)]
            else:
                wait_all(self.ag_copies(bit + 1))
            start_all(self.ag_copies(bit))

        def x(self):
            wait_all(self.ag_copies(0))
            start_all(self.x_copies())

        def c(self):
            wait_all(self.x_copies())
            start_all(self.c_copies())

        def done(self):
            wait_all(self.c_copies())

    class Late:
        def __init__(self, out, rows, names, bufs):
            self.out, self.rows, self.names, self.begun = out, rows, names, set()
            self.src, self.b0, self.b1, self.b2, self.b3 = bufs
            self.rc, self.rb, self.share = rows // 2, rows // 4, rows // 4 // lines
            self.i0, self.iy, self.i2 = take(1), take(shards - 1), take(1)
            self.irs, self.iag, self.ix, self.ic = take(lines - 1), take(lines - 1), take(1), take(1)

        def c0_copies(self):
            return [remote(self.src.at[:, aligned((1 - core) * self.rc, self.rc)], self.b0, self.i0, core_peer)]

        def y_copies(self):
            return [
                remote(self.b0.at[lax.rem(w + s, shards)], self.b1.at[s - 1], self.iy + s - 1, shard_peer(s))
                for s in range(1, shards)
            ]

        def x0_copies(self):
            return [remote(self.b1.at[0, aligned((1 - b) * self.rb, self.rb)], self.b2, self.i2, b_peer)]

        def rs_copies(self):
            return [
                remote(
                    self.b2.at[aligned(lax.rem(a + s, lines) * self.share, self.share)],
                    self.b3.at[s - 1], self.irs + s - 1, line_peer(s),
                )
                for s in range(1, lines)
            ]

        def ag_copies(self):
            own = aligned(self.out + core * self.rc + b * self.rb + a * self.share, self.share)
            return [remote(sums_ref.at[own], sums_ref.at[own], self.iag + s - 1, line_peer(s)) for s in range(1, lines)]

        def x_copies(self):
            own = aligned(self.out + core * self.rc + b * self.rb, self.rb)
            return [remote(sums_ref.at[own], sums_ref.at[own], self.ix, b_peer)]

        def c_copies(self):
            own = aligned(self.out + core * self.rc, self.rc)
            return [remote(sums_ref.at[own], sums_ref.at[own], self.ic, core_peer)]

        def c0(self):
            for m, name in enumerate(self.names):
                grad = gradient(name)
                for s in range(shards):
                    self.src[s, m * rows_out : (m + 1) * rows_out] = grad[s * rows_out : (s + 1) * rows_out].astype(BF16)
            used = len(self.names) * rows_out
            if used < rows_l:
                self.src[:, used:] = jnp.zeros((shards, rows_l - used, width), BF16)
            start_all(self.c0_copies())

        def y(self):
            wait_all(self.c0_copies())
            own = self.src[:, aligned(core * self.rc, self.rc)]
            self.b0[...] = (self.b0[...].astype(F32) + own.astype(F32)).astype(BF16)
            start_all(self.y_copies())

        def x0(self):
            wait_all(self.y_copies())
            total = self.b0[w].astype(F32)
            for s in range(shards - 1):
                total = total + self.b1[s].astype(F32)
            self.b1[0] = total.astype(BF16)
            start_all(self.x0_copies())

        def rs(self):
            wait_all(self.x0_copies())
            own = self.b1[0, aligned(b * self.rb, self.rb)]
            self.b2[...] = (self.b2[...].astype(F32) + own.astype(F32)).astype(BF16)
            start_all(self.rs_copies())

        def ag(self):
            wait_all(self.rs_copies())
            total = self.b2[aligned(a * self.share, self.share)].astype(F32)
            for s in range(lines - 1):
                total = total + self.b3[s].astype(F32)
            own = aligned(self.out + core * self.rc + b * self.rb + a * self.share, self.share)
            sums_ref[own] = total.astype(BF16)
            start_all(self.ag_copies())

        def x(self):
            wait_all(self.ag_copies())
            start_all(self.x_copies())

        def c(self):
            wait_all(self.x_copies())
            start_all(self.c_copies())

        def done(self):
            wait_all(self.c_copies())

    rows_f = 4 * sum(chunks_f)
    rows_out = width // shards
    feeds = []
    begin = 0
    for index, rows in enumerate(chunks_f):
        feeds.append(Feed(begin, rows, rows_f, bufs_f[3 * index : 3 * index + 3]))
        begin += rows
    lates = {}
    for index, names in enumerate(sets):
        late = Late(rows_f + index * rows_l, rows_l, names, bufs_l[5 * index : 5 * index + 5])
        for name in names:
            lates[name] = late

    def late_step(name, step):
        late = lates[name]
        if step not in late.begun:
            late.begun.add(step)
            getattr(late, step)()

    values = x_ref[...].astype(F32)
    center = values - jnp.mean(values, axis=1, keepdims=True)
    inverse = lax.rsqrt(jnp.mean(center * center, axis=1, keepdims=True) + epsilon)
    unit = center * inverse

    def gradient(name):
        cols = vectors_ref[0:8].T
        gain_col, bias_col = cols[:, 0:1], cols[:, 1:2]
        if name == "q":
            m_q[...] = dot_tn(unit.astype(BF16), dq_ref[...])
            cs_q[...] = jnp.broadcast_to(jnp.sum(dq_ref[...].astype(F32), axis=0, keepdims=True), cs_q.shape)
            return gain_col * m_q[...] + bias_col * cs_q[0:1]
        if name == "p":
            total = jnp.zeros((width, width), F32)
            for index, (begin, size) in enumerate(pos_parts):
                if index:
                    start_all(pos_copies(begin, size))
                wait_all(pos_copies(begin, size))
                total = total + dot_nn(dpk_buf[:, 0:size], table_buf[0:size])
            return total.T
        m, cs = (mt_k, cs_k) if name == "k" else (mt_v, cs_v)
        return gain_col * m[...] + bias_col * fold_rows(cs[:, 0:1])

    mt_k[...] = jnp.zeros_like(mt_k)
    mt_v[...] = jnp.zeros_like(mt_v)
    cs_k[...] = jnp.zeros_like(cs_k)
    cs_v[...] = jnp.zeros_like(cs_v)
    pl.semaphore_wait(barrier, len(peers))
    feeds[-1].y()
    weights_copy.wait()

    i_x0, i_x1, i_x2 = take(lines), take(lines), take(lines)

    def copy_x0(j):
        return remote(dxp.at[j, 1 - core], bx0.at[j], i_x0 + j, core_peer)

    def copy_x1(j):
        return remote(bx0.at[j, 1 - b], bx1.at[j], i_x1 + j, b_peer)

    def copy_x2(mask):
        return remote(bx1.at[order.index(mask)], bx2.at[mask - 1], i_x2 + mask, line_at(mask & -mask))

    def after_x0(j):
        copy_x0(j).wait()
        bx0[j] = (bx0[j].astype(F32) + dxp[j, core].astype(F32)).astype(BF16)
        copy_x1(j).start()

    def after_x1(j):
        mask = order[j]
        copy_x1(j).wait()
        total = bx1[j].astype(F32) + bx0[j, b].astype(F32)
        for bit in range(bits):
            if mask and 1 << bit >= (mask & -mask):
                break
            source = mask | 1 << bit
            copy_x2(source).wait()
            total = total + bx2[source - 1].astype(F32)
        if mask:
            bx1[j] = total.astype(BF16)
            copy_x2(mask).start()
        return total

    last = lines - 1
    events = {}

    def plan(j, after, work, *args):
        events.setdefault((min(j, last), after), []).append((work, args))

    one, two = feeds[0], feeds[-1]
    pair = len(feeds) > 1

    def along(feed, stage):
        begin, end = ((1, bits), (bits, bits + 1), (bits + 1, 2 * bits))[stage - 1]
        for step in range(begin, end):
            if step < bits:
                feed.rs(step)
            else:
                feed.ag(2 * bits - 1 - step)

    plan(0, "first", late_step, "q", "c0")
    plan(0, "blocks", after_x0, 0)
    plan(0, "blocks", late_step, "q", "y")
    plan(0, "blocks", late_step, "p", "c0")
    plan(1, "first", late_step, "p", "y")
    plan(1, "first", two.rs, 0)
    if pair:
        plan(1, "first", one.y)
    plan(1, "all", late_step, "q", "x0")
    if lines == 4:
        plan(1, "all", after_x1, 0)
        plan(1, "all", after_x0, 1)
    else:
        for j in range(1, last):
            plan(j + 1, "first", after_x0, j)
    plan(3, "first" if last >= 3 else "all", along, two, 1)
    plan(3, "blocks" if last >= 3 else "all", late_step, "p", "x0")
    plan(3, "blocks" if last >= 3 else "all", late_step, "q", "rs")

    def happen(j, after):
        for (when, place), works in sorted(events.items()):
            if place == after:

                @pl.when(j == when)
                def _():
                    for work, args in works:
                        work(*args)

    def line_step(j, _):
        slot = lax.rem(j, 2)

        @pl.when(j < last)
        def _():
            start_all(fetch(j + 1, 1 - slot))

        wait_all(fetch(j, slot))

        def make_block(core_of, b_of):
            keys = pl.ds(pl.multiple_of((2 * b_of + core_of) * tokens, tokens), tokens)
            part = dot_nn(wk_ref[...], dk_buf[slot, :, keys]) + dot_nn(wv_ref[...], dv_buf[slot, :, keys])
            dxp[j, core_of, b_of] = part.astype(BF16)

        make_block(1 - core, 0)
        make_block(1 - core, 1)
        copy_x0(j).start()
        happen(j, "first")
        make_block(core, 0)
        make_block(core, 1)
        happen(j, "blocks")
        mt_k[...] += dot_nn(dk_buf[slot], un_buf[slot])
        mt_v[...] += dot_nn(dv_buf[slot], un_buf[slot])
        for cs, buf in ((cs_k, dk_buf), (cs_v, dv_buf)):
            total = cs[...]
            for piece in range(group // BLK):
                total = total + buf[slot, :, piece * BLK : (piece + 1) * BLK].astype(F32)
            cs[...] = total
        happen(j, "all")
        return 0

    lax.fori_loop(0, lines, line_step, 0)
    for m, cs in ((mt_k, cs_k), (mt_v, cs_v)):
        m[...] = m[...].T
        cs[...] = jnp.broadcast_to(jnp.sum(cs[...], axis=1, keepdims=True), cs.shape)

    vstages = [[core_peer], [b_peer], [line_peer(s) for s in range(1, lines)], [shard_peer(s) for s in range(1, shards)]]
    vslots = []
    place = 0
    for stage in vstages:
        vslots.append(place)
        place += len(stage)
    vbegin = take(place)

    def v_copy(stage, index):
        slot = vslots[stage] + index
        return remote(vacc.at[pl.ds(stage * 16, 16)], vbuf.at[slot], vbegin + slot, vstages[stage][index])

    def v_start(stage):
        for index in range(len(vstages[stage])):
            v_copy(stage, index).start()

    def v_finish(stage):
        total = vacc[stage * 16 : stage * 16 + 16]
        for index in range(len(vstages[stage])):
            v_copy(stage, index).wait()
            total = total + vbuf[vslots[stage] + index]
        vacc[(stage + 1) * 16 : (stage + 2) * 16] = total

    def vectors_begin():
        vacc[0:16] = vec_ref[...]
        vacc[2:4] = bias_ref[0:2]
        gain_grad = m_q[...] * wq_ref[...].astype(F32)
        gain_grad = gain_grad + mt_k[...] * wk_ref[...].astype(F32) + mt_v[...] * wv_ref[...].astype(F32)
        vacc[0:1] = fold_rows(jnp.sum(gain_grad, axis=1, keepdims=True))
        total = dot_nt(cs_q[...].astype(BF16), wq_ref[...])
        for cs, weight in ((cs_k, wk_ref), (cs_v, wv_ref)):
            row = jnp.broadcast_to(fold_rows(cs[:, 0:1]), (8, width))
            total = total + dot_nt(row.astype(BF16), weight[...])
        vacc[1:2] = total[0:1]
        v_start(0)

    if pair:
        one.rs(0)
    after_x0(last)
    late_step("k", "c0")
    if lines == 4:
        after_x0(2)
    else:
        after_x1(0)
    along(two, 2)
    late_step("p", "rs")
    late_step("v", "c0")
    late_step("k", "y")
    late_step("q", "ag")
    vectors_begin()
    late_step("v", "y")
    if pair:
        along(one, 1)
    along(two, 3)
    late_step("p", "ag")
    v_finish(0)
    v_start(1)
    late_step("k", "x0")
    if pair:
        along(one, 2)
    late_step("v", "x0")
    v_finish(1)
    v_start(2)
    two.x()
    late_step("k", "rs")
    late_step("p", "x")
    late_step("v", "rs")
    if pair:
        along(one, 3)
    late_step("k", "ag")
    late_step("q", "x")
    late_step("v", "ag")
    for j in reversed(range(1, last)) if lines == 4 else range(1, last):
        after_x1(j)
    if pair:
        one.x()
    two.c()
    late_step("k", "x")
    late_step("p", "c")
    v_finish(2)
    v_start(3)
    late_step("v", "x")
    late_step("q", "c")
    if pair:
        one.c()
    own = after_x1(last)
    scaled = (own.T + dot_nt(dq_ref[...], wq_ref[...])) * vectors_ref[0:1]
    hidden_copy.wait()
    grad_ref[...] = hidden_ref[...] + inverse * (
        scaled - jnp.mean(scaled, axis=1, keepdims=True) - unit * jnp.mean(scaled * unit, axis=1, keepdims=True)
    )
    late_step("k", "c")
    late_step("v", "c")
    v_finish(3)
    vsum_ref[...] = vacc[4 * 16 : 5 * 16]
    for feed in feeds:
        feed.done()
    for name in "qpkv":
        late_step(name, "done")


def finish(lines, shards, chunks_f, sets, rows_l, cid, mine, come, dk, dv, unit_all, dpk, table, weights, dq, x, vectors, total, vec, bias, hidden):
    tokens, width = dq.shape
    vmem = pl.BlockSpec(memory_space=pltpu.VMEM)
    hbm = pl.BlockSpec(memory_space=pl.ANY)
    bufs = []
    for rows in chunks_f:
        bufs += [
            pltpu.VMEM((shards, rows, width), BF16),
            pltpu.VMEM((shards - 1, rows, width), BF16),
            pltpu.VMEM((rows, width), BF16),
        ]
    for names in sets:
        bufs += [
            pltpu.VMEM((shards, rows_l, width), BF16),
            pltpu.VMEM((shards, rows_l // 2, width), BF16),
            pltpu.VMEM((shards - 1, rows_l // 2, width), BF16),
            pltpu.VMEM((rows_l // 4, width), BF16),
            pltpu.VMEM((lines - 1, rows_l // 4 // lines, width), BF16),
        ]
    hops = shards - 1 + 2 * (lines - 1)
    copies = len(chunks_f) * (shards + 2 + 2 * (lines.bit_length() - 1)) + len(sets) * (hops + 4) + 3 * lines + 2 + lines - 1 + shards - 1
    total_rows = 4 * sum(chunks_f) + len(sets) * rows_l
    stages = 1 + 1 + (lines - 1) + (shards - 1)
    hold = min(dpk.shape[1], 17 * BLK)
    return pl.pallas_call(
        functools.partial(finish_kernel, lines, shards, tuple(chunks_f), sets, rows_l),
        out_shape=(
            jax.ShapeDtypeStruct((tokens, width), F32),
            jax.ShapeDtypeStruct((total_rows, width), BF16),
            jax.ShapeDtypeStruct((16, width), F32),
        ),
        in_specs=[vmem] * 2 + [hbm] * 6 + [vmem] * 6 + [hbm],
        out_specs=(vmem,) * 3,
        scratch_shapes=[
            pltpu.VMEM((2, width, 4 * tokens), BF16),
            pltpu.VMEM((2, width, 4 * tokens), BF16),
            pltpu.VMEM((2, 4 * tokens, width), BF16),
            pltpu.SemaphoreType.DMA((2, 3)),
            pltpu.VMEM((width, hold), BF16),
            pltpu.VMEM((hold, width), BF16),
            pltpu.VMEM((4, width, width), BF16),
            pltpu.VMEM((tokens, width), F32),
            pltpu.SemaphoreType.DMA((4,)),
            pltpu.VMEM((width, width), F32),
            pltpu.VMEM((width, width), F32),
            pltpu.VMEM((width, width), F32),
            pltpu.VMEM((8, width), F32),
            pltpu.VMEM((width, BLK), F32),
            pltpu.VMEM((width, BLK), F32),
            pltpu.VMEM((lines, 2, 2, width, tokens), BF16),
            pltpu.VMEM((lines, 2, width, tokens), BF16),
            pltpu.VMEM((lines, width, tokens), BF16),
            pltpu.VMEM((lines - 1, width, tokens), BF16),
            pltpu.VMEM((stages, 16, width), F32),
            pltpu.VMEM((5 * 16, width), F32),
        ]
        + bufs
        + [pltpu.SemaphoreType.DMA((copies,)), pltpu.SemaphoreType.DMA((copies,))],
        compiler_params=pltpu.CompilerParams(
            collective_id=cid, has_side_effects=True, vmem_limit_bytes=63 * 2**20
        ),
        cost_estimate=pl.CostEstimate(flops=10**10, bytes_accessed=30 * 2**20, transcendentals=0),
        name="finish",
    )(mine, come, dk, dv, unit_all, dpk, table, weights, dq, x, vectors, total, vec, bias, hidden)


def unpack_kernel(
    shards, rows_f, sets, rows_l, sums_ref, vsum_ref, total_ref, grad_ref, result_ref,
    grad_out, result_out, q_out, k_out, v_out, o_out, p_out, u_out, d_out, g1_out, b1_out, cb_out, pb_out, g2_out, b2_out, bd_out, bu_out,
    loss_out,
    low, wide, up, in_sem, out_sem,
):
    width = vsum_ref.shape[1]
    rows_out, rows_up = q_out.shape[0], d_out.shape[0]
    parts = u_out.shape[1] // width
    w = lax.axis_index("wsh")
    pieces = [(rows_up, d_out), (2 * rows_up, o_out)]
    to = {"q": q_out, "p": p_out, "k": k_out, "v": v_out}
    for index, names in enumerate(sets):
        pieces += [(rows_f + index * rows_l + m * rows_out, to[name]) for m, name in enumerate(names)]
    ins = [pltpu.make_async_copy(sums_ref.at[0:rows_up], low.at[0:rows_up], in_sem.at[0])]
    for index, (begin, out) in enumerate(pieces):
        size = out.shape[0]
        ins.append(pltpu.make_async_copy(sums_ref.at[begin : begin + size], low.at[begin : begin + size], in_sem.at[1 + index]))
    for copy in ins:
        copy.start()
    outs = [
        pltpu.make_async_copy(grad_ref, grad_out, out_sem.at[7]),
        pltpu.make_async_copy(result_ref, result_out, out_sem.at[8]),
    ]
    for copy in outs:
        copy.start()
    ins[0].wait()
    for c in range(parts):
        up[:, c * width : (c + 1) * width] = low[c * rows_out : (c + 1) * rows_out].astype(F32)
    outs.append(pltpu.make_async_copy(up, u_out, out_sem.at[0]))
    outs[2].start()
    for index, (begin, out) in enumerate(pieces):
        size = out.shape[0]
        ins[1 + index].wait()
        wide[begin : begin + size] = low[begin : begin + size].astype(F32)
        copy = pltpu.make_async_copy(wide.at[begin : begin + size], out, out_sem.at[1 + index])
        copy.start()
        outs.append(copy)

    def share(row):
        part = vsum_ref[row : row + 1, 0:rows_out]
        for s in range(1, shards):
            part = jnp.where(w == s, vsum_ref[row : row + 1, s * rows_out : (s + 1) * rows_out], part)
        return part.reshape(rows_out)

    for row, ref in enumerate((g1_out, b1_out, cb_out, pb_out, g2_out, b2_out, bd_out)):
        ref[...] = share(row)
    per = rows_up // rows_out
    for q in range(per):
        part = None
        for s in range(shards):
            group = s * per + q
            row, place = 7 + group // shards, group % shards
            piece = vsum_ref[row : row + 1, place * rows_out : (place + 1) * rows_out]
            part = piece if part is None else jnp.where(w == s, piece, part)
        bu_out[q * rows_out : (q + 1) * rows_out] = part.reshape(rows_out)
    loss_out[0, 0] = vsum_ref[7 + parts, 0] / (total_ref[0, 0] * width)
    for copy in outs:
        copy.wait()


def unpack(shards, rows_f, sets, rows_l, hidden, sums, vsum, total, grad, result):
    tokens, width = grad.shape
    rows_out, rows_up = width // shards, hidden // shards
    vmem = pl.BlockSpec(memory_space=pltpu.VMEM)
    hbm = pl.BlockSpec(memory_space=pl.ANY)
    square = jax.ShapeDtypeStruct((rows_out, width), F32)
    vector = jax.ShapeDtypeStruct((rows_out,), F32)
    return pl.pallas_call(
        functools.partial(unpack_kernel, shards, rows_f, sets, rows_l),
        out_shape=(
            jax.ShapeDtypeStruct((tokens, width), F32), jax.ShapeDtypeStruct((tokens, width), BF16), square, square, square, square, square,
            jax.ShapeDtypeStruct((rows_out, hidden), F32), jax.ShapeDtypeStruct((rows_up, width), F32),
            vector, vector, vector, vector, vector, vector, vector, jax.ShapeDtypeStruct((rows_up,), F32),
            jax.ShapeDtypeStruct((1, 1), F32),
        ),
        in_specs=[hbm, vmem, vmem, vmem, vmem],
        out_specs=(hbm,) * 9 + (vmem,) * 8 + (pl.BlockSpec(memory_space=pltpu.SMEM),),
        scratch_shapes=[
            pltpu.VMEM(sums.shape, BF16),
            pltpu.VMEM(sums.shape, F32),
            pltpu.VMEM((rows_out, hidden), F32),
            pltpu.SemaphoreType.DMA((7,)),
            pltpu.SemaphoreType.DMA((9,)),
        ],
        compiler_params=pltpu.CompilerParams(vmem_limit_bytes=62 * 2**20),
        cost_estimate=pl.CostEstimate(flops=10**6, bytes_accessed=12 * 2**20, transcendentals=0),
        name="unpack",
    )(sums, vsum, total, grad, result)


PARTS = 2


def start_kernel(
    lines, shards, x_ref, wk_ref, wv_ref, wp_ref, wq_ref, wo_ref, wu_ref, wd_ref,
    g1_ref, b1_ref, cb_ref, pb_ref, g2_ref, b2_ref, bd_ref, bu_ref, mask_ref, far_ref, near_ref,
    k_ref, v_ref, unit_ref, pk_ref, table_ref, qc_ref, qp_ref, weights_ref, wo_out, wu_out, wd_out, vectors_ref, total_ref,
    x_all, k_buf, v_buf, pk_buf, t_buf, wo_buf, wu_buf, wd_buf, vec_src, vec_buf, cnt_buf, cnt_acc,
    up_send, up_recv, down_send, down_recv, b_send, b_recv, c_send, c_recv,
    y_send, y_recv, yc_send, yc_recv, d_send, d_recv, s_send, s_recv, out_sem, pos_sem, own_sem,
):
    tokens, width = x_ref.shape
    piece = tokens // PARTS
    half = width // 2
    chunks = pk_buf.shape[0] // BLK
    ctx = lax.axis_index("ctx")
    w = lax.axis_index("wsh")
    core = lax.rem(ctx, 2)
    b = lax.rem(ctx // 2, 2)
    a = ctx // 4

    def at(a_to, b_to, core_to):
        return (a_to * 2 + b_to) * 2 + core_to

    def shard_peer(s):
        return (ctx, lax.rem(w + s, shards))

    def line_peer(s):
        return (at(lax.rem(a + s, lines), b, core), w)

    core_peer = (at(a, b, 1 - core), w)
    b_peer = (at(a, 1 - b, core), w)
    peers = [core_peer, b_peer] + [line_peer(s) for s in range(1, lines)] + [shard_peer(s) for s in range(1, shards)]
    barrier = pltpu.get_barrier_semaphore()
    for peer in peers:
        pl.semaphore_signal(barrier, inc=1, device_id=peer, device_id_type=MESH)

    def remote(src, dst, send, recv, peer):
        return pltpu.make_async_remote_copy(
            src_ref=src, dst_ref=dst, send_sem=send, recv_sem=recv, device_id=peer, device_id_type=MESH
        )

    def block(slot):
        return aligned(slot * tokens, tokens)

    def unit_of(rows):
        values = rows.astype(F32)
        center = values - jnp.mean(values, axis=1, keepdims=True)
        return center * lax.rsqrt(jnp.mean(center * center, axis=1, keepdims=True) + epsilon)

    x_all[block(ctx)] = unit_of(x_ref[...]).astype(BF16)
    rows_out = wq_ref.shape[0]
    quarter = rows_out // 2
    rows_up = wd_ref.shape[0]
    weight_in = (wk_ref, wv_ref, wp_ref, wq_ref, wo_ref, wu_ref)
    weight_to = tuple(weights_ref.at[m] for m in range(4)) + (wo_buf, wu_buf)
    own_copies = [
        pltpu.make_async_copy(ref, to.at[aligned(w * rows_out, rows_out)], own_sem.at[m])
        for m, (ref, to) in enumerate(zip(weight_in[:4], weight_to))
    ]
    for copy in own_copies:
        copy.start()
    vec_src[...] = jnp.zeros_like(vec_src)
    for row, ref in enumerate((g1_ref, b1_ref, cb_ref, pb_ref, g2_ref, b2_ref, bd_ref)):
        vec_src[row : row + 1] = ref[...].astype(F32).reshape(1, rows_out)
    bias_rows = rows_up // rows_out
    for q in range(bias_rows):
        vec_src[7 + q : 8 + q] = bu_ref[q * rows_out : (q + 1) * rows_out].astype(F32).reshape(1, rows_out)
    cnt_acc[0:8] = jnp.broadcast_to(jnp.sum(mask_ref[...].astype(F32), axis=1, keepdims=True), (8, BLK))
    pl.semaphore_wait(barrier, len(peers))

    def x_copy(slot, h, send, recv, peer):
        rows = aligned(slot * tokens + h * piece, piece)
        return remote(x_all.at[rows], x_all.at[rows], send, recv, peer)

    def up_copy(p, h):
        peer = (at(jnp.minimum(a + 1, lines - 1), b, core), w)
        return x_copy(at(p, b, core), h, up_send.at[p, h], up_recv.at[p, h], peer)

    def down_copy(p, h):
        peer = (at(jnp.maximum(a - 1, 0), b, core), w)
        return x_copy(at(p, b, core), h, down_send.at[p, h], down_recv.at[p, h], peer)

    def b_copy(p, h, b_from):
        return x_copy(at(p, b_from, core), h, b_send.at[p, h], b_recv.at[p, h], b_peer)

    def c_copy(p, far, b_from, core_from):
        rows = block(at(p, b_from, core_from))
        return remote(x_all.at[rows], x_all.at[rows], c_send.at[far, p], c_recv.at[far, p], core_peer)

    def weight_copy(m, s):
        rows = aligned(w * rows_out + core * quarter, quarter)
        src = weight_in[m].at[aligned(core * quarter, quarter)]
        return remote(src, weight_to[m].at[rows], y_send.at[m, s - 1], y_recv.at[m, s - 1], shard_peer(s))

    def weight_pass(m, s):
        rows = aligned(lax.rem(w + shards - s, shards) * rows_out + core * quarter, quarter)
        return remote(
            weight_to[m].at[rows], weight_to[m].at[rows], yc_send.at[m, s - 1], yc_recv.at[m, s - 1], core_peer
        )

    low = lax.rem(a, 2)
    quarter_in, quarter_to = (wd_ref,), (wd_buf,)
    pair_peer = (at(a + 1 - 2 * low, b, core), w)

    def quarter_rows(m, s, low_of):
        size = quarter_in[m].shape[0]
        owner = lax.rem(w + shards - s, shards)
        return aligned(owner * size + (low_of * 2 + core) * (size // 4), size // 4)

    def quarter_copy(m, s):
        size = quarter_in[m].shape[0]
        src = quarter_in[m].at[aligned((low * 2 + core) * (size // 4), size // 4)]
        dst = quarter_to[m].at[quarter_rows(m, 0, low)]
        return remote(src, dst, d_send.at[m, 0, s - 1], d_recv.at[m, 0, s - 1], shard_peer(s))

    def quarter_pass(m, kind, s):
        rows = quarter_rows(m, s, 1 - low if kind == 3 else low)
        peer = pair_peer if kind == 1 else core_peer
        ref = quarter_to[m].at[rows]
        return remote(ref, ref, d_send.at[m, kind, s - 1], d_recv.at[m, kind, s - 1], peer)

    def quarter_on(m):
        for s in range(1, shards):
            quarter_copy(m, s).wait()
            quarter_pass(m, 1, s).start()
            quarter_pass(m, 2, s).start()

    def vec_copy(s):
        return remote(vec_src, vec_buf.at[s - 1], s_send.at[s - 1], s_recv.at[s - 1], shard_peer(s))

    stages = [[shard_peer(s) for s in range(1, shards)], [core_peer], [b_peer], [line_peer(s) for s in range(1, lines)]]
    slots = []
    place = 0
    for stage in stages:
        slots.append(place)
        place += len(stage)

    def cnt_copy(stage, index):
        slot = slots[stage] + index
        sem = shards - 1 + slot
        return remote(cnt_acc.at[pl.ds(stage * 8, 8)], cnt_buf.at[slot], s_send.at[sem], s_recv.at[sem], stages[stage][index])

    def cnt_start(stage):
        for index in range(len(stages[stage])):
            cnt_copy(stage, index).start()

    def cnt_finish(stage):
        total = cnt_acc[stage * 8 : stage * 8 + 8]
        for index in range(len(stages[stage])):
            cnt_copy(stage, index).wait()
            total = total + cnt_buf[slots[stage] + index]
        cnt_acc[(stage + 1) * 8 : (stage + 2) * 8] = total

    for s in range(1, shards):
        vec_copy(s).start()
    cnt_start(0)
    for h in range(PARTS):

        @pl.when(a + 1 < lines)
        def _():
            up_copy(a, h).start()

        @pl.when(a >= 1)
        def _():
            down_copy(a, h).start()

        b_copy(a, h, b).start()
    c_copy(a, 0, b, core).start()
    for kind, m in ((0, 0), (0, 1), (1, 0), (0, 2), (0, 3), (0, 5), (0, 4)):
        for s in range(1, shards):
            (quarter_copy if kind else weight_copy)(m, s).start()


    def table_step(d, _):
        sin_far, cos_far = far_ref[0, pl.ds(d, 1)], far_ref[1, pl.ds(d, 1)]
        sin_near, cos_near = near_ref[0], near_ref[1]
        rows = aligned(d * BLK, BLK)
        t_buf[rows, :half] = (sin_far * cos_near - cos_far * sin_near).astype(BF16)
        t_buf[rows, half:] = (cos_far * cos_near + sin_far * sin_near).astype(BF16)
        return 0

    lax.fori_loop(0, chunks, table_step, 0)
    table_out = pltpu.make_async_copy(t_buf, table_ref, pos_sem.at[0])
    table_out.start()
    lane_to = lax.broadcasted_iota(jnp.int32, (rows_out, width), 1)
    lane_from = lax.broadcasted_iota(jnp.int32, (rows_out, width), 0)
    row_at = lax.broadcasted_iota(jnp.int32, (16, width), 0)

    def spread(values, place):
        return dot_nn(values.astype(BF16), (lane_to == lane_from + place * rows_out).astype(BF16))

    def placed(values, owner):
        full = jnp.where(row_at < 7, spread(values, owner), 0.0)
        for q in range(bias_rows):
            group = owner * bias_rows + q
            row = jnp.broadcast_to(values[7 + q : 8 + q], values.shape)
            full = full + jnp.where(row_at == 7 + group // shards, spread(row, lax.rem(group, shards)), 0.0)
        return full

    vectors = placed(vec_src[...], w)
    for s in range(1, shards):
        vec_copy(s).wait()
        vectors = vectors + placed(vec_buf[s - 1], lax.rem(w + shards - s, shards))
    vectors_ref[...] = vectors
    cnt_finish(0)
    cnt_start(1)

    def out_copies(slot):
        rows = block(slot)
        return (
            pltpu.make_async_copy(k_buf.at[rows], k_ref.at[rows], out_sem.at[0, slot]),
            pltpu.make_async_copy(v_buf.at[rows], v_ref.at[rows], out_sem.at[1, slot]),
            pltpu.make_async_copy(x_all.at[rows], unit_ref.at[rows], out_sem.at[2, slot]),
        )

    def project(p):
        def one(q, _):
            other_b = lax.rem(q, 2)
            other_core = q // 2

            @pl.when(q == 1)
            def _():
                for h in range(PARTS):
                    b_copy(p, h, b).wait()
                c_copy(p, 1, 1 - b, core).start()

            @pl.when(q == 2)
            def _():
                c_copy(p, 0, b, core).wait()

            @pl.when(q == 3)
            def _():
                c_copy(p, 1, 1 - b, core).wait()

            slot = at(p, b + other_b - 2 * b * other_b, core + other_core - 2 * core * other_core)
            rows = block(slot)
            normed = (x_all[rows].astype(F32) * vectors_ref[0:1] + vectors_ref[1:2]).astype(BF16)
            k_buf[rows] = dot_nn(normed, weights_ref[0]).astype(BF16)
            v_buf[rows] = dot_nn(normed, weights_ref[1]).astype(BF16)
            for copy in out_copies(slot):
                copy.start()
            return 0

        lax.fori_loop(0, 4, one, 0)

    def pos_step(d, _):
        rows = aligned(d * BLK, BLK)
        pk_buf[rows] = dot_nn(t_buf[rows], weights_ref[2]).astype(BF16)
        return 0

    last = lines - 1

    def line_step(s, _):
        below, high = a - 1 - s, a + 1 + s

        for h in range(PARTS):

            @pl.when((s < lines - 1) & (below >= 0))
            def _():
                p = jnp.maximum(below, 0)
                up_copy(p, h).wait_recv()

                @pl.when(a + 1 < lines)
                def _():
                    up_copy(p, h).start()

                b_copy(p, h, b).start()
                if h == PARTS - 1:
                    c_copy(p, 0, b, core).start()

            @pl.when((s < lines - 1) & (high < lines))
            def _():
                p = jnp.minimum(high, lines - 1)
                down_copy(p, h).wait_recv()

                @pl.when(a >= 1)
                def _():
                    down_copy(p, h).start()

                b_copy(p, h, b).start()
                if h == PARTS - 1:
                    c_copy(p, 0, b, core).start()

        @pl.when(s == 0)
        def _():
            cnt_finish(1)
            cnt_start(2)

        @pl.when(s == 1)
        def _():
            for copy in own_copies:
                copy.wait()
            for m in range(2):
                for t in range(1, shards):
                    weight_copy(m, t).wait()
                    weight_pass(m, t).start()
            cnt_finish(2)
            cnt_start(3)
            for m in range(2):
                for t in range(1, shards):
                    weight_pass(m, t).wait()

        @pl.when(s == min(2, last))
        def _():
            for t in range(1, shards):
                weight_copy(2, t).wait()
                weight_pass(2, t).start()

        @pl.when((s >= 1) & (a - s + 1 >= 0))
        def _():
            project(jnp.maximum(a - s + 1, 0))

        @pl.when((s >= 2) & (a + s - 1 < lines))
        def _():
            project(jnp.minimum(a + s - 1, lines - 1))

        @pl.when(s == min(2, last))
        def _():
            quarter_on(0)
            for t in range(1, shards):
                weight_pass(2, t).wait()
            lax.fori_loop(0, chunks // 2, pos_step, 0)

        @pl.when(s == last)
        def _():
            for t in range(1, shards):
                weight_copy(3, t).wait()
                weight_pass(3, t).start()
            lax.fori_loop(chunks // 2, chunks, pos_step, 0)

        return 0

    lax.fori_loop(0, lines + 1, line_step, 0)
    for m in (5, 4):
        for s in range(1, shards):
            weight_copy(m, s).wait()
            weight_pass(m, s).start()
    for s in range(1, shards):
        weight_pass(3, s).wait()
    pos_out = pltpu.make_async_copy(pk_buf, pk_ref, pos_sem.at[1])
    pos_out.start()
    normed = (x_all[block(ctx)].astype(F32) * vectors_ref[0:1] + vectors_ref[1:2]).astype(BF16)
    queries = dot_nn(normed, weights_ref[3]).astype(BF16).astype(F32)
    qc_ref[...] = ((queries + vectors_ref[2:3]) * 0.125).astype(BF16)
    qp_ref[...] = ((queries + vectors_ref[3:4]) * 0.125).astype(BF16)
    cnt_finish(3)
    total_ref[...] = cnt_acc[4 * 8 : 5 * 8]

    def sends_done(p, _):
        for h in range(PARTS):

            @pl.when((a + 1 < lines) & (p <= a))
            def _():
                up_copy(p, h).wait_send()

            @pl.when((a >= 1) & (p >= a))
            def _():
                down_copy(p, h).wait_send()

        return 0

    lax.fori_loop(0, lines, sends_done, 0)

    def outs_done(slot, _):
        for copy in out_copies(slot):
            copy.wait()
        return 0

    lax.fori_loop(0, 4 * lines, outs_done, 0)
    for s in range(1, shards):
        weight_pass(4, s).wait()
        weight_pass(5, s).wait()
        quarter_pass(0, 1, s).wait()
        quarter_pass(0, 3, s).start()
    for s in range(1, shards):
        quarter_pass(0, 2, s).wait()
        quarter_pass(0, 3, s).wait()
    far_copies = []
    for m, (buf, to) in enumerate(((wo_buf, wo_out), (wu_buf, wu_out), (wd_buf, wd_out))):
        size = buf.shape[0] // shards
        for s in range(1, shards):
            rows = aligned(lax.rem(w + s, shards) * size, size)
            far_copies.append(pltpu.make_async_copy(buf.at[rows], to.at[rows], own_sem.at[4 + m * (shards - 1) + s - 1]))
    for copy in far_copies:
        copy.start()
    for copy in far_copies:
        copy.wait()
    table_out.wait()
    pos_out.wait()


def start(lines, shards, cid, limit, x, weights, vectors, mask, far, near):
    tokens, width = x.shape
    hidden = weights[5].shape[1]
    rows_out = weights[0].shape[0]
    members = 4 * lines
    keys = members * tokens
    span = limit * BLK
    vmem = pl.BlockSpec(memory_space=pltpu.VMEM)
    hbm = pl.BlockSpec(memory_space=pl.ANY)
    small = 2 * (shards - 1) + 1 + 1 + lines - 1
    dma = pltpu.SemaphoreType.DMA
    other = shards - 1
    return pl.pallas_call(
        functools.partial(start_kernel, lines, shards),
        out_shape=(
            jax.ShapeDtypeStruct((keys, width), BF16),
            jax.ShapeDtypeStruct((keys, width), BF16),
            jax.ShapeDtypeStruct((keys, width), BF16),
            jax.ShapeDtypeStruct((span, width), BF16),
            jax.ShapeDtypeStruct((span, width), BF16),
            jax.ShapeDtypeStruct((tokens, width), BF16),
            jax.ShapeDtypeStruct((tokens, width), BF16),
            jax.ShapeDtypeStruct((4, width, width), BF16),
            jax.ShapeDtypeStruct((width, width), BF16),
            jax.ShapeDtypeStruct((width, hidden), BF16),
            jax.ShapeDtypeStruct((hidden, width), BF16),
            jax.ShapeDtypeStruct((16, width), F32),
            jax.ShapeDtypeStruct((8, BLK), F32),
        ),
        in_specs=[vmem] + [hbm] * 7 + [vmem] * 11,
        out_specs=(hbm,) * 5 + (vmem,) * 3 + (hbm,) * 3 + (vmem,) * 2,
        scratch_shapes=[
            pltpu.VMEM((keys, width), BF16),
            pltpu.VMEM((keys, width), BF16),
            pltpu.VMEM((keys, width), BF16),
            pltpu.VMEM((span, width), BF16),
            pltpu.VMEM((span, width), BF16),
            pltpu.VMEM((width, width), BF16),
            pltpu.VMEM((width, hidden), BF16),
            pltpu.VMEM((hidden, width), BF16),
            pltpu.VMEM((16, rows_out), F32),
            pltpu.VMEM((other, 16, rows_out), F32),
            pltpu.VMEM((lines + shards, 8, BLK), F32),
            pltpu.VMEM((5 * 8, BLK), F32),
        ]
        + [dma((lines, PARTS))] * 6
        + [dma((2, lines))] * 2
        + [dma((6, other))] * 4
        + [dma((1, 4, other))] * 2
        + [dma((small,))] * 2
        + [dma((3, members)), dma((2,)), dma((4 + 3 * other,))],
        compiler_params=pltpu.CompilerParams(collective_id=cid, has_side_effects=True, vmem_limit_bytes=60 * 2**20),
        cost_estimate=pl.CostEstimate(flops=6 * 10**9, bytes_accessed=20 * 2**20, transcendentals=0),
        name="start",
    )(x, *weights, *vectors, mask, far, near)


GELU_SCALE = math.sqrt(2.0 / math.pi)


def middle_kernel(
    shards, rows_f, mask_ref, x_ref, mixed_ref, teacher_ref, out_grad_ref, vectors_ref, total_ref,
    wo_own, wu_own, wd_own, wo_ref, wu_ref, wd_ref,
    out_ref, hidden_ref, gm_ref, mine_ref, theirs_ref, vec_ref,
    wo, wu, wd, slope, act, gf_ref, landed, sem, send_sem, recv_sem,
):
    tokens, width = x_ref.shape
    parts = wu.shape[1] // width
    ctx = lax.axis_index("ctx")
    core = lax.rem(ctx, 2)
    core_peer = (ctx + 1 - 2 * core, lax.axis_index("wsh"))
    barrier = pltpu.get_barrier_semaphore()
    pl.semaphore_signal(barrier, inc=1, device_id=core_peer, device_id_type=MESH)
    w = lax.axis_index("wsh")
    copies = []
    for k, (own, gathered, full) in enumerate(((wo_own, wo_ref, wo), (wu_own, wu_ref, wu), (wd_own, wd_ref, wd))):
        size = own.shape[0]
        part = [pltpu.make_async_copy(own, full.at[aligned(w * size, size)], sem.at[k, 0])]
        for s in range(1, shards):
            rows = aligned(lax.rem(w + s, shards) * size, size)
            part.append(pltpu.make_async_copy(gathered.at[rows], full.at[rows], sem.at[k, s]))
        for copy in part:
            copy.start()
        copies.append(part)

    def arrive(k):
        for copy in copies[k]:
            copy.wait()

    b = lax.rem(ctx // 2, 2)
    half, quarter = rows_f // 2, rows_f // 4

    def give(begin, size, index):
        rows = aligned((1 - core) * half + begin, size)
        return pltpu.make_async_remote_copy(
            src_ref=gf_ref.at[:, rows], dst_ref=landed.at[:, begin : begin + size],
            send_sem=send_sem.at[index], recv_sem=recv_sem.at[index], device_id=core_peer, device_id_type=MESH,
        )

    gain, offset, down_bias = vectors_ref[4:5], vectors_ref[5:6], vectors_ref[6:7]
    mixed = mixed_ref[...].astype(BF16)
    arrive(0)
    hidden = x_ref[...].astype(F32) + dot_nn(mixed, wo[...])
    center = hidden - jnp.mean(hidden, axis=1, keepdims=True)
    inverse = lax.rsqrt(jnp.mean(center * center, axis=1, keepdims=True) + epsilon)
    unit = center * inverse
    normed = (unit * gain + offset).astype(BF16)
    result = hidden + down_bias
    arrive(1)
    arrive(2)
    for c in range(parts):
        cols = slice(c * width, (c + 1) * width)
        v = dot_nn(normed, wu[:, cols]) + vectors_ref[7 + c : 8 + c]
        square = v * v
        t = jnp.tanh(GELU_SCALE * (v + 0.044715 * (square * v)))
        act[:, cols] = (0.5 * v * (1.0 + t)).astype(BF16)
        slope[:, cols] = 0.5 * (1.0 + t) + 0.5 * v * (1.0 - t * t) * (GELU_SCALE * (1.0 + 3.0 * 0.044715 * square))
        result = result + dot_nn(act[:, cols], wd[cols])
    out_ref[...] = result.astype(BF16)
    mask = jnp.broadcast_to(mask_ref[...].astype(F32), (8, tokens)).T[:, 0:1]
    error = result - teacher_ref[...].astype(F32)
    masked = mask * error
    count = jnp.sum(total_ref[0:1, 0:1], axis=1, keepdims=True)
    grad_result = out_grad_ref[...].astype(F32) + (2.0 / (count * width)) * masked
    branch = grad_result.astype(BF16)
    vec_ref[...] = jnp.zeros_like(vec_ref)
    vec_ref[7 + parts : 8 + parts] = jnp.broadcast_to(
        jnp.sum(jnp.sum(masked * error, axis=1, keepdims=True), axis=0, keepdims=True), (1, width)
    )
    vec_ref[6:7] = jnp.sum(branch.astype(F32), axis=0, keepdims=True)
    rows_up = wd.shape[0] // shards
    rows_out = width // shards
    used = 2 * rows_up + rows_out
    if used < rows_f:
        gf_ref[:, used:] = jnp.zeros((shards, rows_f - used, width), BF16)
    grad_normed = jnp.zeros((tokens, width), F32)
    for c in range(parts):
        cols = slice(c * width, (c + 1) * width)
        grad_pre = (dot_nt(branch, wd[cols]) * slope[:, cols]).astype(BF16)
        vec_ref[7 + c : 8 + c] = jnp.sum(grad_pre.astype(F32), axis=0, keepdims=True)
        grad_normed = grad_normed + dot_nt(grad_pre, wu[:, cols])
        up = dot_tn(normed, grad_pre).astype(BF16)
        down = dot_tn(act[:, cols], branch).astype(BF16)
        for s in range(shards):
            gf_ref[s, c * rows_out : (c + 1) * rows_out] = up[s * rows_out : (s + 1) * rows_out]
        step = min(rows_up, width)
        for begin in range(0, width, step):
            row = c * width + begin
            place = rows_up + row % rows_up
            gf_ref[row // rows_up, place : place + step] = down[begin : begin + step]
    pl.semaphore_wait(barrier, 1)
    early = max(0, 2 * rows_up - half)
    if early:
        give(0, early, 0).start()
    vec_ref[4:5] = jnp.sum(grad_normed * unit, axis=0, keepdims=True)
    vec_ref[5:6] = jnp.sum(grad_normed, axis=0, keepdims=True)
    scaled = grad_normed * gain
    grad_hidden = grad_result + inverse * (
        scaled - jnp.mean(scaled, axis=1, keepdims=True) - unit * jnp.mean(scaled * unit, axis=1, keepdims=True)
    )
    hidden_ref[...] = grad_hidden
    attn = grad_hidden.astype(BF16)
    gm_ref[...] = dot_nt(attn, wo[...]).astype(BF16)
    outer = dot_tn(mixed, attn).astype(BF16)
    for s in range(shards):
        gf_ref[s, 2 * rows_up : used] = outer[s * rows_out : (s + 1) * rows_out]
    give(early, half - early, 1).start()
    if early:
        give(0, early, 0).wait()
    give(early, half - early, 1).wait()
    for ref, place in ((theirs_ref, 1 - b), (mine_ref, b)):
        own = gf_ref[:, aligned(core * half + place * quarter, quarter)].astype(F32)
        ref[...] = (own + landed[:, aligned(place * quarter, quarter)].astype(F32)).astype(BF16)


def middle(shards, rows_f, cid, mask, x, mixed, teacher, out_grad, vectors, total, own, gathered):
    tokens, width = x.shape
    hidden = own[1].shape[1]
    vmem = pl.BlockSpec(memory_space=pltpu.VMEM)
    hbm = pl.BlockSpec(memory_space=pl.ANY)
    return pl.pallas_call(
        functools.partial(middle_kernel, shards, rows_f),
        out_shape=(
            jax.ShapeDtypeStruct((tokens, width), BF16),
            jax.ShapeDtypeStruct((tokens, width), F32),
            jax.ShapeDtypeStruct((tokens, width), BF16),
            jax.ShapeDtypeStruct((shards, rows_f // 4, width), BF16),
            jax.ShapeDtypeStruct((shards, rows_f // 4, width), BF16),
            jax.ShapeDtypeStruct((16, width), F32),
        ),
        in_specs=[vmem] * 7 + [hbm] * 6,
        out_specs=(vmem,) * 6,
        scratch_shapes=[
            pltpu.VMEM((width, width), BF16),
            pltpu.VMEM((width, hidden), BF16),
            pltpu.VMEM((hidden, width), BF16),
            pltpu.VMEM((tokens, hidden), F32),
            pltpu.VMEM((tokens, hidden), BF16),
            pltpu.VMEM((shards, rows_f, width), BF16),
            pltpu.VMEM((shards, rows_f // 2, width), BF16),
            pltpu.SemaphoreType.DMA((3, shards)),
            pltpu.SemaphoreType.DMA((2,)),
            pltpu.SemaphoreType.DMA((2,)),
        ],
        compiler_params=pltpu.CompilerParams(collective_id=cid, has_side_effects=True, vmem_limit_bytes=56 * 2**20),
        cost_estimate=pl.CostEstimate(flops=4 * 10**9, bytes_accessed=20 * 2**20, transcendentals=10**6),
        name="middle",
    )(mask, x, mixed, teacher, out_grad, vectors, total, *own, *gathered)


def body(
    inputs, block_perm, seq_lengths, loss_mask, teacher, out_grad, gain_one, bias_one, w_query, w_key, w_value,
    w_output, w_pos, content_bias, position_bias, gain_two, bias_two, w_up, bias_up, w_down, bias_down,
):
    width = inputs.shape[2]
    shards = lax.axis_size("wsh")
    members = lax.axis_size("ctx")
    lines = members // 4
    hidden = bias_up.shape[0] * shards
    blocks = block_perm.shape[1]
    limit = blocks // 2 + 1
    rows_up, rows_out = hidden // shards, width // shards

    frequency = np.exp(np.arange(width // 2) * (-2.0 * math.log(10000.0) / width))
    far_angle = (np.arange(-(-limit // 8) * 8) * BLK + (BLK - 1))[:, None] * frequency[None]
    near_angle = np.arange(BLK)[:, None] * frequency[None]
    far = jnp.asarray(np.stack([np.sin(far_angle), np.cos(far_angle)]), F32)
    near = jnp.asarray(np.stack([np.sin(near_angle), np.cos(near_angle)]), F32)

    keys, values, unit_all, pos_keys, table, qc, qp, weights, wo, wu, wd, vectors, total = start(
        lines, shards, 0, limit, inputs[0], (w_key, w_value, w_pos, w_query, w_output, w_up, w_down),
        (gain_one, bias_one, content_bias, position_bias, gain_two, bias_two, bias_down, bias_up), loss_mask, far, near,
    )
    mixed, linv, probs = attn_fwd(block_perm, seq_lengths, qc, qp, keys, values, pos_keys, blocks, limit)

    step = 16 * lines
    pieces = -(-(2 * rows_up + rows_out) // (4 * step))
    split = min(2, pieces)
    chunks_f = tuple((pieces * (i + 1) // split - pieces * i // split) * step for i in range(split))
    rows_f = 4 * step * pieces
    if rows_out % (32 * lines):
        sets, rows_l = (("q", "p"), ("k", "v")), -(-2 * rows_out // (32 * lines)) * 32 * lines
    else:
        sets, rows_l = (("q",), ("p",), ("k",), ("v",)), rows_out
    output, grad_hidden, grad_mixed, mine, theirs, vec = middle(
        shards, rows_f, 2, loss_mask, inputs[0], mixed, teacher[0], out_grad[0], vectors, total,
        (w_output, w_up, w_down), (wo, wu, wd),
    )
    come = lax.ppermute(theirs, "ctx", [(i, i ^ 2) for i in range(members)])
    grad_query, bias_grads, dk_t, dv_t, dpk_t = attn_bwd(
        block_perm, seq_lengths, qc, qp, keys, values, pos_keys, probs, linv, grad_mixed, mixed, blocks, limit
    )
    grad_input, sums, vsum = finish(
        lines, shards, chunks_f, sets, rows_l, 1, mine, come, dk_t, dv_t, unit_all, dpk_t, table, weights, grad_query,
        inputs[0], vectors, total, vec, bias_grads, grad_hidden,
    )
    (
        grad_input, output, g_query, g_key, g_value, g_output, g_pos, g_up, g_down,
        v_g1, v_b1, v_cb, v_pb, v_g2, v_b2, v_bd, v_bu, loss,
    ) = unpack(shards, rows_f, sets, rows_l, hidden, sums, vsum, total, grad_input, output)
    return (
        output[None], loss.reshape(()), grad_input[None], v_g1, v_b1, g_query, g_key, g_value, g_output, g_pos,
        v_cb, v_pb, v_g2, v_b2, g_up, v_bu, g_down, v_bd,
    )


def solution(mesh):
    rows = P("wsh", "ctx", None)
    vector = P("wsh")
    matrix = P("wsh", None)
    placed = (
        rows, matrix, matrix, P("wsh", "ctx"), rows, rows, vector, vector, matrix, matrix, matrix, matrix, matrix,
        vector, vector, vector, vector, matrix, vector, matrix, vector,
    )
    out = (
        rows, P(), rows, vector, vector, matrix, matrix, matrix, matrix, matrix, vector, vector, vector, vector,
        matrix, vector, matrix, vector,
    )
    return jax.shard_map(body, mesh=mesh, in_specs=placed, out_specs=out, check_vma=False)
```

```python
import functools
import math

import jax
import jax.numpy as jnp
import numpy as np
from jax import lax
from jax.experimental import pallas as pl
from jax.experimental.pallas import tpu as pltpu
from jax.sharding import PartitionSpec as P

HEADS = 8
HEAD = 64
PAIRS = HEADS // 2
BLK = 128
ROWS = HEADS * BLK
NEG = -1e30
epsilon = 1e-05
F32 = jnp.float32
BF16 = jnp.bfloat16


def dot_nt(a, b):
    return lax.dot_general(a, b, (((1,), (1,)), ((), ())), preferred_element_type=F32)


def dot_nn(a, b):
    return lax.dot_general(a, b, (((1,), (0,)), ((), ())), preferred_element_type=F32)


def dot_tn(a, b):
    return lax.dot_general(a, b, (((0,), (0,)), ((), ())), preferred_element_type=F32)


def iotas():
    row = lax.broadcasted_iota(jnp.int32, (BLK, BLK), 0)
    col = lax.broadcasted_iota(jnp.int32, (BLK, BLK), 1)
    return row, col


def read_places(perm_ref, lengths_ref, meta, blocks, count):
    device = lax.axis_index("ctx")
    meta[0] = perm_ref[0, 2 * device]
    meta[1] = perm_ref[0, 2 * device + 1]

    def place(slot, _):
        meta[2 + perm_ref[0, slot]] = slot
        return 0

    lax.fori_loop(0, blocks, place, 0, unroll=True)
    end = jnp.int32(0)
    for e in range(count):
        end = end + lengths_ref[0, e]
        meta[2 + blocks + e] = end


def block_range(meta, a, blocks, limit):
    qb = meta[a]
    first = qb * BLK
    low = jnp.int32(0)
    for e in range(meta.shape[0] - 2 - blocks):
        end = meta[2 + blocks + e]
        low = jnp.where(first >= end, jnp.maximum(low, end), low)
    lowest = low // BLK
    return qb, lowest, jnp.minimum(qb - lowest + 1, limit)


def stack_heads(pair):
    lane = lax.broadcasted_iota(jnp.int32, pair.shape, 1)
    zero = jnp.zeros_like(pair)
    return jnp.concatenate([jnp.where(lane < HEAD, pair, zero), jnp.where(lane >= HEAD, pair, zero)], axis=0)


def flip_rows(x):
    index = 7 - lax.broadcasted_iota(jnp.int32, (8, BLK), 0)
    slabs = [jnp.take_along_axis(x[8 * g : 8 * g + 8], index, axis=0) for g in reversed(range(BLK // 8))]
    return jnp.concatenate(slabs, axis=0)


def flip_two(x):
    return jnp.concatenate([flip_rows(x[:BLK]), flip_rows(x[BLK:])], axis=0)


def needed_blocks(meta, blocks, limit):
    ranges = []
    for a in range(2):
        qb, lowest, count = block_range(meta, a, blocks, limit)
        ranges.append((qb + 1 - 2 * ((count + 1) // 2), qb))
    return ranges


def load_keys(meta, blocks, limit, pairs, sem):
    (low0, high0), (low1, high1) = needed_blocks(meta, blocks, limit)
    for hbm, ref in pairs:
        ref[0:BLK] = jnp.zeros((BLK, ref.shape[1]), ref.dtype)

    def copies(kb):
        slot = pl.ds(pl.multiple_of(meta[2 + kb] * BLK, BLK), BLK)
        place = pl.ds(pl.multiple_of((kb + 1) * BLK, BLK), BLK)
        return [
            pltpu.make_async_copy(hbm.at[slot], ref.at[place], sem.at[index, kb]) for index, (hbm, ref) in enumerate(pairs)
        ]

    def begin(kb, _):
        @pl.when(((kb >= low0) & (kb <= high0)) | ((kb >= low1) & (kb <= high1)))
        def _():
            for copy in copies(kb):
                copy.start()

        return 0

    lax.fori_loop(0, blocks, begin, 0)

    def arrive(a):
        low, high = (jnp.where(a == 0, x, y) for x, y in ((low0, low1), (high0, high1)))

        def one(kb, _):
            @pl.when((a == 0) | (kb < low0) | (kb > high0))
            def _():
                for copy in copies(kb):
                    copy.wait()

            return 0

        lax.fori_loop(jnp.maximum(low, 0), high + 1, one, 0)

    return arrive


def wide_iotas():
    row = lax.broadcasted_iota(jnp.int32, (BLK, 2 * BLK), 0)
    col = lax.broadcasted_iota(jnp.int32, (BLK, 2 * BLK), 1)
    return row, col


def attn_fwd_kernel(
    blocks, limit, perm_ref, lengths_ref, qc_ref, qp_ref, k_in, v_in, pk_in, mixed_ref, linv_ref, p_ref,
    meta, k_ref, v_ref, pk_ref, q2c, q2p, prev, top, total, acc, s_scr, p_buf, kv_sem, pk_sem, p_sem,
):
    read_places(perm_ref, lengths_ref, meta, blocks, lengths_ref.shape[1])
    span = pk_in.shape[0]
    pk_copy = pltpu.make_async_copy(pk_in, pk_ref.at[0:span], pk_sem)
    pk_copy.start()
    arrive = load_keys(meta, blocks, limit, ((k_in, k_ref), (v_in, v_ref)), kv_sem)
    pk_ref[span:] = jnp.zeros((BLK, pk_ref.shape[1]), BF16)
    row, col = iotas()
    tri = col <= row
    wide_row, wide_col = wide_iotas()
    tiles = s_scr.shape[0]

    def p_copy(slot, index):
        return pltpu.make_async_copy(p_buf.at[slot], p_ref.at[index], p_sem.at[slot])

    def one_query_block(a, _):
        qb, lowest, count = block_range(meta, a, blocks, limit)
        pairs = (count + 1) // 2
        rows_a = pl.ds(pl.multiple_of(a * BLK, BLK), BLK)
        pos = qb * BLK + wide_row
        start = jnp.zeros((BLK, 2 * BLK), jnp.int32)
        for e in range(meta.shape[0] - 2 - blocks):
            end = meta[2 + blocks + e]
            start = jnp.where(pos >= end, jnp.maximum(start, end), start)
        for hp in range(PAIRS):
            lanes = slice(hp * BLK, (hp + 1) * BLK)
            q2c[hp] = stack_heads(qc_ref[rows_a, lanes].astype(F32)).astype(BF16)
            q2p[hp] = stack_heads(qp_ref[rows_a, lanes].astype(F32)).astype(BF16)
        prev[...] = jnp.zeros_like(prev)
        top[...] = jnp.full_like(top, NEG)
        total[...] = jnp.zeros_like(total)
        acc[...] = jnp.zeros_like(acc)
        arrive(a)

        @pl.when(a == 0)
        def _():
            pk_copy.wait()

        def score_step(t, _):
            kb = qb - 2 * t
            keys = pl.ds(pl.multiple_of(kb * BLK, BLK), 2 * BLK)
            place = (kb - 1) * BLK + wide_col
            bias = jnp.where((place >= start) & (place <= pos), 0.0, NEG).astype(F32)
            drows = pl.ds(pl.multiple_of(2 * t * BLK, BLK), 2 * BLK)
            for hp in range(PAIRS):
                lanes = slice(hp * BLK, (hp + 1) * BLK)
                s = dot_nt(q2c[hp], k_ref[keys, lanes])
                r = dot_nt(q2p[hp], pk_ref[drows, lanes])
                for half in range(2):
                    part = slice(half * BLK, (half + 1) * BLK)
                    rows = slice((2 * hp + half) * BLK, (2 * hp + half + 1) * BLK)
                    near = pltpu.roll(r[part, :BLK], 1, 1, stride=1, stride_axis=0)
                    far = pltpu.roll(r[part, BLK:], 1, 1, stride=1, stride_axis=0)
                    late = s[part, BLK:] + jnp.where(tri, near, prev[rows]) + bias[:, BLK:]
                    early = s[part, :BLK] + jnp.where(tri, far, near) + bias[:, :BLK]
                    prev[rows] = far
                    s_scr[t, rows, :BLK] = early
                    s_scr[t, rows, BLK:] = late
                    top[rows] = jnp.maximum(top[rows], jnp.maximum(early, late))
            return 0

        lax.fori_loop(0, pairs, score_step, 0)
        for h in range(HEADS):
            rows = slice(h * BLK, (h + 1) * BLK)
            top[rows] = jnp.broadcast_to(jnp.max(top[rows], axis=1, keepdims=True), (BLK, BLK))

        def mix_step(t, _):
            kb = qb - 2 * t
            keys = pl.ds(pl.multiple_of(kb * BLK, BLK), 2 * BLK)
            slot = lax.rem(t, 2)

            @pl.when(t >= 2)
            def _():
                p_copy(slot, 0).wait()

            for hp in range(PAIRS):
                lanes = slice(hp * BLK, (hp + 1) * BLK)
                rows = slice(2 * hp * BLK, 2 * (hp + 1) * BLK)
                early = jnp.exp(s_scr[t, rows, :BLK] - top[rows])
                late = jnp.exp(s_scr[t, rows, BLK:] - top[rows])
                total[rows] += early + late
                p_buf[slot, rows, :BLK] = flip_two(early).astype(BF16)
                p_buf[slot, rows, BLK:] = flip_two(late).astype(BF16)
                low = jnp.concatenate([early.astype(BF16), late.astype(BF16)], axis=1)
                acc[hp] += dot_nn(low, v_ref[keys, lanes])
            p_copy(slot, a * tiles + t).start()
            return 0

        lax.fori_loop(0, pairs, mix_step, 0)
        p_copy(lax.rem(pairs - 1, 2), 0).wait()

        @pl.when(pairs >= 2)
        def _():
            p_copy(lax.rem(pairs, 2), 0).wait()

        lane = lax.broadcasted_iota(jnp.int32, (BLK, BLK), 1)
        for hp in range(PAIRS):
            lanes = slice(hp * BLK, (hp + 1) * BLK)
            parts = []
            for half in range(2):
                h = 2 * hp + half
                rows = slice(h * BLK, (h + 1) * BLK)
                inv = 1.0 / jnp.sum(total[rows], axis=1, keepdims=True)
                inv = jnp.broadcast_to(inv, (BLK, BLK))
                linv_ref[a, rows] = inv
                parts.append(acc[hp, half * BLK : (half + 1) * BLK] * inv)
            mixed_ref[rows_a, lanes] = jnp.where(lane < HEAD, parts[0], parts[1])
        return 0

    lax.fori_loop(0, 2, one_query_block, 0)


def attn_fwd(perm, lengths, qc, qp, k, v, pk, blocks, limit):
    tokens, width = qc.shape
    keys, span = k.shape[0], pk.shape[0]
    tiles = (limit + 1) // 2
    vmem = pl.BlockSpec(memory_space=pltpu.VMEM)
    hbm = pl.BlockSpec(memory_space=pl.ANY)
    return pl.pallas_call(
        functools.partial(attn_fwd_kernel, blocks, limit),
        out_shape=(
            jax.ShapeDtypeStruct((tokens, width), F32),
            jax.ShapeDtypeStruct((2, ROWS, BLK), F32),
            jax.ShapeDtypeStruct((2 * tiles, ROWS, 2 * BLK), BF16),
        ),
        in_specs=[pl.BlockSpec(memory_space=pltpu.SMEM)] * 2 + [vmem] * 2 + [hbm] * 3,
        out_specs=(vmem, vmem, hbm),
        scratch_shapes=[
            pltpu.SMEM((2 + blocks + lengths.shape[1],), jnp.int32),
            pltpu.VMEM((keys + BLK, width), BF16),
            pltpu.VMEM((keys + BLK, width), BF16),
            pltpu.VMEM((span + BLK, width), BF16),
            pltpu.VMEM((PAIRS, 2 * BLK, BLK), BF16),
            pltpu.VMEM((PAIRS, 2 * BLK, BLK), BF16),
            pltpu.VMEM((ROWS, BLK), F32),
            pltpu.VMEM((ROWS, BLK), F32),
            pltpu.VMEM((ROWS, BLK), F32),
            pltpu.VMEM((PAIRS, 2 * BLK, BLK), F32),
            pltpu.VMEM((tiles, ROWS, 2 * BLK), F32),
            pltpu.VMEM((2, ROWS, 2 * BLK), BF16),
            pltpu.SemaphoreType.DMA((2, blocks)),
            pltpu.SemaphoreType.DMA,
            pltpu.SemaphoreType.DMA((2,)),
        ],
        compiler_params=pltpu.CompilerParams(vmem_limit_bytes=60 * 2**20),
        cost_estimate=pl.CostEstimate(flops=3 * 10**9, bytes_accessed=20 * 2**20, transcendentals=4 * 10**6),
        name="attn_fwd",
    )(perm, lengths, qc, qp, k, v, pk)


def attn_bwd_kernel(
    blocks, limit, perm_ref, lengths_ref, qc_ref, qp_ref, k_in, v_in, pk_in, p_ref, linv_ref, gm_ref, mixed_ref,
    dq_ref, bias_ref, dk_out, dv_out, dpk_ref,
    meta, k_ref, v_ref, pk_ref, dk_ref, dv_ref, q2c_t, q2p_t, gm2, gm2_t, dd, carry, dqk, dqp, dpk, p_buf,
    empty, kv_sem, pk_sem, p_sem, out_sem,
):
    read_places(perm_ref, lengths_ref, meta, blocks, lengths_ref.shape[1])
    span = pk_in.shape[0]
    pk_copy = pltpu.make_async_copy(pk_in, pk_ref.at[0:span], pk_sem)
    pk_copy.start()
    arrive = load_keys(meta, blocks, limit, ((k_in, k_ref), (v_in, v_ref)), kv_sem)
    pk_ref[span:] = jnp.zeros((BLK, pk_ref.shape[1]), BF16)
    row, col = iotas()
    tri = col <= BLK - 1 - row
    tiles = p_ref.shape[0] // 2
    (low0, high0), (low1, high1) = needed_blocks(meta, blocks, limit)

    def out_copies(kb, nothing=False):
        slot = pl.ds(pl.multiple_of(meta[2 + kb] * BLK, BLK), BLK)
        place = pl.ds(pl.multiple_of((kb + 1) * BLK, BLK), BLK)
        return [
            pltpu.make_async_copy(empty if nothing else ref.at[:, place], out.at[:, slot], out_sem.at[index, kb])
            for index, (ref, out) in enumerate(((dk_ref, dk_out), (dv_ref, dv_out)))
        ]

    empty[...] = jnp.zeros_like(empty)
    for ref in (dk_ref, dv_ref):
        ref[:, 0:BLK] = jnp.zeros((ref.shape[0], BLK), BF16)

    def prepare(kb, _):
        used = ((kb >= low0) & (kb <= high0)) | ((kb >= low1) & (kb <= high1))

        @pl.when(used)
        def _():
            place = pl.ds(pl.multiple_of((kb + 1) * BLK, BLK), BLK)
            for ref in (dk_ref, dv_ref):
                ref[:, place] = jnp.zeros((ref.shape[0], BLK), BF16)

        @pl.when(jnp.logical_not(used))
        def _():
            for copy in out_copies(kb, True):
                copy.start()

        return 0

    lax.fori_loop(0, blocks, prepare, 0)
    dpk[...] = jnp.zeros_like(dpk)
    bias_ref[...] = jnp.zeros_like(bias_ref)

    def p_copy(slot, index):
        return pltpu.make_async_copy(p_ref.at[index], p_buf.at[slot], p_sem.at[slot])

    def one_query_block(a, _):
        qb, lowest, count = block_range(meta, a, blocks, limit)
        pairs = (count + 1) // 2
        rows_a = pl.ds(pl.multiple_of(a * BLK, BLK), BLK)
        p_copy(0, a * tiles + pairs - 1).start()
        for hp in range(PAIRS):
            lanes = slice(hp * BLK, (hp + 1) * BLK)
            rows = slice(2 * hp * BLK, 2 * (hp + 1) * BLK)
            q2c_t[hp] = stack_heads(flip_rows(qc_ref[rows_a, lanes].astype(F32))).T.astype(BF16)
            q2p_t[hp] = stack_heads(flip_rows(qp_ref[rows_a, lanes].astype(F32))).T.astype(BF16)
            g = stack_heads(gm_ref[rows_a, lanes].astype(F32))
            scaled = flip_two(g * linv_ref[a, rows])
            gm2[hp] = scaled.astype(BF16)
            gm2_t[hp] = scaled.T.astype(BF16)
            pair = flip_rows(mixed_ref[rows_a, lanes])
            dd[rows] = jnp.broadcast_to(
                jnp.sum(scaled * jnp.concatenate([pair, pair], axis=0), axis=1, keepdims=True), (2 * BLK, BLK)
            )
        carry[...] = jnp.zeros_like(carry)
        dqk[...] = jnp.zeros_like(dqk)
        dqp[...] = jnp.zeros_like(dqp)
        arrive(a)

        @pl.when(a == 0)
        def _():
            pk_copy.wait()

        def step(t, _):
            tile = pairs - 1 - t
            kb = qb - 2 * tile
            keys = pl.ds(pl.multiple_of(kb * BLK, BLK), 2 * BLK)
            drows = pl.ds(pl.multiple_of(2 * tile * BLK, BLK), 2 * BLK)
            slot = lax.rem(t, 2)
            p_copy(slot, 0).wait()

            @pl.when(tile >= 1)
            def _():
                p_copy(1 - slot, a * tiles + tile - 1).start()

            for hp in range(PAIRS):
                lanes = slice(hp * BLK, (hp + 1) * BLK)
                rows = slice(2 * hp * BLK, 2 * (hp + 1) * BLK)
                p = p_buf[slot, rows]
                g = dot_nt(gm2[hp], v_ref[keys, lanes])
                early = (p[:, :BLK].astype(F32) * (g[:, :BLK] - dd[rows])).astype(BF16)
                late = (p[:, BLK:].astype(F32) * (g[:, BLK:] - dd[rows])).astype(BF16)
                gs = jnp.concatenate([early, late], axis=1)
                early, late = early.astype(F32), late.astype(F32)
                rots = []
                for half in range(2):
                    part = slice(half * BLK, (half + 1) * BLK)
                    crow = slice((2 * hp + half) * BLK, (2 * hp + half + 1) * BLK)
                    far = jnp.where(tri, early[part], carry[crow])
                    near = jnp.where(tri, late[part], early[part])
                    carry[crow] = late[part]
                    rots.append(
                        jnp.concatenate(
                            [
                                pltpu.roll(near, 0, 1, stride=1, stride_axis=0).astype(BF16),
                                pltpu.roll(far, 0, 1, stride=1, stride_axis=0).astype(BF16),
                            ],
                            axis=1,
                        )
                    )
                rot = jnp.concatenate(rots, axis=0)
                dqk[hp] += dot_nn(gs, k_ref[keys, lanes])
                dqp[hp] += dot_nn(rot, pk_ref[drows, lanes])
                dk_ref[lanes, keys] = (dk_ref[lanes, keys].astype(F32) + dot_nn(q2c_t[hp], gs)).astype(BF16)
                dv_ref[lanes, keys] = (dv_ref[lanes, keys].astype(F32) + dot_nn(gm2_t[hp], p)).astype(BF16)
                dpk[lanes, drows] += dot_nn(q2p_t[hp], rot)
            for block in (kb - 1, kb):

                @pl.when((block >= 0) & ((a == 1) | (block < low1) | (block > high1)))
                def _():
                    for copy in out_copies(jnp.maximum(block, 0)):
                        copy.start()

            return 0

        lax.fori_loop(0, pairs, step, 0)
        lane = lax.broadcasted_iota(jnp.int32, (BLK, BLK), 1)
        for hp in range(PAIRS):
            lanes = slice(hp * BLK, (hp + 1) * BLK)
            ck = jnp.where(lane < HEAD, dqk[hp, :BLK], dqk[hp, BLK:]) * 0.125
            cp = jnp.where(lane < HEAD, dqp[hp, :BLK], dqp[hp, BLK:]) * 0.125
            dq_ref[rows_a, lanes] = flip_rows(ck + cp).astype(BF16)
            bias_ref[0:1, lanes] += jnp.sum(ck, axis=0, keepdims=True)
            bias_ref[1:2, lanes] += jnp.sum(cp, axis=0, keepdims=True)
        return 0

    lax.fori_loop(0, 2, one_query_block, 0)

    def given(kb, _):
        for copy in out_copies(kb):
            copy.wait()
        return 0

    dpk_ref[...] = dpk[:, 0:span].astype(BF16)
    lax.fori_loop(0, blocks, given, 0)


def attn_bwd(perm, lengths, qc, qp, k, v, pk, p, linv, gm, mixed, blocks, limit):
    tokens, width = qc.shape
    keys, span = k.shape[0], pk.shape[0]
    vmem = pl.BlockSpec(memory_space=pltpu.VMEM)
    hbm = pl.BlockSpec(memory_space=pl.ANY)
    return pl.pallas_call(
        functools.partial(attn_bwd_kernel, blocks, limit),
        out_shape=(
            jax.ShapeDtypeStruct((tokens, width), BF16),
            jax.ShapeDtypeStruct((8, width), F32),
            jax.ShapeDtypeStruct((width, keys), BF16),
            jax.ShapeDtypeStruct((width, keys), BF16),
            jax.ShapeDtypeStruct((width, span), BF16),
        ),
        in_specs=[pl.BlockSpec(memory_space=pltpu.SMEM)] * 2 + [vmem] * 2 + [hbm] * 4 + [vmem] * 3,
        out_specs=(vmem, vmem, hbm, hbm, vmem),
        scratch_shapes=[
            pltpu.SMEM((2 + blocks + lengths.shape[1],), jnp.int32),
            pltpu.VMEM((keys + BLK, width), BF16),
            pltpu.VMEM((keys + BLK, width), BF16),
            pltpu.VMEM((span + BLK, width), BF16),
            pltpu.VMEM((width, keys + BLK), BF16),
            pltpu.VMEM((width, keys + BLK), BF16),
            pltpu.VMEM((PAIRS, BLK, 2 * BLK), BF16),
            pltpu.VMEM((PAIRS, BLK, 2 * BLK), BF16),
            pltpu.VMEM((PAIRS, 2 * BLK, BLK), BF16),
            pltpu.VMEM((PAIRS, BLK, 2 * BLK), BF16),
            pltpu.VMEM((ROWS, BLK), F32),
            pltpu.VMEM((ROWS, BLK), F32),
            pltpu.VMEM((PAIRS, 2 * BLK, BLK), F32),
            pltpu.VMEM((PAIRS, 2 * BLK, BLK), F32),
            pltpu.VMEM((width, span + BLK), F32),
            pltpu.VMEM((2, ROWS, 2 * BLK), BF16),
            pltpu.VMEM((width, BLK), BF16),
            pltpu.SemaphoreType.DMA((2, blocks)),
            pltpu.SemaphoreType.DMA,
            pltpu.SemaphoreType.DMA((2,)),
            pltpu.SemaphoreType.DMA((2, blocks)),
        ],
        compiler_params=pltpu.CompilerParams(vmem_limit_bytes=62 * 2**20),
        cost_estimate=pl.CostEstimate(flops=6 * 10**9, bytes_accessed=30 * 2**20, transcendentals=0),
        name="attn_bwd",
    )(perm, lengths, qc, qp, k, v, pk, p, linv, gm, mixed)


MESH = pl.DeviceIdType.MESH


def fold_rows(x):
    return jnp.broadcast_to(x, (x.shape[0], BLK)).T[0:1]


def aligned(begin, size):
    return pl.ds(pl.multiple_of(begin, math.gcd(size, 16)), size)


def finish_kernel(
    lines, shards, chunks_f, sets, rows_l,
    mine_in, come_in, dk_ref, dv_ref, unit_all_ref, dpk_ref, table_ref, weights_in, dq_ref, x_ref,
    vectors_ref, total_ref, vec_ref, bias_ref, hidden_in,
    grad_ref, sums_out, vsum_ref,
    mine_ref, come_ref, sums_ref, sums_sem, dk_buf, dv_buf, un_buf, in_sem, dpk_buf, table_buf, weights_ref, hidden_ref, pos_sem, m_q, mt_k, mt_v, cs_q, cs_k, cs_v, dxp, bx0, bx1, bx2, vbuf, vacc,
    *rest,
):
    wk_ref, wv_ref, wq_ref = weights_ref.at[0], weights_ref.at[1], weights_ref.at[3]
    tokens, width = dq_ref.shape
    bufs_f = rest[: 3 * len(chunks_f)]
    bufs_l = rest[3 * len(chunks_f) : -2]
    send_sem, recv_sem = rest[-2:]
    ctx = lax.axis_index("ctx")
    w = lax.axis_index("wsh")
    core = lax.rem(ctx, 2)
    b = lax.rem(ctx // 2, 2)
    a = ctx // 4

    def at(a_to, b_to, core_to):
        return (a_to * 2 + b_to) * 2 + core_to

    def line_peer(s):
        return (at(lax.rem(a + s, lines), b, core), w)

    def shard_peer(s):
        return (ctx, lax.rem(w + s, shards))

    core_peer = (at(a, b, 1 - core), w)
    b_peer = (at(a, 1 - b, core), w)
    peers = [core_peer, b_peer] + [line_peer(s) for s in range(1, lines)] + [shard_peer(s) for s in range(1, shards)]
    barrier = pltpu.get_barrier_semaphore()
    for peer in peers:
        pl.semaphore_signal(barrier, inc=1, device_id=peer, device_id_type=MESH)

    counter = [0]

    def take(number):
        begin = counter[0]
        counter[0] += number
        return begin

    def remote(src, dst, index, peer):
        return pltpu.make_async_remote_copy(
            src_ref=src, dst_ref=dst, send_sem=send_sem.at[index], recv_sem=recv_sem.at[index],
            device_id=peer, device_id_type=MESH,
        )

    bits = lines.bit_length() - 1
    order = []
    for bit in range(bits):
        order += [m for m in reversed(range(lines)) if m & ((1 << (bit + 1)) - 1) == 1 << bit]
    order.append(0)

    def other(mask):
        place = 0
        for bit in range(bits):
            own = lax.rem(a // (1 << bit), 2)
            place = place + (1 << bit) * ((1 - own) if mask >> bit & 1 else own)
        return place

    def line_place(j):
        place = jnp.int32(0)
        for index, mask in enumerate(order):
            place = place + jnp.where(j == index, other(mask), 0)
        return place

    def line_at(mask):
        return (at(other(mask), b, core), w)

    group = 4 * tokens

    def fetch(j, slot):
        begin = pl.multiple_of(line_place(j) * group, group)
        return (
            pltpu.make_async_copy(dk_ref.at[:, pl.ds(begin, group)], dk_buf.at[slot], in_sem.at[slot, 0]),
            pltpu.make_async_copy(dv_ref.at[:, pl.ds(begin, group)], dv_buf.at[slot], in_sem.at[slot, 1]),
            pltpu.make_async_copy(unit_all_ref.at[pl.ds(begin, group)], un_buf.at[slot], in_sem.at[slot, 2]),
        )

    span, hold = table_ref.shape[0], table_buf.shape[0]
    pos_parts = [(begin, min(hold, span - begin)) for begin in range(0, span, hold)]

    def pos_copies(begin, size):
        rows = pl.ds(begin, size)
        return [
            pltpu.make_async_copy(dpk_ref.at[:, rows], dpk_buf.at[:, 0:size], pos_sem.at[0]),
            pltpu.make_async_copy(table_ref.at[rows], table_buf.at[0:size], pos_sem.at[1]),
        ]

    weights_copy = pltpu.make_async_copy(weights_in, weights_ref, pos_sem.at[2])
    hidden_copy = pltpu.make_async_copy(hidden_in, hidden_ref, pos_sem.at[3])
    feed_copies = [
        pltpu.make_async_copy(mine_in, mine_ref, pos_sem.at[4]),
        pltpu.make_async_copy(come_in, come_ref, pos_sem.at[5]),
    ]
    for copy in feed_copies:
        copy.start()
    weights_copy.start()
    for copy in fetch(0, 0):
        copy.start()
    for copy in pos_copies(*pos_parts[0]):
        copy.start()
    hidden_copy.start()

    def start_all(copies):
        for copy in copies:
            copy.start()

    def wait_all(copies):
        for copy in copies:
            copy.wait()

    def own_bit(bit):
        return lax.rem(a // (1 << bit), 2)

    def bit_peer(bit):
        return line_at(1 << bit)

    class Feed:
        def __init__(self, begin, rows, total_rows, bufs):
            self.begin, self.rows = begin, rows
            self.rc, self.rb = total_rows // 2, total_rows // 4
            self.b0, self.b1, self.b2 = bufs
            self.iy, self.irs, self.iag, self.ix, self.ic = take(shards - 1), take(bits), take(bits), take(1), take(2)

        def region(self, bit):
            start = 0
            for k in range(bit):
                start = start + own_bit(k) * (self.rows >> (k + 1))
            return start, self.rows >> bit

        def y_copies(self):
            return [
                remote(self.b0.at[lax.rem(w + s, shards)], self.b1.at[s - 1], self.iy + s - 1, shard_peer(s))
                for s in range(1, shards)
            ]

        def rs_copies(self, bit):
            start, size = self.region(bit)
            size = size // 2
            give = aligned(start + (1 - own_bit(bit)) * size, size)
            begin = sum(self.rows >> (k + 1) for k in range(bit))
            return [remote(self.b1.at[0, give], self.b2.at[begin : begin + size], self.irs + bit, bit_peer(bit))]

        def place(self, b_of, begin, size):
            return aligned(core * self.rc + b_of * self.rb + self.begin + begin, size)

        def ag_copies(self, bit):
            own = self.place(b, *self.region(bit + 1))
            return [remote(sums_ref.at[own], sums_ref.at[own], self.iag + bit, bit_peer(bit))]

        def x_copies(self):
            own = self.place(b, 0, self.rows)
            return [remote(sums_ref.at[own], sums_ref.at[own], self.ix, b_peer)]

        def c_copies(self):
            return [
                remote(sums_ref.at[rows], sums_ref.at[rows], self.ic + k, core_peer)
                for k, rows in enumerate((self.place(b, 0, self.rows), self.place(1 - b, 0, self.rows)))
            ]

        def y(self):
            rows = pl.ds(self.begin, self.rows)
            self.b0[...] = (mine_ref[:, rows].astype(F32) + come_ref[:, rows].astype(F32)).astype(BF16)
            start_all(self.y_copies())

        def rs(self, bit):
            if bit == 0:
                wait_all(self.y_copies())
                total = self.b0[w].astype(F32)
                for s in range(shards - 1):
                    total = total + self.b1[s].astype(F32)
                self.b1[0] = total.astype(BF16)
            else:
                self.add(bit - 1)
            start_all(self.rs_copies(bit))

        def add(self, bit):
            wait_all(self.rs_copies(bit))
            start, size = self.region(bit + 1)
            begin = sum(self.rows >> (k + 1) for k in range(bit))
            rows = aligned(start, size)
            self.b1[0, rows] = (self.b1[0, rows].astype(F32) + self.b2[begin : begin + size].astype(F32)).astype(BF16)

        def ag(self, bit):
            if bit == bits - 1:
                self.add(bit)
                start, size = self.region(bits)
                sums_ref[self.place(b, start, size)] = self.b1[0, aligned(start, size)]
            else:
                wait_all(self.ag_copies(bit + 1))
            start_all(self.ag_copies(bit))

        def x(self):
            wait_all(self.ag_copies(0))
            start_all(self.x_copies())

        def c(self):
            wait_all(self.x_copies())
            start_all(self.c_copies())

        def done(self):
            wait_all(self.c_copies())

    class Late:
        def __init__(self, out, rows, names, bufs):
            self.out, self.rows, self.names, self.begun = out, rows, names, set()
            self.src, self.b0, self.b1, self.b2, self.b3 = bufs
            self.rc, self.rb, self.share = rows // 2, rows // 4, rows // 4 // lines
            self.i0, self.iy, self.i2 = take(1), take(shards - 1), take(1)
            self.irs, self.iag, self.ix, self.ic = take(lines - 1), take(lines - 1), take(1), take(1)

        def c0_copies(self):
            return [remote(self.src.at[:, aligned((1 - core) * self.rc, self.rc)], self.b0, self.i0, core_peer)]

        def y_copies(self):
            return [
                remote(self.b0.at[lax.rem(w + s, shards)], self.b1.at[s - 1], self.iy + s - 1, shard_peer(s))
                for s in range(1, shards)
            ]

        def x0_copies(self):
            return [remote(self.b1.at[0, aligned((1 - b) * self.rb, self.rb)], self.b2, self.i2, b_peer)]

        def rs_copies(self):
            return [
                remote(
                    self.b2.at[aligned(lax.rem(a + s, lines) * self.share, self.share)],
                    self.b3.at[s - 1], self.irs + s - 1, line_peer(s),
                )
                for s in range(1, lines)
            ]

        def ag_copies(self):
            own = aligned(self.out + core * self.rc + b * self.rb + a * self.share, self.share)
            return [remote(sums_ref.at[own], sums_ref.at[own], self.iag + s - 1, line_peer(s)) for s in range(1, lines)]

        def x_copies(self):
            own = aligned(self.out + core * self.rc + b * self.rb, self.rb)
            return [remote(sums_ref.at[own], sums_ref.at[own], self.ix, b_peer)]

        def c_copies(self):
            own = aligned(self.out + core * self.rc, self.rc)
            return [remote(sums_ref.at[own], sums_ref.at[own], self.ic, core_peer)]

        def c0(self):
            for m, name in enumerate(self.names):
                grad = gradient(name)
                for s in range(shards):
                    self.src[s, m * rows_out : (m + 1) * rows_out] = grad[s * rows_out : (s + 1) * rows_out].astype(BF16)
            used = len(self.names) * rows_out
            if used < rows_l:
                self.src[:, used:] = jnp.zeros((shards, rows_l - used, width), BF16)
            start_all(self.c0_copies())

        def y(self):
            wait_all(self.c0_copies())
            own = self.src[:, aligned(core * self.rc, self.rc)]
            self.b0[...] = (self.b0[...].astype(F32) + own.astype(F32)).astype(BF16)
            start_all(self.y_copies())

        def x0(self):
            wait_all(self.y_copies())
            total = self.b0[w].astype(F32)
            for s in range(shards - 1):
                total = total + self.b1[s].astype(F32)
            self.b1[0] = total.astype(BF16)
            start_all(self.x0_copies())

        def rs(self):
            wait_all(self.x0_copies())
            own = self.b1[0, aligned(b * self.rb, self.rb)]
            self.b2[...] = (self.b2[...].astype(F32) + own.astype(F32)).astype(BF16)
            start_all(self.rs_copies())

        def ag(self):
            wait_all(self.rs_copies())
            total = self.b2[aligned(a * self.share, self.share)].astype(F32)
            for s in range(lines - 1):
                total = total + self.b3[s].astype(F32)
            own = aligned(self.out + core * self.rc + b * self.rb + a * self.share, self.share)
            sums_ref[own] = total.astype(BF16)
            start_all(self.ag_copies())

        def x(self):
            wait_all(self.ag_copies())
            start_all(self.x_copies())

        def c(self):
            wait_all(self.x_copies())
            start_all(self.c_copies())

        def done(self):
            wait_all(self.c_copies())

    rows_f = 4 * sum(chunks_f)
    rows_out = width // shards
    feeds = []
    begin = 0
    for index, rows in enumerate(chunks_f):
        feeds.append(Feed(begin, rows, rows_f, bufs_f[3 * index : 3 * index + 3]))
        begin += rows
    lates = {}
    for index, names in enumerate(sets):
        late = Late(rows_f + index * rows_l, rows_l, names, bufs_l[5 * index : 5 * index + 5])
        for name in names:
            lates[name] = late

    def late_step(name, step):
        late = lates[name]
        if step not in late.begun:
            late.begun.add(step)
            getattr(late, step)()

    values = x_ref[...].astype(F32)
    center = values - jnp.mean(values, axis=1, keepdims=True)
    inverse = lax.rsqrt(jnp.mean(center * center, axis=1, keepdims=True) + epsilon)
    unit = center * inverse

    def gradient(name):
        cols = vectors_ref[0:8].T
        gain_col, bias_col = cols[:, 0:1], cols[:, 1:2]
        if name == "q":
            m_q[...] = dot_tn(unit.astype(BF16), dq_ref[...])
            cs_q[...] = jnp.broadcast_to(jnp.sum(dq_ref[...].astype(F32), axis=0, keepdims=True), cs_q.shape)
            return gain_col * m_q[...] + bias_col * cs_q[0:1]
        if name == "p":
            total = jnp.zeros((width, width), F32)
            for index, (begin, size) in enumerate(pos_parts):
                if index:
                    start_all(pos_copies(begin, size))
                wait_all(pos_copies(begin, size))
                total = total + dot_nn(dpk_buf[:, 0:size], table_buf[0:size])
            return total.T
        m, cs = (mt_k, cs_k) if name == "k" else (mt_v, cs_v)
        return gain_col * m[...] + bias_col * fold_rows(cs[:, 0:1])

    mt_k[...] = jnp.zeros_like(mt_k)
    mt_v[...] = jnp.zeros_like(mt_v)
    cs_k[...] = jnp.zeros_like(cs_k)
    cs_v[...] = jnp.zeros_like(cs_v)
    pl.semaphore_wait(barrier, len(peers))
    wait_all(feed_copies)
    feeds[-1].y()
    weights_copy.wait()

    i_x0, i_x1, i_x2 = take(lines), take(lines), take(lines)

    def copy_x0(j):
        return remote(dxp.at[j, 1 - core], bx0.at[j], i_x0 + j, core_peer)

    def copy_x1(j):
        return remote(bx0.at[j, 1 - b], bx1.at[j], i_x1 + j, b_peer)

    def copy_x2(mask):
        return remote(bx1.at[order.index(mask)], bx2.at[mask - 1], i_x2 + mask, line_at(mask & -mask))

    def after_x0(j):
        copy_x0(j).wait()
        bx0[j] = (bx0[j].astype(F32) + dxp[j, core].astype(F32)).astype(BF16)
        copy_x1(j).start()

    def after_x1(j):
        mask = order[j]
        copy_x1(j).wait()
        total = bx1[j].astype(F32) + bx0[j, b].astype(F32)
        for bit in range(bits):
            if mask and 1 << bit >= (mask & -mask):
                break
            source = mask | 1 << bit
            copy_x2(source).wait()
            total = total + bx2[source - 1].astype(F32)
        if mask:
            bx1[j] = total.astype(BF16)
            copy_x2(mask).start()
        return total

    last = lines - 1
    events = {}

    def plan(j, after, work, *args):
        events.setdefault((min(j, last), after), []).append((work, args))

    one, two = feeds[0], feeds[-1]
    pair = len(feeds) > 1

    def along(feed, stage):
        begin, end = ((1, bits), (bits, bits + 1), (bits + 1, 2 * bits))[stage - 1]
        for step in range(begin, end):
            if step < bits:
                feed.rs(step)
            else:
                feed.ag(2 * bits - 1 - step)

    plan(0, "first", late_step, "q", "c0")
    plan(0, "blocks", after_x0, 0)
    plan(0, "blocks", late_step, "q", "y")
    plan(0, "blocks", late_step, "p", "c0")
    plan(1, "first", late_step, "p", "y")
    plan(1, "first", two.rs, 0)
    if pair:
        plan(1, "first", one.y)
    plan(1, "all", late_step, "q", "x0")
    if lines == 4:
        plan(1, "all", after_x1, 0)
        plan(1, "all", after_x0, 1)
    else:
        for j in range(1, last):
            plan(j + 1, "first", after_x0, j)
    plan(3, "first" if last >= 3 else "all", along, two, 1)
    plan(3, "blocks" if last >= 3 else "all", late_step, "p", "x0")
    plan(3, "blocks" if last >= 3 else "all", late_step, "q", "rs")

    def happen(j, after):
        for (when, place), works in sorted(events.items()):
            if place == after:

                @pl.when(j == when)
                def _():
                    for work, args in works:
                        work(*args)

    def line_step(j, _):
        slot = lax.rem(j, 2)

        @pl.when(j < last)
        def _():
            start_all(fetch(j + 1, 1 - slot))

        wait_all(fetch(j, slot))

        def make_block(core_of, b_of):
            keys = pl.ds(pl.multiple_of((2 * b_of + core_of) * tokens, tokens), tokens)
            part = dot_nn(wk_ref[...], dk_buf[slot, :, keys]) + dot_nn(wv_ref[...], dv_buf[slot, :, keys])
            dxp[j, core_of, b_of] = part.astype(BF16)

        make_block(1 - core, 0)
        make_block(1 - core, 1)
        copy_x0(j).start()
        happen(j, "first")
        make_block(core, 0)
        make_block(core, 1)
        happen(j, "blocks")
        mt_k[...] += dot_nn(dk_buf[slot], un_buf[slot])
        mt_v[...] += dot_nn(dv_buf[slot], un_buf[slot])
        for cs, buf in ((cs_k, dk_buf), (cs_v, dv_buf)):
            total = cs[...]
            for piece in range(group // BLK):
                total = total + buf[slot, :, piece * BLK : (piece + 1) * BLK].astype(F32)
            cs[...] = total
        happen(j, "all")
        return 0

    lax.fori_loop(0, lines, line_step, 0)
    for m, cs in ((mt_k, cs_k), (mt_v, cs_v)):
        m[...] = m[...].T
        cs[...] = jnp.broadcast_to(jnp.sum(cs[...], axis=1, keepdims=True), cs.shape)

    vstages = [[core_peer], [b_peer], [line_peer(s) for s in range(1, lines)], [shard_peer(s) for s in range(1, shards)]]
    vslots = []
    place = 0
    for stage in vstages:
        vslots.append(place)
        place += len(stage)
    vbegin = take(place)

    def v_copy(stage, index):
        slot = vslots[stage] + index
        return remote(vacc.at[pl.ds(stage * 16, 16)], vbuf.at[slot], vbegin + slot, vstages[stage][index])

    def v_start(stage):
        for index in range(len(vstages[stage])):
            v_copy(stage, index).start()

    def v_finish(stage):
        total = vacc[stage * 16 : stage * 16 + 16]
        for index in range(len(vstages[stage])):
            v_copy(stage, index).wait()
            total = total + vbuf[vslots[stage] + index]
        vacc[(stage + 1) * 16 : (stage + 2) * 16] = total

    def vectors_begin():
        vacc[0:16] = vec_ref[...]
        vacc[2:4] = bias_ref[0:2]
        gain_grad = m_q[...] * wq_ref[...].astype(F32)
        gain_grad = gain_grad + mt_k[...] * wk_ref[...].astype(F32) + mt_v[...] * wv_ref[...].astype(F32)
        vacc[0:1] = fold_rows(jnp.sum(gain_grad, axis=1, keepdims=True))
        total = dot_nt(cs_q[...].astype(BF16), wq_ref[...])
        for cs, weight in ((cs_k, wk_ref), (cs_v, wv_ref)):
            row = jnp.broadcast_to(fold_rows(cs[:, 0:1]), (8, width))
            total = total + dot_nt(row.astype(BF16), weight[...])
        vacc[1:2] = total[0:1]
        v_start(0)

    if pair:
        one.rs(0)
    after_x0(last)
    late_step("k", "c0")
    if lines == 4:
        after_x0(2)
    else:
        after_x1(0)
    along(two, 2)
    late_step("p", "rs")
    late_step("v", "c0")
    late_step("k", "y")
    late_step("q", "ag")
    vectors_begin()
    late_step("v", "y")
    if pair:
        along(one, 1)
    along(two, 3)
    late_step("p", "ag")
    v_finish(0)
    v_start(1)
    late_step("k", "x0")
    if pair:
        along(one, 2)
    late_step("v", "x0")
    v_finish(1)
    v_start(2)
    two.x()
    late_step("k", "rs")
    late_step("p", "x")
    late_step("v", "rs")
    if pair:
        along(one, 3)
    late_step("k", "ag")
    late_step("q", "x")
    late_step("v", "ag")
    for j in reversed(range(1, last)) if lines == 4 else range(1, last):
        after_x1(j)
    if pair:
        one.x()
    two.c()
    late_step("k", "x")
    late_step("p", "c")
    v_finish(2)
    v_start(3)
    late_step("v", "x")
    late_step("q", "c")
    if pair:
        one.c()
    leaving = []

    def leave(rows):
        copy = pltpu.make_async_copy(sums_ref.at[rows], sums_out.at[rows], sums_sem.at[len(leaving)])
        copy.start()
        leaving.append(copy)

    def feed_leaves(feed):
        feed.done()
        for quarter in range(4):
            leave(pl.ds(quarter * feed.rb + feed.begin, feed.rows))

    feed_leaves(two)
    own = after_x1(last)
    scaled = (own.T + dot_nt(dq_ref[...], wq_ref[...])) * vectors_ref[0:1]
    hidden_copy.wait()
    grad_ref[...] = hidden_ref[...] + inverse * (
        scaled - jnp.mean(scaled, axis=1, keepdims=True) - unit * jnp.mean(scaled * unit, axis=1, keepdims=True)
    )
    late_step("k", "c")
    late_step("v", "c")
    if pair:
        feed_leaves(one)
    v_finish(3)
    vsum_ref[...] = vacc[4 * 16 : 5 * 16]
    for name in "qpkv":
        if "done" not in lates[name].begun:
            late_step(name, "done")
            leave(pl.ds(lates[name].out, rows_l))
    wait_all(leaving)


def finish(lines, shards, chunks_f, sets, rows_l, cid, mine, come, dk, dv, unit_all, dpk, table, weights, dq, x, vectors, total, vec, bias, hidden):
    tokens, width = dq.shape
    vmem = pl.BlockSpec(memory_space=pltpu.VMEM)
    hbm = pl.BlockSpec(memory_space=pl.ANY)
    bufs = []
    for rows in chunks_f:
        bufs += [
            pltpu.VMEM((shards, rows, width), BF16),
            pltpu.VMEM((shards - 1, rows, width), BF16),
            pltpu.VMEM((rows, width), BF16),
        ]
    for names in sets:
        bufs += [
            pltpu.VMEM((shards, rows_l, width), BF16),
            pltpu.VMEM((shards, rows_l // 2, width), BF16),
            pltpu.VMEM((shards - 1, rows_l // 2, width), BF16),
            pltpu.VMEM((rows_l // 4, width), BF16),
            pltpu.VMEM((lines - 1, rows_l // 4 // lines, width), BF16),
        ]
    hops = shards - 1 + 2 * (lines - 1)
    copies = len(chunks_f) * (shards + 2 + 2 * (lines.bit_length() - 1)) + len(sets) * (hops + 4) + 3 * lines + 2 + lines - 1 + shards - 1
    total_rows = 4 * sum(chunks_f) + len(sets) * rows_l
    stages = 1 + 1 + (lines - 1) + (shards - 1)
    hold = min(dpk.shape[1], 17 * BLK)
    return pl.pallas_call(
        functools.partial(finish_kernel, lines, shards, tuple(chunks_f), sets, rows_l),
        out_shape=(
            jax.ShapeDtypeStruct((tokens, width), F32),
            jax.ShapeDtypeStruct((total_rows, width), BF16),
            jax.ShapeDtypeStruct((16, width), F32),
        ),
        in_specs=[hbm] * 8 + [vmem] * 6 + [hbm],
        out_specs=(vmem, hbm, vmem),
        scratch_shapes=[
            pltpu.VMEM(mine.shape, BF16),
            pltpu.VMEM(mine.shape, BF16),
            pltpu.VMEM((total_rows, width), BF16),
            pltpu.SemaphoreType.DMA((4 * len(chunks_f) + len(sets),)),
            pltpu.VMEM((2, width, 4 * tokens), BF16),
            pltpu.VMEM((2, width, 4 * tokens), BF16),
            pltpu.VMEM((2, 4 * tokens, width), BF16),
            pltpu.SemaphoreType.DMA((2, 3)),
            pltpu.VMEM((width, hold), BF16),
            pltpu.VMEM((hold, width), BF16),
            pltpu.VMEM((4, width, width), BF16),
            pltpu.VMEM((tokens, width), F32),
            pltpu.SemaphoreType.DMA((6,)),
            pltpu.VMEM((width, width), F32),
            pltpu.VMEM((width, width), F32),
            pltpu.VMEM((width, width), F32),
            pltpu.VMEM((8, width), F32),
            pltpu.VMEM((width, BLK), F32),
            pltpu.VMEM((width, BLK), F32),
            pltpu.VMEM((lines, 2, 2, width, tokens), BF16),
            pltpu.VMEM((lines, 2, width, tokens), BF16),
            pltpu.VMEM((lines, width, tokens), BF16),
            pltpu.VMEM((lines - 1, width, tokens), BF16),
            pltpu.VMEM((stages, 16, width), F32),
            pltpu.VMEM((5 * 16, width), F32),
        ]
        + bufs
        + [pltpu.SemaphoreType.DMA((copies,)), pltpu.SemaphoreType.DMA((copies,))],
        compiler_params=pltpu.CompilerParams(
            collective_id=cid, has_side_effects=True, vmem_limit_bytes=63 * 2**20
        ),
        cost_estimate=pl.CostEstimate(flops=10**10, bytes_accessed=30 * 2**20, transcendentals=0),
        name="finish",
    )(mine, come, dk, dv, unit_all, dpk, table, weights, dq, x, vectors, total, vec, bias, hidden)


def unpack_kernel(
    shards, rows_f, sets, rows_l, sums_ref, vsum_ref, total_ref, grad_ref, result_ref,
    grad_out, result_out, q_out, k_out, v_out, o_out, p_out, u_out, d_out, g1_out, b1_out, cb_out, pb_out, g2_out, b2_out, bd_out, bu_out,
    loss_out,
    low, wide, up, in_sem, out_sem,
):
    width = vsum_ref.shape[1]
    rows_out, rows_up = q_out.shape[0], d_out.shape[0]
    parts = u_out.shape[1] // width
    w = lax.axis_index("wsh")
    half = rows_f // 2
    step = min(rows_up, width)
    part_out, part_step = rows_out // 2, step // 2
    to = {"q": q_out, "p": p_out, "k": k_out, "v": v_out}
    pieces = []
    for index, names in enumerate(sets):
        pieces += [(rows_f + index * rows_l + m * rows_out, rows_out, to[name]) for m, name in enumerate(names)]
    ins = []
    for begin, size in [
        (h * half + begin, size)
        for begin, size in ((0, rows_up // 2), (rows_up // 2, rows_up // 2), (rows_up, part_out))
        for h in range(2)
    ] + [(begin, size) for begin, size, out in pieces]:
        rows = slice(begin, begin + size)
        ins.append(pltpu.make_async_copy(sums_ref.at[rows], low.at[rows], in_sem.at[len(ins)]))
    for copy in ins:
        copy.start()
    outs = []

    def send(src, dst):
        copy = pltpu.make_async_copy(src, dst, out_sem.at[len(outs)])
        copy.start()
        outs.append(copy)

    send(grad_ref, grad_out)
    send(result_ref, result_out)
    for h in range(2):
        ins[h].wait()
        for c in range(parts):
            begin = h * half + c * part_out
            up[h * part_out : (h + 1) * part_out, c * width : (c + 1) * width] = low[begin : begin + part_out].astype(F32)
    send(up, u_out)
    for h in range(2):
        ins[2 + h].wait()
        for j in range(rows_up // step):
            begin = h * half + rows_up // 2 + j * part_step
            wide[j * step + h * part_step : j * step + (h + 1) * part_step] = low[begin : begin + part_step].astype(F32)
    send(wide.at[0:rows_up], d_out)
    for h in range(2):
        ins[4 + h].wait()
        begin = h * half + rows_up
        wide[rows_up + h * part_out : rows_up + (h + 1) * part_out] = low[begin : begin + part_out].astype(F32)
    send(wide.at[rows_up : rows_up + rows_out], o_out)
    for index, (begin, size, out) in enumerate(pieces):
        ins[6 + index].wait()
        wide[begin : begin + size] = low[begin : begin + size].astype(F32)
        send(wide.at[begin : begin + size], out)

    def share(row):
        part = vsum_ref[row : row + 1, 0:rows_out]
        for s in range(1, shards):
            part = jnp.where(w == s, vsum_ref[row : row + 1, s * rows_out : (s + 1) * rows_out], part)
        return part.reshape(rows_out)

    for row, ref in enumerate((g1_out, b1_out, cb_out, pb_out, g2_out, b2_out, bd_out)):
        ref[...] = share(row)
    per = rows_up // rows_out
    for q in range(per):
        part = None
        for s in range(shards):
            group = s * per + q
            row, place = 7 + group // shards, group % shards
            piece = vsum_ref[row : row + 1, place * rows_out : (place + 1) * rows_out]
            part = piece if part is None else jnp.where(w == s, piece, part)
        bu_out[q * rows_out : (q + 1) * rows_out] = part.reshape(rows_out)
    loss_out[0, 0] = vsum_ref[7 + parts, 0] / (total_ref[0, 0] * width)
    for copy in outs:
        copy.wait()


def unpack(shards, rows_f, sets, rows_l, hidden, sums, vsum, total, grad, result):
    tokens, width = grad.shape
    rows_out, rows_up = width // shards, hidden // shards
    vmem = pl.BlockSpec(memory_space=pltpu.VMEM)
    hbm = pl.BlockSpec(memory_space=pl.ANY)
    square = jax.ShapeDtypeStruct((rows_out, width), F32)
    vector = jax.ShapeDtypeStruct((rows_out,), F32)
    return pl.pallas_call(
        functools.partial(unpack_kernel, shards, rows_f, sets, rows_l),
        out_shape=(
            jax.ShapeDtypeStruct((tokens, width), F32), jax.ShapeDtypeStruct((tokens, width), BF16), square, square, square, square, square,
            jax.ShapeDtypeStruct((rows_out, hidden), F32), jax.ShapeDtypeStruct((rows_up, width), F32),
            vector, vector, vector, vector, vector, vector, vector, jax.ShapeDtypeStruct((rows_up,), F32),
            jax.ShapeDtypeStruct((1, 1), F32),
        ),
        in_specs=[hbm, vmem, vmem, vmem, vmem],
        out_specs=(hbm,) * 9 + (vmem,) * 8 + (pl.BlockSpec(memory_space=pltpu.SMEM),),
        scratch_shapes=[
            pltpu.VMEM(sums.shape, BF16),
            pltpu.VMEM(sums.shape, F32),
            pltpu.VMEM((rows_out, hidden), F32),
            pltpu.SemaphoreType.DMA((10,)),
            pltpu.SemaphoreType.DMA((9,)),
        ],
        compiler_params=pltpu.CompilerParams(vmem_limit_bytes=62 * 2**20),
        cost_estimate=pl.CostEstimate(flops=10**6, bytes_accessed=12 * 2**20, transcendentals=0),
        name="unpack",
    )(sums, vsum, total, grad, result)


PARTS = 2


def start_kernel(
    lines, shards, x_ref, wk_ref, wv_ref, wp_ref, wq_ref, wo_ref, wu_ref, wd_ref,
    g1_ref, b1_ref, cb_ref, pb_ref, g2_ref, b2_ref, bd_ref, bu_ref, mask_ref, far_ref, near_ref,
    k_ref, v_ref, unit_ref, pk_ref, table_ref, qc_ref, qp_ref, weights_out, wo_out, wu_out, wd_out, vectors_ref, total_ref,
    weights_ref, x_all, k_buf, v_buf, pk_buf, t_buf, wo_buf, wu_buf, wd_buf, vec_src, vec_buf, cnt_buf, cnt_acc,
    up_send, up_recv, down_send, down_recv, b_send, b_recv, c_send, c_recv,
    y_send, y_recv, yc_send, yc_recv, d_send, d_recv, s_send, s_recv, out_sem, pos_sem, own_sem,
):
    tokens, width = x_ref.shape
    piece = tokens // PARTS
    half = width // 2
    chunks = pk_buf.shape[0] // BLK
    ctx = lax.axis_index("ctx")
    w = lax.axis_index("wsh")
    core = lax.rem(ctx, 2)
    b = lax.rem(ctx // 2, 2)
    a = ctx // 4

    def at(a_to, b_to, core_to):
        return (a_to * 2 + b_to) * 2 + core_to

    def shard_peer(s):
        return (ctx, lax.rem(w + s, shards))

    def line_peer(s):
        return (at(lax.rem(a + s, lines), b, core), w)

    core_peer = (at(a, b, 1 - core), w)
    b_peer = (at(a, 1 - b, core), w)
    peers = [core_peer, b_peer] + [line_peer(s) for s in range(1, lines)] + [shard_peer(s) for s in range(1, shards)]
    barrier = pltpu.get_barrier_semaphore()
    for peer in peers:
        pl.semaphore_signal(barrier, inc=1, device_id=peer, device_id_type=MESH)

    def remote(src, dst, send, recv, peer):
        return pltpu.make_async_remote_copy(
            src_ref=src, dst_ref=dst, send_sem=send, recv_sem=recv, device_id=peer, device_id_type=MESH
        )

    def block(slot):
        return aligned(slot * tokens, tokens)

    def unit_of(rows):
        values = rows.astype(F32)
        center = values - jnp.mean(values, axis=1, keepdims=True)
        return center * lax.rsqrt(jnp.mean(center * center, axis=1, keepdims=True) + epsilon)

    x_all[block(ctx)] = unit_of(x_ref[...]).astype(BF16)
    rows_out = wq_ref.shape[0]
    quarter = rows_out // 2
    rows_up = wd_ref.shape[0]
    weight_in = (wk_ref, wv_ref, wp_ref, wq_ref, wo_ref, wu_ref)
    weight_to = tuple(weights_ref.at[m] for m in range(4)) + (wo_buf, wu_buf)
    own_copies = [
        pltpu.make_async_copy(ref, to.at[aligned(w * rows_out, rows_out)], own_sem.at[m])
        for m, (ref, to) in enumerate(zip(weight_in[:4], weight_to))
    ]
    for copy in own_copies:
        copy.start()
    vec_src[...] = jnp.zeros_like(vec_src)
    for row, ref in enumerate((g1_ref, b1_ref, cb_ref, pb_ref, g2_ref, b2_ref, bd_ref)):
        vec_src[row : row + 1] = ref[...].astype(F32).reshape(1, rows_out)
    bias_rows = rows_up // rows_out
    for q in range(bias_rows):
        vec_src[7 + q : 8 + q] = bu_ref[q * rows_out : (q + 1) * rows_out].astype(F32).reshape(1, rows_out)
    cnt_acc[0:8] = jnp.broadcast_to(jnp.sum(mask_ref[...].astype(F32), axis=1, keepdims=True), (8, BLK))
    pl.semaphore_wait(barrier, len(peers))

    def x_copy(slot, h, send, recv, peer):
        rows = aligned(slot * tokens + h * piece, piece)
        return remote(x_all.at[rows], x_all.at[rows], send, recv, peer)

    def up_copy(p, h):
        peer = (at(jnp.minimum(a + 1, lines - 1), b, core), w)
        return x_copy(at(p, b, core), h, up_send.at[p, h], up_recv.at[p, h], peer)

    def down_copy(p, h):
        peer = (at(jnp.maximum(a - 1, 0), b, core), w)
        return x_copy(at(p, b, core), h, down_send.at[p, h], down_recv.at[p, h], peer)

    def b_copy(p, h, b_from):
        return x_copy(at(p, b_from, core), h, b_send.at[p, h], b_recv.at[p, h], b_peer)

    def c_copy(p, far, b_from, core_from):
        rows = block(at(p, b_from, core_from))
        return remote(x_all.at[rows], x_all.at[rows], c_send.at[far, p], c_recv.at[far, p], core_peer)

    def weight_copy(m, s):
        rows = aligned(w * rows_out + core * quarter, quarter)
        src = weight_in[m].at[aligned(core * quarter, quarter)]
        return remote(src, weight_to[m].at[rows], y_send.at[m, s - 1], y_recv.at[m, s - 1], shard_peer(s))

    def weight_pass(m, s):
        rows = aligned(lax.rem(w + shards - s, shards) * rows_out + core * quarter, quarter)
        return remote(
            weight_to[m].at[rows], weight_to[m].at[rows], yc_send.at[m, s - 1], yc_recv.at[m, s - 1], core_peer
        )

    low = lax.rem(a, 2)
    quarter_in, quarter_to = (wd_ref,), (wd_buf,)
    pair_peer = (at(a + 1 - 2 * low, b, core), w)

    def quarter_rows(m, s, low_of):
        size = quarter_in[m].shape[0]
        owner = lax.rem(w + shards - s, shards)
        return aligned(owner * size + (low_of * 2 + core) * (size // 4), size // 4)

    def quarter_copy(m, s):
        size = quarter_in[m].shape[0]
        src = quarter_in[m].at[aligned((low * 2 + core) * (size // 4), size // 4)]
        dst = quarter_to[m].at[quarter_rows(m, 0, low)]
        return remote(src, dst, d_send.at[m, 0, s - 1], d_recv.at[m, 0, s - 1], shard_peer(s))

    def quarter_pass(m, kind, s):
        rows = quarter_rows(m, s, 1 - low if kind == 3 else low)
        peer = pair_peer if kind == 1 else core_peer
        ref = quarter_to[m].at[rows]
        return remote(ref, ref, d_send.at[m, kind, s - 1], d_recv.at[m, kind, s - 1], peer)

    def quarter_on(m):
        for s in range(1, shards):
            quarter_copy(m, s).wait()
            quarter_pass(m, 1, s).start()
            quarter_pass(m, 2, s).start()

    def vec_copy(s):
        return remote(vec_src, vec_buf.at[s - 1], s_send.at[s - 1], s_recv.at[s - 1], shard_peer(s))

    stages = [[shard_peer(s) for s in range(1, shards)], [core_peer], [b_peer], [line_peer(s) for s in range(1, lines)]]
    slots = []
    place = 0
    for stage in stages:
        slots.append(place)
        place += len(stage)

    def cnt_copy(stage, index):
        slot = slots[stage] + index
        sem = shards - 1 + slot
        return remote(cnt_acc.at[pl.ds(stage * 8, 8)], cnt_buf.at[slot], s_send.at[sem], s_recv.at[sem], stages[stage][index])

    def cnt_start(stage):
        for index in range(len(stages[stage])):
            cnt_copy(stage, index).start()

    def cnt_finish(stage):
        total = cnt_acc[stage * 8 : stage * 8 + 8]
        for index in range(len(stages[stage])):
            cnt_copy(stage, index).wait()
            total = total + cnt_buf[slots[stage] + index]
        cnt_acc[(stage + 1) * 8 : (stage + 2) * 8] = total

    for s in range(1, shards):
        vec_copy(s).start()
    cnt_start(0)
    for h in range(PARTS):

        @pl.when(a + 1 < lines)
        def _():
            up_copy(a, h).start()

        @pl.when(a >= 1)
        def _():
            down_copy(a, h).start()

        b_copy(a, h, b).start()
    c_copy(a, 0, b, core).start()
    for kind, m in ((0, 0), (0, 1), (1, 0), (0, 2), (0, 3), (0, 5), (0, 4)):
        for s in range(1, shards):
            (quarter_copy if kind else weight_copy)(m, s).start()


    def table_step(d, _):
        sin_far, cos_far = far_ref[0, pl.ds(d, 1)], far_ref[1, pl.ds(d, 1)]
        sin_near, cos_near = near_ref[0], near_ref[1]
        rows = aligned(d * BLK, BLK)
        t_buf[rows, :half] = (sin_far * cos_near - cos_far * sin_near).astype(BF16)
        t_buf[rows, half:] = (cos_far * cos_near + sin_far * sin_near).astype(BF16)
        return 0

    lax.fori_loop(0, chunks, table_step, 0)
    table_out = pltpu.make_async_copy(t_buf, table_ref, pos_sem.at[0])
    table_out.start()
    lane_to = lax.broadcasted_iota(jnp.int32, (rows_out, width), 1)
    lane_from = lax.broadcasted_iota(jnp.int32, (rows_out, width), 0)
    row_at = lax.broadcasted_iota(jnp.int32, (16, width), 0)

    def spread(values, place):
        return dot_nn(values.astype(BF16), (lane_to == lane_from + place * rows_out).astype(BF16))

    def placed(values, owner):
        full = jnp.where(row_at < 7, spread(values, owner), 0.0)
        for q in range(bias_rows):
            group = owner * bias_rows + q
            row = jnp.broadcast_to(values[7 + q : 8 + q], values.shape)
            full = full + jnp.where(row_at == 7 + group // shards, spread(row, lax.rem(group, shards)), 0.0)
        return full

    vectors = placed(vec_src[...], w)
    for s in range(1, shards):
        vec_copy(s).wait()
        vectors = vectors + placed(vec_buf[s - 1], lax.rem(w + shards - s, shards))
    vectors_ref[...] = vectors
    cnt_finish(0)
    cnt_start(1)

    def out_copies(slot):
        rows = block(slot)
        return (
            pltpu.make_async_copy(k_buf.at[rows], k_ref.at[rows], out_sem.at[0, slot]),
            pltpu.make_async_copy(v_buf.at[rows], v_ref.at[rows], out_sem.at[1, slot]),
            pltpu.make_async_copy(x_all.at[rows], unit_ref.at[rows], out_sem.at[2, slot]),
        )

    def project(p):
        def one(q, _):
            other_b = q // 2
            other_core = lax.rem(q, 2)

            @pl.when(q == 1)
            def _():
                c_copy(p, 0, b, core).wait()

            @pl.when(q == 2)
            def _():
                for h in range(PARTS):
                    b_copy(p, h, b).wait()
                c_copy(p, 1, 1 - b, core).start()

            @pl.when(q == 3)
            def _():
                c_copy(p, 1, 1 - b, core).wait()

            slot = at(p, b + other_b - 2 * b * other_b, core + other_core - 2 * core * other_core)
            rows = block(slot)
            normed = (x_all[rows].astype(F32) * vectors_ref[0:1] + vectors_ref[1:2]).astype(BF16)
            k_buf[rows] = dot_nn(normed, weights_ref[0]).astype(BF16)
            v_buf[rows] = dot_nn(normed, weights_ref[1]).astype(BF16)
            for copy in out_copies(slot):
                copy.start()
            return 0

        lax.fori_loop(0, 4, one, 0)

    def pos_step(d, _):
        rows = aligned(d * BLK, BLK)
        pk_buf[rows] = dot_nn(t_buf[rows], weights_ref[2]).astype(BF16)
        return 0

    last = lines - 1

    def line_step(s, _):
        below, high = a - 1 - s, a + 1 + s

        for h in range(PARTS):

            @pl.when((s < lines - 1) & (below >= 0))
            def _():
                p = jnp.maximum(below, 0)
                up_copy(p, h).wait_recv()

                @pl.when(a + 1 < lines)
                def _():
                    up_copy(p, h).start()

                b_copy(p, h, b).start()
                if h == PARTS - 1:
                    c_copy(p, 0, b, core).start()

            @pl.when((s < lines - 1) & (high < lines))
            def _():
                p = jnp.minimum(high, lines - 1)
                down_copy(p, h).wait_recv()

                @pl.when(a >= 1)
                def _():
                    down_copy(p, h).start()

                b_copy(p, h, b).start()
                if h == PARTS - 1:
                    c_copy(p, 0, b, core).start()

        @pl.when(s == 0)
        def _():
            cnt_finish(1)
            cnt_start(2)

        @pl.when(s == 1)
        def _():
            for copy in own_copies:
                copy.wait()
            for m in range(2):
                for t in range(1, shards):
                    weight_copy(m, t).wait()
                    weight_pass(m, t).start()
            cnt_finish(2)
            cnt_start(3)
            for m in range(2):
                for t in range(1, shards):
                    weight_pass(m, t).wait()

        @pl.when(s == min(2, last))
        def _():
            quarter_on(0)
            for t in range(1, shards):
                weight_copy(2, t).wait()
                weight_pass(2, t).start()

        @pl.when((s >= 1) & (a - s + 1 >= 0))
        def _():
            project(jnp.maximum(a - s + 1, 0))

        @pl.when((s >= 2) & (a + s - 1 < lines))
        def _():
            project(jnp.minimum(a + s - 1, lines - 1))

        @pl.when(s == min(2, last))
        def _():
            for t in range(1, shards):
                weight_pass(2, t).wait()
            lax.fori_loop(0, chunks // 2, pos_step, 0)

        @pl.when(s == last)
        def _():
            for t in range(1, shards):
                weight_copy(3, t).wait()
                weight_pass(3, t).start()
            lax.fori_loop(chunks // 2, chunks, pos_step, 0)
            for t in range(1, shards):
                weight_pass(3, t).wait()
            normed = (x_all[block(ctx)].astype(F32) * vectors_ref[0:1] + vectors_ref[1:2]).astype(BF16)
            queries = dot_nn(normed, weights_ref[3]).astype(BF16).astype(F32)
            qc_ref[...] = ((queries + vectors_ref[2:3]) * 0.125).astype(BF16)
            qp_ref[...] = ((queries + vectors_ref[3:4]) * 0.125).astype(BF16)

        return 0

    lax.fori_loop(0, lines + 1, line_step, 0)
    for m in (5, 4):
        for s in range(1, shards):
            weight_copy(m, s).wait()
            weight_pass(m, s).start()
    pos_out = pltpu.make_async_copy(pk_buf, pk_ref, pos_sem.at[1])
    pos_out.start()
    weights_leave = pltpu.make_async_copy(weights_ref, weights_out, pos_sem.at[2])
    weights_leave.start()
    cnt_finish(3)
    total_ref[...] = cnt_acc[4 * 8 : 5 * 8]

    def sends_done(p, _):
        for h in range(PARTS):

            @pl.when((a + 1 < lines) & (p <= a))
            def _():
                up_copy(p, h).wait_send()

            @pl.when((a >= 1) & (p >= a))
            def _():
                down_copy(p, h).wait_send()

        return 0

    lax.fori_loop(0, lines, sends_done, 0)

    def outs_done(slot, _):
        for copy in out_copies(slot):
            copy.wait()
        return 0

    lax.fori_loop(0, 4 * lines, outs_done, 0)
    for s in range(1, shards):
        weight_pass(4, s).wait()
        weight_pass(5, s).wait()
        quarter_pass(0, 1, s).wait()
        quarter_pass(0, 3, s).start()
    for s in range(1, shards):
        quarter_pass(0, 2, s).wait()
        quarter_pass(0, 3, s).wait()
    far_copies = []
    for m, (buf, to) in enumerate(((wo_buf, wo_out), (wu_buf, wu_out), (wd_buf, wd_out))):
        size = buf.shape[0] // shards
        for s in range(1, shards):
            rows = aligned(lax.rem(w + s, shards) * size, size)
            far_copies.append(pltpu.make_async_copy(buf.at[rows], to.at[rows], own_sem.at[4 + m * (shards - 1) + s - 1]))
    for copy in far_copies:
        copy.start()
    for copy in far_copies:
        copy.wait()
    table_out.wait()
    pos_out.wait()
    weights_leave.wait()


def start(lines, shards, cid, limit, x, weights, vectors, mask, far, near):
    tokens, width = x.shape
    hidden = weights[5].shape[1]
    rows_out = weights[0].shape[0]
    members = 4 * lines
    keys = members * tokens
    span = limit * BLK
    vmem = pl.BlockSpec(memory_space=pltpu.VMEM)
    hbm = pl.BlockSpec(memory_space=pl.ANY)
    small = 2 * (shards - 1) + 1 + 1 + lines - 1
    dma = pltpu.SemaphoreType.DMA
    other = shards - 1
    return pl.pallas_call(
        functools.partial(start_kernel, lines, shards),
        out_shape=(
            jax.ShapeDtypeStruct((keys, width), BF16),
            jax.ShapeDtypeStruct((keys, width), BF16),
            jax.ShapeDtypeStruct((keys, width), BF16),
            jax.ShapeDtypeStruct((span, width), BF16),
            jax.ShapeDtypeStruct((span, width), BF16),
            jax.ShapeDtypeStruct((tokens, width), BF16),
            jax.ShapeDtypeStruct((tokens, width), BF16),
            jax.ShapeDtypeStruct((4, width, width), BF16),
            jax.ShapeDtypeStruct((width, width), BF16),
            jax.ShapeDtypeStruct((width, hidden), BF16),
            jax.ShapeDtypeStruct((hidden, width), BF16),
            jax.ShapeDtypeStruct((16, width), F32),
            jax.ShapeDtypeStruct((8, BLK), F32),
        ),
        in_specs=[vmem] + [hbm] * 7 + [vmem] * 11,
        out_specs=(hbm,) * 5 + (vmem,) * 2 + (hbm,) * 4 + (vmem,) * 2,
        scratch_shapes=[
            pltpu.VMEM((4, width, width), BF16),
            pltpu.VMEM((keys, width), BF16),
            pltpu.VMEM((keys, width), BF16),
            pltpu.VMEM((keys, width), BF16),
            pltpu.VMEM((span, width), BF16),
            pltpu.VMEM((span, width), BF16),
            pltpu.VMEM((width, width), BF16),
            pltpu.VMEM((width, hidden), BF16),
            pltpu.VMEM((hidden, width), BF16),
            pltpu.VMEM((16, rows_out), F32),
            pltpu.VMEM((other, 16, rows_out), F32),
            pltpu.VMEM((lines + shards, 8, BLK), F32),
            pltpu.VMEM((5 * 8, BLK), F32),
        ]
        + [dma((lines, PARTS))] * 6
        + [dma((2, lines))] * 2
        + [dma((6, other))] * 4
        + [dma((1, 4, other))] * 2
        + [dma((small,))] * 2
        + [dma((3, members)), dma((3,)), dma((4 + 3 * other,))],
        compiler_params=pltpu.CompilerParams(collective_id=cid, has_side_effects=True, vmem_limit_bytes=60 * 2**20),
        cost_estimate=pl.CostEstimate(flops=6 * 10**9, bytes_accessed=20 * 2**20, transcendentals=0),
        name="start",
    )(x, *weights, *vectors, mask, far, near)


GELU_SCALE = math.sqrt(2.0 / math.pi)


def middle_kernel(
    shards, rows_f, mask_ref, x_ref, mixed_ref, teacher_ref, out_grad_ref, vectors_ref, total_ref,
    wo_own, wu_own, wd_own, wo_ref, wu_ref, wd_ref,
    out_ref, hidden_ref, gm_ref, mine_ref, theirs_ref, vec_ref,
    wo, wu, wd, slope, act, gf_ref, landed, sem, send_sem, recv_sem,
):
    tokens, width = x_ref.shape
    parts = wu.shape[1] // width
    ctx = lax.axis_index("ctx")
    core = lax.rem(ctx, 2)
    core_peer = (ctx + 1 - 2 * core, lax.axis_index("wsh"))
    barrier = pltpu.get_barrier_semaphore()
    pl.semaphore_signal(barrier, inc=1, device_id=core_peer, device_id_type=MESH)
    w = lax.axis_index("wsh")
    copies = []
    for k, (own, gathered, full) in enumerate(((wo_own, wo_ref, wo), (wu_own, wu_ref, wu), (wd_own, wd_ref, wd))):
        size = own.shape[0]
        part = [pltpu.make_async_copy(own, full.at[aligned(w * size, size)], sem.at[k, 0])]
        for s in range(1, shards):
            rows = aligned(lax.rem(w + s, shards) * size, size)
            part.append(pltpu.make_async_copy(gathered.at[rows], full.at[rows], sem.at[k, s]))
        for copy in part:
            copy.start()
        copies.append(part)

    def arrive(k):
        for copy in copies[k]:
            copy.wait()

    b = lax.rem(ctx // 2, 2)
    half, quarter = rows_f // 2, rows_f // 4

    rows_up, rows_out = wd_own.shape[0], wo_own.shape[0]
    step = min(rows_up, width)
    part_out, part_step = rows_out // 2, step // 2
    gives = []

    def give(begin, size, owner=None):
        owners = slice(None) if owner is None else owner
        rows = aligned((1 - core) * half + begin, size)
        index = len(gives)
        copy = pltpu.make_async_remote_copy(
            src_ref=gf_ref.at[owners, rows], dst_ref=landed.at[owners, pl.ds(begin, size)],
            send_sem=send_sem.at[index], recv_sem=recv_sem.at[index], device_id=core_peer, device_id_type=MESH,
        )
        copy.start()
        gives.append(copy)

    gain, offset, down_bias = vectors_ref[4:5], vectors_ref[5:6], vectors_ref[6:7]
    mixed = mixed_ref[...].astype(BF16)
    arrive(0)
    hidden = x_ref[...].astype(F32) + dot_nn(mixed, wo[...])
    center = hidden - jnp.mean(hidden, axis=1, keepdims=True)
    inverse = lax.rsqrt(jnp.mean(center * center, axis=1, keepdims=True) + epsilon)
    unit = center * inverse
    normed = (unit * gain + offset).astype(BF16)
    result = hidden + down_bias
    arrive(1)
    for c in range(parts):
        cols = slice(c * width, (c + 1) * width)
        v = dot_nn(normed, wu[:, cols]) + vectors_ref[7 + c : 8 + c]
        square = v * v
        t = jnp.tanh(GELU_SCALE * (v + 0.044715 * (square * v)))
        act[:, cols] = (0.5 * v * (1.0 + t)).astype(BF16)
        slope[:, cols] = 0.5 * (1.0 + t) + 0.5 * v * (1.0 - t * t) * (GELU_SCALE * (1.0 + 3.0 * 0.044715 * square))
        if c == 0:
            arrive(2)
        result = result + dot_nn(act[:, cols], wd[cols])
    out_ref[...] = result.astype(BF16)
    mask = jnp.broadcast_to(mask_ref[...].astype(F32), (8, tokens)).T[:, 0:1]
    error = result - teacher_ref[...].astype(F32)
    masked = mask * error
    count = jnp.sum(total_ref[0:1, 0:1], axis=1, keepdims=True)
    grad_result = out_grad_ref[...].astype(F32) + (2.0 / (count * width)) * masked
    branch = grad_result.astype(BF16)
    vec_ref[...] = jnp.zeros_like(vec_ref)
    vec_ref[7 + parts : 8 + parts] = jnp.broadcast_to(
        jnp.sum(jnp.sum(masked * error, axis=1, keepdims=True), axis=0, keepdims=True), (1, width)
    )
    vec_ref[6:7] = jnp.sum(branch.astype(F32), axis=0, keepdims=True)
    used = rows_up + part_out
    if used < half:
        for h in range(2):
            gf_ref[:, h * half + used : (h + 1) * half] = jnp.zeros((shards, half - used, width), BF16)
    pl.semaphore_wait(barrier, 1)
    grad_normed = jnp.zeros((tokens, width), F32)
    for c in range(parts):
        cols = slice(c * width, (c + 1) * width)
        grad_pre = (dot_nt(branch, wd[cols]) * slope[:, cols]).astype(BF16)
        vec_ref[7 + c : 8 + c] = jnp.sum(grad_pre.astype(F32), axis=0, keepdims=True)
        grad_normed = grad_normed + dot_nt(grad_pre, wu[:, cols])
        up = dot_tn(normed, grad_pre).astype(BF16)
        down = dot_tn(act[:, cols], branch).astype(BF16)
        for s in range(shards):
            for h in range(2):
                begin = s * rows_out + h * part_out
                gf_ref[s, h * half + c * part_out : h * half + (c + 1) * part_out] = up[begin : begin + part_out]
        give(c * part_out, part_out)
        for begin in range(0, width, step):
            row = c * width + begin
            owner, place = row // rows_up, rows_up // 2 + row % rows_up // 2
            for h in range(2):
                piece = down[begin + h * part_step : begin + (h + 1) * part_step]
                gf_ref[owner, h * half + place : h * half + place + part_step] = piece
            give(place, part_step, owner)
    vec_ref[4:5] = jnp.sum(grad_normed * unit, axis=0, keepdims=True)
    vec_ref[5:6] = jnp.sum(grad_normed, axis=0, keepdims=True)
    scaled = grad_normed * gain
    grad_hidden = grad_result + inverse * (
        scaled - jnp.mean(scaled, axis=1, keepdims=True) - unit * jnp.mean(scaled * unit, axis=1, keepdims=True)
    )
    hidden_ref[...] = grad_hidden
    attn = grad_hidden.astype(BF16)
    gm_ref[...] = dot_nt(attn, wo[...]).astype(BF16)
    outer = dot_tn(mixed, attn).astype(BF16)
    for s in range(shards):
        for h in range(2):
            begin = s * rows_out + h * part_out
            gf_ref[s, h * half + rows_up : h * half + used] = outer[begin : begin + part_out]
    give(rows_up, half - rows_up)
    for copy in gives:
        copy.wait()
    for ref, place in ((theirs_ref, 1 - b), (mine_ref, b)):
        own = gf_ref[:, aligned(core * half + place * quarter, quarter)].astype(F32)
        ref[...] = (own + landed[:, aligned(place * quarter, quarter)].astype(F32)).astype(BF16)


def middle(shards, rows_f, cid, mask, x, mixed, teacher, out_grad, vectors, total, own, gathered):
    tokens, width = x.shape
    hidden = own[1].shape[1]
    pieces = hidden // width + hidden // min(own[2].shape[0], width) + 1
    vmem = pl.BlockSpec(memory_space=pltpu.VMEM)
    hbm = pl.BlockSpec(memory_space=pl.ANY)
    return pl.pallas_call(
        functools.partial(middle_kernel, shards, rows_f),
        out_shape=(
            jax.ShapeDtypeStruct((tokens, width), BF16),
            jax.ShapeDtypeStruct((tokens, width), F32),
            jax.ShapeDtypeStruct((tokens, width), BF16),
            jax.ShapeDtypeStruct((shards, rows_f // 4, width), BF16),
            jax.ShapeDtypeStruct((shards, rows_f // 4, width), BF16),
            jax.ShapeDtypeStruct((16, width), F32),
        ),
        in_specs=[vmem] * 7 + [hbm] * 6,
        out_specs=(vmem,) * 6,
        scratch_shapes=[
            pltpu.VMEM((width, width), BF16),
            pltpu.VMEM((width, hidden), BF16),
            pltpu.VMEM((hidden, width), BF16),
            pltpu.VMEM((tokens, hidden), F32),
            pltpu.VMEM((tokens, hidden), BF16),
            pltpu.VMEM((shards, rows_f, width), BF16),
            pltpu.VMEM((shards, rows_f // 2, width), BF16),
            pltpu.SemaphoreType.DMA((3, shards)),
            pltpu.SemaphoreType.DMA((pieces,)),
            pltpu.SemaphoreType.DMA((pieces,)),
        ],
        compiler_params=pltpu.CompilerParams(collective_id=cid, has_side_effects=True, vmem_limit_bytes=56 * 2**20),
        cost_estimate=pl.CostEstimate(flops=4 * 10**9, bytes_accessed=20 * 2**20, transcendentals=10**6),
        name="middle",
    )(mask, x, mixed, teacher, out_grad, vectors, total, *own, *gathered)


def body(
    inputs, block_perm, seq_lengths, loss_mask, teacher, out_grad, gain_one, bias_one, w_query, w_key, w_value,
    w_output, w_pos, content_bias, position_bias, gain_two, bias_two, w_up, bias_up, w_down, bias_down,
):
    width = inputs.shape[2]
    shards = lax.axis_size("wsh")
    members = lax.axis_size("ctx")
    lines = members // 4
    hidden = bias_up.shape[0] * shards
    blocks = block_perm.shape[1]
    limit = blocks // 2 + 1
    rows_up, rows_out = hidden // shards, width // shards

    frequency = np.exp(np.arange(width // 2) * (-2.0 * math.log(10000.0) / width))
    far_angle = (np.arange(-(-limit // 8) * 8) * BLK + (BLK - 1))[:, None] * frequency[None]
    near_angle = np.arange(BLK)[:, None] * frequency[None]
    far = jnp.asarray(np.stack([np.sin(far_angle), np.cos(far_angle)]), F32)
    near = jnp.asarray(np.stack([np.sin(near_angle), np.cos(near_angle)]), F32)

    keys, values, unit_all, pos_keys, table, qc, qp, weights, wo, wu, wd, vectors, total = start(
        lines, shards, 0, limit, inputs[0], (w_key, w_value, w_pos, w_query, w_output, w_up, w_down),
        (gain_one, bias_one, content_bias, position_bias, gain_two, bias_two, bias_down, bias_up), loss_mask, far, near,
    )
    mixed, linv, probs = attn_fwd(block_perm, seq_lengths, qc, qp, keys, values, pos_keys, blocks, limit)

    step = 16 * lines
    pieces = -(-(2 * rows_up + rows_out) // (4 * step))
    split = min(2, pieces)
    chunks_f = tuple((pieces * (i + 1) // split - pieces * i // split) * step for i in range(split))
    rows_f = 4 * step * pieces
    if rows_out % (32 * lines):
        sets, rows_l = (("q", "p"), ("k", "v")), -(-2 * rows_out // (32 * lines)) * 32 * lines
    else:
        sets, rows_l = (("q",), ("p",), ("k",), ("v",)), rows_out
    output, grad_hidden, grad_mixed, mine, theirs, vec = middle(
        shards, rows_f, 2, loss_mask, inputs[0], mixed, teacher[0], out_grad[0], vectors, total,
        (w_output, w_up, w_down), (wo, wu, wd),
    )
    come = lax.ppermute(theirs, "ctx", [(i, i ^ 2) for i in range(members)])
    grad_query, bias_grads, dk_t, dv_t, dpk_t = attn_bwd(
        block_perm, seq_lengths, qc, qp, keys, values, pos_keys, probs, linv, grad_mixed, mixed, blocks, limit
    )
    grad_input, sums, vsum = finish(
        lines, shards, chunks_f, sets, rows_l, 1, mine, come, dk_t, dv_t, unit_all, dpk_t, table, weights, grad_query,
        inputs[0], vectors, total, vec, bias_grads, grad_hidden,
    )
    (
        grad_input, output, g_query, g_key, g_value, g_output, g_pos, g_up, g_down,
        v_g1, v_b1, v_cb, v_pb, v_g2, v_b2, v_bd, v_bu, loss,
    ) = unpack(shards, rows_f, sets, rows_l, hidden, sums, vsum, total, grad_input, output)
    return (
        output[None], loss.reshape(()), grad_input[None], v_g1, v_b1, g_query, g_key, g_value, g_output, g_pos,
        v_cb, v_pb, v_g2, v_b2, g_up, v_bu, g_down, v_bd,
    )


def solution(mesh):
    rows = P("wsh", "ctx", None)
    vector = P("wsh")
    matrix = P("wsh", None)
    placed = (
        rows, matrix, matrix, P("wsh", "ctx"), rows, rows, vector, vector, matrix, matrix, matrix, matrix, matrix,
        vector, vector, vector, vector, matrix, vector, matrix, vector,
    )
    out = (
        rows, P(), rows, vector, vector, matrix, matrix, matrix, matrix, matrix, vector, vector, vector, vector,
        matrix, vector, matrix, vector,
    )
    return jax.shard_map(body, mesh=mesh, in_specs=placed, out_specs=out, check_vma=False)
```

```python
import functools
import math

import jax
import jax.numpy as jnp
import numpy as np
from jax import lax
from jax.experimental import pallas as pl
from jax.experimental.pallas import tpu as pltpu
from jax.sharding import PartitionSpec as P

HEADS = 8
HEAD = 64
PAIRS = HEADS // 2
BLK = 128
ROWS = HEADS * BLK
NEG = -1e30
epsilon = 1e-05
F32 = jnp.float32
BF16 = jnp.bfloat16


def dot_nt(a, b):
    return lax.dot_general(a, b, (((1,), (1,)), ((), ())), preferred_element_type=F32)


def dot_nn(a, b):
    return lax.dot_general(a, b, (((1,), (0,)), ((), ())), preferred_element_type=F32)


def dot_tn(a, b):
    return lax.dot_general(a, b, (((0,), (0,)), ((), ())), preferred_element_type=F32)


def iotas():
    row = lax.broadcasted_iota(jnp.int32, (BLK, BLK), 0)
    col = lax.broadcasted_iota(jnp.int32, (BLK, BLK), 1)
    return row, col


def read_places(perm_ref, lengths_ref, meta, blocks, count):
    device = lax.axis_index("ctx")
    meta[0] = perm_ref[0, 2 * device]
    meta[1] = perm_ref[0, 2 * device + 1]

    def place(slot, _):
        meta[2 + perm_ref[0, slot]] = slot
        return 0

    lax.fori_loop(0, blocks, place, 0, unroll=True)
    end = jnp.int32(0)
    for e in range(count):
        end = end + lengths_ref[0, e]
        meta[2 + blocks + e] = end


def block_range(meta, a, blocks, limit):
    qb = meta[a]
    first = qb * BLK
    low = jnp.int32(0)
    for e in range(meta.shape[0] - 2 - blocks):
        end = meta[2 + blocks + e]
        low = jnp.where(first >= end, jnp.maximum(low, end), low)
    lowest = low // BLK
    return qb, lowest, jnp.minimum(qb - lowest + 1, limit)


def stack_heads(pair):
    lane = lax.broadcasted_iota(jnp.int32, pair.shape, 1)
    zero = jnp.zeros_like(pair)
    return jnp.concatenate([jnp.where(lane < HEAD, pair, zero), jnp.where(lane >= HEAD, pair, zero)], axis=0)


def flip_rows(x):
    index = 7 - lax.broadcasted_iota(jnp.int32, (8, BLK), 0)
    slabs = [jnp.take_along_axis(x[8 * g : 8 * g + 8], index, axis=0) for g in reversed(range(BLK // 8))]
    return jnp.concatenate(slabs, axis=0)


def flip_two(x):
    return jnp.concatenate([flip_rows(x[:BLK]), flip_rows(x[BLK:])], axis=0)


def needed_blocks(meta, blocks, limit):
    ranges = []
    for a in range(2):
        qb, lowest, count = block_range(meta, a, blocks, limit)
        ranges.append((qb + 1 - 2 * ((count + 1) // 2), qb))
    return ranges


def load_keys(meta, blocks, limit, pairs, sem):
    (low0, high0), (low1, high1) = needed_blocks(meta, blocks, limit)
    for hbm, ref in pairs:
        ref[0:BLK] = jnp.zeros((BLK, ref.shape[1]), ref.dtype)

    def copies(kb):
        slot = pl.ds(pl.multiple_of(meta[2 + kb] * BLK, BLK), BLK)
        place = pl.ds(pl.multiple_of((kb + 1) * BLK, BLK), BLK)
        return [
            pltpu.make_async_copy(hbm.at[slot], ref.at[place], sem.at[index, kb]) for index, (hbm, ref) in enumerate(pairs)
        ]

    def begin(kb, _):
        @pl.when(((kb >= low0) & (kb <= high0)) | ((kb >= low1) & (kb <= high1)))
        def _():
            for copy in copies(kb):
                copy.start()

        return 0

    lax.fori_loop(0, blocks, begin, 0)

    def arrive(a):
        low, high = (jnp.where(a == 0, x, y) for x, y in ((low0, low1), (high0, high1)))

        def one(kb, _):
            @pl.when((a == 0) | (kb < low0) | (kb > high0))
            def _():
                for copy in copies(kb):
                    copy.wait()

            return 0

        lax.fori_loop(jnp.maximum(low, 0), high + 1, one, 0)

    return arrive


def wide_iotas():
    row = lax.broadcasted_iota(jnp.int32, (BLK, 2 * BLK), 0)
    col = lax.broadcasted_iota(jnp.int32, (BLK, 2 * BLK), 1)
    return row, col


def attn_fwd_kernel(
    blocks, limit, perm_ref, lengths_ref, qc_ref, qp_ref, k_in, v_in, pk_in, mixed_ref, linv_ref, p_ref,
    meta, k_ref, v_ref, pk_ref, q2c, q2p, prev, top, total, acc, s_scr, p_buf, kv_sem, pk_sem, p_sem,
):
    read_places(perm_ref, lengths_ref, meta, blocks, lengths_ref.shape[1])
    span = pk_in.shape[0]
    pk_copy = pltpu.make_async_copy(pk_in, pk_ref.at[0:span], pk_sem)
    pk_copy.start()
    arrive = load_keys(meta, blocks, limit, ((k_in, k_ref), (v_in, v_ref)), kv_sem)
    pk_ref[span:] = jnp.zeros((BLK, pk_ref.shape[1]), BF16)
    row, col = iotas()
    tri = col <= row
    wide_row, wide_col = wide_iotas()
    tiles = s_scr.shape[0]

    def p_copy(slot, index):
        return pltpu.make_async_copy(p_buf.at[slot], p_ref.at[index], p_sem.at[slot])

    def one_query_block(a, _):
        qb, lowest, count = block_range(meta, a, blocks, limit)
        pairs = (count + 1) // 2
        rows_a = pl.ds(pl.multiple_of(a * BLK, BLK), BLK)
        pos = qb * BLK + wide_row
        start = jnp.zeros((BLK, 2 * BLK), jnp.int32)
        for e in range(meta.shape[0] - 2 - blocks):
            end = meta[2 + blocks + e]
            start = jnp.where(pos >= end, jnp.maximum(start, end), start)
        for hp in range(PAIRS):
            lanes = slice(hp * BLK, (hp + 1) * BLK)
            q2c[hp] = stack_heads(qc_ref[rows_a, lanes].astype(F32)).astype(BF16)
            q2p[hp] = stack_heads(qp_ref[rows_a, lanes].astype(F32)).astype(BF16)
        prev[...] = jnp.zeros_like(prev)
        top[...] = jnp.full_like(top, NEG)
        total[...] = jnp.zeros_like(total)
        acc[...] = jnp.zeros_like(acc)
        arrive(a)

        @pl.when(a == 0)
        def _():
            pk_copy.wait()

        def score_step(t, _):
            kb = qb - 2 * t
            keys = pl.ds(pl.multiple_of(kb * BLK, BLK), 2 * BLK)
            place = (kb - 1) * BLK + wide_col
            bias = jnp.where((place >= start) & (place <= pos), 0.0, NEG).astype(F32)
            drows = pl.ds(pl.multiple_of(2 * t * BLK, BLK), 2 * BLK)
            for hp in range(PAIRS):
                lanes = slice(hp * BLK, (hp + 1) * BLK)
                s = dot_nt(q2c[hp], k_ref[keys, lanes])
                r = dot_nt(q2p[hp], pk_ref[drows, lanes])
                for half in range(2):
                    part = slice(half * BLK, (half + 1) * BLK)
                    rows = slice((2 * hp + half) * BLK, (2 * hp + half + 1) * BLK)
                    near = pltpu.roll(r[part, :BLK], 1, 1, stride=1, stride_axis=0)
                    far = pltpu.roll(r[part, BLK:], 1, 1, stride=1, stride_axis=0)
                    late = s[part, BLK:] + jnp.where(tri, near, prev[rows]) + bias[:, BLK:]
                    early = s[part, :BLK] + jnp.where(tri, far, near) + bias[:, :BLK]
                    prev[rows] = far
                    s_scr[t, rows, :BLK] = early
                    s_scr[t, rows, BLK:] = late
                    top[rows] = jnp.maximum(top[rows], jnp.maximum(early, late))
            return 0

        lax.fori_loop(0, pairs, score_step, 0)
        for h in range(HEADS):
            rows = slice(h * BLK, (h + 1) * BLK)
            top[rows] = jnp.broadcast_to(jnp.max(top[rows], axis=1, keepdims=True), (BLK, BLK))

        def mix_step(t, _):
            kb = qb - 2 * t
            keys = pl.ds(pl.multiple_of(kb * BLK, BLK), 2 * BLK)
            slot = lax.rem(t, 2)

            @pl.when(t >= 2)
            def _():
                p_copy(slot, 0).wait()

            for hp in range(PAIRS):
                lanes = slice(hp * BLK, (hp + 1) * BLK)
                rows = slice(2 * hp * BLK, 2 * (hp + 1) * BLK)
                early = jnp.exp(s_scr[t, rows, :BLK] - top[rows])
                late = jnp.exp(s_scr[t, rows, BLK:] - top[rows])
                total[rows] += early + late
                p_buf[slot, rows, :BLK] = flip_two(early).astype(BF16)
                p_buf[slot, rows, BLK:] = flip_two(late).astype(BF16)
                low = jnp.concatenate([early.astype(BF16), late.astype(BF16)], axis=1)
                acc[hp] += dot_nn(low, v_ref[keys, lanes])
            p_copy(slot, a * tiles + t).start()
            return 0

        lax.fori_loop(0, pairs, mix_step, 0)
        p_copy(lax.rem(pairs - 1, 2), 0).wait()

        @pl.when(pairs >= 2)
        def _():
            p_copy(lax.rem(pairs, 2), 0).wait()

        lane = lax.broadcasted_iota(jnp.int32, (BLK, BLK), 1)
        for hp in range(PAIRS):
            lanes = slice(hp * BLK, (hp + 1) * BLK)
            parts = []
            for half in range(2):
                h = 2 * hp + half
                rows = slice(h * BLK, (h + 1) * BLK)
                inv = 1.0 / jnp.sum(total[rows], axis=1, keepdims=True)
                inv = jnp.broadcast_to(inv, (BLK, BLK))
                linv_ref[a, rows] = inv
                parts.append(acc[hp, half * BLK : (half + 1) * BLK] * inv)
            mixed_ref[rows_a, lanes] = jnp.where(lane < HEAD, parts[0], parts[1])
        return 0

    lax.fori_loop(0, 2, one_query_block, 0)


def attn_fwd(perm, lengths, qc, qp, k, v, pk, blocks, limit):
    tokens, width = qc.shape
    keys, span = k.shape[0], pk.shape[0]
    tiles = (limit + 1) // 2
    vmem = pl.BlockSpec(memory_space=pltpu.VMEM)
    hbm = pl.BlockSpec(memory_space=pl.ANY)
    return pl.pallas_call(
        functools.partial(attn_fwd_kernel, blocks, limit),
        out_shape=(
            jax.ShapeDtypeStruct((tokens, width), F32),
            jax.ShapeDtypeStruct((2, ROWS, BLK), F32),
            jax.ShapeDtypeStruct((2 * tiles, ROWS, 2 * BLK), BF16),
        ),
        in_specs=[pl.BlockSpec(memory_space=pltpu.SMEM)] * 2 + [vmem] * 2 + [hbm] * 3,
        out_specs=(vmem, vmem, hbm),
        scratch_shapes=[
            pltpu.SMEM((2 + blocks + lengths.shape[1],), jnp.int32),
            pltpu.VMEM((keys + BLK, width), BF16),
            pltpu.VMEM((keys + BLK, width), BF16),
            pltpu.VMEM((span + BLK, width), BF16),
            pltpu.VMEM((PAIRS, 2 * BLK, BLK), BF16),
            pltpu.VMEM((PAIRS, 2 * BLK, BLK), BF16),
            pltpu.VMEM((ROWS, BLK), F32),
            pltpu.VMEM((ROWS, BLK), F32),
            pltpu.VMEM((ROWS, BLK), F32),
            pltpu.VMEM((PAIRS, 2 * BLK, BLK), F32),
            pltpu.VMEM((tiles, ROWS, 2 * BLK), F32),
            pltpu.VMEM((2, ROWS, 2 * BLK), BF16),
            pltpu.SemaphoreType.DMA((2, blocks)),
            pltpu.SemaphoreType.DMA,
            pltpu.SemaphoreType.DMA((2,)),
        ],
        compiler_params=pltpu.CompilerParams(vmem_limit_bytes=60 * 2**20),
        cost_estimate=pl.CostEstimate(flops=3 * 10**9, bytes_accessed=20 * 2**20, transcendentals=4 * 10**6),
        name="attn_fwd",
    )(perm, lengths, qc, qp, k, v, pk)


def attn_bwd_kernel(
    blocks, limit, perm_ref, lengths_ref, qc_ref, qp_ref, k_in, v_in, pk_in, p_ref, linv_ref, gm_ref, mixed_ref,
    dq_ref, bias_ref, dk_out, dv_out, dpk_out,
    meta, k_ref, v_ref, pk_ref, dk_ref, dv_ref, q2c_t, q2p_t, gm2, gm2_t, dd, carry, dqk, dqp, dpk, p_buf,
    empty, dpk_low, kv_sem, pk_sem, p_sem, out_sem, dpk_sem,
):
    read_places(perm_ref, lengths_ref, meta, blocks, lengths_ref.shape[1])
    span = pk_in.shape[0]
    pk_copy = pltpu.make_async_copy(pk_in, pk_ref.at[0:span], pk_sem)
    pk_copy.start()
    arrive = load_keys(meta, blocks, limit, ((k_in, k_ref), (v_in, v_ref)), kv_sem)
    pk_ref[span:] = jnp.zeros((BLK, pk_ref.shape[1]), BF16)
    row, col = iotas()
    tri = col <= BLK - 1 - row
    tiles = p_ref.shape[0] // 2
    (low0, high0), (low1, high1) = needed_blocks(meta, blocks, limit)

    def out_copies(kb, nothing=False):
        slot = pl.ds(pl.multiple_of(meta[2 + kb] * BLK, BLK), BLK)
        place = pl.ds(pl.multiple_of((kb + 1) * BLK, BLK), BLK)
        return [
            pltpu.make_async_copy(empty if nothing else ref.at[:, place], out.at[:, slot], out_sem.at[index, kb])
            for index, (ref, out) in enumerate(((dk_ref, dk_out), (dv_ref, dv_out)))
        ]

    empty[...] = jnp.zeros_like(empty)
    for ref in (dk_ref, dv_ref):
        ref[:, 0:BLK] = jnp.zeros((ref.shape[0], BLK), BF16)

    def prepare(kb, _):
        used = ((kb >= low0) & (kb <= high0)) | ((kb >= low1) & (kb <= high1))

        @pl.when(used)
        def _():
            place = pl.ds(pl.multiple_of((kb + 1) * BLK, BLK), BLK)
            for ref in (dk_ref, dv_ref):
                ref[:, place] = jnp.zeros((ref.shape[0], BLK), BF16)

        @pl.when(jnp.logical_not(used))
        def _():
            for copy in out_copies(kb, True):
                copy.start()

        return 0

    lax.fori_loop(0, blocks, prepare, 0)
    dpk[...] = jnp.zeros_like(dpk)
    bias_ref[...] = jnp.zeros_like(bias_ref)

    def p_copy(slot, index):
        return pltpu.make_async_copy(p_ref.at[index], p_buf.at[slot], p_sem.at[slot])

    def one_query_block(a, _):
        qb, lowest, count = block_range(meta, a, blocks, limit)
        pairs = (count + 1) // 2
        rows_a = pl.ds(pl.multiple_of(a * BLK, BLK), BLK)
        p_copy(0, a * tiles + pairs - 1).start()
        for hp in range(PAIRS):
            lanes = slice(hp * BLK, (hp + 1) * BLK)
            rows = slice(2 * hp * BLK, 2 * (hp + 1) * BLK)
            q2c_t[hp] = stack_heads(flip_rows(qc_ref[rows_a, lanes].astype(F32))).T.astype(BF16)
            q2p_t[hp] = stack_heads(flip_rows(qp_ref[rows_a, lanes].astype(F32))).T.astype(BF16)
            g = stack_heads(gm_ref[rows_a, lanes].astype(F32))
            scaled = flip_two(g * linv_ref[a, rows])
            gm2[hp] = scaled.astype(BF16)
            gm2_t[hp] = scaled.T.astype(BF16)
            pair = flip_rows(mixed_ref[rows_a, lanes])
            dd[rows] = jnp.broadcast_to(
                jnp.sum(scaled * jnp.concatenate([pair, pair], axis=0), axis=1, keepdims=True), (2 * BLK, BLK)
            )
        carry[...] = jnp.zeros_like(carry)
        dqk[...] = jnp.zeros_like(dqk)
        dqp[...] = jnp.zeros_like(dqp)
        arrive(a)

        @pl.when(a == 0)
        def _():
            pk_copy.wait()

        def step(t, _):
            tile = pairs - 1 - t
            kb = qb - 2 * tile
            keys = pl.ds(pl.multiple_of(kb * BLK, BLK), 2 * BLK)
            drows = pl.ds(pl.multiple_of(2 * tile * BLK, BLK), 2 * BLK)
            slot = lax.rem(t, 2)
            p_copy(slot, 0).wait()

            @pl.when(tile >= 1)
            def _():
                p_copy(1 - slot, a * tiles + tile - 1).start()

            for hp in range(PAIRS):
                lanes = slice(hp * BLK, (hp + 1) * BLK)
                rows = slice(2 * hp * BLK, 2 * (hp + 1) * BLK)
                p = p_buf[slot, rows]
                g = dot_nt(gm2[hp], v_ref[keys, lanes])
                early = (p[:, :BLK].astype(F32) * (g[:, :BLK] - dd[rows])).astype(BF16)
                late = (p[:, BLK:].astype(F32) * (g[:, BLK:] - dd[rows])).astype(BF16)
                gs = jnp.concatenate([early, late], axis=1)
                early, late = early.astype(F32), late.astype(F32)
                rots = []
                for half in range(2):
                    part = slice(half * BLK, (half + 1) * BLK)
                    crow = slice((2 * hp + half) * BLK, (2 * hp + half + 1) * BLK)
                    far = jnp.where(tri, early[part], carry[crow])
                    near = jnp.where(tri, late[part], early[part])
                    carry[crow] = late[part]
                    rots.append(
                        jnp.concatenate(
                            [
                                pltpu.roll(near, 0, 1, stride=1, stride_axis=0).astype(BF16),
                                pltpu.roll(far, 0, 1, stride=1, stride_axis=0).astype(BF16),
                            ],
                            axis=1,
                        )
                    )
                rot = jnp.concatenate(rots, axis=0)
                dqk[hp] += dot_nn(gs, k_ref[keys, lanes])
                dqp[hp] += dot_nn(rot, pk_ref[drows, lanes])
                dk_ref[lanes, keys] = (dk_ref[lanes, keys].astype(F32) + dot_nn(q2c_t[hp], gs)).astype(BF16)
                dv_ref[lanes, keys] = (dv_ref[lanes, keys].astype(F32) + dot_nn(gm2_t[hp], p)).astype(BF16)
                dpk[lanes, drows] += dot_nn(q2p_t[hp], rot)
            for block in (kb - 1, kb):

                @pl.when((block >= 0) & ((a == 1) | (block < low1) | (block > high1)))
                def _():
                    for copy in out_copies(jnp.maximum(block, 0)):
                        copy.start()

            return 0

        lax.fori_loop(0, pairs, step, 0)
        lane = lax.broadcasted_iota(jnp.int32, (BLK, BLK), 1)
        for hp in range(PAIRS):
            lanes = slice(hp * BLK, (hp + 1) * BLK)
            ck = jnp.where(lane < HEAD, dqk[hp, :BLK], dqk[hp, BLK:]) * 0.125
            cp = jnp.where(lane < HEAD, dqp[hp, :BLK], dqp[hp, BLK:]) * 0.125
            dq_ref[rows_a, lanes] = flip_rows(ck + cp).astype(BF16)
            bias_ref[0:1, lanes] += jnp.sum(ck, axis=0, keepdims=True)
            bias_ref[1:2, lanes] += jnp.sum(cp, axis=0, keepdims=True)
        return 0

    lax.fori_loop(0, 2, one_query_block, 0)

    def given(kb, _):
        for copy in out_copies(kb):
            copy.wait()
        return 0

    pieces = [(begin, min(4 * BLK, span - begin)) for begin in range(0, span, 4 * BLK)]
    copies = []
    for index, (begin, size) in enumerate(pieces):
        cols = slice(begin, begin + size)
        dpk_low[:, cols] = dpk[:, cols].astype(BF16)
        copy = pltpu.make_async_copy(dpk_low.at[:, cols], dpk_out.at[:, cols], dpk_sem.at[index])
        copy.start()
        copies.append(copy)
    lax.fori_loop(0, blocks, given, 0)
    for copy in copies:
        copy.wait()


def attn_bwd(perm, lengths, qc, qp, k, v, pk, p, linv, gm, mixed, blocks, limit):
    tokens, width = qc.shape
    keys, span = k.shape[0], pk.shape[0]
    vmem = pl.BlockSpec(memory_space=pltpu.VMEM)
    hbm = pl.BlockSpec(memory_space=pl.ANY)
    return pl.pallas_call(
        functools.partial(attn_bwd_kernel, blocks, limit),
        out_shape=(
            jax.ShapeDtypeStruct((tokens, width), BF16),
            jax.ShapeDtypeStruct((8, width), F32),
            jax.ShapeDtypeStruct((width, keys), BF16),
            jax.ShapeDtypeStruct((width, keys), BF16),
            jax.ShapeDtypeStruct((width, span), BF16),
        ),
        in_specs=[pl.BlockSpec(memory_space=pltpu.SMEM)] * 2 + [vmem] * 2 + [hbm] * 4 + [vmem] * 3,
        out_specs=(vmem, vmem, hbm, hbm, hbm),
        scratch_shapes=[
            pltpu.SMEM((2 + blocks + lengths.shape[1],), jnp.int32),
            pltpu.VMEM((keys + BLK, width), BF16),
            pltpu.VMEM((keys + BLK, width), BF16),
            pltpu.VMEM((span + BLK, width), BF16),
            pltpu.VMEM((width, keys + BLK), BF16),
            pltpu.VMEM((width, keys + BLK), BF16),
            pltpu.VMEM((PAIRS, BLK, 2 * BLK), BF16),
            pltpu.VMEM((PAIRS, BLK, 2 * BLK), BF16),
            pltpu.VMEM((PAIRS, 2 * BLK, BLK), BF16),
            pltpu.VMEM((PAIRS, BLK, 2 * BLK), BF16),
            pltpu.VMEM((ROWS, BLK), F32),
            pltpu.VMEM((ROWS, BLK), F32),
            pltpu.VMEM((PAIRS, 2 * BLK, BLK), F32),
            pltpu.VMEM((PAIRS, 2 * BLK, BLK), F32),
            pltpu.VMEM((width, span + BLK), F32),
            pltpu.VMEM((2, ROWS, 2 * BLK), BF16),
            pltpu.VMEM((width, BLK), BF16),
            pltpu.VMEM((width, span), BF16),
            pltpu.SemaphoreType.DMA((2, blocks)),
            pltpu.SemaphoreType.DMA,
            pltpu.SemaphoreType.DMA((2,)),
            pltpu.SemaphoreType.DMA((2, blocks)),
            pltpu.SemaphoreType.DMA((span // (4 * BLK) + 1,)),
        ],
        compiler_params=pltpu.CompilerParams(vmem_limit_bytes=62 * 2**20),
        cost_estimate=pl.CostEstimate(flops=6 * 10**9, bytes_accessed=30 * 2**20, transcendentals=0),
        name="attn_bwd",
    )(perm, lengths, qc, qp, k, v, pk, p, linv, gm, mixed)


MESH = pl.DeviceIdType.MESH


def fold_rows(x):
    return jnp.broadcast_to(x, (x.shape[0], BLK)).T[0:1]


def aligned(begin, size):
    return pl.ds(pl.multiple_of(begin, math.gcd(size, 16)), size)


def finish_kernel(
    lines, shards, chunks_f, sets, rows_l,
    mine_in, come_in, dk_ref, dv_ref, unit_all_ref, dpk_ref, table_ref, weights_in, dq_ref, x_ref,
    vectors_ref, total_ref, vec_ref, bias_ref, hidden_in,
    grad_ref, sums_out, vsum_ref,
    mine_ref, come_ref, sums_ref, sums_sem, dk_buf, dv_buf, un_buf, in_sem, dpk_buf, table_buf, weights_ref, hidden_ref, pos_sem, m_q, mt_k, mt_v, cs_q, cs_k, cs_v, dxp, bx0, bx1, bx2, vbuf, vacc,
    *rest,
):
    wk_ref, wv_ref, wq_ref = weights_ref.at[0], weights_ref.at[1], weights_ref.at[3]
    tokens, width = dq_ref.shape
    bufs_f = rest[: 3 * len(chunks_f)]
    bufs_l = rest[3 * len(chunks_f) : -2]
    send_sem, recv_sem = rest[-2:]
    ctx = lax.axis_index("ctx")
    w = lax.axis_index("wsh")
    core = lax.rem(ctx, 2)
    b = lax.rem(ctx // 2, 2)
    a = ctx // 4

    def at(a_to, b_to, core_to):
        return (a_to * 2 + b_to) * 2 + core_to

    def line_peer(s):
        return (at(lax.rem(a + s, lines), b, core), w)

    def shard_peer(s):
        return (ctx, lax.rem(w + s, shards))

    core_peer = (at(a, b, 1 - core), w)
    b_peer = (at(a, 1 - b, core), w)
    peers = [core_peer, b_peer] + [line_peer(s) for s in range(1, lines)] + [shard_peer(s) for s in range(1, shards)]
    barrier = pltpu.get_barrier_semaphore()
    for peer in peers:
        pl.semaphore_signal(barrier, inc=1, device_id=peer, device_id_type=MESH)

    counter = [0]

    def take(number):
        begin = counter[0]
        counter[0] += number
        return begin

    def remote(src, dst, index, peer):
        return pltpu.make_async_remote_copy(
            src_ref=src, dst_ref=dst, send_sem=send_sem.at[index], recv_sem=recv_sem.at[index],
            device_id=peer, device_id_type=MESH,
        )

    bits = lines.bit_length() - 1
    order = []
    for bit in range(bits):
        order += [m for m in reversed(range(lines)) if m & ((1 << (bit + 1)) - 1) == 1 << bit]
    order.append(0)

    def other(mask):
        place = 0
        for bit in range(bits):
            own = lax.rem(a // (1 << bit), 2)
            place = place + (1 << bit) * ((1 - own) if mask >> bit & 1 else own)
        return place

    def line_place(j):
        place = jnp.int32(0)
        for index, mask in enumerate(order):
            place = place + jnp.where(j == index, other(mask), 0)
        return place

    def line_at(mask):
        return (at(other(mask), b, core), w)

    group = 4 * tokens

    def fetch(j, slot):
        begin = pl.multiple_of(line_place(j) * group, group)
        return (
            pltpu.make_async_copy(dk_ref.at[:, pl.ds(begin, group)], dk_buf.at[slot], in_sem.at[slot, 0]),
            pltpu.make_async_copy(dv_ref.at[:, pl.ds(begin, group)], dv_buf.at[slot], in_sem.at[slot, 1]),
            pltpu.make_async_copy(unit_all_ref.at[pl.ds(begin, group)], un_buf.at[slot], in_sem.at[slot, 2]),
        )

    span, hold = table_ref.shape[0], table_buf.shape[0]
    pos_parts = [(begin, min(hold, span - begin)) for begin in range(0, span, hold)]

    def pos_copies(begin, size):
        rows = pl.ds(begin, size)
        return [
            pltpu.make_async_copy(dpk_ref.at[:, rows], dpk_buf.at[:, 0:size], pos_sem.at[0]),
            pltpu.make_async_copy(table_ref.at[rows], table_buf.at[0:size], pos_sem.at[1]),
        ]

    weights_copy = pltpu.make_async_copy(weights_in, weights_ref, pos_sem.at[2])
    hidden_copy = pltpu.make_async_copy(hidden_in, hidden_ref, pos_sem.at[3])
    feed_copies = [
        pltpu.make_async_copy(mine_in, mine_ref, pos_sem.at[4]),
        pltpu.make_async_copy(come_in, come_ref, pos_sem.at[5]),
    ]
    for copy in feed_copies:
        copy.start()
    weights_copy.start()
    for copy in fetch(0, 0):
        copy.start()
    for copy in pos_copies(*pos_parts[0]):
        copy.start()
    hidden_copy.start()

    def start_all(copies):
        for copy in copies:
            copy.start()

    def wait_all(copies):
        for copy in copies:
            copy.wait()

    def own_bit(bit):
        return lax.rem(a // (1 << bit), 2)

    def bit_peer(bit):
        return line_at(1 << bit)

    class Feed:
        def __init__(self, begin, rows, total_rows, bufs):
            self.begin, self.rows = begin, rows
            self.rc, self.rb = total_rows // 2, total_rows // 4
            self.b0, self.b1, self.b2 = bufs
            self.iy, self.irs, self.iag, self.ix, self.ic = take(shards - 1), take(bits), take(bits), take(1), take(2)

        def region(self, bit):
            start = 0
            for k in range(bit):
                start = start + own_bit(k) * (self.rows >> (k + 1))
            return start, self.rows >> bit

        def y_copies(self):
            return [
                remote(self.b0.at[lax.rem(w + s, shards)], self.b1.at[s - 1], self.iy + s - 1, shard_peer(s))
                for s in range(1, shards)
            ]

        def rs_copies(self, bit):
            start, size = self.region(bit)
            size = size // 2
            give = aligned(start + (1 - own_bit(bit)) * size, size)
            begin = sum(self.rows >> (k + 1) for k in range(bit))
            return [remote(self.b1.at[0, give], self.b2.at[begin : begin + size], self.irs + bit, bit_peer(bit))]

        def place(self, b_of, begin, size):
            return aligned(core * self.rc + b_of * self.rb + self.begin + begin, size)

        def ag_copies(self, bit):
            own = self.place(b, *self.region(bit + 1))
            return [remote(sums_ref.at[own], sums_ref.at[own], self.iag + bit, bit_peer(bit))]

        def x_copies(self):
            own = self.place(b, 0, self.rows)
            return [remote(sums_ref.at[own], sums_ref.at[own], self.ix, b_peer)]

        def c_copies(self):
            return [
                remote(sums_ref.at[rows], sums_ref.at[rows], self.ic + k, core_peer)
                for k, rows in enumerate((self.place(b, 0, self.rows), self.place(1 - b, 0, self.rows)))
            ]

        def y(self):
            rows = pl.ds(self.begin, self.rows)
            self.b0[...] = (mine_ref[:, rows].astype(F32) + come_ref[:, rows].astype(F32)).astype(BF16)
            start_all(self.y_copies())

        def rs(self, bit):
            if bit == 0:
                wait_all(self.y_copies())
                total = self.b0[w].astype(F32)
                for s in range(shards - 1):
                    total = total + self.b1[s].astype(F32)
                self.b1[0] = total.astype(BF16)
            else:
                self.add(bit - 1)
            start_all(self.rs_copies(bit))

        def add(self, bit):
            wait_all(self.rs_copies(bit))
            start, size = self.region(bit + 1)
            begin = sum(self.rows >> (k + 1) for k in range(bit))
            rows = aligned(start, size)
            self.b1[0, rows] = (self.b1[0, rows].astype(F32) + self.b2[begin : begin + size].astype(F32)).astype(BF16)

        def ag(self, bit):
            if bit == bits - 1:
                self.add(bit)
                start, size = self.region(bits)
                sums_ref[self.place(b, start, size)] = self.b1[0, aligned(start, size)]
            else:
                wait_all(self.ag_copies(bit + 1))
            start_all(self.ag_copies(bit))

        def x(self):
            wait_all(self.ag_copies(0))
            start_all(self.x_copies())

        def c(self):
            wait_all(self.x_copies())
            start_all(self.c_copies())

        def done(self):
            wait_all(self.c_copies())

    class Late:
        def __init__(self, out, rows, names, bufs):
            self.out, self.rows, self.names, self.begun = out, rows, names, set()
            self.src, self.b0, self.b1, self.b2, self.b3 = bufs
            self.rc, self.rb, self.share = rows // 2, rows // 4, rows // 4 // lines
            self.i0, self.iy, self.i2 = take(1), take(shards - 1), take(1)
            self.irs, self.iag, self.ix, self.ic = take(lines - 1), take(lines - 1), take(1), take(1)

        def c0_copies(self):
            return [remote(self.src.at[:, aligned((1 - core) * self.rc, self.rc)], self.b0, self.i0, core_peer)]

        def y_copies(self):
            return [
                remote(self.b0.at[lax.rem(w + s, shards)], self.b1.at[s - 1], self.iy + s - 1, shard_peer(s))
                for s in range(1, shards)
            ]

        def x0_copies(self):
            return [remote(self.b1.at[0, aligned((1 - b) * self.rb, self.rb)], self.b2, self.i2, b_peer)]

        def rs_copies(self):
            return [
                remote(
                    self.b2.at[aligned(lax.rem(a + s, lines) * self.share, self.share)],
                    self.b3.at[s - 1], self.irs + s - 1, line_peer(s),
                )
                for s in range(1, lines)
            ]

        def ag_copies(self):
            own = aligned(self.out + core * self.rc + b * self.rb + a * self.share, self.share)
            return [remote(sums_ref.at[own], sums_ref.at[own], self.iag + s - 1, line_peer(s)) for s in range(1, lines)]

        def x_copies(self):
            own = aligned(self.out + core * self.rc + b * self.rb, self.rb)
            return [remote(sums_ref.at[own], sums_ref.at[own], self.ix, b_peer)]

        def c_copies(self):
            own = aligned(self.out + core * self.rc, self.rc)
            return [remote(sums_ref.at[own], sums_ref.at[own], self.ic, core_peer)]

        def c0(self):
            for m, name in enumerate(self.names):
                grad = gradient(name)
                for s in range(shards):
                    self.src[s, m * rows_out : (m + 1) * rows_out] = grad[s * rows_out : (s + 1) * rows_out].astype(BF16)
            used = len(self.names) * rows_out
            if used < rows_l:
                self.src[:, used:] = jnp.zeros((shards, rows_l - used, width), BF16)
            start_all(self.c0_copies())

        def y(self):
            wait_all(self.c0_copies())
            own = self.src[:, aligned(core * self.rc, self.rc)]
            self.b0[...] = (self.b0[...].astype(F32) + own.astype(F32)).astype(BF16)
            start_all(self.y_copies())

        def x0(self):
            wait_all(self.y_copies())
            total = self.b0[w].astype(F32)
            for s in range(shards - 1):
                total = total + self.b1[s].astype(F32)
            self.b1[0] = total.astype(BF16)
            start_all(self.x0_copies())

        def rs(self):
            wait_all(self.x0_copies())
            own = self.b1[0, aligned(b * self.rb, self.rb)]
            self.b2[...] = (self.b2[...].astype(F32) + own.astype(F32)).astype(BF16)
            start_all(self.rs_copies())

        def ag(self):
            wait_all(self.rs_copies())
            total = self.b2[aligned(a * self.share, self.share)].astype(F32)
            for s in range(lines - 1):
                total = total + self.b3[s].astype(F32)
            own = aligned(self.out + core * self.rc + b * self.rb + a * self.share, self.share)
            sums_ref[own] = total.astype(BF16)
            start_all(self.ag_copies())

        def x(self):
            wait_all(self.ag_copies())
            start_all(self.x_copies())

        def c(self):
            wait_all(self.x_copies())
            start_all(self.c_copies())

        def done(self):
            wait_all(self.c_copies())

    rows_f = 4 * sum(chunks_f)
    rows_out = width // shards
    feeds = []
    begin = 0
    for index, rows in enumerate(chunks_f):
        feeds.append(Feed(begin, rows, rows_f, bufs_f[3 * index : 3 * index + 3]))
        begin += rows
    lates = {}
    for index, names in enumerate(sets):
        late = Late(rows_f + index * rows_l, rows_l, names, bufs_l[5 * index : 5 * index + 5])
        for name in names:
            lates[name] = late

    def late_step(name, step):
        late = lates[name]
        if step not in late.begun:
            late.begun.add(step)
            getattr(late, step)()

    values = x_ref[...].astype(F32)
    center = values - jnp.mean(values, axis=1, keepdims=True)
    inverse = lax.rsqrt(jnp.mean(center * center, axis=1, keepdims=True) + epsilon)
    unit = center * inverse

    def gradient(name):
        cols = vectors_ref[0:8].T
        gain_col, bias_col = cols[:, 0:1], cols[:, 1:2]
        if name == "q":
            m_q[...] = dot_tn(unit.astype(BF16), dq_ref[...])
            cs_q[...] = jnp.broadcast_to(jnp.sum(dq_ref[...].astype(F32), axis=0, keepdims=True), cs_q.shape)
            return gain_col * m_q[...] + bias_col * cs_q[0:1]
        if name == "p":
            total = jnp.zeros((width, width), F32)
            for index, (begin, size) in enumerate(pos_parts):
                if index:
                    start_all(pos_copies(begin, size))
                wait_all(pos_copies(begin, size))
                total = total + dot_nn(dpk_buf[:, 0:size], table_buf[0:size])
            return total.T
        m, cs = (mt_k, cs_k) if name == "k" else (mt_v, cs_v)
        return gain_col * m[...] + bias_col * fold_rows(cs[:, 0:1])

    mt_k[...] = jnp.zeros_like(mt_k)
    mt_v[...] = jnp.zeros_like(mt_v)
    cs_k[...] = jnp.zeros_like(cs_k)
    cs_v[...] = jnp.zeros_like(cs_v)
    pl.semaphore_wait(barrier, len(peers))
    wait_all(feed_copies)
    feeds[-1].y()
    weights_copy.wait()

    i_x0, i_x1, i_x2 = take(lines), take(lines), take(lines)

    def copy_x0(j):
        return remote(dxp.at[j, 1 - core], bx0.at[j], i_x0 + j, core_peer)

    def copy_x1(j):
        return remote(bx0.at[j, 1 - b], bx1.at[j], i_x1 + j, b_peer)

    def copy_x2(mask):
        return remote(bx1.at[order.index(mask)], bx2.at[mask - 1], i_x2 + mask, line_at(mask & -mask))

    def after_x0(j):
        copy_x0(j).wait()
        bx0[j] = (bx0[j].astype(F32) + dxp[j, core].astype(F32)).astype(BF16)
        copy_x1(j).start()

    def after_x1(j):
        mask = order[j]
        copy_x1(j).wait()
        total = bx1[j].astype(F32) + bx0[j, b].astype(F32)
        for bit in range(bits):
            if mask and 1 << bit >= (mask & -mask):
                break
            source = mask | 1 << bit
            copy_x2(source).wait()
            total = total + bx2[source - 1].astype(F32)
        if mask:
            bx1[j] = total.astype(BF16)
            copy_x2(mask).start()
        return total

    last = lines - 1
    events = {}

    def plan(j, after, work, *args):
        events.setdefault((min(j, last), after), []).append((work, args))

    one, two = feeds[0], feeds[-1]
    pair = len(feeds) > 1

    def along(feed, stage):
        begin, end = ((1, bits), (bits, bits + 1), (bits + 1, 2 * bits))[stage - 1]
        for step in range(begin, end):
            if step < bits:
                feed.rs(step)
            else:
                feed.ag(2 * bits - 1 - step)

    plan(0, "first", late_step, "q", "c0")
    plan(0, "blocks", after_x0, 0)
    plan(0, "blocks", late_step, "q", "y")
    plan(0, "blocks", late_step, "p", "c0")
    plan(1, "first", late_step, "p", "y")
    plan(1, "first", two.rs, 0)
    if pair:
        plan(1, "first", one.y)
    plan(1, "all", late_step, "q", "x0")
    if lines == 4:
        plan(1, "all", after_x1, 0)
        plan(1, "all", after_x0, 1)
    else:
        for j in range(1, last):
            plan(j + 1, "first", after_x0, j)
    plan(3, "first" if last >= 3 else "all", along, two, 1)
    plan(3, "blocks" if last >= 3 else "all", late_step, "p", "x0")
    plan(3, "blocks" if last >= 3 else "all", late_step, "q", "rs")

    def happen(j, after):
        for (when, place), works in sorted(events.items()):
            if place == after:

                @pl.when(j == when)
                def _():
                    for work, args in works:
                        work(*args)

    def line_step(j, _):
        slot = lax.rem(j, 2)

        @pl.when(j < last)
        def _():
            start_all(fetch(j + 1, 1 - slot))

        wait_all(fetch(j, slot))

        def make_block(core_of, b_of):
            keys = pl.ds(pl.multiple_of((2 * b_of + core_of) * tokens, tokens), tokens)
            part = dot_nn(wk_ref[...], dk_buf[slot, :, keys]) + dot_nn(wv_ref[...], dv_buf[slot, :, keys])
            dxp[j, core_of, b_of] = part.astype(BF16)

        make_block(1 - core, 0)
        make_block(1 - core, 1)
        copy_x0(j).start()
        happen(j, "first")
        make_block(core, 0)
        make_block(core, 1)
        happen(j, "blocks")
        mt_k[...] += dot_nn(dk_buf[slot], un_buf[slot])
        mt_v[...] += dot_nn(dv_buf[slot], un_buf[slot])
        for cs, buf in ((cs_k, dk_buf), (cs_v, dv_buf)):
            total = cs[...]
            for piece in range(group // BLK):
                total = total + buf[slot, :, piece * BLK : (piece + 1) * BLK].astype(F32)
            cs[...] = total
        happen(j, "all")
        return 0

    lax.fori_loop(0, lines, line_step, 0)
    for m, cs in ((mt_k, cs_k), (mt_v, cs_v)):
        m[...] = m[...].T
        cs[...] = jnp.broadcast_to(jnp.sum(cs[...], axis=1, keepdims=True), cs.shape)

    vstages = [[core_peer], [b_peer], [line_peer(s) for s in range(1, lines)], [shard_peer(s) for s in range(1, shards)]]
    vslots = []
    place = 0
    for stage in vstages:
        vslots.append(place)
        place += len(stage)
    vbegin = take(place)

    def v_copy(stage, index):
        slot = vslots[stage] + index
        return remote(vacc.at[pl.ds(stage * 16, 16)], vbuf.at[slot], vbegin + slot, vstages[stage][index])

    def v_start(stage):
        for index in range(len(vstages[stage])):
            v_copy(stage, index).start()

    def v_finish(stage):
        total = vacc[stage * 16 : stage * 16 + 16]
        for index in range(len(vstages[stage])):
            v_copy(stage, index).wait()
            total = total + vbuf[vslots[stage] + index]
        vacc[(stage + 1) * 16 : (stage + 2) * 16] = total

    def vectors_begin():
        vacc[0:16] = vec_ref[...]
        vacc[2:4] = bias_ref[0:2]
        gain_grad = m_q[...] * wq_ref[...].astype(F32)
        gain_grad = gain_grad + mt_k[...] * wk_ref[...].astype(F32) + mt_v[...] * wv_ref[...].astype(F32)
        vacc[0:1] = fold_rows(jnp.sum(gain_grad, axis=1, keepdims=True))
        total = dot_nt(cs_q[...].astype(BF16), wq_ref[...])
        for cs, weight in ((cs_k, wk_ref), (cs_v, wv_ref)):
            row = jnp.broadcast_to(fold_rows(cs[:, 0:1]), (8, width))
            total = total + dot_nt(row.astype(BF16), weight[...])
        vacc[1:2] = total[0:1]
        v_start(0)

    if pair:
        one.rs(0)
    after_x0(last)
    late_step("k", "c0")
    if lines == 4:
        after_x0(2)
    else:
        after_x1(0)
    along(two, 2)
    late_step("p", "rs")
    late_step("v", "c0")
    late_step("k", "y")
    late_step("q", "ag")
    vectors_begin()
    late_step("v", "y")
    if pair:
        along(one, 1)
    along(two, 3)
    late_step("p", "ag")
    v_finish(0)
    v_start(1)
    late_step("k", "x0")
    if pair:
        along(one, 2)
    late_step("v", "x0")
    v_finish(1)
    v_start(2)
    two.x()
    late_step("k", "rs")
    late_step("p", "x")
    late_step("v", "rs")
    if pair:
        along(one, 3)
    late_step("k", "ag")
    late_step("q", "x")
    late_step("v", "ag")
    for j in reversed(range(1, last)) if lines == 4 else range(1, last):
        after_x1(j)
    if pair:
        one.x()
    two.c()
    late_step("k", "x")
    late_step("p", "c")
    v_finish(2)
    v_start(3)
    late_step("v", "x")
    late_step("q", "c")
    if pair:
        one.c()
    leaving = []

    def leave(rows):
        copy = pltpu.make_async_copy(sums_ref.at[rows], sums_out.at[rows], sums_sem.at[len(leaving)])
        copy.start()
        leaving.append(copy)

    def feed_leaves(feed):
        feed.done()
        for quarter in range(4):
            leave(pl.ds(quarter * feed.rb + feed.begin, feed.rows))

    feed_leaves(two)
    own = after_x1(last)
    scaled = (own.T + dot_nt(dq_ref[...], wq_ref[...])) * vectors_ref[0:1]
    hidden_copy.wait()
    grad_ref[...] = hidden_ref[...] + inverse * (
        scaled - jnp.mean(scaled, axis=1, keepdims=True) - unit * jnp.mean(scaled * unit, axis=1, keepdims=True)
    )
    late_step("k", "c")
    late_step("v", "c")
    if pair:
        feed_leaves(one)
    v_finish(3)
    vsum_ref[...] = vacc[4 * 16 : 5 * 16]
    for name in "qpkv":
        if "done" not in lates[name].begun:
            late_step(name, "done")
            leave(pl.ds(lates[name].out, rows_l))
    wait_all(leaving)


def finish(lines, shards, chunks_f, sets, rows_l, cid, mine, come, dk, dv, unit_all, dpk, table, weights, dq, x, vectors, total, vec, bias, hidden):
    tokens, width = dq.shape
    vmem = pl.BlockSpec(memory_space=pltpu.VMEM)
    hbm = pl.BlockSpec(memory_space=pl.ANY)
    bufs = []
    for rows in chunks_f:
        bufs += [
            pltpu.VMEM((shards, rows, width), BF16),
            pltpu.VMEM((shards - 1, rows, width), BF16),
            pltpu.VMEM((rows, width), BF16),
        ]
    for names in sets:
        bufs += [
            pltpu.VMEM((shards, rows_l, width), BF16),
            pltpu.VMEM((shards, rows_l // 2, width), BF16),
            pltpu.VMEM((shards - 1, rows_l // 2, width), BF16),
            pltpu.VMEM((rows_l // 4, width), BF16),
            pltpu.VMEM((lines - 1, rows_l // 4 // lines, width), BF16),
        ]
    hops = shards - 1 + 2 * (lines - 1)
    copies = len(chunks_f) * (shards + 2 + 2 * (lines.bit_length() - 1)) + len(sets) * (hops + 4) + 3 * lines + 2 + lines - 1 + shards - 1
    total_rows = 4 * sum(chunks_f) + len(sets) * rows_l
    stages = 1 + 1 + (lines - 1) + (shards - 1)
    hold = min(dpk.shape[1], 17 * BLK)
    return pl.pallas_call(
        functools.partial(finish_kernel, lines, shards, tuple(chunks_f), sets, rows_l),
        out_shape=(
            jax.ShapeDtypeStruct((tokens, width), F32),
            jax.ShapeDtypeStruct((total_rows, width), BF16),
            jax.ShapeDtypeStruct((16, width), F32),
        ),
        in_specs=[hbm] * 8 + [vmem] * 6 + [hbm],
        out_specs=(vmem, hbm, vmem),
        scratch_shapes=[
            pltpu.VMEM(mine.shape, BF16),
            pltpu.VMEM(mine.shape, BF16),
            pltpu.VMEM((total_rows, width), BF16),
            pltpu.SemaphoreType.DMA((4 * len(chunks_f) + len(sets),)),
            pltpu.VMEM((2, width, 4 * tokens), BF16),
            pltpu.VMEM((2, width, 4 * tokens), BF16),
            pltpu.VMEM((2, 4 * tokens, width), BF16),
            pltpu.SemaphoreType.DMA((2, 3)),
            pltpu.VMEM((width, hold), BF16),
            pltpu.VMEM((hold, width), BF16),
            pltpu.VMEM((4, width, width), BF16),
            pltpu.VMEM((tokens, width), F32),
            pltpu.SemaphoreType.DMA((6,)),
            pltpu.VMEM((width, width), F32),
            pltpu.VMEM((width, width), F32),
            pltpu.VMEM((width, width), F32),
            pltpu.VMEM((8, width), F32),
            pltpu.VMEM((width, BLK), F32),
            pltpu.VMEM((width, BLK), F32),
            pltpu.VMEM((lines, 2, 2, width, tokens), BF16),
            pltpu.VMEM((lines, 2, width, tokens), BF16),
            pltpu.VMEM((lines, width, tokens), BF16),
            pltpu.VMEM((lines - 1, width, tokens), BF16),
            pltpu.VMEM((stages, 16, width), F32),
            pltpu.VMEM((5 * 16, width), F32),
        ]
        + bufs
        + [pltpu.SemaphoreType.DMA((copies,)), pltpu.SemaphoreType.DMA((copies,))],
        compiler_params=pltpu.CompilerParams(
            collective_id=cid, has_side_effects=True, vmem_limit_bytes=63 * 2**20
        ),
        cost_estimate=pl.CostEstimate(flops=10**10, bytes_accessed=30 * 2**20, transcendentals=0),
        name="finish",
    )(mine, come, dk, dv, unit_all, dpk, table, weights, dq, x, vectors, total, vec, bias, hidden)


def unpack_kernel(
    shards, rows_f, sets, rows_l, sums_ref, vsum_ref, total_ref, grad_ref, result_ref,
    grad_out, result_out, q_out, k_out, v_out, o_out, p_out, u_out, d_out, g1_out, b1_out, cb_out, pb_out, g2_out, b2_out, bd_out, bu_out,
    loss_out,
    low, wide, up, in_sem, out_sem,
):
    width = vsum_ref.shape[1]
    rows_out, rows_up = q_out.shape[0], d_out.shape[0]
    parts = u_out.shape[1] // width
    w = lax.axis_index("wsh")
    half = rows_f // 2
    step = min(rows_up, width)
    part_out, part_step = rows_out // 2, step // 2
    to = {"q": q_out, "p": p_out, "k": k_out, "v": v_out}
    pieces = []
    for index, names in enumerate(sets):
        pieces += [(rows_f + index * rows_l + m * rows_out, rows_out, to[name]) for m, name in enumerate(names)]
    ins = []
    for begin, size in [
        (h * half + begin, size)
        for begin, size in ((0, rows_up // 2), (rows_up // 2, rows_up // 2), (rows_up, part_out))
        for h in range(2)
    ] + [(begin, size) for begin, size, out in pieces]:
        rows = slice(begin, begin + size)
        ins.append(pltpu.make_async_copy(sums_ref.at[rows], low.at[rows], in_sem.at[len(ins)]))
    for copy in ins:
        copy.start()
    outs = []

    def send(src, dst):
        copy = pltpu.make_async_copy(src, dst, out_sem.at[len(outs)])
        copy.start()
        outs.append(copy)

    send(grad_ref, grad_out)
    send(result_ref, result_out)
    for h in range(2):
        ins[h].wait()
        for c in range(parts):
            begin = h * half + c * part_out
            up[h * part_out : (h + 1) * part_out, c * width : (c + 1) * width] = low[begin : begin + part_out].astype(F32)
        rows = slice(h * part_out, (h + 1) * part_out)
        send(up.at[rows], u_out.at[rows])
    for h in range(2):
        ins[2 + h].wait()
        for j in range(rows_up // step):
            begin = h * half + rows_up // 2 + j * part_step
            rows = slice(j * step + h * part_step, j * step + (h + 1) * part_step)
            wide[rows] = low[begin : begin + part_step].astype(F32)
            send(wide.at[rows], d_out.at[rows])
    for h in range(2):
        ins[4 + h].wait()
        begin = h * half + rows_up
        wide[rows_up + h * part_out : rows_up + (h + 1) * part_out] = low[begin : begin + part_out].astype(F32)
    send(wide.at[rows_up : rows_up + rows_out], o_out)
    for index, (begin, size, out) in enumerate(pieces):
        ins[6 + index].wait()
        wide[begin : begin + size] = low[begin : begin + size].astype(F32)
        send(wide.at[begin : begin + size], out)

    def share(row):
        part = vsum_ref[row : row + 1, 0:rows_out]
        for s in range(1, shards):
            part = jnp.where(w == s, vsum_ref[row : row + 1, s * rows_out : (s + 1) * rows_out], part)
        return part.reshape(rows_out)

    for row, ref in enumerate((g1_out, b1_out, cb_out, pb_out, g2_out, b2_out, bd_out)):
        ref[...] = share(row)
    per = rows_up // rows_out
    for q in range(per):
        part = None
        for s in range(shards):
            group = s * per + q
            row, place = 7 + group // shards, group % shards
            piece = vsum_ref[row : row + 1, place * rows_out : (place + 1) * rows_out]
            part = piece if part is None else jnp.where(w == s, piece, part)
        bu_out[q * rows_out : (q + 1) * rows_out] = part.reshape(rows_out)
    loss_out[0, 0] = vsum_ref[7 + parts, 0] / (total_ref[0, 0] * width)
    for copy in outs:
        copy.wait()


def unpack(shards, rows_f, sets, rows_l, hidden, sums, vsum, total, grad, result):
    tokens, width = grad.shape
    rows_out, rows_up = width // shards, hidden // shards
    vmem = pl.BlockSpec(memory_space=pltpu.VMEM)
    hbm = pl.BlockSpec(memory_space=pl.ANY)
    square = jax.ShapeDtypeStruct((rows_out, width), F32)
    vector = jax.ShapeDtypeStruct((rows_out,), F32)
    return pl.pallas_call(
        functools.partial(unpack_kernel, shards, rows_f, sets, rows_l),
        out_shape=(
            jax.ShapeDtypeStruct((tokens, width), F32), jax.ShapeDtypeStruct((tokens, width), BF16), square, square, square, square, square,
            jax.ShapeDtypeStruct((rows_out, hidden), F32), jax.ShapeDtypeStruct((rows_up, width), F32),
            vector, vector, vector, vector, vector, vector, vector, jax.ShapeDtypeStruct((rows_up,), F32),
            jax.ShapeDtypeStruct((1, 1), F32),
        ),
        in_specs=[hbm, vmem, vmem, vmem, vmem],
        out_specs=(hbm,) * 9 + (vmem,) * 8 + (pl.BlockSpec(memory_space=pltpu.SMEM),),
        scratch_shapes=[
            pltpu.VMEM(sums.shape, BF16),
            pltpu.VMEM(sums.shape, F32),
            pltpu.VMEM((rows_out, hidden), F32),
            pltpu.SemaphoreType.DMA((10,)),
            pltpu.SemaphoreType.DMA((9 + 2 * (rows_up // min(rows_up, width)),)),
        ],
        compiler_params=pltpu.CompilerParams(vmem_limit_bytes=62 * 2**20),
        cost_estimate=pl.CostEstimate(flops=10**6, bytes_accessed=12 * 2**20, transcendentals=0),
        name="unpack",
    )(sums, vsum, total, grad, result)


PARTS = 2


def start_kernel(
    lines, shards, x_ref, wk_ref, wv_ref, wp_ref, wq_ref, wo_ref, wu_ref, wd_ref,
    g1_ref, b1_ref, cb_ref, pb_ref, g2_ref, b2_ref, bd_ref, bu_ref, mask_ref, far_ref, near_ref,
    k_ref, v_ref, unit_ref, pk_ref, table_ref, qc_ref, qp_ref, weights_out, wo_out, wu_out, wd_out, vectors_ref, total_ref,
    weights_ref, x_all, k_buf, v_buf, pk_buf, t_buf, wo_buf, wu_buf, wd_buf, vec_src, vec_buf, cnt_buf, cnt_acc,
    up_send, up_recv, down_send, down_recv, b_send, b_recv, c_send, c_recv,
    y_send, y_recv, yc_send, yc_recv, d_send, d_recv, s_send, s_recv, out_sem, pos_sem, own_sem,
):
    tokens, width = x_ref.shape
    piece = tokens // PARTS
    half = width // 2
    chunks = pk_buf.shape[0] // BLK
    ctx = lax.axis_index("ctx")
    w = lax.axis_index("wsh")
    core = lax.rem(ctx, 2)
    b = lax.rem(ctx // 2, 2)
    a = ctx // 4

    def at(a_to, b_to, core_to):
        return (a_to * 2 + b_to) * 2 + core_to

    def shard_peer(s):
        return (ctx, lax.rem(w + s, shards))

    def line_peer(s):
        return (at(lax.rem(a + s, lines), b, core), w)

    core_peer = (at(a, b, 1 - core), w)
    b_peer = (at(a, 1 - b, core), w)
    peers = [core_peer, b_peer] + [line_peer(s) for s in range(1, lines)] + [shard_peer(s) for s in range(1, shards)]
    barrier = pltpu.get_barrier_semaphore()
    for peer in peers:
        pl.semaphore_signal(barrier, inc=1, device_id=peer, device_id_type=MESH)

    def remote(src, dst, send, recv, peer):
        return pltpu.make_async_remote_copy(
            src_ref=src, dst_ref=dst, send_sem=send, recv_sem=recv, device_id=peer, device_id_type=MESH
        )

    def block(slot):
        return aligned(slot * tokens, tokens)

    def unit_of(rows):
        values = rows.astype(F32)
        center = values - jnp.mean(values, axis=1, keepdims=True)
        return center * lax.rsqrt(jnp.mean(center * center, axis=1, keepdims=True) + epsilon)

    x_all[block(ctx)] = unit_of(x_ref[...]).astype(BF16)
    rows_out = wq_ref.shape[0]
    quarter = rows_out // 2
    rows_up = wd_ref.shape[0]
    weight_in = (wk_ref, wv_ref, wp_ref, wq_ref, wo_ref, wu_ref)
    weight_to = tuple(weights_ref.at[m] for m in range(4)) + (wo_buf, wu_buf)
    own_copies = [
        pltpu.make_async_copy(ref, to.at[aligned(w * rows_out, rows_out)], own_sem.at[m])
        for m, (ref, to) in enumerate(zip(weight_in[:4], weight_to))
    ]
    for copy in own_copies:
        copy.start()
    vec_src[...] = jnp.zeros_like(vec_src)
    for row, ref in enumerate((g1_ref, b1_ref, cb_ref, pb_ref, g2_ref, b2_ref, bd_ref)):
        vec_src[row : row + 1] = ref[...].astype(F32).reshape(1, rows_out)
    bias_rows = rows_up // rows_out
    for q in range(bias_rows):
        vec_src[7 + q : 8 + q] = bu_ref[q * rows_out : (q + 1) * rows_out].astype(F32).reshape(1, rows_out)
    cnt_acc[0:8] = jnp.broadcast_to(jnp.sum(mask_ref[...].astype(F32), axis=1, keepdims=True), (8, BLK))
    pl.semaphore_wait(barrier, len(peers))

    def x_copy(slot, h, send, recv, peer):
        rows = aligned(slot * tokens + h * piece, piece)
        return remote(x_all.at[rows], x_all.at[rows], send, recv, peer)

    def up_copy(p, h):
        peer = (at(jnp.minimum(a + 1, lines - 1), b, core), w)
        return x_copy(at(p, b, core), h, up_send.at[p, h], up_recv.at[p, h], peer)

    def down_copy(p, h):
        peer = (at(jnp.maximum(a - 1, 0), b, core), w)
        return x_copy(at(p, b, core), h, down_send.at[p, h], down_recv.at[p, h], peer)

    def b_copy(p, h, b_from):
        return x_copy(at(p, b_from, core), h, b_send.at[p, h], b_recv.at[p, h], b_peer)

    def c_copy(p, far, b_from, core_from):
        rows = block(at(p, b_from, core_from))
        return remote(x_all.at[rows], x_all.at[rows], c_send.at[far, p], c_recv.at[far, p], core_peer)

    def weight_copy(m, s):
        rows = aligned(w * rows_out + core * quarter, quarter)
        src = weight_in[m].at[aligned(core * quarter, quarter)]
        return remote(src, weight_to[m].at[rows], y_send.at[m, s - 1], y_recv.at[m, s - 1], shard_peer(s))

    def weight_pass(m, s):
        rows = aligned(lax.rem(w + shards - s, shards) * rows_out + core * quarter, quarter)
        return remote(
            weight_to[m].at[rows], weight_to[m].at[rows], yc_send.at[m, s - 1], yc_recv.at[m, s - 1], core_peer
        )

    low = lax.rem(a, 2)
    quarter_in, quarter_to = (wd_ref,), (wd_buf,)
    pair_peer = (at(a + 1 - 2 * low, b, core), w)

    def quarter_rows(m, s, low_of):
        size = quarter_in[m].shape[0]
        owner = lax.rem(w + shards - s, shards)
        return aligned(owner * size + (low_of * 2 + core) * (size // 4), size // 4)

    def quarter_copy(m, s):
        size = quarter_in[m].shape[0]
        src = quarter_in[m].at[aligned((low * 2 + core) * (size // 4), size // 4)]
        dst = quarter_to[m].at[quarter_rows(m, 0, low)]
        return remote(src, dst, d_send.at[m, 0, s - 1], d_recv.at[m, 0, s - 1], shard_peer(s))

    def quarter_pass(m, kind, s):
        rows = quarter_rows(m, s, 1 - low if kind == 3 else low)
        peer = pair_peer if kind == 1 else core_peer
        ref = quarter_to[m].at[rows]
        return remote(ref, ref, d_send.at[m, kind, s - 1], d_recv.at[m, kind, s - 1], peer)

    def quarter_on(m):
        for s in range(1, shards):
            quarter_copy(m, s).wait()
            quarter_pass(m, 1, s).start()
            quarter_pass(m, 2, s).start()

    def vec_copy(s):
        return remote(vec_src, vec_buf.at[s - 1], s_send.at[s - 1], s_recv.at[s - 1], shard_peer(s))

    stages = [[shard_peer(s) for s in range(1, shards)], [core_peer], [b_peer], [line_peer(s) for s in range(1, lines)]]
    slots = []
    place = 0
    for stage in stages:
        slots.append(place)
        place += len(stage)

    def cnt_copy(stage, index):
        slot = slots[stage] + index
        sem = shards - 1 + slot
        return remote(cnt_acc.at[pl.ds(stage * 8, 8)], cnt_buf.at[slot], s_send.at[sem], s_recv.at[sem], stages[stage][index])

    def cnt_start(stage):
        for index in range(len(stages[stage])):
            cnt_copy(stage, index).start()

    def cnt_finish(stage):
        total = cnt_acc[stage * 8 : stage * 8 + 8]
        for index in range(len(stages[stage])):
            cnt_copy(stage, index).wait()
            total = total + cnt_buf[slots[stage] + index]
        cnt_acc[(stage + 1) * 8 : (stage + 2) * 8] = total

    for s in range(1, shards):
        vec_copy(s).start()
    cnt_start(0)
    for h in range(PARTS):

        @pl.when(a + 1 < lines)
        def _():
            up_copy(a, h).start()

        @pl.when(a >= 1)
        def _():
            down_copy(a, h).start()

        b_copy(a, h, b).start()
    c_copy(a, 0, b, core).start()
    for kind, m in ((0, 0), (0, 1), (1, 0), (0, 2), (0, 3), (0, 5), (0, 4)):
        for s in range(1, shards):
            (quarter_copy if kind else weight_copy)(m, s).start()


    def table_step(d, _):
        sin_far, cos_far = far_ref[0, pl.ds(d, 1)], far_ref[1, pl.ds(d, 1)]
        sin_near, cos_near = near_ref[0], near_ref[1]
        rows = aligned(d * BLK, BLK)
        t_buf[rows, :half] = (sin_far * cos_near - cos_far * sin_near).astype(BF16)
        t_buf[rows, half:] = (cos_far * cos_near + sin_far * sin_near).astype(BF16)
        return 0

    lax.fori_loop(0, chunks, table_step, 0)
    table_out = pltpu.make_async_copy(t_buf, table_ref, pos_sem.at[0])
    table_out.start()
    lane_to = lax.broadcasted_iota(jnp.int32, (rows_out, width), 1)
    lane_from = lax.broadcasted_iota(jnp.int32, (rows_out, width), 0)
    row_at = lax.broadcasted_iota(jnp.int32, (16, width), 0)

    def spread(values, place):
        return dot_nn(values.astype(BF16), (lane_to == lane_from + place * rows_out).astype(BF16))

    def placed(values, owner):
        full = jnp.where(row_at < 7, spread(values, owner), 0.0)
        for q in range(bias_rows):
            group = owner * bias_rows + q
            row = jnp.broadcast_to(values[7 + q : 8 + q], values.shape)
            full = full + jnp.where(row_at == 7 + group // shards, spread(row, lax.rem(group, shards)), 0.0)
        return full

    vectors = placed(vec_src[...], w)
    for s in range(1, shards):
        vec_copy(s).wait()
        vectors = vectors + placed(vec_buf[s - 1], lax.rem(w + shards - s, shards))
    vectors_ref[...] = vectors
    cnt_finish(0)
    cnt_start(1)

    def out_copies(slot):
        rows = block(slot)
        return (
            pltpu.make_async_copy(k_buf.at[rows], k_ref.at[rows], out_sem.at[0, slot]),
            pltpu.make_async_copy(v_buf.at[rows], v_ref.at[rows], out_sem.at[1, slot]),
            pltpu.make_async_copy(x_all.at[rows], unit_ref.at[rows], out_sem.at[2, slot]),
        )

    def project(p):
        def one(q, _):
            other_b = q // 2
            other_core = lax.rem(q, 2)

            @pl.when(q == 1)
            def _():
                c_copy(p, 0, b, core).wait()

            @pl.when(q == 2)
            def _():
                for h in range(PARTS):
                    b_copy(p, h, b).wait()
                c_copy(p, 1, 1 - b, core).start()

            @pl.when(q == 3)
            def _():
                c_copy(p, 1, 1 - b, core).wait()

            slot = at(p, b + other_b - 2 * b * other_b, core + other_core - 2 * core * other_core)
            rows = block(slot)
            normed = (x_all[rows].astype(F32) * vectors_ref[0:1] + vectors_ref[1:2]).astype(BF16)
            k_buf[rows] = dot_nn(normed, weights_ref[0]).astype(BF16)
            v_buf[rows] = dot_nn(normed, weights_ref[1]).astype(BF16)
            for copy in out_copies(slot):
                copy.start()
            return 0

        lax.fori_loop(0, 4, one, 0)

    def pos_step(d, _):
        rows = aligned(d * BLK, BLK)
        pk_buf[rows] = dot_nn(t_buf[rows], weights_ref[2]).astype(BF16)
        return 0

    last = lines - 1

    def line_step(s, _):
        below, high = a - 1 - s, a + 1 + s

        for h in range(PARTS):

            @pl.when((s < lines - 1) & (below >= 0))
            def _():
                p = jnp.maximum(below, 0)
                up_copy(p, h).wait_recv()

                @pl.when(a + 1 < lines)
                def _():
                    up_copy(p, h).start()

                b_copy(p, h, b).start()
                if h == PARTS - 1:
                    c_copy(p, 0, b, core).start()

            @pl.when((s < lines - 1) & (high < lines))
            def _():
                p = jnp.minimum(high, lines - 1)
                down_copy(p, h).wait_recv()

                @pl.when(a >= 1)
                def _():
                    down_copy(p, h).start()

                b_copy(p, h, b).start()
                if h == PARTS - 1:
                    c_copy(p, 0, b, core).start()

        @pl.when(s == 0)
        def _():
            cnt_finish(1)
            cnt_start(2)

        @pl.when(s == 1)
        def _():
            for copy in own_copies:
                copy.wait()
            for m in range(2):
                for t in range(1, shards):
                    weight_copy(m, t).wait()
                    weight_pass(m, t).start()
            cnt_finish(2)
            cnt_start(3)
            for m in range(2):
                for t in range(1, shards):
                    weight_pass(m, t).wait()

        @pl.when(s == min(2, last))
        def _():
            quarter_on(0)
            for t in range(1, shards):
                weight_copy(2, t).wait()
                weight_pass(2, t).start()

        @pl.when((s >= 1) & (a - s + 1 >= 0))
        def _():
            project(jnp.maximum(a - s + 1, 0))

        @pl.when((s >= 2) & (a + s - 1 < lines))
        def _():
            project(jnp.minimum(a + s - 1, lines - 1))

        @pl.when(s == min(2, last))
        def _():
            for t in range(1, shards):
                weight_pass(2, t).wait()
            lax.fori_loop(0, chunks // 2, pos_step, 0)

        @pl.when(s == last)
        def _():
            for t in range(1, shards):
                weight_copy(3, t).wait()
                weight_pass(3, t).start()
            lax.fori_loop(chunks // 2, chunks, pos_step, 0)
            for t in range(1, shards):
                weight_pass(3, t).wait()
            normed = (x_all[block(ctx)].astype(F32) * vectors_ref[0:1] + vectors_ref[1:2]).astype(BF16)
            queries = dot_nn(normed, weights_ref[3]).astype(BF16).astype(F32)
            qc_ref[...] = ((queries + vectors_ref[2:3]) * 0.125).astype(BF16)
            qp_ref[...] = ((queries + vectors_ref[3:4]) * 0.125).astype(BF16)

        return 0

    lax.fori_loop(0, lines + 1, line_step, 0)
    for m in (5, 4):
        for s in range(1, shards):
            weight_copy(m, s).wait()
            weight_pass(m, s).start()
    pos_out = pltpu.make_async_copy(pk_buf, pk_ref, pos_sem.at[1])
    pos_out.start()
    weights_leave = pltpu.make_async_copy(weights_ref, weights_out, pos_sem.at[2])
    weights_leave.start()
    cnt_finish(3)
    total_ref[...] = cnt_acc[4 * 8 : 5 * 8]

    def sends_done(p, _):
        for h in range(PARTS):

            @pl.when((a + 1 < lines) & (p <= a))
            def _():
                up_copy(p, h).wait_send()

            @pl.when((a >= 1) & (p >= a))
            def _():
                down_copy(p, h).wait_send()

        return 0

    lax.fori_loop(0, lines, sends_done, 0)

    def outs_done(slot, _):
        for copy in out_copies(slot):
            copy.wait()
        return 0

    lax.fori_loop(0, 4 * lines, outs_done, 0)
    for s in range(1, shards):
        weight_pass(4, s).wait()
        weight_pass(5, s).wait()
        quarter_pass(0, 1, s).wait()
        quarter_pass(0, 3, s).start()
    for s in range(1, shards):
        quarter_pass(0, 2, s).wait()
        quarter_pass(0, 3, s).wait()
    far_copies = []
    for m, (buf, to) in enumerate(((wo_buf, wo_out), (wu_buf, wu_out), (wd_buf, wd_out))):
        size = buf.shape[0] // shards
        for s in range(1, shards):
            rows = aligned(lax.rem(w + s, shards) * size, size)
            far_copies.append(pltpu.make_async_copy(buf.at[rows], to.at[rows], own_sem.at[4 + m * (shards - 1) + s - 1]))
    for copy in far_copies:
        copy.start()
    for copy in far_copies:
        copy.wait()
    table_out.wait()
    pos_out.wait()
    weights_leave.wait()


def start(lines, shards, cid, limit, x, weights, vectors, mask, far, near):
    tokens, width = x.shape
    hidden = weights[5].shape[1]
    rows_out = weights[0].shape[0]
    members = 4 * lines
    keys = members * tokens
    span = limit * BLK
    vmem = pl.BlockSpec(memory_space=pltpu.VMEM)
    hbm = pl.BlockSpec(memory_space=pl.ANY)
    small = 2 * (shards - 1) + 1 + 1 + lines - 1
    dma = pltpu.SemaphoreType.DMA
    other = shards - 1
    return pl.pallas_call(
        functools.partial(start_kernel, lines, shards),
        out_shape=(
            jax.ShapeDtypeStruct((keys, width), BF16),
            jax.ShapeDtypeStruct((keys, width), BF16),
            jax.ShapeDtypeStruct((keys, width), BF16),
            jax.ShapeDtypeStruct((span, width), BF16),
            jax.ShapeDtypeStruct((span, width), BF16),
            jax.ShapeDtypeStruct((tokens, width), BF16),
            jax.ShapeDtypeStruct((tokens, width), BF16),
            jax.ShapeDtypeStruct((4, width, width), BF16),
            jax.ShapeDtypeStruct((width, width), BF16),
            jax.ShapeDtypeStruct((width, hidden), BF16),
            jax.ShapeDtypeStruct((hidden, width), BF16),
            jax.ShapeDtypeStruct((16, width), F32),
            jax.ShapeDtypeStruct((8, BLK), F32),
        ),
        in_specs=[vmem] + [hbm] * 7 + [vmem] * 11,
        out_specs=(hbm,) * 5 + (vmem,) * 2 + (hbm,) * 4 + (vmem,) * 2,
        scratch_shapes=[
            pltpu.VMEM((4, width, width), BF16),
            pltpu.VMEM((keys, width), BF16),
            pltpu.VMEM((keys, width), BF16),
            pltpu.VMEM((keys, width), BF16),
            pltpu.VMEM((span, width), BF16),
            pltpu.VMEM((span, width), BF16),
            pltpu.VMEM((width, width), BF16),
            pltpu.VMEM((width, hidden), BF16),
            pltpu.VMEM((hidden, width), BF16),
            pltpu.VMEM((16, rows_out), F32),
            pltpu.VMEM((other, 16, rows_out), F32),
            pltpu.VMEM((lines + shards, 8, BLK), F32),
            pltpu.VMEM((5 * 8, BLK), F32),
        ]
        + [dma((lines, PARTS))] * 6
        + [dma((2, lines))] * 2
        + [dma((6, other))] * 4
        + [dma((1, 4, other))] * 2
        + [dma((small,))] * 2
        + [dma((3, members)), dma((3,)), dma((4 + 3 * other,))],
        compiler_params=pltpu.CompilerParams(collective_id=cid, has_side_effects=True, vmem_limit_bytes=60 * 2**20),
        cost_estimate=pl.CostEstimate(flops=6 * 10**9, bytes_accessed=20 * 2**20, transcendentals=0),
        name="start",
    )(x, *weights, *vectors, mask, far, near)


GELU_SCALE = math.sqrt(2.0 / math.pi)


def middle_kernel(
    shards, rows_f, mask_ref, x_ref, mixed_ref, teacher_ref, out_grad_ref, vectors_ref, total_ref,
    wo_own, wu_own, wd_own, wo_ref, wu_ref, wd_ref,
    out_ref, hidden_ref, gm_ref, mine_ref, theirs_ref, vec_ref,
    wo, wu, wd, slope, act, gf_ref, landed, sem, send_sem, recv_sem,
):
    tokens, width = x_ref.shape
    parts = wu.shape[1] // width
    ctx = lax.axis_index("ctx")
    core = lax.rem(ctx, 2)
    core_peer = (ctx + 1 - 2 * core, lax.axis_index("wsh"))
    barrier = pltpu.get_barrier_semaphore()
    pl.semaphore_signal(barrier, inc=1, device_id=core_peer, device_id_type=MESH)
    w = lax.axis_index("wsh")
    copies = []
    for k, (own, gathered, full) in enumerate(((wo_own, wo_ref, wo), (wu_own, wu_ref, wu), (wd_own, wd_ref, wd))):
        size = own.shape[0]
        part = [pltpu.make_async_copy(own, full.at[aligned(w * size, size)], sem.at[k, 0])]
        for s in range(1, shards):
            rows = aligned(lax.rem(w + s, shards) * size, size)
            part.append(pltpu.make_async_copy(gathered.at[rows], full.at[rows], sem.at[k, s]))
        for copy in part:
            copy.start()
        copies.append(part)

    def arrive(k):
        for copy in copies[k]:
            copy.wait()

    b = lax.rem(ctx // 2, 2)
    half, quarter = rows_f // 2, rows_f // 4

    rows_up, rows_out = wd_own.shape[0], wo_own.shape[0]
    step = min(rows_up, width)
    part_out, part_step = rows_out // 2, step // 2
    gives = []

    def give(begin, size, owner=None):
        owners = slice(None) if owner is None else owner
        rows = aligned((1 - core) * half + begin, size)
        index = len(gives)
        copy = pltpu.make_async_remote_copy(
            src_ref=gf_ref.at[owners, rows], dst_ref=landed.at[owners, pl.ds(begin, size)],
            send_sem=send_sem.at[index], recv_sem=recv_sem.at[index], device_id=core_peer, device_id_type=MESH,
        )
        copy.start()
        gives.append(copy)

    gain, offset, down_bias = vectors_ref[4:5], vectors_ref[5:6], vectors_ref[6:7]
    mixed = mixed_ref[...].astype(BF16)
    arrive(0)
    hidden = x_ref[...].astype(F32) + dot_nn(mixed, wo[...])
    center = hidden - jnp.mean(hidden, axis=1, keepdims=True)
    inverse = lax.rsqrt(jnp.mean(center * center, axis=1, keepdims=True) + epsilon)
    unit = center * inverse
    normed = (unit * gain + offset).astype(BF16)
    result = hidden + down_bias
    arrive(1)
    for c in range(parts):
        cols = slice(c * width, (c + 1) * width)
        v = dot_nn(normed, wu[:, cols]) + vectors_ref[7 + c : 8 + c]
        square = v * v
        t = jnp.tanh(GELU_SCALE * (v + 0.044715 * (square * v)))
        act[:, cols] = (0.5 * v * (1.0 + t)).astype(BF16)
        slope[:, cols] = 0.5 * (1.0 + t) + 0.5 * v * (1.0 - t * t) * (GELU_SCALE * (1.0 + 3.0 * 0.044715 * square))
        if c == 0:
            arrive(2)
        result = result + dot_nn(act[:, cols], wd[cols])
    out_ref[...] = result.astype(BF16)
    mask = jnp.broadcast_to(mask_ref[...].astype(F32), (8, tokens)).T[:, 0:1]
    error = result - teacher_ref[...].astype(F32)
    masked = mask * error
    count = jnp.sum(total_ref[0:1, 0:1], axis=1, keepdims=True)
    grad_result = out_grad_ref[...].astype(F32) + (2.0 / (count * width)) * masked
    branch = grad_result.astype(BF16)
    vec_ref[...] = jnp.zeros_like(vec_ref)
    vec_ref[7 + parts : 8 + parts] = jnp.broadcast_to(
        jnp.sum(jnp.sum(masked * error, axis=1, keepdims=True), axis=0, keepdims=True), (1, width)
    )
    vec_ref[6:7] = jnp.sum(branch.astype(F32), axis=0, keepdims=True)
    used = rows_up + part_out
    if used < half:
        for h in range(2):
            gf_ref[:, h * half + used : (h + 1) * half] = jnp.zeros((shards, half - used, width), BF16)
    pl.semaphore_wait(barrier, 1)
    grad_normed = jnp.zeros((tokens, width), F32)
    for c in range(parts):
        cols = slice(c * width, (c + 1) * width)
        grad_pre = (dot_nt(branch, wd[cols]) * slope[:, cols]).astype(BF16)
        vec_ref[7 + c : 8 + c] = jnp.sum(grad_pre.astype(F32), axis=0, keepdims=True)
        grad_normed = grad_normed + dot_nt(grad_pre, wu[:, cols])
        up = dot_tn(normed, grad_pre).astype(BF16)
        down = dot_tn(act[:, cols], branch).astype(BF16)
        for s in range(shards):
            for h in range(2):
                begin = s * rows_out + h * part_out
                gf_ref[s, h * half + c * part_out : h * half + (c + 1) * part_out] = up[begin : begin + part_out]
        give(c * part_out, part_out)
        for begin in range(0, width, step):
            row = c * width + begin
            owner, place = row // rows_up, rows_up // 2 + row % rows_up // 2
            for h in range(2):
                piece = down[begin + h * part_step : begin + (h + 1) * part_step]
                gf_ref[owner, h * half + place : h * half + place + part_step] = piece
            give(place, part_step, owner)
    vec_ref[4:5] = jnp.sum(grad_normed * unit, axis=0, keepdims=True)
    vec_ref[5:6] = jnp.sum(grad_normed, axis=0, keepdims=True)
    scaled = grad_normed * gain
    grad_hidden = grad_result + inverse * (
        scaled - jnp.mean(scaled, axis=1, keepdims=True) - unit * jnp.mean(scaled * unit, axis=1, keepdims=True)
    )
    hidden_ref[...] = grad_hidden
    attn = grad_hidden.astype(BF16)
    gm_ref[...] = dot_nt(attn, wo[...]).astype(BF16)
    outer = dot_tn(mixed, attn).astype(BF16)
    for s in range(shards):
        for h in range(2):
            begin = s * rows_out + h * part_out
            gf_ref[s, h * half + rows_up : h * half + used] = outer[begin : begin + part_out]
    give(rows_up, half - rows_up)
    for copy in gives:
        copy.wait()
    for ref, place in ((theirs_ref, 1 - b), (mine_ref, b)):
        own = gf_ref[:, aligned(core * half + place * quarter, quarter)].astype(F32)
        ref[...] = (own + landed[:, aligned(place * quarter, quarter)].astype(F32)).astype(BF16)


def middle(shards, rows_f, cid, mask, x, mixed, teacher, out_grad, vectors, total, own, gathered):
    tokens, width = x.shape
    hidden = own[1].shape[1]
    pieces = hidden // width + hidden // min(own[2].shape[0], width) + 1
    vmem = pl.BlockSpec(memory_space=pltpu.VMEM)
    hbm = pl.BlockSpec(memory_space=pl.ANY)
    return pl.pallas_call(
        functools.partial(middle_kernel, shards, rows_f),
        out_shape=(
            jax.ShapeDtypeStruct((tokens, width), BF16),
            jax.ShapeDtypeStruct((tokens, width), F32),
            jax.ShapeDtypeStruct((tokens, width), BF16),
            jax.ShapeDtypeStruct((shards, rows_f // 4, width), BF16),
            jax.ShapeDtypeStruct((shards, rows_f // 4, width), BF16),
            jax.ShapeDtypeStruct((16, width), F32),
        ),
        in_specs=[vmem] * 7 + [hbm] * 6,
        out_specs=(vmem,) * 6,
        scratch_shapes=[
            pltpu.VMEM((width, width), BF16),
            pltpu.VMEM((width, hidden), BF16),
            pltpu.VMEM((hidden, width), BF16),
            pltpu.VMEM((tokens, hidden), F32),
            pltpu.VMEM((tokens, hidden), BF16),
            pltpu.VMEM((shards, rows_f, width), BF16),
            pltpu.VMEM((shards, rows_f // 2, width), BF16),
            pltpu.SemaphoreType.DMA((3, shards)),
            pltpu.SemaphoreType.DMA((pieces,)),
            pltpu.SemaphoreType.DMA((pieces,)),
        ],
        compiler_params=pltpu.CompilerParams(collective_id=cid, has_side_effects=True, vmem_limit_bytes=56 * 2**20),
        cost_estimate=pl.CostEstimate(flops=4 * 10**9, bytes_accessed=20 * 2**20, transcendentals=10**6),
        name="middle",
    )(mask, x, mixed, teacher, out_grad, vectors, total, *own, *gathered)


def body(
    inputs, block_perm, seq_lengths, loss_mask, teacher, out_grad, gain_one, bias_one, w_query, w_key, w_value,
    w_output, w_pos, content_bias, position_bias, gain_two, bias_two, w_up, bias_up, w_down, bias_down,
):
    width = inputs.shape[2]
    shards = lax.axis_size("wsh")
    members = lax.axis_size("ctx")
    lines = members // 4
    hidden = bias_up.shape[0] * shards
    blocks = block_perm.shape[1]
    limit = blocks // 2 + 1
    rows_up, rows_out = hidden // shards, width // shards

    frequency = np.exp(np.arange(width // 2) * (-2.0 * math.log(10000.0) / width))
    far_angle = (np.arange(-(-limit // 8) * 8) * BLK + (BLK - 1))[:, None] * frequency[None]
    near_angle = np.arange(BLK)[:, None] * frequency[None]
    far = jnp.asarray(np.stack([np.sin(far_angle), np.cos(far_angle)]), F32)
    near = jnp.asarray(np.stack([np.sin(near_angle), np.cos(near_angle)]), F32)

    keys, values, unit_all, pos_keys, table, qc, qp, weights, wo, wu, wd, vectors, total = start(
        lines, shards, 0, limit, inputs[0], (w_key, w_value, w_pos, w_query, w_output, w_up, w_down),
        (gain_one, bias_one, content_bias, position_bias, gain_two, bias_two, bias_down, bias_up), loss_mask, far, near,
    )
    mixed, linv, probs = attn_fwd(block_perm, seq_lengths, qc, qp, keys, values, pos_keys, blocks, limit)

    step = 16 * lines
    pieces = -(-(2 * rows_up + rows_out) // (4 * step))
    split = min(2, pieces)
    chunks_f = tuple((pieces * (i + 1) // split - pieces * i // split) * step for i in range(split))
    rows_f = 4 * step * pieces
    if rows_out % (32 * lines):
        sets, rows_l = (("q", "p"), ("k", "v")), -(-2 * rows_out // (32 * lines)) * 32 * lines
    else:
        sets, rows_l = (("q",), ("p",), ("k",), ("v",)), rows_out
    output, grad_hidden, grad_mixed, mine, theirs, vec = middle(
        shards, rows_f, 2, loss_mask, inputs[0], mixed, teacher[0], out_grad[0], vectors, total,
        (w_output, w_up, w_down), (wo, wu, wd),
    )
    come = lax.ppermute(theirs, "ctx", [(i, i ^ 2) for i in range(members)])
    grad_query, bias_grads, dk_t, dv_t, dpk_t = attn_bwd(
        block_perm, seq_lengths, qc, qp, keys, values, pos_keys, probs, linv, grad_mixed, mixed, blocks, limit
    )
    grad_input, sums, vsum = finish(
        lines, shards, chunks_f, sets, rows_l, 1, mine, come, dk_t, dv_t, unit_all, dpk_t, table, weights, grad_query,
        inputs[0], vectors, total, vec, bias_grads, grad_hidden,
    )
    (
        grad_input, output, g_query, g_key, g_value, g_output, g_pos, g_up, g_down,
        v_g1, v_b1, v_cb, v_pb, v_g2, v_b2, v_bd, v_bu, loss,
    ) = unpack(shards, rows_f, sets, rows_l, hidden, sums, vsum, total, grad_input, output)
    return (
        output[None], loss.reshape(()), grad_input[None], v_g1, v_b1, g_query, g_key, g_value, g_output, g_pos,
        v_cb, v_pb, v_g2, v_b2, g_up, v_bu, g_down, v_bd,
    )


def solution(mesh):
    rows = P("wsh", "ctx", None)
    vector = P("wsh")
    matrix = P("wsh", None)
    placed = (
        rows, matrix, matrix, P("wsh", "ctx"), rows, rows, vector, vector, matrix, matrix, matrix, matrix, matrix,
        vector, vector, vector, vector, matrix, vector, matrix, vector,
    )
    out = (
        rows, P(), rows, vector, vector, matrix, matrix, matrix, matrix, matrix, vector, vector, vector, vector,
        matrix, vector, matrix, vector,
    )
    return jax.shard_map(body, mesh=mesh, in_specs=placed, out_specs=out, check_vma=False)
```
